256 devices in a mesh: depth: 4 (over x), row: 16 (over z, core), col: 4 (over y).
Axes of the slice: x: 4, y: 4, z: 8, core: 2. Of those that a mesh axis runs over, the one named last changes fastest.
Arguments:
- tokens: float32 [8192, 8192], P(('depth', 'col'), 'row'), may hold values from -16 to 16
- w_query: float32 [8192, 4096], P('row', 'col'), may hold values from -0.0625 to 0.0625
- w_key: float32 [8192, 512], P('row', 'col'), may hold values from -0.0625 to 0.0625
- w_value: float32 [8192, 512], P('row', 'col'), may hold values from -0.0625 to 0.0625
- w_out: float32 [4096, 8192], P('col', 'row'), may hold values from -0.09375 to 0.09375
Outputs:
- mixed: float32 [8192, 8192], P(('depth', 'col'), 'row')
The draws below stay inside these ranges and needn't reach their ends.
All inputs are finite; a program needn't handle non-finite values.
Results may differ from the reference program's by a relative error of at most 0.0003.
Values sent between devices are 32-bit elements; how exact they have to be, the bound alone decides.
A program may use at most 64 MiB of HBM per device.

```python
import math
import jax
import jax.numpy as jnp
from jax import lax

D = 8192
QUERY_HEADS = 32
KEY_VALUE_HEADS = 4
HEAD_SIZE_DIM = 128
TOKENS_PER_SET = 2048
TOKEN_TOTAL = 8192
QUERY_WIDTH = 4096
KW = 512
N_DEPTH = 4


def draw_tokens(key, part):
    normal_part = jnp.clip(jax.random.normal(key, (TOKEN_TOTAL, D), jnp.float32), -5.0, 5.0)
    return normal_part


def steps_of(key, extent, split, low, largest):
    def one(position, blocks):
        heights = jax.random.uniform(jax.random.fold_in(jax.random.fold_in(key, 6), position), (blocks,), jnp.float32, low / len(split), largest / len(split))
        return jnp.repeat(jnp.exp(heights), extent[position] // blocks).reshape((-1,) + (1,) * (len(extent) - position - 1))

    level = one(*split[0])
    for cut in split[1:]:
        level = level * one(*cut)
    return level


def centred(rng, extent, scale, reach, cuts=(), held_as=jnp.bfloat16):
    array = jax.random.normal(rng, extent, jnp.float32) * scale
    if len(cuts) > 0:
        array = steps_of(rng, extent, cuts, -0.22, 0.18) * array
    return jnp.clip(array, min=-reach, max=reach).astype(held_as)


def setup_inputs(seed: int = 0) -> dict:
    arg_keys = jax.random.split(jax.random.key(seed), 6)
    return {
        "tokens": draw_tokens(jax.random.fold_in(arg_keys[5], 71), 0),
        "w_query": centred(arg_keys[1], (D, QUERY_WIDTH), D ** -0.5, 0.0625, ((0, 16), (1, 4)), jnp.float32),
        "w_key": centred(arg_keys[2], (D, KW), D ** -0.5, 0.0625, ((0, 16), (1, 4)), jnp.float32),
        "w_value": centred(arg_keys[3], (D, KW), D ** -0.5, 0.0625, ((0, 16), (1, 4)), jnp.float32),
        "w_out": centred(arg_keys[4], (QUERY_WIDTH, D), QUERY_WIDTH ** -0.5, 0.09375, ((0, 4), (1, 16)), jnp.float32),
    }


def reference(tokens, w_query, w_key, w_value, w_out):
    highest = lax.Precision.HIGHEST
    query_rows = jnp.dot(tokens, w_query, preferred_element_type=jnp.float32, precision=highest)
    key_rows = jnp.dot(tokens, w_key, preferred_element_type=jnp.float32, precision=highest)
    value_rows = jnp.dot(tokens, w_value, preferred_element_type=jnp.float32, precision=highest)
    queries_per_group = QUERY_HEADS // KEY_VALUE_HEADS
    score_scale = 1.0 / math.sqrt(HEAD_SIZE_DIM)
    query_head_rows = query_rows.reshape(N_DEPTH, TOKENS_PER_SET, KEY_VALUE_HEADS, queries_per_group, HEAD_SIZE_DIM).transpose(0, 2, 1, 3, 4).reshape(N_DEPTH * KEY_VALUE_HEADS, TOKENS_PER_SET, queries_per_group, HEAD_SIZE_DIM)
    key_head_rows = key_rows.reshape(N_DEPTH, TOKENS_PER_SET, KEY_VALUE_HEADS, HEAD_SIZE_DIM).transpose(0, 2, 1, 3).reshape(N_DEPTH * KEY_VALUE_HEADS, TOKENS_PER_SET, HEAD_SIZE_DIM)
    value_head_rows = value_rows.reshape(N_DEPTH, TOKENS_PER_SET, KEY_VALUE_HEADS, HEAD_SIZE_DIM).transpose(0, 2, 1, 3).reshape(N_DEPTH * KEY_VALUE_HEADS, TOKENS_PER_SET, HEAD_SIZE_DIM)

    def one_group(triple):
        head_query, head_key, head_value = triple
        scores = jnp.einsum('tgd,sd->gts', head_query, head_key, precision=highest) * score_scale
        weights = jax.nn.softmax(scores, axis=-1)
        return jnp.einsum('gts,sd->tgd', weights, head_value, precision=highest)
    attention_output = lax.map(one_group, (query_head_rows, key_head_rows, value_head_rows))
    attention_output = attention_output.reshape(N_DEPTH, KEY_VALUE_HEADS, TOKENS_PER_SET, queries_per_group, HEAD_SIZE_DIM).transpose(0, 2, 1, 3, 4).reshape(TOKEN_TOTAL, QUERY_WIDTH)
    return jnp.dot(attention_output, w_out, preferred_element_type=jnp.float32, precision=highest)
```

```python
import math

import jax
import numpy as np
import jax.numpy as jnp
from jax import lax
from jax.sharding import PartitionSpec as P

QUERY_HEADS = 32
KEY_VALUE_HEADS = 4
HEAD_SIZE_DIM = 128


def start_state(query_rows, kv_width):
    count_of_heads = kv_width // HEAD_SIZE_DIM
    queries_per_group = QUERY_HEADS // KEY_VALUE_HEADS
    count_of_rows = query_rows.shape[0]
    running_max = jnp.full((count_of_heads, queries_per_group, count_of_rows), -1e30, jnp.float32)
    running_sum = jnp.zeros((count_of_heads, queries_per_group, count_of_rows), jnp.float32)
    weighted = jnp.zeros(
        (count_of_heads, queries_per_group, count_of_rows, HEAD_SIZE_DIM), jnp.float32
    )
    return (running_max, running_sum, weighted)


def fold_keys(query_rows, state_now, block_pair):
    highest = lax.Precision.HIGH
    running_max, running_sum, weighted = state_now
    key_block, value_block = block_pair
    count_of_heads = key_block.shape[1] // HEAD_SIZE_DIM
    count_of_rows = query_rows.shape[0]
    query_head_rows = query_rows.reshape(
        count_of_rows, count_of_heads, QUERY_HEADS // KEY_VALUE_HEADS, HEAD_SIZE_DIM
    )
    key_head_rows = key_block.reshape(-1, count_of_heads, HEAD_SIZE_DIM)
    value_head_rows = value_block.reshape(-1, count_of_heads, HEAD_SIZE_DIM)
    scores = jnp.einsum("rkgd,nkd->kgrn", query_head_rows, key_head_rows, precision=highest) * (
        1.0 / math.sqrt(HEAD_SIZE_DIM)
    )
    newest = jnp.maximum(running_max, jnp.max(scores, axis=-1))
    weights = jnp.exp(scores - newest[..., None])
    running_sum = jnp.sum(weights, axis=-1)
    weighted = jnp.einsum("kgrn,nkd->kgrd", weights, value_head_rows, precision=highest)
    return (newest, running_sum, weighted)


def finish(state_now):
    running_max, running_sum, weighted = state_now
    attention_output = weighted / running_sum[..., None]
    count_of_heads, queries_per_group, count_of_rows, head_size = attention_output.shape
    return attention_output.transpose(2, 0, 1, 3).reshape(
        count_of_rows, count_of_heads * queries_per_group * head_size
    )


def on_device(tokens, w_query, w_key, w_value, w_out):
    highest = lax.Precision.HIGH
    gathered = lax.all_gather(tokens, "col", axis=0, tiled=True)
    q_width = w_query.shape[1]
    kv_width = w_key.shape[1]

    def product(weight):
        return jnp.dot(gathered, weight, preferred_element_type=jnp.float32, precision=highest)

    partial = jnp.concatenate([product(w_query), product(w_key), product(w_value)], axis=1)
    on_chip = lax.psum_scatter(partial, "rc", scatter_dimension=0, tiled=True)
    joined = lax.psum_scatter(on_chip, "rz", scatter_dimension=0, tiled=True)
    query_rows = joined[:, :q_width]
    local_kv = joined[:, q_width:]
    all_kv = lax.all_gather(lax.all_gather(local_kv, "rz", axis=0, tiled=True), "rc", axis=0, tiled=True)
    state_end = fold_keys(
        query_rows,
        start_state(query_rows, kv_width),
        (all_kv[:, :kv_width], all_kv[:, kv_width:]),
    )
    attention_output = finish(state_end)
    set_attended = lax.all_gather(
        lax.all_gather(attention_output, "rz", axis=0, tiled=True), "rc", axis=0, tiled=True
    )
    return lax.psum_scatter(
        jnp.dot(set_attended, w_out, preferred_element_type=jnp.float32, precision=highest),
        "col",
        scatter_dimension=0,
        tiled=True,
    )


def solution(mesh):
    depth, row, col = (mesh.shape[a] for a in ("depth", "row", "col"))
    split = jax.sharding.Mesh(
        np.asarray(mesh.devices).reshape(depth, row // 2, 2, col), ("depth", "rz", "rc", "col")
    )
    rows = ("rz", "rc")
    placed = (
        P(("depth", "col"), rows),
        P(rows, "col"),
        P(rows, "col"),
        P(rows, "col"),
        P("col", rows),
    )
    return jax.shard_map(
        on_device, mesh=split, in_specs=placed, out_specs=P(("depth", "col"), rows), check_vma=False
    )
```

```python
import functools
import math

import jax
import numpy as np
import jax.numpy as jnp
from jax import lax
from jax.experimental import pallas as pl
from jax.experimental.pallas import tpu as pltpu
from jax.sharding import PartitionSpec as P

QUERY_HEADS = 32
KEY_VALUE_HEADS = 4
HEAD_SIZE_DIM = 128


def start_state(query_rows, kv_width):
    count_of_heads = kv_width // HEAD_SIZE_DIM
    queries_per_group = QUERY_HEADS // KEY_VALUE_HEADS
    count_of_rows = query_rows.shape[0]
    running_max = jnp.full((count_of_heads, queries_per_group, count_of_rows), -1e30, jnp.float32)
    running_sum = jnp.zeros((count_of_heads, queries_per_group, count_of_rows), jnp.float32)
    weighted = jnp.zeros(
        (count_of_heads, queries_per_group, count_of_rows, HEAD_SIZE_DIM), jnp.float32
    )
    return (running_max, running_sum, weighted)


def fold_keys(query_rows, state_now, block_pair):
    highest = lax.Precision.HIGH
    running_max, running_sum, weighted = state_now
    key_block, value_block = block_pair
    count_of_heads = key_block.shape[1] // HEAD_SIZE_DIM
    count_of_rows = query_rows.shape[0]
    query_head_rows = query_rows.reshape(
        count_of_rows, count_of_heads, QUERY_HEADS // KEY_VALUE_HEADS, HEAD_SIZE_DIM
    )
    key_head_rows = key_block.reshape(-1, count_of_heads, HEAD_SIZE_DIM)
    value_head_rows = value_block.reshape(-1, count_of_heads, HEAD_SIZE_DIM)
    scores = jnp.einsum("rkgd,nkd->kgrn", query_head_rows, key_head_rows, precision=highest) * (
        1.0 / math.sqrt(HEAD_SIZE_DIM)
    )
    newest = jnp.maximum(running_max, jnp.max(scores, axis=-1))
    weights = jnp.exp(scores - newest[..., None])
    running_sum = jnp.sum(weights, axis=-1)
    weighted = jnp.einsum("kgrn,nkd->kgrd", weights, value_head_rows, precision=highest)
    return (newest, running_sum, weighted)


def finish(state_now):
    running_max, running_sum, weighted = state_now
    attention_output = weighted / running_sum[..., None]
    count_of_heads, queries_per_group, count_of_rows, head_size = attention_output.shape
    return attention_output.transpose(2, 0, 1, 3).reshape(
        count_of_rows, count_of_heads * queries_per_group * head_size
    )


def gather_kernel(ring, n, x_ref, out_ref, local_sem, send_sems, recv_sems):
    mesh_id = pl.DeviceIdType.MESH
    d = lax.axis_index("depth")
    z = lax.axis_index("rz")
    c = lax.axis_index("rc")
    y = lax.axis_index("col")
    right = lax.rem(z + 1, ring)
    left = lax.rem(z + ring - 1, ring)
    sib = (d, z, 1 - c, y)

    barrier = pltpu.get_barrier_semaphore()
    for peer in ((d, left, c, y), (d, right, c, y), sib):
        pl.semaphore_signal(barrier, inc=1, device_id=peer, device_id_type=mesh_id)
    pl.semaphore_wait(barrier, 3)

    def rows(zz, lo=0, size=n):
        return pl.ds(pl.multiple_of((zz * 2 + c) * n + lo, 8), size)

    def remote(src, dst_rows, peer, idx):
        cp = pltpu.make_async_remote_copy(
            src_ref=src,
            dst_ref=out_ref.at[dst_rows],
            send_sem=send_sems.at[idx],
            recv_sem=recv_sems.at[idx],
            device_id=peer,
            device_id_type=mesh_id,
        )
        cp.start()
        return cp

    local = pltpu.make_async_copy(x_ref, out_ref.at[rows(z)], local_sem)
    local.start()
    sib_copies = [remote(x_ref, rows(z), sib, ring)]
    half = ring // 2
    for s in range(1, half + 1):
        origin_r = lax.rem(z - (s - 1) + ring, ring)
        origin_l = lax.rem(z + (s - 1), ring)
        src_r = x_ref if s == 1 else out_ref.at[rows(origin_r)]
        src_l = x_ref if s == 1 else out_ref.at[rows(origin_l)]
        if s < half:
            cr = remote(src_r, rows(origin_r), (d, right, c, y), 2 * (s - 1))
            cl = remote(src_l, rows(origin_l), (d, left, c, y), 2 * (s - 1) + 1)
            cr.wait()
            cl.wait()
            got_l = lax.rem(z - s + ring, ring)
            got_r = lax.rem(z + s, ring)
            sib_copies.append(remote(out_ref.at[rows(got_l)], rows(got_l), sib, ring + 2 * s - 1))
            sib_copies.append(remote(out_ref.at[rows(got_r)], rows(got_r), sib, ring + 2 * s))
        else:
            h = n // 2
            cr = remote(src_r.at[pl.ds(0, h)], rows(origin_r, 0, h), (d, right, c, y), 2 * (s - 1))
            cl = remote(src_l.at[pl.ds(h, h)], rows(origin_l, h, h), (d, left, c, y), 2 * (s - 1) + 1)
            cr.wait()
            cl.wait()
            opp = lax.rem(z + half, ring)
            sib_copies.append(remote(out_ref.at[rows(opp)], rows(opp), sib, ring + 2 * s - 1))
    local.wait()
    for cp in sib_copies:
        cp.wait()


def ring_gather(block, ring, collective_id):
    n, w = block.shape
    return pl.pallas_call(
        functools.partial(gather_kernel, ring, n),
        out_shape=jax.ShapeDtypeStruct((2 * ring * n, w), block.dtype),
        in_specs=[pl.BlockSpec(memory_space=pl.ANY)],
        out_specs=pl.BlockSpec(memory_space=pl.ANY),
        scratch_shapes=[
            pltpu.SemaphoreType.DMA(()),
            pltpu.SemaphoreType.DMA((2 * ring,)),
            pltpu.SemaphoreType.DMA((2 * ring,)),
        ],
        compiler_params=pltpu.CompilerParams(collective_id=collective_id, has_side_effects=True),
    )(block)


def on_device(ring, tokens, w_query, w_key, w_value, w_out):
    highest = lax.Precision.HIGH
    gathered = lax.all_gather(tokens, "col", axis=0, tiled=True)
    q_width = w_query.shape[1]
    kv_width = w_key.shape[1]

    def product(weight):
        return jnp.dot(gathered, weight, preferred_element_type=jnp.float32, precision=highest)

    partial = jnp.concatenate([product(w_query), product(w_key), product(w_value)], axis=1)
    joined = lax.psum_scatter(partial, ("rz", "rc"), scatter_dimension=0, tiled=True)
    query_rows = joined[:, :q_width]
    all_kv = ring_gather(joined[:, q_width:], ring, 0)
    state_end = fold_keys(
        query_rows,
        start_state(query_rows, kv_width),
        (all_kv[:, :kv_width], all_kv[:, kv_width:]),
    )
    set_attended = ring_gather(finish(state_end), ring, 1)
    return lax.psum_scatter(
        jnp.dot(set_attended, w_out, preferred_element_type=jnp.float32, precision=highest),
        "col",
        scatter_dimension=0,
        tiled=True,
    )


def solution(mesh):
    depth, row, col = (mesh.shape[a] for a in ("depth", "row", "col"))
    split = jax.sharding.Mesh(
        np.asarray(mesh.devices).reshape(depth, row // 2, 2, col), ("depth", "rz", "rc", "col")
    )
    rows = ("rz", "rc")
    placed = (
        P(("depth", "col"), rows),
        P(rows, "col"),
        P(rows, "col"),
        P(rows, "col"),
        P("col", rows),
    )
    return jax.shard_map(
        functools.partial(on_device, row // 2),
        mesh=split,
        in_specs=placed,
        out_specs=P(("depth", "col"), rows),
        check_vma=False,
    )
```

```python
import functools
import math

import jax
import numpy as np
import jax.numpy as jnp
from jax import lax
from jax.experimental import pallas as pl
from jax.experimental.pallas import tpu as pltpu
from jax.sharding import PartitionSpec as P

QUERY_HEADS = 32
KEY_VALUE_HEADS = 4
HEAD_SIZE_DIM = 128


def start_state(query_rows, kv_width):
    count_of_heads = kv_width // HEAD_SIZE_DIM
    queries_per_group = QUERY_HEADS // KEY_VALUE_HEADS
    count_of_rows = query_rows.shape[0]
    running_max = jnp.full((count_of_heads, queries_per_group, count_of_rows), -1e30, jnp.float32)
    running_sum = jnp.zeros((count_of_heads, queries_per_group, count_of_rows), jnp.float32)
    weighted = jnp.zeros(
        (count_of_heads, queries_per_group, count_of_rows, HEAD_SIZE_DIM), jnp.float32
    )
    return (running_max, running_sum, weighted)


def fold_keys(query_rows, state_now, block_pair):
    highest = lax.Precision.HIGH
    running_max, running_sum, weighted = state_now
    key_block, value_block = block_pair
    count_of_heads = key_block.shape[1] // HEAD_SIZE_DIM
    count_of_rows = query_rows.shape[0]
    query_head_rows = query_rows.reshape(
        count_of_rows, count_of_heads, QUERY_HEADS // KEY_VALUE_HEADS, HEAD_SIZE_DIM
    )
    key_head_rows = key_block.reshape(-1, count_of_heads, HEAD_SIZE_DIM)
    value_head_rows = value_block.reshape(-1, count_of_heads, HEAD_SIZE_DIM)
    scores = jnp.einsum("rkgd,nkd->kgrn", query_head_rows, key_head_rows, precision=highest) * (
        1.0 / math.sqrt(HEAD_SIZE_DIM)
    )
    newest = jnp.maximum(running_max, jnp.max(scores, axis=-1))
    weights = jnp.exp(scores - newest[..., None])
    running_sum = jnp.sum(weights, axis=-1)
    weighted = jnp.einsum("kgrn,nkd->kgrd", weights, value_head_rows, precision=highest)
    return (newest, running_sum, weighted)


def finish(state_now):
    running_max, running_sum, weighted = state_now
    attention_output = weighted / running_sum[..., None]
    count_of_heads, queries_per_group, count_of_rows, head_size = attention_output.shape
    return attention_output.transpose(2, 0, 1, 3).reshape(
        count_of_rows, count_of_heads * queries_per_group * head_size
    )


def gather_kernel(axis, ring, n, with_sib, x_ref, out_ref, local_sem, send_sems, recv_sems):
    mesh_id = pl.DeviceIdType.MESH
    names = ("depth", "rz", "rc", "col")
    me = {a: lax.axis_index(a) for a in names}
    pos = me[axis]

    def device(**moved):
        return tuple(moved.get(a, me[a]) for a in names)

    right = device(**{axis: lax.rem(pos + 1, ring)})
    left = device(**{axis: lax.rem(pos + ring - 1, ring)})
    sib = device(rc=1 - me["rc"])
    peers = (left, right, sib) if with_sib else (left, right)

    barrier = pltpu.get_barrier_semaphore()
    for peer in peers:
        pl.semaphore_signal(barrier, inc=1, device_id=peer, device_id_type=mesh_id)
    pl.semaphore_wait(barrier, len(peers))

    def rows(at, lo=0, size=n):
        slot = at * 2 + me["rc"] if with_sib else at
        return pl.ds(pl.multiple_of(slot * n + lo, 8), size)

    def remote(src, dst_rows, peer, idx):
        cp = pltpu.make_async_remote_copy(
            src_ref=src,
            dst_ref=out_ref.at[dst_rows],
            send_sem=send_sems.at[idx],
            recv_sem=recv_sems.at[idx],
            device_id=peer,
            device_id_type=mesh_id,
        )
        cp.start()
        return cp

    def to_sib(at, idx):
        if with_sib:
            sib_copies.append(remote(out_ref.at[rows(at)], rows(at), sib, idx))

    local = pltpu.make_async_copy(x_ref, out_ref.at[rows(pos)], local_sem)
    local.start()
    sib_copies = [remote(x_ref, rows(pos), sib, ring)] if with_sib else []
    half = ring // 2
    for s in range(1, half + 1):
        origin_r = lax.rem(pos - (s - 1) + ring, ring)
        origin_l = lax.rem(pos + (s - 1), ring)
        src_r = x_ref if s == 1 else out_ref.at[rows(origin_r)]
        src_l = x_ref if s == 1 else out_ref.at[rows(origin_l)]
        if s < half:
            cr = remote(src_r, rows(origin_r), right, 2 * (s - 1))
            cl = remote(src_l, rows(origin_l), left, 2 * (s - 1) + 1)
            cr.wait()
            cl.wait()
            to_sib(lax.rem(pos - s + ring, ring), ring + 2 * s - 1)
            to_sib(lax.rem(pos + s, ring), ring + 2 * s)
        else:
            h = n // 2
            cr = remote(src_r.at[pl.ds(0, h)], rows(origin_r, 0, h), right, 2 * (s - 1))
            cl = remote(src_l.at[pl.ds(h, h)], rows(origin_l, h, h), left, 2 * (s - 1) + 1)
            cr.wait()
            cl.wait()
            to_sib(lax.rem(pos + half, ring), ring + 2 * s - 1)
    local.wait()
    for cp in sib_copies:
        cp.wait()


def ring_gather(block, axis, ring, with_sib, collective_id):
    n, w = block.shape
    copies = 2 if with_sib else 1
    return pl.pallas_call(
        functools.partial(gather_kernel, axis, ring, n, with_sib),
        out_shape=jax.ShapeDtypeStruct((copies * ring * n, w), block.dtype),
        in_specs=[pl.BlockSpec(memory_space=pl.ANY)],
        out_specs=pl.BlockSpec(memory_space=pl.ANY),
        scratch_shapes=[
            pltpu.SemaphoreType.DMA(()),
            pltpu.SemaphoreType.DMA((2 * ring,)),
            pltpu.SemaphoreType.DMA((2 * ring,)),
        ],
        compiler_params=pltpu.CompilerParams(collective_id=collective_id, has_side_effects=True),
    )(block)


def on_device(ring, cols, tokens, w_query, w_key, w_value, w_out):
    highest = lax.Precision.HIGH
    gathered = ring_gather(tokens, "col", cols, False, 2)
    q_width = w_query.shape[1]
    kv_width = w_key.shape[1]

    def product(weight):
        return jnp.dot(gathered, weight, preferred_element_type=jnp.float32, precision=highest)

    partial = jnp.concatenate([product(w_query), product(w_key), product(w_value)], axis=1)
    joined = lax.psum_scatter(partial, ("rz", "rc"), scatter_dimension=0, tiled=True)
    query_rows = joined[:, :q_width]
    all_kv = ring_gather(joined[:, q_width:], "rz", ring, True, 0)
    state_end = fold_keys(
        query_rows,
        start_state(query_rows, kv_width),
        (all_kv[:, :kv_width], all_kv[:, kv_width:]),
    )
    set_attended = ring_gather(finish(state_end), "rz", ring, True, 1)
    return lax.psum_scatter(
        jnp.dot(set_attended, w_out, preferred_element_type=jnp.float32, precision=highest),
        "col",
        scatter_dimension=0,
        tiled=True,
    )


def solution(mesh):
    depth, row, col = (mesh.shape[a] for a in ("depth", "row", "col"))
    split = jax.sharding.Mesh(
        np.asarray(mesh.devices).reshape(depth, row // 2, 2, col), ("depth", "rz", "rc", "col")
    )
    rows = ("rz", "rc")
    placed = (
        P(("depth", "col"), rows),
        P(rows, "col"),
        P(rows, "col"),
        P(rows, "col"),
        P("col", rows),
    )
    return jax.shard_map(
        functools.partial(on_device, row // 2, col),
        mesh=split,
        in_specs=placed,
        out_specs=P(("depth", "col"), rows),
        check_vma=False,
    )
```

```python
import functools
import math

import jax
import numpy as np
import jax.numpy as jnp
from jax import lax
from jax.experimental import pallas as pl
from jax.experimental.pallas import tpu as pltpu
from jax.sharding import PartitionSpec as P

QUERY_HEADS = 32
KEY_VALUE_HEADS = 4
HEAD_SIZE_DIM = 128


def start_state(query_rows, kv_width):
    count_of_heads = kv_width // HEAD_SIZE_DIM
    queries_per_group = QUERY_HEADS // KEY_VALUE_HEADS
    count_of_rows = query_rows.shape[0]
    running_max = jnp.full((count_of_heads, queries_per_group, count_of_rows), -1e30, jnp.float32)
    running_sum = jnp.zeros((count_of_heads, queries_per_group, count_of_rows), jnp.float32)
    weighted = jnp.zeros(
        (count_of_heads, queries_per_group, count_of_rows, HEAD_SIZE_DIM), jnp.float32
    )
    return (running_max, running_sum, weighted)


def fold_keys(query_rows, state_now, block_pair):
    highest = lax.Precision.HIGH
    running_max, running_sum, weighted = state_now
    key_block, value_block = block_pair
    count_of_heads = key_block.shape[1] // HEAD_SIZE_DIM
    count_of_rows = query_rows.shape[0]
    query_head_rows = query_rows.reshape(
        count_of_rows, count_of_heads, QUERY_HEADS // KEY_VALUE_HEADS, HEAD_SIZE_DIM
    )
    key_head_rows = key_block.reshape(-1, count_of_heads, HEAD_SIZE_DIM)
    value_head_rows = value_block.reshape(-1, count_of_heads, HEAD_SIZE_DIM)
    scores = jnp.einsum("rkgd,nkd->kgrn", query_head_rows, key_head_rows, precision=highest) * (
        1.0 / math.sqrt(HEAD_SIZE_DIM)
    )
    newest = jnp.maximum(running_max, jnp.max(scores, axis=-1))
    weights = jnp.exp(scores - newest[..., None])
    running_sum = jnp.sum(weights, axis=-1)
    weighted = jnp.einsum("kgrn,nkd->kgrd", weights, value_head_rows, precision=highest)
    return (newest, running_sum, weighted)


def finish(state_now):
    running_max, running_sum, weighted = state_now
    attention_output = weighted / running_sum[..., None]
    count_of_heads, queries_per_group, count_of_rows, head_size = attention_output.shape
    return attention_output.transpose(2, 0, 1, 3).reshape(
        count_of_rows, count_of_heads * queries_per_group * head_size
    )


def gather_kernel(axis, ring, n, with_sib, x_ref, out_ref, local_sem, send_sems, recv_sems):
    mesh_id = pl.DeviceIdType.MESH
    names = ("depth", "rz", "rc", "col")
    me = {a: lax.axis_index(a) for a in names}
    pos = me[axis]

    def device(**moved):
        return tuple(moved.get(a, me[a]) for a in names)

    right = device(**{axis: lax.rem(pos + 1, ring)})
    left = device(**{axis: lax.rem(pos + ring - 1, ring)})
    sib = device(rc=1 - me["rc"])
    peers = (left, right, sib) if with_sib else (left, right)

    barrier = pltpu.get_barrier_semaphore()
    for peer in peers:
        pl.semaphore_signal(barrier, inc=1, device_id=peer, device_id_type=mesh_id)
    pl.semaphore_wait(barrier, len(peers))

    def rows(at, lo=0, size=n):
        slot = at * 2 + me["rc"] if with_sib else at
        return pl.ds(pl.multiple_of(slot * n + lo, 8), size)

    def remote(src, dst_rows, peer, idx):
        cp = pltpu.make_async_remote_copy(
            src_ref=src,
            dst_ref=out_ref.at[dst_rows],
            send_sem=send_sems.at[idx],
            recv_sem=recv_sems.at[idx],
            device_id=peer,
            device_id_type=mesh_id,
        )
        cp.start()
        return cp

    def to_sib(at, idx):
        if with_sib:
            sib_copies.append(remote(out_ref.at[rows(at)], rows(at), sib, idx))

    local = pltpu.make_async_copy(x_ref, out_ref.at[rows(pos)], local_sem)
    local.start()
    sib_copies = [remote(x_ref, rows(pos), sib, ring)] if with_sib else []
    half = ring // 2
    for s in range(1, half + 1):
        origin_r = lax.rem(pos - (s - 1) + ring, ring)
        origin_l = lax.rem(pos + (s - 1), ring)
        src_r = x_ref if s == 1 else out_ref.at[rows(origin_r)]
        src_l = x_ref if s == 1 else out_ref.at[rows(origin_l)]
        if s < half:
            cr = remote(src_r, rows(origin_r), right, 2 * (s - 1))
            cl = remote(src_l, rows(origin_l), left, 2 * (s - 1) + 1)
            cr.wait()
            cl.wait()
            to_sib(lax.rem(pos - s + ring, ring), ring + 2 * s - 1)
            to_sib(lax.rem(pos + s, ring), ring + 2 * s)
        else:
            h = n // 2
            cr = remote(src_r.at[pl.ds(0, h)], rows(origin_r, 0, h), right, 2 * (s - 1))
            cl = remote(src_l.at[pl.ds(h, h)], rows(origin_l, h, h), left, 2 * (s - 1) + 1)
            cr.wait()
            cl.wait()
            to_sib(lax.rem(pos + half, ring), ring + 2 * s - 1)
    local.wait()
    for cp in sib_copies:
        cp.wait()


def ring_gather(block, axis, ring, with_sib, collective_id):
    n, w = block.shape
    copies = 2 if with_sib else 1
    return pl.pallas_call(
        functools.partial(gather_kernel, axis, ring, n, with_sib),
        out_shape=jax.ShapeDtypeStruct((copies * ring * n, w), block.dtype),
        in_specs=[pl.BlockSpec(memory_space=pl.ANY)],
        out_specs=pl.BlockSpec(memory_space=pl.ANY),
        scratch_shapes=[
            pltpu.SemaphoreType.DMA(()),
            pltpu.SemaphoreType.DMA((2 * ring,)),
            pltpu.SemaphoreType.DMA((2 * ring,)),
        ],
        compiler_params=pltpu.CompilerParams(collective_id=collective_id, has_side_effects=True),
    )(block)


def scatter_kernel(axis, ring, m, with_sib, x_ref, out_ref, sbuf, rbuf, sibbuf, send_sems, recv_sems, sib_sems):
    mesh_id = pl.DeviceIdType.MESH
    names = ("depth", "rz", "rc", "col")
    me = {a: lax.axis_index(a) for a in names}
    pos = me[axis]
    h = m // 2

    def device(**moved):
        return tuple(moved.get(a, me[a]) for a in names)

    right = device(**{axis: lax.rem(pos + 1, ring)})
    left = device(**{axis: lax.rem(pos + ring - 1, ring)})
    sib = device(rc=1 - me["rc"])
    peers = (left, right, sib) if with_sib else (left, right)

    barrier = pltpu.get_barrier_semaphore()
    for peer in peers:
        pl.semaphore_signal(barrier, inc=1, device_id=peer, device_id_type=mesh_id)
    pl.semaphore_wait(barrier, len(peers))

    def rows_of(at, half, owner):
        slot = at * 2 + owner if with_sib else at
        return pl.ds(pl.multiple_of(slot * m + half * h, 8), h)

    def remote(src, dst, peer, sems, idx):
        cp = pltpu.make_async_remote_copy(
            src_ref=src,
            dst_ref=dst,
            send_sem=sems[0].at[idx],
            recv_sem=sems[1].at[idx],
            device_id=peer,
            device_id_type=mesh_id,
        )
        cp.start()
        return cp

    def need(s, half):
        sign = -1 if half == 0 else 1
        return lax.rem(pos + sign * s + ring * ring, ring)

    sib_copies = {}
    if with_sib:
        order = [(s, half) for s in range(1, ring) for half in (0, 1)] + [(ring, 0), (ring, 1)]
        for idx, (s, half) in enumerate(order):
            at = need(s % ring, half)
            dst = sibbuf.at[pl.ds(pl.multiple_of(at * m + half * h, 8), h)]
            sib_copies[(s, half)] = remote(
                x_ref.at[rows_of(at, half, 1 - me["rc"])], dst, sib, (sib_sems[0], sib_sems[1]), idx
            )

    def contribution(s, half):
        at = need(s % ring, half)
        own = x_ref[rows_of(at, half, me["rc"])]
        if with_sib:
            sib_copies[(s, half)].wait()
            own = own + sibbuf[pl.ds(pl.multiple_of(at * m + half * h, 8), h)]
        return own

    ring_copies = {}
    for s in range(1, ring):
        for half in (0, 1):
            value = contribution(s, half)
            if s > 1:
                ring_copies[(s - 1, half)].wait()
                value = value + rbuf[half, s - 2]
            sbuf[half, s - 1] = value
            ring_copies[(s, half)] = remote(
                sbuf.at[half, s - 1],
                rbuf.at[half, s - 1],
                right if half == 0 else left,
                (send_sems, recv_sems),
                half * (ring - 1) + s - 1,
            )
    for half in (0, 1):
        value = contribution(ring, half)
        ring_copies[(ring - 1, half)].wait()
        out_ref[pl.ds(half * h, h)] = value + rbuf[half, ring - 2]


def ring_scatter(x, axis, ring, with_sib, collective_id):
    total, w = x.shape
    copies = 2 if with_sib else 1
    m = total // (copies * ring)
    sib_rows = ring * m if with_sib else 8
    return pl.pallas_call(
        functools.partial(scatter_kernel, axis, ring, m, with_sib),
        out_shape=jax.ShapeDtypeStruct((m, w), x.dtype),
        in_specs=[pl.BlockSpec(memory_space=pltpu.VMEM)],
        out_specs=pl.BlockSpec(memory_space=pltpu.VMEM),
        scratch_shapes=[
            pltpu.VMEM((2, ring - 1, m // 2, w), x.dtype),
            pltpu.VMEM((2, ring - 1, m // 2, w), x.dtype),
            pltpu.VMEM((sib_rows, w), x.dtype),
            pltpu.SemaphoreType.DMA((2 * ring,)),
            pltpu.SemaphoreType.DMA((2 * ring,)),
            (pltpu.SemaphoreType.DMA((2 * ring,)), pltpu.SemaphoreType.DMA((2 * ring,))),
        ],
        compiler_params=pltpu.CompilerParams(
            collective_id=collective_id, has_side_effects=True, vmem_limit_bytes=60 * 1024 * 1024
        ),
    )(x)


def on_device(ring, cols, tokens, w_query, w_key, w_value, w_out):
    highest = lax.Precision.HIGH
    gathered = ring_gather(tokens, "col", cols, False, 2)
    q_width = w_query.shape[1]
    kv_width = w_key.shape[1]

    def product(weight):
        return jnp.dot(gathered, weight, preferred_element_type=jnp.float32, precision=highest)

    partial = jnp.concatenate([product(w_query), product(w_key), product(w_value)], axis=1)
    joined = ring_scatter(partial, "rz", ring, True, 3)
    query_rows = joined[:, :q_width]
    all_kv = ring_gather(joined[:, q_width:], "rz", ring, True, 0)
    state_end = fold_keys(
        query_rows,
        start_state(query_rows, kv_width),
        (all_kv[:, :kv_width], all_kv[:, kv_width:]),
    )
    set_attended = ring_gather(finish(state_end), "rz", ring, True, 1)
    return ring_scatter(
        jnp.dot(set_attended, w_out, preferred_element_type=jnp.float32, precision=highest),
        "col",
        cols,
        False,
        4,
    )


def solution(mesh):
    depth, row, col = (mesh.shape[a] for a in ("depth", "row", "col"))
    split = jax.sharding.Mesh(
        np.asarray(mesh.devices).reshape(depth, row // 2, 2, col), ("depth", "rz", "rc", "col")
    )
    rows = ("rz", "rc")
    placed = (
        P(("depth", "col"), rows),
        P(rows, "col"),
        P(rows, "col"),
        P(rows, "col"),
        P("col", rows),
    )
    return jax.shard_map(
        functools.partial(on_device, row // 2, col),
        mesh=split,
        in_specs=placed,
        out_specs=P(("depth", "col"), rows),
        check_vma=False,
    )
```

```python
import functools
import math

import jax
import numpy as np
import jax.numpy as jnp
from jax import lax
from jax.experimental import pallas as pl
from jax.experimental.pallas import tpu as pltpu
from jax.sharding import PartitionSpec as P

QUERY_HEADS = 32
KEY_VALUE_HEADS = 4
HEAD_SIZE_DIM = 128


def start_state(query_rows, kv_width):
    count_of_heads = kv_width // HEAD_SIZE_DIM
    queries_per_group = QUERY_HEADS // KEY_VALUE_HEADS
    count_of_rows = query_rows.shape[0]
    running_max = jnp.full((count_of_heads, queries_per_group, count_of_rows), -1e30, jnp.float32)
    running_sum = jnp.zeros((count_of_heads, queries_per_group, count_of_rows), jnp.float32)
    weighted = jnp.zeros(
        (count_of_heads, queries_per_group, count_of_rows, HEAD_SIZE_DIM), jnp.float32
    )
    return (running_max, running_sum, weighted)


def fold_keys(query_rows, state_now, block_pair):
    highest = lax.Precision.HIGH
    running_max, running_sum, weighted = state_now
    key_block, value_block = block_pair
    count_of_heads = key_block.shape[1] // HEAD_SIZE_DIM
    count_of_rows = query_rows.shape[0]
    query_head_rows = query_rows.reshape(
        count_of_rows, count_of_heads, QUERY_HEADS // KEY_VALUE_HEADS, HEAD_SIZE_DIM
    )
    key_head_rows = key_block.reshape(-1, count_of_heads, HEAD_SIZE_DIM)
    value_head_rows = value_block.reshape(-1, count_of_heads, HEAD_SIZE_DIM)
    scores = jnp.einsum("rkgd,nkd->kgrn", query_head_rows, key_head_rows, precision=highest) * (
        1.0 / math.sqrt(HEAD_SIZE_DIM)
    )
    newest = jnp.maximum(running_max, jnp.max(scores, axis=-1))
    weights = jnp.exp(scores - newest[..., None])
    running_sum = jnp.sum(weights, axis=-1)
    weighted = jnp.einsum("kgrn,nkd->kgrd", weights, value_head_rows, precision=highest)
    return (newest, running_sum, weighted)


def finish(state_now):
    running_max, running_sum, weighted = state_now
    attention_output = weighted / running_sum[..., None]
    count_of_heads, queries_per_group, count_of_rows, head_size = attention_output.shape
    return attention_output.transpose(2, 0, 1, 3).reshape(
        count_of_rows, count_of_heads * queries_per_group * head_size
    )


def gather_kernel(axis, ring, n, with_sib, x_ref, out_ref, local_sem, send_sems, recv_sems):
    mesh_id = pl.DeviceIdType.MESH
    names = ("depth", "rz", "rc", "col")
    me = {a: lax.axis_index(a) for a in names}
    pos = me[axis]

    def device(**moved):
        return tuple(moved.get(a, me[a]) for a in names)

    right = device(**{axis: lax.rem(pos + 1, ring)})
    left = device(**{axis: lax.rem(pos + ring - 1, ring)})
    sib = device(rc=1 - me["rc"])
    peers = (left, right, sib) if with_sib else (left, right)

    barrier = pltpu.get_barrier_semaphore()
    for peer in peers:
        pl.semaphore_signal(barrier, inc=1, device_id=peer, device_id_type=mesh_id)
    pl.semaphore_wait(barrier, len(peers))

    def rows(at, lo=0, size=n):
        slot = at * 2 + me["rc"] if with_sib else at
        return pl.ds(pl.multiple_of(slot * n + lo, 8), size)

    def remote(src, dst_rows, peer, idx):
        cp = pltpu.make_async_remote_copy(
            src_ref=src,
            dst_ref=out_ref.at[dst_rows],
            send_sem=send_sems.at[idx],
            recv_sem=recv_sems.at[idx],
            device_id=peer,
            device_id_type=mesh_id,
        )
        cp.start()
        return cp

    def to_sib(at, idx):
        if with_sib:
            sib_copies.append(remote(out_ref.at[rows(at)], rows(at), sib, idx))

    local = pltpu.make_async_copy(x_ref, out_ref.at[rows(pos)], local_sem)
    local.start()
    sib_copies = [remote(x_ref, rows(pos), sib, ring)] if with_sib else []
    half = ring // 2
    for s in range(1, half + 1):
        origin_r = lax.rem(pos - (s - 1) + ring, ring)
        origin_l = lax.rem(pos + (s - 1), ring)
        src_r = x_ref if s == 1 else out_ref.at[rows(origin_r)]
        src_l = x_ref if s == 1 else out_ref.at[rows(origin_l)]
        if s < half:
            cr = remote(src_r, rows(origin_r), right, 2 * (s - 1))
            cl = remote(src_l, rows(origin_l), left, 2 * (s - 1) + 1)
            cr.wait()
            cl.wait()
            to_sib(lax.rem(pos - s + ring, ring), ring + 2 * s - 1)
            to_sib(lax.rem(pos + s, ring), ring + 2 * s)
        else:
            h = n // 2
            cr = remote(src_r.at[pl.ds(0, h)], rows(origin_r, 0, h), right, 2 * (s - 1))
            cl = remote(src_l.at[pl.ds(h, h)], rows(origin_l, h, h), left, 2 * (s - 1) + 1)
            cr.wait()
            cl.wait()
            to_sib(lax.rem(pos + half, ring), ring + 2 * s - 1)
    local.wait()
    for cp in sib_copies:
        cp.wait()


def ring_gather(block, axis, ring, with_sib, collective_id):
    n, w = block.shape
    copies = 2 if with_sib else 1
    return pl.pallas_call(
        functools.partial(gather_kernel, axis, ring, n, with_sib),
        out_shape=jax.ShapeDtypeStruct((copies * ring * n, w), block.dtype),
        in_specs=[pl.BlockSpec(memory_space=pl.ANY)],
        out_specs=pl.BlockSpec(memory_space=pl.ANY),
        scratch_shapes=[
            pltpu.SemaphoreType.DMA(()),
            pltpu.SemaphoreType.DMA((2 * ring,)),
            pltpu.SemaphoreType.DMA((2 * ring,)),
        ],
        compiler_params=pltpu.CompilerParams(collective_id=collective_id, has_side_effects=True),
    )(block)


def scatter_kernel(axis, ring, m, with_sib, parts, x_ref, out_ref, sbuf, rbuf, sibbuf, send_sems, recv_sems, sib_sems):
    mesh_id = pl.DeviceIdType.MESH
    names = ("depth", "rz", "rc", "col")
    me = {a: lax.axis_index(a) for a in names}
    pos = me[axis]
    h = m // 2
    q = h // parts

    def device(**moved):
        return tuple(moved.get(a, me[a]) for a in names)

    right = device(**{axis: lax.rem(pos + 1, ring)})
    left = device(**{axis: lax.rem(pos + ring - 1, ring)})
    sib = device(rc=1 - me["rc"])
    peers = (left, right, sib) if with_sib else (left, right)

    barrier = pltpu.get_barrier_semaphore()
    for peer in peers:
        pl.semaphore_signal(barrier, inc=1, device_id=peer, device_id_type=mesh_id)
    pl.semaphore_wait(barrier, len(peers))

    def rows_of(at, half, part, owner):
        slot = at * 2 + owner if with_sib else at
        return pl.ds(pl.multiple_of(slot * m + half * h + part * q, 8), q)

    def sib_rows(at, half, part):
        return pl.ds(pl.multiple_of(at * m + half * h + part * q, 8), q)

    def remote(src, dst, peer, sems, idx):
        cp = pltpu.make_async_remote_copy(
            src_ref=src,
            dst_ref=dst,
            send_sem=sems[0].at[idx],
            recv_sem=sems[1].at[idx],
            device_id=peer,
            device_id_type=mesh_id,
        )
        cp.start()
        return cp

    def need(s, half):
        sign = -1 if half == 0 else 1
        return lax.rem(pos + sign * (s % ring) + ring * ring, ring)

    sib_copies = {}
    if with_sib:
        order = [(s, half) for s in range(1, ring + 1) for half in (0, 1)]
        for idx, (s, half) in enumerate(order):
            at = need(s, half)
            sib_copies[(s, half)] = remote(
                x_ref.at[pl.ds(pl.multiple_of((at * 2 + 1 - me["rc"]) * m + half * h, 8), h)],
                sibbuf.at[pl.ds(pl.multiple_of(at * m + half * h, 8), h)],
                sib,
                (sib_sems[0], sib_sems[1]),
                idx,
            )

    def contribution(s, half, part):
        at = need(s, half)
        own = x_ref[rows_of(at, half, part, me["rc"])]
        if with_sib:
            if part == 0:
                sib_copies[(s, half)].wait()
            own = own + sibbuf[sib_rows(at, half, part)]
        return own

    ring_copies = {}
    for s in range(1, ring):
        for part in range(parts):
            for half in (0, 1):
                value = contribution(s, half, part)
                if s > 1:
                    ring_copies[(s - 1, half, part)].wait()
                    value = value + rbuf[half, s - 2, part]
                sbuf[half, s - 1, part] = value
                ring_copies[(s, half, part)] = remote(
                    sbuf.at[half, s - 1, part],
                    rbuf.at[half, s - 1, part],
                    right if half == 0 else left,
                    (send_sems, recv_sems),
                    (half * (ring - 1) + s - 1) * parts + part,
                )
    for part in range(parts):
        for half in (0, 1):
            value = contribution(ring, half, part)
            ring_copies[(ring - 1, half, part)].wait()
            out_ref[pl.ds(half * h + part * q, q)] = value + rbuf[half, ring - 2, part]


def ring_scatter(x, axis, ring, with_sib, parts, collective_id):
    total, w = x.shape
    copies = 2 if with_sib else 1
    m = total // (copies * ring)
    sib_rows = ring * m if with_sib else 8
    return pl.pallas_call(
        functools.partial(scatter_kernel, axis, ring, m, with_sib, parts),
        out_shape=jax.ShapeDtypeStruct((m, w), x.dtype),
        in_specs=[pl.BlockSpec(memory_space=pltpu.VMEM)],
        out_specs=pl.BlockSpec(memory_space=pltpu.VMEM),
        scratch_shapes=[
            pltpu.VMEM((2, ring - 1, parts, m // 2 // parts, w), x.dtype),
            pltpu.VMEM((2, ring - 1, parts, m // 2 // parts, w), x.dtype),
            pltpu.VMEM((sib_rows, w), x.dtype),
            pltpu.SemaphoreType.DMA((2 * ring * parts,)),
            pltpu.SemaphoreType.DMA((2 * ring * parts,)),
            (pltpu.SemaphoreType.DMA((2 * ring,)), pltpu.SemaphoreType.DMA((2 * ring,))),
        ],
        compiler_params=pltpu.CompilerParams(
            collective_id=collective_id, has_side_effects=True, vmem_limit_bytes=60 * 1024 * 1024
        ),
    )(x)


def on_device(ring, cols, tokens, w_query, w_key, w_value, w_out):
    highest = lax.Precision.HIGH
    gathered = ring_gather(tokens, "col", cols, False, 2)
    q_width = w_query.shape[1]
    kv_width = w_key.shape[1]

    def product(weight):
        return jnp.dot(gathered, weight, preferred_element_type=jnp.float32, precision=highest)

    partial = product(jnp.concatenate([w_query, w_key, w_value], axis=1))
    joined = ring_scatter(partial, "rz", ring, True, 4, 3)
    query_rows = joined[:, :q_width]
    all_kv = ring_gather(joined[:, q_width:], "rz", ring, True, 0)
    state_end = fold_keys(
        query_rows,
        start_state(query_rows, kv_width),
        (all_kv[:, :kv_width], all_kv[:, kv_width:]),
    )
    set_attended = ring_gather(finish(state_end), "rz", ring, True, 1)
    return ring_scatter(
        jnp.dot(set_attended, w_out, preferred_element_type=jnp.float32, precision=highest),
        "col",
        cols,
        False,
        4,
        4,
    )


def solution(mesh):
    depth, row, col = (mesh.shape[a] for a in ("depth", "row", "col"))
    split = jax.sharding.Mesh(
        np.asarray(mesh.devices).reshape(depth, row // 2, 2, col), ("depth", "rz", "rc", "col")
    )
    rows = ("rz", "rc")
    placed = (
        P(("depth", "col"), rows),
        P(rows, "col"),
        P(rows, "col"),
        P(rows, "col"),
        P("col", rows),
    )
    return jax.shard_map(
        functools.partial(on_device, row // 2, col),
        mesh=split,
        in_specs=placed,
        out_specs=P(("depth", "col"), rows),
        check_vma=False,
    )
```

```python
import functools
import math

import jax
import numpy as np
import jax.numpy as jnp
from jax import lax
from jax.experimental import pallas as pl
from jax.experimental.pallas import tpu as pltpu
from jax.sharding import PartitionSpec as P

QUERY_HEADS = 32
KEY_VALUE_HEADS = 4
HEAD_SIZE_DIM = 128


def start_state(query_rows, kv_width):
    count_of_heads = kv_width // HEAD_SIZE_DIM
    queries_per_group = QUERY_HEADS // KEY_VALUE_HEADS
    count_of_rows = query_rows.shape[0]
    running_max = jnp.full((count_of_heads, queries_per_group, count_of_rows), -1e30, jnp.float32)
    running_sum = jnp.zeros((count_of_heads, queries_per_group, count_of_rows), jnp.float32)
    weighted = jnp.zeros(
        (count_of_heads, queries_per_group, count_of_rows, HEAD_SIZE_DIM), jnp.float32
    )
    return (running_max, running_sum, weighted)


def fold_keys(query_rows, state_now, block_pair):
    highest = lax.Precision.HIGH
    running_max, running_sum, weighted = state_now
    key_block, value_block = block_pair
    count_of_heads = key_block.shape[1] // HEAD_SIZE_DIM
    count_of_rows = query_rows.shape[0]
    query_head_rows = query_rows.reshape(
        count_of_rows, count_of_heads, QUERY_HEADS // KEY_VALUE_HEADS, HEAD_SIZE_DIM
    )
    key_head_rows = key_block.reshape(-1, count_of_heads, HEAD_SIZE_DIM)
    value_head_rows = value_block.reshape(-1, count_of_heads, HEAD_SIZE_DIM)
    scores = jnp.einsum("rkgd,nkd->kgrn", query_head_rows, key_head_rows, precision=highest) * (
        1.0 / math.sqrt(HEAD_SIZE_DIM)
    )
    newest = jnp.maximum(running_max, jnp.max(scores, axis=-1))
    weights = jnp.exp(scores - newest[..., None])
    running_sum = jnp.sum(weights, axis=-1)
    weighted = jnp.einsum("kgrn,nkd->kgrd", weights, value_head_rows, precision=highest)
    return (newest, running_sum, weighted)


def finish(state_now):
    running_max, running_sum, weighted = state_now
    attention_output = weighted / running_sum[..., None]
    count_of_heads, queries_per_group, count_of_rows, head_size = attention_output.shape
    return attention_output.transpose(2, 0, 1, 3).reshape(
        count_of_rows, count_of_heads * queries_per_group * head_size
    )


def gather_kernel(axis, ring, n, with_sib, x_ref, out_ref, local_sem, send_sems, recv_sems):
    mesh_id = pl.DeviceIdType.MESH
    names = ("depth", "rz", "rc", "col")
    me = {a: lax.axis_index(a) for a in names}
    pos = me[axis]

    def device(**moved):
        return tuple(moved.get(a, me[a]) for a in names)

    right = device(**{axis: lax.rem(pos + 1, ring)})
    left = device(**{axis: lax.rem(pos + ring - 1, ring)})
    sib = device(rc=1 - me["rc"])
    peers = (left, right, sib) if with_sib else (left, right)

    barrier = pltpu.get_barrier_semaphore()
    for peer in peers:
        pl.semaphore_signal(barrier, inc=1, device_id=peer, device_id_type=mesh_id)
    pl.semaphore_wait(barrier, len(peers))

    def rows(at, lo=0, size=n):
        slot = at * 2 + me["rc"] if with_sib else at
        return pl.ds(pl.multiple_of(slot * n + lo, 8), size)

    def remote(src, dst_rows, peer, idx):
        cp = pltpu.make_async_remote_copy(
            src_ref=src,
            dst_ref=out_ref.at[dst_rows],
            send_sem=send_sems.at[idx],
            recv_sem=recv_sems.at[idx],
            device_id=peer,
            device_id_type=mesh_id,
        )
        cp.start()
        return cp

    def to_sib(at, idx):
        if with_sib:
            sib_copies.append(remote(out_ref.at[rows(at)], rows(at), sib, idx))

    local = pltpu.make_async_copy(x_ref, out_ref.at[rows(pos)], local_sem)
    local.start()
    sib_copies = [remote(x_ref, rows(pos), sib, ring)] if with_sib else []
    half = ring // 2
    for s in range(1, half + 1):
        origin_r = lax.rem(pos - (s - 1) + ring, ring)
        origin_l = lax.rem(pos + (s - 1), ring)
        src_r = x_ref if s == 1 else out_ref.at[rows(origin_r)]
        src_l = x_ref if s == 1 else out_ref.at[rows(origin_l)]
        if s < half:
            cr = remote(src_r, rows(origin_r), right, 2 * (s - 1))
            cl = remote(src_l, rows(origin_l), left, 2 * (s - 1) + 1)
            cr.wait()
            cl.wait()
            to_sib(lax.rem(pos - s + ring, ring), ring + 2 * s - 1)
            to_sib(lax.rem(pos + s, ring), ring + 2 * s)
        else:
            h = n // 2
            cr = remote(src_r.at[pl.ds(0, h)], rows(origin_r, 0, h), right, 2 * (s - 1))
            cl = remote(src_l.at[pl.ds(h, h)], rows(origin_l, h, h), left, 2 * (s - 1) + 1)
            cr.wait()
            cl.wait()
            to_sib(lax.rem(pos + half, ring), ring + 2 * s - 1)
    local.wait()
    for cp in sib_copies:
        cp.wait()


def ring_gather(block, axis, ring, with_sib, collective_id):
    n, w = block.shape
    copies = 2 if with_sib else 1
    return pl.pallas_call(
        functools.partial(gather_kernel, axis, ring, n, with_sib),
        out_shape=jax.ShapeDtypeStruct((copies * ring * n, w), block.dtype),
        in_specs=[pl.BlockSpec(memory_space=pl.ANY)],
        out_specs=pl.BlockSpec(memory_space=pl.ANY),
        scratch_shapes=[
            pltpu.SemaphoreType.DMA(()),
            pltpu.SemaphoreType.DMA((2 * ring,)),
            pltpu.SemaphoreType.DMA((2 * ring,)),
        ],
        compiler_params=pltpu.CompilerParams(collective_id=collective_id, has_side_effects=True),
    )(block)


def scatter_kernel(axis, ring, m, with_sib, parts, x_ref, out_ref, sbuf, rbuf, sibbuf, send_sems, recv_sems, sib_sems):
    mesh_id = pl.DeviceIdType.MESH
    names = ("depth", "rz", "rc", "col")
    me = {a: lax.axis_index(a) for a in names}
    pos = me[axis]
    h = m // 2
    q = h // parts

    def device(**moved):
        return tuple(moved.get(a, me[a]) for a in names)

    right = device(**{axis: lax.rem(pos + 1, ring)})
    left = device(**{axis: lax.rem(pos + ring - 1, ring)})
    sib = device(rc=1 - me["rc"])
    peers = (left, right, sib) if with_sib else (left, right)

    barrier = pltpu.get_barrier_semaphore()
    for peer in peers:
        pl.semaphore_signal(barrier, inc=1, device_id=peer, device_id_type=mesh_id)
    pl.semaphore_wait(barrier, len(peers))

    def rows_of(at, half, part, owner):
        slot = at * 2 + owner if with_sib else at
        return pl.ds(pl.multiple_of(slot * m + half * h + part * q, 8), q)

    def sib_rows(at, half, part):
        return pl.ds(pl.multiple_of(at * m + half * h + part * q, 8), q)

    def remote(src, dst, peer, sems, idx):
        cp = pltpu.make_async_remote_copy(
            src_ref=src,
            dst_ref=dst,
            send_sem=sems[0].at[idx],
            recv_sem=sems[1].at[idx],
            device_id=peer,
            device_id_type=mesh_id,
        )
        cp.start()
        return cp

    def need(s, half):
        sign = -1 if half == 0 else 1
        return lax.rem(pos + sign * (s % ring) + ring * ring, ring)

    sib_copies = {}
    if with_sib:
        order = [(s, half) for s in range(1, ring + 1) for half in (0, 1)]
        for idx, (s, half) in enumerate(order):
            at = need(s, half)
            sib_copies[(s, half)] = remote(
                x_ref.at[pl.ds(pl.multiple_of((at * 2 + 1 - me["rc"]) * m + half * h, 8), h)],
                sibbuf.at[pl.ds(pl.multiple_of(at * m + half * h, 8), h)],
                sib,
                (sib_sems[0], sib_sems[1]),
                idx,
            )

    def contribution(s, half, part):
        at = need(s, half)
        own = x_ref[rows_of(at, half, part, me["rc"])]
        if with_sib:
            if part == 0:
                sib_copies[(s, half)].wait()
            own = own + sibbuf[sib_rows(at, half, part)]
        return own

    ring_copies = {}
    for s in range(1, ring):
        for part in range(parts):
            for half in (0, 1):
                value = contribution(s, half, part)
                if s > 1:
                    ring_copies[(s - 1, half, part)].wait()
                    value = value + rbuf[half, s - 2, part]
                sbuf[half, s - 1, part] = value
                ring_copies[(s, half, part)] = remote(
                    sbuf.at[half, s - 1, part],
                    rbuf.at[half, s - 1, part],
                    right if half == 0 else left,
                    (send_sems, recv_sems),
                    (half * (ring - 1) + s - 1) * parts + part,
                )
    for part in range(parts):
        for half in (0, 1):
            value = contribution(ring, half, part)
            ring_copies[(ring - 1, half, part)].wait()
            out_ref[pl.ds(half * h + part * q, q)] = value + rbuf[half, ring - 2, part]


def ring_scatter(x, axis, ring, with_sib, parts, collective_id):
    total, w = x.shape
    copies = 2 if with_sib else 1
    m = total // (copies * ring)
    sib_rows = ring * m if with_sib else 8
    return pl.pallas_call(
        functools.partial(scatter_kernel, axis, ring, m, with_sib, parts),
        out_shape=jax.ShapeDtypeStruct((m, w), x.dtype),
        in_specs=[pl.BlockSpec(memory_space=pltpu.VMEM)],
        out_specs=pl.BlockSpec(memory_space=pltpu.VMEM),
        scratch_shapes=[
            pltpu.VMEM((2, ring - 1, parts, m // 2 // parts, w), x.dtype),
            pltpu.VMEM((2, ring - 1, parts, m // 2 // parts, w), x.dtype),
            pltpu.VMEM((sib_rows, w), x.dtype),
            pltpu.SemaphoreType.DMA((2 * ring * parts,)),
            pltpu.SemaphoreType.DMA((2 * ring * parts,)),
            (pltpu.SemaphoreType.DMA((2 * ring,)), pltpu.SemaphoreType.DMA((2 * ring,))),
        ],
        compiler_params=pltpu.CompilerParams(
            collective_id=collective_id, has_side_effects=True, vmem_limit_bytes=60 * 1024 * 1024
        ),
    )(x)


def mix_kernel(ring, cols, n, o_ref, wo_ref, out_ref, ogath, part, recv, send_sems, recv_sems, y_send, y_recv):
    mesh_id = pl.DeviceIdType.MESH
    names = ("depth", "rz", "rc", "col")
    me = {a: lax.axis_index(a) for a in names}
    z, c, y = me["rz"], me["rc"], me["col"]
    per_col = 2 * ring // cols

    def device(**moved):
        return tuple(moved.get(a, me[a]) for a in names)

    right = device(rz=lax.rem(z + 1, ring))
    left = device(rz=lax.rem(z + ring - 1, ring))
    sib = device(rc=1 - c)
    peers = [left, right, sib] + [device(col=lax.rem(y + d, cols)) for d in range(1, cols)]

    barrier = pltpu.get_barrier_semaphore()
    for peer in peers:
        pl.semaphore_signal(barrier, inc=1, device_id=peer, device_id_type=mesh_id)
    pl.semaphore_wait(barrier, len(peers))

    def remote(src, dst, peer, send, recv_sem):
        cp = pltpu.make_async_remote_copy(
            src_ref=src, dst_ref=dst, send_sem=send, recv_sem=recv_sem, device_id=peer, device_id_type=mesh_id
        )
        cp.start()
        return cp

    def project(block, k):
        part[k] = jnp.dot(block, wo_ref[...], preferred_element_type=jnp.float32, precision=lax.Precision.HIGH)
        dest = k // per_col

        @pl.when(dest != y)
        def _():
            remote(
                part.at[k],
                recv.at[lax.rem(y - dest + cols, cols), lax.rem(k, per_col)],
                device(col=dest),
                y_send.at[k],
                y_recv.at[lax.rem(y - dest + cols, cols) * per_col + lax.rem(k, per_col)],
            )

    def slot(zz, cc):
        return zz * 2 + cc

    def z_copy(src, dst_slot, lo, size, peer, idx):
        return remote(src, ogath.at[dst_slot, pl.ds(lo, size)], peer, send_sems.at[idx], recv_sems.at[idx])

    project(o_ref[...], slot(z, c))
    pending_sib = [(z_copy(o_ref, slot(z, c), 0, n, sib, ring), z)]
    half = ring // 2
    for s in range(1, half + 1):
        origin_r = lax.rem(z - (s - 1) + ring, ring)
        origin_l = lax.rem(z + (s - 1), ring)
        src_r = o_ref if s == 1 else ogath.at[slot(origin_r, c)]
        src_l = o_ref if s == 1 else ogath.at[slot(origin_l, c)]
        if s < half:
            cr = z_copy(src_r, slot(origin_r, c), 0, n, right, 2 * (s - 1))
            cl = z_copy(src_l, slot(origin_l, c), 0, n, left, 2 * (s - 1) + 1)
        else:
            h = n // 2
            cr = z_copy(src_r.at[pl.ds(0, h)], slot(origin_r, c), 0, h, right, 2 * (s - 1))
            cl = z_copy(src_l.at[pl.ds(h, h)], slot(origin_l, c), h, h, left, 2 * (s - 1) + 1)
        for cp, at in pending_sib:
            cp.wait()
            project(ogath[slot(at, 1 - c)], slot(at, 1 - c))
        pending_sib = []
        cr.wait()
        cl.wait()
        if s < half:
            arrived = [(lax.rem(z - s + ring, ring), ring + 2 * s - 1), (lax.rem(z + s, ring), ring + 2 * s)]
        else:
            arrived = [(lax.rem(z + half, ring), ring + 2 * s - 1)]
        for at, idx in arrived:
            pending_sib.append((z_copy(ogath.at[slot(at, c)], slot(at, c), 0, n, sib, idx), at))
            project(ogath[slot(at, c)], slot(at, c))
    for cp, at in pending_sib:
        cp.wait()
        project(ogath[slot(at, 1 - c)], slot(at, 1 - c))
    for i in range(per_col):
        total = part[y * per_col + i]
        for d in range(1, cols):
            pltpu.make_async_remote_copy(
                src_ref=part.at[0],
                dst_ref=recv.at[d, i],
                send_sem=y_send.at[0],
                recv_sem=y_recv.at[d * per_col + i],
                device_id=device(col=lax.rem(y + d, cols)),
                device_id_type=mesh_id,
            ).wait_recv()
            total = total + recv[d, i]
        out_ref[pl.ds(i * n, n)] = total
    for k in range(2 * ring):
        @pl.when(k // per_col != y)
        def _():
            pltpu.make_async_remote_copy(
                src_ref=part.at[k],
                dst_ref=recv.at[0, 0],
                send_sem=y_send.at[k],
                recv_sem=y_recv.at[0],
                device_id=device(col=lax.rem(y + 1, cols)),
                device_id_type=mesh_id,
            ).wait_send()


def gather_mix(o, w_out, ring, cols, collective_id):
    n, width = o.shape
    out_w = w_out.shape[1]
    per_col = 2 * ring // cols
    return pl.pallas_call(
        functools.partial(mix_kernel, ring, cols, n),
        out_shape=jax.ShapeDtypeStruct((per_col * n, out_w), jnp.float32),
        in_specs=[pl.BlockSpec(memory_space=pltpu.VMEM), pl.BlockSpec(memory_space=pltpu.VMEM)],
        out_specs=pl.BlockSpec(memory_space=pltpu.VMEM),
        scratch_shapes=[
            pltpu.VMEM((2 * ring, n, width), jnp.float32),
            pltpu.VMEM((2 * ring, n, out_w), jnp.float32),
            pltpu.VMEM((cols, per_col, n, out_w), jnp.float32),
            pltpu.SemaphoreType.DMA((2 * ring,)),
            pltpu.SemaphoreType.DMA((2 * ring,)),
            pltpu.SemaphoreType.DMA((2 * ring,)),
            pltpu.SemaphoreType.DMA((cols * per_col,)),
        ],
        compiler_params=pltpu.CompilerParams(
            collective_id=collective_id, has_side_effects=True, vmem_limit_bytes=60 * 1024 * 1024
        ),
    )(o, w_out)


def on_device(ring, cols, tokens, w_query, w_key, w_value, w_out):
    highest = lax.Precision.HIGH
    gathered = ring_gather(tokens, "col", cols, False, 2)
    q_width = w_query.shape[1]
    kv_width = w_key.shape[1]

    def product(weight):
        return jnp.dot(gathered, weight, preferred_element_type=jnp.float32, precision=highest)

    partial = product(jnp.concatenate([w_query, w_key, w_value], axis=1))
    joined = ring_scatter(partial, "rz", ring, True, 4, 3)
    query_rows = joined[:, :q_width]
    all_kv = ring_gather(joined[:, q_width:], "rz", ring, True, 0)
    state_end = fold_keys(
        query_rows,
        start_state(query_rows, kv_width),
        (all_kv[:, :kv_width], all_kv[:, kv_width:]),
    )
    return gather_mix(finish(state_end), w_out, ring, cols, 5)


def solution(mesh):
    depth, row, col = (mesh.shape[a] for a in ("depth", "row", "col"))
    split = jax.sharding.Mesh(
        np.asarray(mesh.devices).reshape(depth, row // 2, 2, col), ("depth", "rz", "rc", "col")
    )
    rows = ("rz", "rc")
    placed = (
        P(("depth", "col"), rows),
        P(rows, "col"),
        P(rows, "col"),
        P(rows, "col"),
        P("col", rows),
    )
    return jax.shard_map(
        functools.partial(on_device, row // 2, col),
        mesh=split,
        in_specs=placed,
        out_specs=P(("depth", "col"), rows),
        check_vma=False,
    )
```

```python
import functools
import math

import jax
import numpy as np
import jax.numpy as jnp
from jax import lax
from jax.experimental import pallas as pl
from jax.experimental.pallas import tpu as pltpu
from jax.sharding import PartitionSpec as P

QUERY_HEADS = 32
KEY_VALUE_HEADS = 4
HEAD_SIZE_DIM = 128


def start_state(query_rows, kv_width):
    count_of_heads = kv_width // HEAD_SIZE_DIM
    queries_per_group = QUERY_HEADS // KEY_VALUE_HEADS
    count_of_rows = query_rows.shape[0]
    running_max = jnp.full((count_of_heads, queries_per_group, count_of_rows), -1e30, jnp.float32)
    running_sum = jnp.zeros((count_of_heads, queries_per_group, count_of_rows), jnp.float32)
    weighted = jnp.zeros(
        (count_of_heads, queries_per_group, count_of_rows, HEAD_SIZE_DIM), jnp.float32
    )
    return (running_max, running_sum, weighted)


def fold_keys(query_rows, state_now, block_pair):
    highest = lax.Precision.HIGH
    running_max, running_sum, weighted = state_now
    key_block, value_block = block_pair
    count_of_heads = key_block.shape[1] // HEAD_SIZE_DIM
    count_of_rows = query_rows.shape[0]
    query_head_rows = query_rows.reshape(
        count_of_rows, count_of_heads, QUERY_HEADS // KEY_VALUE_HEADS, HEAD_SIZE_DIM
    )
    key_head_rows = key_block.reshape(-1, count_of_heads, HEAD_SIZE_DIM)
    value_head_rows = value_block.reshape(-1, count_of_heads, HEAD_SIZE_DIM)
    scores = jnp.einsum("rkgd,nkd->kgrn", query_head_rows, key_head_rows, precision=highest) * (
        1.0 / math.sqrt(HEAD_SIZE_DIM)
    )
    newest = jnp.maximum(running_max, jnp.max(scores, axis=-1))
    weights = jnp.exp(scores - newest[..., None])
    running_sum = jnp.sum(weights, axis=-1)
    weighted = jnp.einsum("kgrn,nkd->kgrd", weights, value_head_rows, precision=highest)
    return (newest, running_sum, weighted)


def finish(state_now):
    running_max, running_sum, weighted = state_now
    attention_output = weighted / running_sum[..., None]
    count_of_heads, queries_per_group, count_of_rows, head_size = attention_output.shape
    return attention_output.transpose(2, 0, 1, 3).reshape(
        count_of_rows, count_of_heads * queries_per_group * head_size
    )


def gather_kernel(axis, ring, n, with_sib, x_ref, out_ref, local_sem, send_sems, recv_sems):
    mesh_id = pl.DeviceIdType.MESH
    names = ("depth", "rz", "rc", "col")
    me = {a: lax.axis_index(a) for a in names}
    pos = me[axis]

    def device(**moved):
        return tuple(moved.get(a, me[a]) for a in names)

    right = device(**{axis: lax.rem(pos + 1, ring)})
    left = device(**{axis: lax.rem(pos + ring - 1, ring)})
    sib = device(rc=1 - me["rc"])
    peers = (left, right, sib) if with_sib else (left, right)

    barrier = pltpu.get_barrier_semaphore()
    for peer in peers:
        pl.semaphore_signal(barrier, inc=1, device_id=peer, device_id_type=mesh_id)
    pl.semaphore_wait(barrier, len(peers))

    def rows(at, lo=0, size=n):
        slot = at * 2 + me["rc"] if with_sib else at
        return pl.ds(pl.multiple_of(slot * n + lo, 8), size)

    def remote(src, dst_rows, peer, idx):
        cp = pltpu.make_async_remote_copy(
            src_ref=src,
            dst_ref=out_ref.at[dst_rows],
            send_sem=send_sems.at[idx],
            recv_sem=recv_sems.at[idx],
            device_id=peer,
            device_id_type=mesh_id,
        )
        cp.start()
        return cp

    def to_sib(at, idx):
        if with_sib:
            sib_copies.append(remote(out_ref.at[rows(at)], rows(at), sib, idx))

    local = pltpu.make_async_copy(x_ref, out_ref.at[rows(pos)], local_sem)
    local.start()
    sib_copies = [remote(x_ref, rows(pos), sib, ring)] if with_sib else []
    half = ring // 2
    for s in range(1, half + 1):
        origin_r = lax.rem(pos - (s - 1) + ring, ring)
        origin_l = lax.rem(pos + (s - 1), ring)
        src_r = x_ref if s == 1 else out_ref.at[rows(origin_r)]
        src_l = x_ref if s == 1 else out_ref.at[rows(origin_l)]
        if s < half:
            cr = remote(src_r, rows(origin_r), right, 2 * (s - 1))
            cl = remote(src_l, rows(origin_l), left, 2 * (s - 1) + 1)
            cr.wait()
            cl.wait()
            to_sib(lax.rem(pos - s + ring, ring), ring + 2 * s - 1)
            to_sib(lax.rem(pos + s, ring), ring + 2 * s)
        else:
            h = n // 2
            cr = remote(src_r.at[pl.ds(0, h)], rows(origin_r, 0, h), right, 2 * (s - 1))
            cl = remote(src_l.at[pl.ds(h, h)], rows(origin_l, h, h), left, 2 * (s - 1) + 1)
            cr.wait()
            cl.wait()
            to_sib(lax.rem(pos + half, ring), ring + 2 * s - 1)
    local.wait()
    for cp in sib_copies:
        cp.wait()


def ring_gather(block, axis, ring, with_sib, collective_id):
    n, w = block.shape
    copies = 2 if with_sib else 1
    return pl.pallas_call(
        functools.partial(gather_kernel, axis, ring, n, with_sib),
        out_shape=jax.ShapeDtypeStruct((copies * ring * n, w), block.dtype),
        in_specs=[pl.BlockSpec(memory_space=pl.ANY)],
        out_specs=pl.BlockSpec(memory_space=pl.ANY),
        scratch_shapes=[
            pltpu.SemaphoreType.DMA(()),
            pltpu.SemaphoreType.DMA((2 * ring,)),
            pltpu.SemaphoreType.DMA((2 * ring,)),
        ],
        compiler_params=pltpu.CompilerParams(collective_id=collective_id, has_side_effects=True),
    )(block)


def scatter_kernel(axis, ring, m, with_sib, parts, x_ref, out_ref, sbuf, rbuf, sibbuf, send_sems, recv_sems, sib_sems):
    mesh_id = pl.DeviceIdType.MESH
    names = ("depth", "rz", "rc", "col")
    me = {a: lax.axis_index(a) for a in names}
    pos = me[axis]
    h = m // 2
    q = h // parts

    def device(**moved):
        return tuple(moved.get(a, me[a]) for a in names)

    right = device(**{axis: lax.rem(pos + 1, ring)})
    left = device(**{axis: lax.rem(pos + ring - 1, ring)})
    sib = device(rc=1 - me["rc"])
    peers = (left, right, sib) if with_sib else (left, right)

    barrier = pltpu.get_barrier_semaphore()
    for peer in peers:
        pl.semaphore_signal(barrier, inc=1, device_id=peer, device_id_type=mesh_id)
    pl.semaphore_wait(barrier, len(peers))

    def rows_of(at, half, part, owner):
        slot = at * 2 + owner if with_sib else at
        return pl.ds(pl.multiple_of(slot * m + half * h + part * q, 8), q)

    def sib_rows(at, half, part):
        return pl.ds(pl.multiple_of(at * m + half * h + part * q, 8), q)

    def remote(src, dst, peer, sems, idx):
        cp = pltpu.make_async_remote_copy(
            src_ref=src,
            dst_ref=dst,
            send_sem=sems[0].at[idx],
            recv_sem=sems[1].at[idx],
            device_id=peer,
            device_id_type=mesh_id,
        )
        cp.start()
        return cp

    def need(s, half):
        sign = -1 if half == 0 else 1
        return lax.rem(pos + sign * (s % ring) + ring * ring, ring)

    sib_copies = {}
    if with_sib:
        order = [(s, half) for s in range(1, ring + 1) for half in (0, 1)]
        for idx, (s, half) in enumerate(order):
            at = need(s, half)
            sib_copies[(s, half)] = remote(
                x_ref.at[pl.ds(pl.multiple_of((at * 2 + 1 - me["rc"]) * m + half * h, 8), h)],
                sibbuf.at[pl.ds(pl.multiple_of(at * m + half * h, 8), h)],
                sib,
                (sib_sems[0], sib_sems[1]),
                idx,
            )

    def contribution(s, half, part):
        at = need(s, half)
        own = x_ref[rows_of(at, half, part, me["rc"])]
        if with_sib:
            if part == 0:
                sib_copies[(s, half)].wait()
            own = own + sibbuf[sib_rows(at, half, part)]
        return own

    ring_copies = {}
    for s in range(1, ring):
        for part in range(parts):
            for half in (0, 1):
                value = contribution(s, half, part)
                if s > 1:
                    ring_copies[(s - 1, half, part)].wait()
                    value = value + rbuf[half, s - 2, part]
                sbuf[half, s - 1, part] = value
                ring_copies[(s, half, part)] = remote(
                    sbuf.at[half, s - 1, part],
                    rbuf.at[half, s - 1, part],
                    right if half == 0 else left,
                    (send_sems, recv_sems),
                    (half * (ring - 1) + s - 1) * parts + part,
                )
    for part in range(parts):
        for half in (0, 1):
            value = contribution(ring, half, part)
            ring_copies[(ring - 1, half, part)].wait()
            out_ref[pl.ds(half * h + part * q, q)] = value + rbuf[half, ring - 2, part]


def ring_scatter(x, axis, ring, with_sib, parts, collective_id):
    total, w = x.shape
    copies = 2 if with_sib else 1
    m = total // (copies * ring)
    sib_rows = ring * m if with_sib else 8
    return pl.pallas_call(
        functools.partial(scatter_kernel, axis, ring, m, with_sib, parts),
        out_shape=jax.ShapeDtypeStruct((m, w), x.dtype),
        in_specs=[pl.BlockSpec(memory_space=pltpu.VMEM)],
        out_specs=pl.BlockSpec(memory_space=pltpu.VMEM),
        scratch_shapes=[
            pltpu.VMEM((2, ring - 1, parts, m // 2 // parts, w), x.dtype),
            pltpu.VMEM((2, ring - 1, parts, m // 2 // parts, w), x.dtype),
            pltpu.VMEM((sib_rows, w), x.dtype),
            pltpu.SemaphoreType.DMA((2 * ring * parts,)),
            pltpu.SemaphoreType.DMA((2 * ring * parts,)),
            (pltpu.SemaphoreType.DMA((2 * ring,)), pltpu.SemaphoreType.DMA((2 * ring,))),
        ],
        compiler_params=pltpu.CompilerParams(
            collective_id=collective_id, has_side_effects=True, vmem_limit_bytes=60 * 1024 * 1024
        ),
    )(x)


def mix_kernel(ring, cols, n, o_ref, wo_ref, out_ref, ogath, part, recv, send_sems, recv_sems, y_send, y_recv):
    mesh_id = pl.DeviceIdType.MESH
    names = ("depth", "rz", "rc", "col")
    me = {a: lax.axis_index(a) for a in names}
    z, c, y = me["rz"], me["rc"], me["col"]
    per_col = 2 * ring // cols

    def device(**moved):
        return tuple(moved.get(a, me[a]) for a in names)

    right = device(rz=lax.rem(z + 1, ring))
    left = device(rz=lax.rem(z + ring - 1, ring))
    sib = device(rc=1 - c)
    peers = [left, right, sib] + [device(col=lax.rem(y + d, cols)) for d in range(1, cols)]

    barrier = pltpu.get_barrier_semaphore()
    for peer in peers:
        pl.semaphore_signal(barrier, inc=1, device_id=peer, device_id_type=mesh_id)
    pl.semaphore_wait(barrier, len(peers))

    def remote(src, dst, peer, send, recv_sem):
        cp = pltpu.make_async_remote_copy(
            src_ref=src, dst_ref=dst, send_sem=send, recv_sem=recv_sem, device_id=peer, device_id_type=mesh_id
        )
        cp.start()
        return cp

    piece = n // cols

    def project(block, k):
        part[k] = jnp.dot(block, wo_ref[...], preferred_element_type=jnp.float32, precision=lax.Precision.HIGH)
        for d in range(1, cols):
            dest = lax.rem(y + d, cols)
            remote(
                part.at[k, pl.ds(pl.multiple_of(dest * piece, 8), piece)],
                recv.at[cols - d, k],
                device(col=dest),
                y_send.at[k * cols + d],
                y_recv.at[(cols - d) * 2 * ring + k],
            )

    def slot(zz, cc):
        return zz * 2 + cc

    def z_copy(src, dst_slot, lo, size, peer, idx):
        return remote(src, ogath.at[dst_slot, pl.ds(lo, size)], peer, send_sems.at[idx], recv_sems.at[idx])

    project(o_ref[...], slot(z, c))
    pending_sib = [(z_copy(o_ref, slot(z, c), 0, n, sib, ring), z)]
    half = ring // 2
    for s in range(1, half + 1):
        origin_r = lax.rem(z - (s - 1) + ring, ring)
        origin_l = lax.rem(z + (s - 1), ring)
        src_r = o_ref if s == 1 else ogath.at[slot(origin_r, c)]
        src_l = o_ref if s == 1 else ogath.at[slot(origin_l, c)]
        if s < half:
            cr = z_copy(src_r, slot(origin_r, c), 0, n, right, 2 * (s - 1))
            cl = z_copy(src_l, slot(origin_l, c), 0, n, left, 2 * (s - 1) + 1)
        else:
            h = n // 2
            cr = z_copy(src_r.at[pl.ds(0, h)], slot(origin_r, c), 0, h, right, 2 * (s - 1))
            cl = z_copy(src_l.at[pl.ds(h, h)], slot(origin_l, c), h, h, left, 2 * (s - 1) + 1)
        for cp, at in pending_sib:
            cp.wait()
            project(ogath[slot(at, 1 - c)], slot(at, 1 - c))
        pending_sib = []
        cr.wait()
        cl.wait()
        if s < half:
            arrived = [(lax.rem(z - s + ring, ring), ring + 2 * s - 1), (lax.rem(z + s, ring), ring + 2 * s)]
        else:
            arrived = [(lax.rem(z + half, ring), ring + 2 * s - 1)]
        for at, idx in arrived:
            pending_sib.append((z_copy(ogath.at[slot(at, c)], slot(at, c), 0, n, sib, idx), at))
            project(ogath[slot(at, c)], slot(at, c))
    for cp, at in pending_sib:
        cp.wait()
        project(ogath[slot(at, 1 - c)], slot(at, 1 - c))
    for k in range(2 * ring):
        total = part[k, pl.ds(pl.multiple_of(y * piece, 8), piece)]
        for d in range(1, cols):
            pltpu.make_async_remote_copy(
                src_ref=part.at[k, pl.ds(0, piece)],
                dst_ref=recv.at[d, k],
                send_sem=y_send.at[0],
                recv_sem=y_recv.at[d * 2 * ring + k],
                device_id=device(col=lax.rem(y + d, cols)),
                device_id_type=mesh_id,
            ).wait_recv()
            total = total + recv[d, k]
        out_ref[pl.ds(k * piece, piece)] = total
    for k in range(2 * ring):
        for d in range(1, cols):
            pltpu.make_async_remote_copy(
                src_ref=part.at[k, pl.ds(0, piece)],
                dst_ref=recv.at[0, 0],
                send_sem=y_send.at[k * cols + d],
                recv_sem=y_recv.at[0],
                device_id=device(col=lax.rem(y + d, cols)),
                device_id_type=mesh_id,
            ).wait_send()


def gather_mix(o, w_out, ring, cols, collective_id):
    n, width = o.shape
    out_w = w_out.shape[1]
    per_col = 2 * ring // cols
    return pl.pallas_call(
        functools.partial(mix_kernel, ring, cols, n),
        out_shape=jax.ShapeDtypeStruct((per_col * n, out_w), jnp.float32),
        in_specs=[pl.BlockSpec(memory_space=pltpu.VMEM), pl.BlockSpec(memory_space=pltpu.VMEM)],
        out_specs=pl.BlockSpec(memory_space=pltpu.VMEM),
        scratch_shapes=[
            pltpu.VMEM((2 * ring, n, width), jnp.float32),
            pltpu.VMEM((2 * ring, n, out_w), jnp.float32),
            pltpu.VMEM((cols, 2 * ring, n // cols, out_w), jnp.float32),
            pltpu.SemaphoreType.DMA((2 * ring,)),
            pltpu.SemaphoreType.DMA((2 * ring,)),
            pltpu.SemaphoreType.DMA((2 * ring * cols,)),
            pltpu.SemaphoreType.DMA((2 * ring * cols,)),
        ],
        compiler_params=pltpu.CompilerParams(
            collective_id=collective_id, has_side_effects=True, vmem_limit_bytes=60 * 1024 * 1024
        ),
    )(o, w_out)


def front_kernel(ring, cols, tok_ref, w_ref, out_ref, tg, partial, sibbuf, sbuf, rbuf, y_sems, z_sems, sib_sems):
    mesh_id = pl.DeviceIdType.MESH
    names = ("depth", "rz", "rc", "col")
    me = {a: lax.axis_index(a) for a in names}
    z, c, y = me["rz"], me["rc"], me["col"]
    rows = tok_ref.shape[0]
    m = rows // (2 * ring)
    h = m // 2

    def device(**moved):
        return tuple(moved.get(a, me[a]) for a in names)

    right = device(rz=lax.rem(z + 1, ring))
    left = device(rz=lax.rem(z + ring - 1, ring))
    sib = device(rc=1 - c)
    y_right = device(col=lax.rem(y + 1, cols))
    y_left = device(col=lax.rem(y + cols - 1, cols))
    peers = [left, right, sib, y_left, y_right]

    barrier = pltpu.get_barrier_semaphore()
    for peer in peers:
        pl.semaphore_signal(barrier, inc=1, device_id=peer, device_id_type=mesh_id)
    pl.semaphore_wait(barrier, len(peers))

    def remote(src, dst, peer, sems, idx):
        cp = pltpu.make_async_remote_copy(
            src_ref=src, dst_ref=dst, send_sem=sems[0].at[idx], recv_sem=sems[1].at[idx],
            device_id=peer, device_id_type=mesh_id,
        )
        cp.start()
        return cp

    def need(s, half):
        sign = -1 if half == 0 else 1
        return lax.rem(z + sign * (s % ring) + ring * ring, ring)

    def round_steps(r, chunk):
        x = partial.at[r]
        base = r * 2 * ring
        sib_copies = {}
        for idx, (s, half) in enumerate((s, half) for s in range(1, ring + 1) for half in (0, 1)):
            at = need(s, half)
            sib_copies[(s, half)] = remote(
                x.at[pl.ds(pl.multiple_of((at * 2 + 1 - c) * m + half * h, 8), h)],
                sibbuf.at[r, pl.ds(pl.multiple_of(at * m + half * h, 8), h)],
                sib, sib_sems, base + idx,
            )
        yield

        def contribution(s, half):
            at = need(s, half)
            sib_copies[(s, half)].wait()
            own = x[pl.ds(pl.multiple_of((at * 2 + c) * m + half * h, 8), h)]
            return own + sibbuf[r, pl.ds(pl.multiple_of(at * m + half * h, 8), h)]

        ring_copies = {}
        for s in range(1, ring):
            for half in (0, 1):
                value = contribution(s, half)
                if s > 1:
                    ring_copies[(s - 1, half)].wait()
                    value = value + rbuf[r, half, s - 2]
                sbuf[r, half, s - 1] = value
                ring_copies[(s, half)] = remote(
                    sbuf.at[r, half, s - 1], rbuf.at[r, half, s - 1],
                    right if half == 0 else left, z_sems, base + half * (ring - 1) + s - 1,
                )
            yield
        for half in (0, 1):
            value = contribution(ring, half)
            ring_copies[(ring - 1, half)].wait()
            out_ref[pl.ds(pl.multiple_of(chunk * m + half * h, 8), h)] = value + rbuf[r, half, ring - 2]
        yield

    def project(r, src):
        partial[r] = jnp.dot(src[...], w_ref[...], preferred_element_type=jnp.float32, precision=lax.Precision.HIGH)

    y1r = remote(tok_ref, tg.at[1], y_right, y_sems, 0)
    y1l = remote(tok_ref, tg.at[2], y_left, y_sems, 1)
    project(0, tok_ref)
    rounds = [round_steps(0, y)]
    next(rounds[0])
    next(rounds[0])
    next(rounds[0])
    y1r.wait()
    y1l.wait()
    half_rows = rows // 2
    y2r = remote(tg.at[1, pl.ds(0, half_rows)], tg.at[3, pl.ds(0, half_rows)], y_right, y_sems, 2)
    y2l = remote(tg.at[2, pl.ds(half_rows, half_rows)], tg.at[3, pl.ds(half_rows, half_rows)], y_left, y_sems, 3)
    project(1, tg.at[1])
    rounds.append(round_steps(1, lax.rem(y + cols - 1, cols)))
    next(rounds[1])
    project(2, tg.at[2])
    rounds.append(round_steps(2, lax.rem(y + 1, cols)))
    next(rounds[2])
    for _ in range(2):
        for g in rounds:
            next(g, None)
    y2r.wait()
    y2l.wait()
    project(3, tg.at[3])
    rounds.append(round_steps(3, lax.rem(y + 2, cols)))
    next(rounds[3])
    live = list(rounds)
    while live:
        live = [g for g in live if next(g, "done") != "done"]


def front(tokens, weights, ring, cols, collective_id):
    rows, width = tokens.shape
    out_w = weights.shape[1]
    m = rows // (2 * ring)
    return pl.pallas_call(
        functools.partial(front_kernel, ring, cols),
        out_shape=jax.ShapeDtypeStruct((cols * m, out_w), jnp.float32),
        in_specs=[pl.BlockSpec(memory_space=pltpu.VMEM), pl.BlockSpec(memory_space=pltpu.VMEM)],
        out_specs=pl.BlockSpec(memory_space=pltpu.VMEM),
        scratch_shapes=[
            pltpu.VMEM((cols, rows, width), jnp.float32),
            pltpu.VMEM((cols, rows, out_w), jnp.float32),
            pltpu.VMEM((cols, ring * m, out_w), jnp.float32),
            pltpu.VMEM((cols, 2, ring - 1, m // 2, out_w), jnp.float32),
            pltpu.VMEM((cols, 2, ring - 1, m // 2, out_w), jnp.float32),
            (pltpu.SemaphoreType.DMA((4,)), pltpu.SemaphoreType.DMA((4,))),
            (pltpu.SemaphoreType.DMA((cols * 2 * ring,)), pltpu.SemaphoreType.DMA((cols * 2 * ring,))),
            (pltpu.SemaphoreType.DMA((cols * 2 * ring,)), pltpu.SemaphoreType.DMA((cols * 2 * ring,))),
        ],
        compiler_params=pltpu.CompilerParams(
            collective_id=collective_id, has_side_effects=True, vmem_limit_bytes=60 * 1024 * 1024
        ),
    )(tokens, weights)


def on_device(ring, cols, tokens, w_query, w_key, w_value, w_out):
    highest = lax.Precision.HIGH
    q_width = w_query.shape[1]
    kv_width = w_key.shape[1]
    joined = front(tokens, jnp.concatenate([w_query, w_key, w_value], axis=1), ring, cols, 3)
    query_rows = joined[:, :q_width]
    all_kv = ring_gather(joined[:, q_width:], "rz", ring, True, 0)
    state_end = fold_keys(
        query_rows,
        start_state(query_rows, kv_width),
        (all_kv[:, :kv_width], all_kv[:, kv_width:]),
    )
    return gather_mix(finish(state_end), w_out, ring, cols, 5)


def solution(mesh):
    depth, row, col = (mesh.shape[a] for a in ("depth", "row", "col"))
    split = jax.sharding.Mesh(
        np.asarray(mesh.devices).reshape(depth, row // 2, 2, col), ("depth", "rz", "rc", "col")
    )
    rows = ("rz", "rc")
    placed = (
        P(("depth", "col"), rows),
        P(rows, "col"),
        P(rows, "col"),
        P(rows, "col"),
        P("col", rows),
    )
    return jax.shard_map(
        functools.partial(on_device, row // 2, col),
        mesh=split,
        in_specs=placed,
        out_specs=P(("depth", "col"), rows),
        check_vma=False,
    )
```

```python
import functools
import math

import jax
import numpy as np
import jax.numpy as jnp
from jax import lax
from jax.experimental import pallas as pl
from jax.experimental.pallas import tpu as pltpu
from jax.sharding import PartitionSpec as P

QUERY_HEADS = 32
KEY_VALUE_HEADS = 4
HEAD_SIZE_DIM = 128


def start_state(query_rows, kv_width):
    count_of_heads = kv_width // HEAD_SIZE_DIM
    queries_per_group = QUERY_HEADS // KEY_VALUE_HEADS
    count_of_rows = query_rows.shape[0]
    running_max = jnp.full((count_of_heads, queries_per_group, count_of_rows), -1e30, jnp.float32)
    running_sum = jnp.zeros((count_of_heads, queries_per_group, count_of_rows), jnp.float32)
    weighted = jnp.zeros(
        (count_of_heads, queries_per_group, count_of_rows, HEAD_SIZE_DIM), jnp.float32
    )
    return (running_max, running_sum, weighted)


def fold_keys(query_rows, state_now, block_pair):
    highest = lax.Precision.HIGH
    running_max, running_sum, weighted = state_now
    key_block, value_block = block_pair
    count_of_heads = key_block.shape[1] // HEAD_SIZE_DIM
    count_of_rows = query_rows.shape[0]
    query_head_rows = query_rows.reshape(
        count_of_rows, count_of_heads, QUERY_HEADS // KEY_VALUE_HEADS, HEAD_SIZE_DIM
    )
    key_head_rows = key_block.reshape(-1, count_of_heads, HEAD_SIZE_DIM)
    value_head_rows = value_block.reshape(-1, count_of_heads, HEAD_SIZE_DIM)
    scores = jnp.einsum("rkgd,nkd->kgrn", query_head_rows, key_head_rows, precision=highest) * (
        1.0 / math.sqrt(HEAD_SIZE_DIM)
    )
    newest = jnp.maximum(running_max, jnp.max(scores, axis=-1))
    weights = jnp.exp(scores - newest[..., None])
    running_sum = jnp.sum(weights, axis=-1)
    weighted = jnp.einsum("kgrn,nkd->kgrd", weights, value_head_rows, precision=highest)
    return (newest, running_sum, weighted)


def finish(state_now):
    running_max, running_sum, weighted = state_now
    attention_output = weighted / running_sum[..., None]
    count_of_heads, queries_per_group, count_of_rows, head_size = attention_output.shape
    return attention_output.transpose(2, 0, 1, 3).reshape(
        count_of_rows, count_of_heads * queries_per_group * head_size
    )


def gather_kernel(axis, ring, n, with_sib, x_ref, out_ref, local_sem, send_sems, recv_sems):
    mesh_id = pl.DeviceIdType.MESH
    names = ("depth", "rz", "rc", "col")
    me = {a: lax.axis_index(a) for a in names}
    pos = me[axis]

    def device(**moved):
        return tuple(moved.get(a, me[a]) for a in names)

    right = device(**{axis: lax.rem(pos + 1, ring)})
    left = device(**{axis: lax.rem(pos + ring - 1, ring)})
    sib = device(rc=1 - me["rc"])
    peers = (left, right, sib) if with_sib else (left, right)

    barrier = pltpu.get_barrier_semaphore()
    for peer in peers:
        pl.semaphore_signal(barrier, inc=1, device_id=peer, device_id_type=mesh_id)
    pl.semaphore_wait(barrier, len(peers))

    def rows(at, lo=0, size=n):
        slot = at * 2 + me["rc"] if with_sib else at
        return pl.ds(pl.multiple_of(slot * n + lo, 8), size)

    def remote(src, dst_rows, peer, idx):
        cp = pltpu.make_async_remote_copy(
            src_ref=src,
            dst_ref=out_ref.at[dst_rows],
            send_sem=send_sems.at[idx],
            recv_sem=recv_sems.at[idx],
            device_id=peer,
            device_id_type=mesh_id,
        )
        cp.start()
        return cp

    def to_sib(at, idx):
        if with_sib:
            sib_copies.append(remote(out_ref.at[rows(at)], rows(at), sib, idx))

    local = pltpu.make_async_copy(x_ref, out_ref.at[rows(pos)], local_sem)
    local.start()
    sib_copies = [remote(x_ref, rows(pos), sib, ring)] if with_sib else []
    half = ring // 2
    for s in range(1, half + 1):
        origin_r = lax.rem(pos - (s - 1) + ring, ring)
        origin_l = lax.rem(pos + (s - 1), ring)
        src_r = x_ref if s == 1 else out_ref.at[rows(origin_r)]
        src_l = x_ref if s == 1 else out_ref.at[rows(origin_l)]
        if s < half:
            cr = remote(src_r, rows(origin_r), right, 2 * (s - 1))
            cl = remote(src_l, rows(origin_l), left, 2 * (s - 1) + 1)
            cr.wait()
            cl.wait()
            to_sib(lax.rem(pos - s + ring, ring), ring + 2 * s - 1)
            to_sib(lax.rem(pos + s, ring), ring + 2 * s)
        else:
            h = n // 2
            cr = remote(src_r.at[pl.ds(0, h)], rows(origin_r, 0, h), right, 2 * (s - 1))
            cl = remote(src_l.at[pl.ds(h, h)], rows(origin_l, h, h), left, 2 * (s - 1) + 1)
            cr.wait()
            cl.wait()
            to_sib(lax.rem(pos + half, ring), ring + 2 * s - 1)
    local.wait()
    for cp in sib_copies:
        cp.wait()


def ring_gather(block, axis, ring, with_sib, collective_id):
    n, w = block.shape
    copies = 2 if with_sib else 1
    return pl.pallas_call(
        functools.partial(gather_kernel, axis, ring, n, with_sib),
        out_shape=jax.ShapeDtypeStruct((copies * ring * n, w), block.dtype),
        in_specs=[pl.BlockSpec(memory_space=pl.ANY)],
        out_specs=pl.BlockSpec(memory_space=pl.ANY),
        scratch_shapes=[
            pltpu.SemaphoreType.DMA(()),
            pltpu.SemaphoreType.DMA((2 * ring,)),
            pltpu.SemaphoreType.DMA((2 * ring,)),
        ],
        compiler_params=pltpu.CompilerParams(collective_id=collective_id, has_side_effects=True),
    )(block)


def scatter_kernel(axis, ring, m, with_sib, parts, x_ref, out_ref, sbuf, rbuf, sibbuf, send_sems, recv_sems, sib_sems):
    mesh_id = pl.DeviceIdType.MESH
    names = ("depth", "rz", "rc", "col")
    me = {a: lax.axis_index(a) for a in names}
    pos = me[axis]
    h = m // 2
    q = h // parts

    def device(**moved):
        return tuple(moved.get(a, me[a]) for a in names)

    right = device(**{axis: lax.rem(pos + 1, ring)})
    left = device(**{axis: lax.rem(pos + ring - 1, ring)})
    sib = device(rc=1 - me["rc"])
    peers = (left, right, sib) if with_sib else (left, right)

    barrier = pltpu.get_barrier_semaphore()
    for peer in peers:
        pl.semaphore_signal(barrier, inc=1, device_id=peer, device_id_type=mesh_id)
    pl.semaphore_wait(barrier, len(peers))

    def rows_of(at, half, part, owner):
        slot = at * 2 + owner if with_sib else at
        return pl.ds(pl.multiple_of(slot * m + half * h + part * q, 8), q)

    def sib_rows(at, half, part):
        return pl.ds(pl.multiple_of(at * m + half * h + part * q, 8), q)

    def remote(src, dst, peer, sems, idx):
        cp = pltpu.make_async_remote_copy(
            src_ref=src,
            dst_ref=dst,
            send_sem=sems[0].at[idx],
            recv_sem=sems[1].at[idx],
            device_id=peer,
            device_id_type=mesh_id,
        )
        cp.start()
        return cp

    def need(s, half):
        sign = -1 if half == 0 else 1
        return lax.rem(pos + sign * (s % ring) + ring * ring, ring)

    sib_copies = {}
    if with_sib:
        order = [(s, half) for s in range(1, ring + 1) for half in (0, 1)]
        for idx, (s, half) in enumerate(order):
            at = need(s, half)
            sib_copies[(s, half)] = remote(
                x_ref.at[pl.ds(pl.multiple_of((at * 2 + 1 - me["rc"]) * m + half * h, 8), h)],
                sibbuf.at[pl.ds(pl.multiple_of(at * m + half * h, 8), h)],
                sib,
                (sib_sems[0], sib_sems[1]),
                idx,
            )

    def contribution(s, half, part):
        at = need(s, half)
        own = x_ref[rows_of(at, half, part, me["rc"])]
        if with_sib:
            if part == 0:
                sib_copies[(s, half)].wait()
            own = own + sibbuf[sib_rows(at, half, part)]
        return own

    ring_copies = {}
    for s in range(1, ring):
        for part in range(parts):
            for half in (0, 1):
                value = contribution(s, half, part)
                if s > 1:
                    ring_copies[(s - 1, half, part)].wait()
                    value = value + rbuf[half, s - 2, part]
                sbuf[half, s - 1, part] = value
                ring_copies[(s, half, part)] = remote(
                    sbuf.at[half, s - 1, part],
                    rbuf.at[half, s - 1, part],
                    right if half == 0 else left,
                    (send_sems, recv_sems),
                    (half * (ring - 1) + s - 1) * parts + part,
                )
    for part in range(parts):
        for half in (0, 1):
            value = contribution(ring, half, part)
            ring_copies[(ring - 1, half, part)].wait()
            out_ref[pl.ds(half * h + part * q, q)] = value + rbuf[half, ring - 2, part]


def ring_scatter(x, axis, ring, with_sib, parts, collective_id):
    total, w = x.shape
    copies = 2 if with_sib else 1
    m = total // (copies * ring)
    sib_rows = ring * m if with_sib else 8
    return pl.pallas_call(
        functools.partial(scatter_kernel, axis, ring, m, with_sib, parts),
        out_shape=jax.ShapeDtypeStruct((m, w), x.dtype),
        in_specs=[pl.BlockSpec(memory_space=pltpu.VMEM)],
        out_specs=pl.BlockSpec(memory_space=pltpu.VMEM),
        scratch_shapes=[
            pltpu.VMEM((2, ring - 1, parts, m // 2 // parts, w), x.dtype),
            pltpu.VMEM((2, ring - 1, parts, m // 2 // parts, w), x.dtype),
            pltpu.VMEM((sib_rows, w), x.dtype),
            pltpu.SemaphoreType.DMA((2 * ring * parts,)),
            pltpu.SemaphoreType.DMA((2 * ring * parts,)),
            (pltpu.SemaphoreType.DMA((2 * ring,)), pltpu.SemaphoreType.DMA((2 * ring,))),
        ],
        compiler_params=pltpu.CompilerParams(
            collective_id=collective_id, has_side_effects=True, vmem_limit_bytes=60 * 1024 * 1024
        ),
    )(x)


def mix_kernel(ring, cols, n, o_ref, wo_ref, out_ref, ogath, part, recv, send_sems, recv_sems, y_send, y_recv):
    mesh_id = pl.DeviceIdType.MESH
    names = ("depth", "rz", "rc", "col")
    me = {a: lax.axis_index(a) for a in names}
    z, c, y = me["rz"], me["rc"], me["col"]
    per_col = 2 * ring // cols

    def device(**moved):
        return tuple(moved.get(a, me[a]) for a in names)

    right = device(rz=lax.rem(z + 1, ring))
    left = device(rz=lax.rem(z + ring - 1, ring))
    sib = device(rc=1 - c)
    peers = [left, right, sib] + [device(col=lax.rem(y + d, cols)) for d in range(1, cols)]

    barrier = pltpu.get_barrier_semaphore()
    for peer in peers:
        pl.semaphore_signal(barrier, inc=1, device_id=peer, device_id_type=mesh_id)
    pl.semaphore_wait(barrier, len(peers))

    def remote(src, dst, peer, send, recv_sem):
        cp = pltpu.make_async_remote_copy(
            src_ref=src, dst_ref=dst, send_sem=send, recv_sem=recv_sem, device_id=peer, device_id_type=mesh_id
        )
        cp.start()
        return cp

    piece = n // cols

    def project(block, k):
        part[k] = jnp.dot(block, wo_ref[...], preferred_element_type=jnp.float32, precision=lax.Precision.HIGH)
        for d in range(1, cols):
            dest = lax.rem(y + d, cols)
            remote(
                part.at[k, pl.ds(pl.multiple_of(dest * piece, 8), piece)],
                recv.at[cols - d, k],
                device(col=dest),
                y_send.at[k * cols + d],
                y_recv.at[(cols - d) * 2 * ring + k],
            )

    def slot(zz, cc):
        return zz * 2 + cc

    def z_copy(src, dst_slot, lo, size, peer, idx):
        return remote(src, ogath.at[dst_slot, pl.ds(lo, size)], peer, send_sems.at[idx], recv_sems.at[idx])

    project(o_ref[...], slot(z, c))
    pending_sib = [(z_copy(o_ref, slot(z, c), 0, n, sib, ring), z)]
    half = ring // 2
    for s in range(1, half + 1):
        origin_r = lax.rem(z - (s - 1) + ring, ring)
        origin_l = lax.rem(z + (s - 1), ring)
        src_r = o_ref if s == 1 else ogath.at[slot(origin_r, c)]
        src_l = o_ref if s == 1 else ogath.at[slot(origin_l, c)]
        if s < half:
            cr = z_copy(src_r, slot(origin_r, c), 0, n, right, 2 * (s - 1))
            cl = z_copy(src_l, slot(origin_l, c), 0, n, left, 2 * (s - 1) + 1)
        else:
            h = n // 2
            cr = z_copy(src_r.at[pl.ds(0, h)], slot(origin_r, c), 0, h, right, 2 * (s - 1))
            cl = z_copy(src_l.at[pl.ds(h, h)], slot(origin_l, c), h, h, left, 2 * (s - 1) + 1)
        for cp, at in pending_sib:
            cp.wait()
            project(ogath[slot(at, 1 - c)], slot(at, 1 - c))
        pending_sib = []
        cr.wait()
        cl.wait()
        if s < half:
            arrived = [(lax.rem(z - s + ring, ring), ring + 2 * s - 1), (lax.rem(z + s, ring), ring + 2 * s)]
        else:
            arrived = [(lax.rem(z + half, ring), ring + 2 * s - 1)]
        for at, idx in arrived:
            pending_sib.append((z_copy(ogath.at[slot(at, c)], slot(at, c), 0, n, sib, idx), at))
            project(ogath[slot(at, c)], slot(at, c))
    for cp, at in pending_sib:
        cp.wait()
        project(ogath[slot(at, 1 - c)], slot(at, 1 - c))
    for k in range(2 * ring):
        total = part[k, pl.ds(pl.multiple_of(y * piece, 8), piece)]
        for d in range(1, cols):
            pltpu.make_async_remote_copy(
                src_ref=part.at[k, pl.ds(0, piece)],
                dst_ref=recv.at[d, k],
                send_sem=y_send.at[0],
                recv_sem=y_recv.at[d * 2 * ring + k],
                device_id=device(col=lax.rem(y + d, cols)),
                device_id_type=mesh_id,
            ).wait_recv()
            total = total + recv[d, k]
        out_ref[pl.ds(k * piece, piece)] = total
    for k in range(2 * ring):
        for d in range(1, cols):
            pltpu.make_async_remote_copy(
                src_ref=part.at[k, pl.ds(0, piece)],
                dst_ref=recv.at[0, 0],
                send_sem=y_send.at[k * cols + d],
                recv_sem=y_recv.at[0],
                device_id=device(col=lax.rem(y + d, cols)),
                device_id_type=mesh_id,
            ).wait_send()


def gather_mix(o, w_out, ring, cols, collective_id):
    n, width = o.shape
    out_w = w_out.shape[1]
    per_col = 2 * ring // cols
    return pl.pallas_call(
        functools.partial(mix_kernel, ring, cols, n),
        out_shape=jax.ShapeDtypeStruct((per_col * n, out_w), jnp.float32),
        in_specs=[pl.BlockSpec(memory_space=pltpu.VMEM), pl.BlockSpec(memory_space=pltpu.VMEM)],
        out_specs=pl.BlockSpec(memory_space=pltpu.VMEM),
        scratch_shapes=[
            pltpu.VMEM((2 * ring, n, width), jnp.float32),
            pltpu.VMEM((2 * ring, n, out_w), jnp.float32),
            pltpu.VMEM((cols, 2 * ring, n // cols, out_w), jnp.float32),
            pltpu.SemaphoreType.DMA((2 * ring,)),
            pltpu.SemaphoreType.DMA((2 * ring,)),
            pltpu.SemaphoreType.DMA((2 * ring * cols,)),
            pltpu.SemaphoreType.DMA((2 * ring * cols,)),
        ],
        compiler_params=pltpu.CompilerParams(
            collective_id=collective_id, has_side_effects=True, vmem_limit_bytes=60 * 1024 * 1024
        ),
    )(o, w_out)


def front_kernel(
    ring, cols, tok_ref, wq_ref, wk_ref, wv_ref, out_ref, kv_out, tg, partial, sibbuf, sbuf, rbuf, kvbuf,
    y_sems, z_sems, sib_sems, kv_sems,
):
    mesh_id = pl.DeviceIdType.MESH
    names = ("depth", "rz", "rc", "col")
    me = {a: lax.axis_index(a) for a in names}
    z, c, y = me["rz"], me["rc"], me["col"]
    rows = tok_ref.shape[0]
    m = rows // (2 * ring)
    h = m // 2

    def device(**moved):
        return tuple(moved.get(a, me[a]) for a in names)

    right = device(rz=lax.rem(z + 1, ring))
    left = device(rz=lax.rem(z + ring - 1, ring))
    sib = device(rc=1 - c)
    y_right = device(col=lax.rem(y + 1, cols))
    y_left = device(col=lax.rem(y + cols - 1, cols))
    peers = [left, right, sib, y_left, y_right]

    barrier = pltpu.get_barrier_semaphore()
    for peer in peers:
        pl.semaphore_signal(barrier, inc=1, device_id=peer, device_id_type=mesh_id)
    pl.semaphore_wait(barrier, len(peers))

    def remote(src, dst, peer, sems, idx):
        cp = pltpu.make_async_remote_copy(
            src_ref=src, dst_ref=dst, send_sem=sems[0].at[idx], recv_sem=sems[1].at[idx],
            device_id=peer, device_id_type=mesh_id,
        )
        cp.start()
        return cp

    def need(s, half):
        sign = -1 if half == 0 else 1
        return lax.rem(z + sign * (s % ring) + ring * ring, ring)

    def round_steps(r, chunk):
        x = partial.at[r]
        base = r * 2 * ring
        sib_copies = {}
        for idx, (s, half) in enumerate((s, half) for s in range(1, ring + 1) for half in (0, 1)):
            at = need(s, half)
            sib_copies[(s, half)] = remote(
                x.at[pl.ds(pl.multiple_of((at * 2 + 1 - c) * m + half * h, 8), h)],
                sibbuf.at[r, pl.ds(pl.multiple_of(at * m + half * h, 8), h)],
                sib, sib_sems, base + idx,
            )
        yield

        def contribution(s, half):
            at = need(s, half)
            sib_copies[(s, half)].wait()
            own = x[pl.ds(pl.multiple_of((at * 2 + c) * m + half * h, 8), h)]
            return own + sibbuf[r, pl.ds(pl.multiple_of(at * m + half * h, 8), h)]

        ring_copies = {}
        for s in range(1, ring):
            for half in (0, 1):
                value = contribution(s, half)
                if s > 1:
                    ring_copies[(s - 1, half)].wait()
                    value = value + rbuf[r, half, s - 2]
                sbuf[r, half, s - 1] = value
                ring_copies[(s, half)] = remote(
                    sbuf.at[r, half, s - 1], rbuf.at[r, half, s - 1],
                    right if half == 0 else left, z_sems, base + half * (ring - 1) + s - 1,
                )
            yield
        for half in (0, 1):
            value = contribution(ring, half)
            ring_copies[(ring - 1, half)].wait()
            value = value + rbuf[r, half, ring - 2]
            out_ref[pl.ds(pl.multiple_of(chunk * m + half * h, 8), h)] = value
            kvbuf[r, z * 2 + c, pl.ds(half * h, h)] = value[:, qw:]
        yield

        def kv_copy(src, at, lo, size, peer, idx):
            return remote(src, kvbuf.at[r, at * 2 + c, pl.ds(lo, size)], peer, kv_sems, base + idx)

        kv_sib = [
            remote(kvbuf.at[r, z * 2 + c], kvbuf.at[r, z * 2 + c], sib, kv_sems, base + ring)
        ]
        half_ring = ring // 2
        for s in range(1, half_ring + 1):
            origin_r = lax.rem(z - (s - 1) + ring, ring)
            origin_l = lax.rem(z + (s - 1), ring)
            src_r = kvbuf.at[r, origin_r * 2 + c]
            src_l = kvbuf.at[r, origin_l * 2 + c]
            if s < half_ring:
                cr = kv_copy(src_r, origin_r, 0, m, right, 2 * (s - 1))
                cl = kv_copy(src_l, origin_l, 0, m, left, 2 * (s - 1) + 1)
            else:
                cr = kv_copy(src_r.at[pl.ds(0, h)], origin_r, 0, h, right, 2 * (s - 1))
                cl = kv_copy(src_l.at[pl.ds(h, h)], origin_l, h, h, left, 2 * (s - 1) + 1)
            yield
            cr.wait()
            cl.wait()
            if s < half_ring:
                got = [(lax.rem(z - s + ring, ring), ring + 2 * s - 1), (lax.rem(z + s, ring), ring + 2 * s)]
            else:
                got = [(lax.rem(z + half_ring, ring), ring + 2 * s - 1)]
            for at, idx in got:
                kv_sib.append(
                    remote(kvbuf.at[r, at * 2 + c], kvbuf.at[r, at * 2 + c], sib, kv_sems, base + idx)
                )
        yield
        for cp in kv_sib:
            cp.wait()
        yield

    qw = wq_ref.shape[1]
    kw = wk_ref.shape[1]

    def project(r, src):
        block = src[...]
        for lo, w_ref in ((0, wq_ref), (qw, wk_ref), (qw + kw, wv_ref)):
            partial[r, :, pl.ds(lo, w_ref.shape[1])] = jnp.dot(
                block, w_ref[...], preferred_element_type=jnp.float32, precision=lax.Precision.HIGH
            )

    y1r = remote(tok_ref, tg.at[1], y_right, y_sems, 0)
    y1l = remote(tok_ref, tg.at[2], y_left, y_sems, 1)
    project(0, tok_ref)
    rounds = [round_steps(0, y)]
    next(rounds[0])
    next(rounds[0])
    next(rounds[0])
    y1r.wait()
    y1l.wait()
    half_rows = rows // 2
    y2r = remote(tg.at[1, pl.ds(0, half_rows)], tg.at[3, pl.ds(0, half_rows)], y_right, y_sems, 2)
    y2l = remote(tg.at[2, pl.ds(half_rows, half_rows)], tg.at[3, pl.ds(half_rows, half_rows)], y_left, y_sems, 3)
    project(1, tg.at[1])
    rounds.append(round_steps(1, lax.rem(y + cols - 1, cols)))
    next(rounds[1])
    project(2, tg.at[2])
    rounds.append(round_steps(2, lax.rem(y + 1, cols)))
    next(rounds[2])
    for _ in range(2):
        for g in rounds:
            next(g, None)
    y2r.wait()
    y2l.wait()
    project(3, tg.at[3])
    rounds.append(round_steps(3, lax.rem(y + 2, cols)))
    next(rounds[3])
    live = list(rounds)
    while live:
        live = [g for g in live if next(g, "done") != "done"]
    kv_out[...] = kvbuf[...]


def front(tokens, w_query, w_key, w_value, ring, cols, collective_id):
    rows, width = tokens.shape
    out_w = w_query.shape[1] + w_key.shape[1] + w_value.shape[1]
    kv_w = w_key.shape[1] + w_value.shape[1]
    m = rows // (2 * ring)
    return pl.pallas_call(
        functools.partial(front_kernel, ring, cols),
        out_shape=(
            jax.ShapeDtypeStruct((cols * m, out_w), jnp.float32),
            jax.ShapeDtypeStruct((cols, 2 * ring, m, kv_w), jnp.float32),
        ),
        in_specs=[pl.BlockSpec(memory_space=pltpu.VMEM)] * 4,
        out_specs=(pl.BlockSpec(memory_space=pltpu.VMEM), pl.BlockSpec(memory_space=pltpu.VMEM)),
        scratch_shapes=[
            pltpu.VMEM((cols, rows, width), jnp.float32),
            pltpu.VMEM((cols, rows, out_w), jnp.float32),
            pltpu.VMEM((cols, ring * m, out_w), jnp.float32),
            pltpu.VMEM((cols, 2, ring - 1, m // 2, out_w), jnp.float32),
            pltpu.VMEM((cols, 2, ring - 1, m // 2, out_w), jnp.float32),
            pltpu.VMEM((cols, 2 * ring, m, kv_w), jnp.float32),
            (pltpu.SemaphoreType.DMA((4,)), pltpu.SemaphoreType.DMA((4,))),
            (pltpu.SemaphoreType.DMA((cols * 2 * ring,)), pltpu.SemaphoreType.DMA((cols * 2 * ring,))),
            (pltpu.SemaphoreType.DMA((cols * 2 * ring,)), pltpu.SemaphoreType.DMA((cols * 2 * ring,))),
            (pltpu.SemaphoreType.DMA((cols * 2 * ring,)), pltpu.SemaphoreType.DMA((cols * 2 * ring,))),
        ],
        compiler_params=pltpu.CompilerParams(
            collective_id=collective_id, has_side_effects=True, vmem_limit_bytes=60 * 1024 * 1024
        ),
    )(tokens, w_query, w_key, w_value)


def on_device(ring, cols, tokens, w_query, w_key, w_value, w_out):
    highest = lax.Precision.HIGH
    q_width = w_query.shape[1]
    kv_width = w_key.shape[1]
    joined, kv_sets = front(tokens, w_query, w_key, w_value, ring, cols, 3)
    query_rows = joined[:, :q_width]
    all_kv = kv_sets.reshape(-1, kv_sets.shape[-1])
    state_end = fold_keys(
        query_rows,
        start_state(query_rows, kv_width),
        (all_kv[:, :kv_width], all_kv[:, kv_width:]),
    )
    return gather_mix(finish(state_end), w_out, ring, cols, 5)


def solution(mesh):
    depth, row, col = (mesh.shape[a] for a in ("depth", "row", "col"))
    split = jax.sharding.Mesh(
        np.asarray(mesh.devices).reshape(depth, row // 2, 2, col), ("depth", "rz", "rc", "col")
    )
    rows = ("rz", "rc")
    placed = (
        P(("depth", "col"), rows),
        P(rows, "col"),
        P(rows, "col"),
        P(rows, "col"),
        P("col", rows),
    )
    return jax.shard_map(
        functools.partial(on_device, row // 2, col),
        mesh=split,
        in_specs=placed,
        out_specs=P(("depth", "col"), rows),
        check_vma=False,
    )
```

```python
import functools
import math

import jax
import numpy as np
import jax.numpy as jnp
from jax import lax
from jax.experimental import pallas as pl
from jax.experimental.pallas import tpu as pltpu
from jax.sharding import PartitionSpec as P

QUERY_HEADS = 32
KEY_VALUE_HEADS = 4
HEAD_SIZE_DIM = 128


def start_state(query_rows, kv_width):
    count_of_heads = kv_width // HEAD_SIZE_DIM
    queries_per_group = QUERY_HEADS // KEY_VALUE_HEADS
    count_of_rows = query_rows.shape[0]
    running_max = jnp.full((count_of_heads, queries_per_group, count_of_rows), -1e30, jnp.float32)
    running_sum = jnp.zeros((count_of_heads, queries_per_group, count_of_rows), jnp.float32)
    weighted = jnp.zeros(
        (count_of_heads, queries_per_group, count_of_rows, HEAD_SIZE_DIM), jnp.float32
    )
    return (running_max, running_sum, weighted)


def fold_keys(query_rows, state_now, block_pair):
    highest = lax.Precision.HIGH
    running_max, running_sum, weighted = state_now
    key_block, value_block = block_pair
    count_of_heads = key_block.shape[1] // HEAD_SIZE_DIM
    count_of_rows = query_rows.shape[0]
    query_head_rows = query_rows.reshape(
        count_of_rows, count_of_heads, QUERY_HEADS // KEY_VALUE_HEADS, HEAD_SIZE_DIM
    )
    key_head_rows = key_block.reshape(-1, count_of_heads, HEAD_SIZE_DIM)
    value_head_rows = value_block.reshape(-1, count_of_heads, HEAD_SIZE_DIM)
    scores = jnp.einsum("rkgd,nkd->kgrn", query_head_rows, key_head_rows, precision=highest) * (
        1.0 / math.sqrt(HEAD_SIZE_DIM)
    )
    newest = jnp.maximum(running_max, jnp.max(scores, axis=-1))
    weights = jnp.exp(scores - newest[..., None])
    running_sum = jnp.sum(weights, axis=-1)
    weighted = jnp.einsum("kgrn,nkd->kgrd", weights, value_head_rows, precision=highest)
    return (newest, running_sum, weighted)


def finish(state_now):
    running_max, running_sum, weighted = state_now
    attention_output = weighted / running_sum[..., None]
    count_of_heads, queries_per_group, count_of_rows, head_size = attention_output.shape
    return attention_output.transpose(2, 0, 1, 3).reshape(
        count_of_rows, count_of_heads * queries_per_group * head_size
    )


def gather_kernel(axis, ring, n, with_sib, x_ref, out_ref, local_sem, send_sems, recv_sems):
    mesh_id = pl.DeviceIdType.MESH
    names = ("depth", "rz", "rc", "col")
    me = {a: lax.axis_index(a) for a in names}
    pos = me[axis]

    def device(**moved):
        return tuple(moved.get(a, me[a]) for a in names)

    right = device(**{axis: lax.rem(pos + 1, ring)})
    left = device(**{axis: lax.rem(pos + ring - 1, ring)})
    sib = device(rc=1 - me["rc"])
    peers = (left, right, sib) if with_sib else (left, right)

    barrier = pltpu.get_barrier_semaphore()
    for peer in peers:
        pl.semaphore_signal(barrier, inc=1, device_id=peer, device_id_type=mesh_id)
    pl.semaphore_wait(barrier, len(peers))

    def rows(at, lo=0, size=n):
        slot = at * 2 + me["rc"] if with_sib else at
        return pl.ds(pl.multiple_of(slot * n + lo, 8), size)

    def remote(src, dst_rows, peer, idx):
        cp = pltpu.make_async_remote_copy(
            src_ref=src,
            dst_ref=out_ref.at[dst_rows],
            send_sem=send_sems.at[idx],
            recv_sem=recv_sems.at[idx],
            device_id=peer,
            device_id_type=mesh_id,
        )
        cp.start()
        return cp

    def to_sib(at, idx):
        if with_sib:
            sib_copies.append(remote(out_ref.at[rows(at)], rows(at), sib, idx))

    local = pltpu.make_async_copy(x_ref, out_ref.at[rows(pos)], local_sem)
    local.start()
    sib_copies = [remote(x_ref, rows(pos), sib, ring)] if with_sib else []
    half = ring // 2
    for s in range(1, half + 1):
        origin_r = lax.rem(pos - (s - 1) + ring, ring)
        origin_l = lax.rem(pos + (s - 1), ring)
        src_r = x_ref if s == 1 else out_ref.at[rows(origin_r)]
        src_l = x_ref if s == 1 else out_ref.at[rows(origin_l)]
        if s < half:
            cr = remote(src_r, rows(origin_r), right, 2 * (s - 1))
            cl = remote(src_l, rows(origin_l), left, 2 * (s - 1) + 1)
            cr.wait()
            cl.wait()
            to_sib(lax.rem(pos - s + ring, ring), ring + 2 * s - 1)
            to_sib(lax.rem(pos + s, ring), ring + 2 * s)
        else:
            h = n // 2
            cr = remote(src_r.at[pl.ds(0, h)], rows(origin_r, 0, h), right, 2 * (s - 1))
            cl = remote(src_l.at[pl.ds(h, h)], rows(origin_l, h, h), left, 2 * (s - 1) + 1)
            cr.wait()
            cl.wait()
            to_sib(lax.rem(pos + half, ring), ring + 2 * s - 1)
    local.wait()
    for cp in sib_copies:
        cp.wait()


def ring_gather(block, axis, ring, with_sib, collective_id):
    n, w = block.shape
    copies = 2 if with_sib else 1
    return pl.pallas_call(
        functools.partial(gather_kernel, axis, ring, n, with_sib),
        out_shape=jax.ShapeDtypeStruct((copies * ring * n, w), block.dtype),
        in_specs=[pl.BlockSpec(memory_space=pl.ANY)],
        out_specs=pl.BlockSpec(memory_space=pl.ANY),
        scratch_shapes=[
            pltpu.SemaphoreType.DMA(()),
            pltpu.SemaphoreType.DMA((2 * ring,)),
            pltpu.SemaphoreType.DMA((2 * ring,)),
        ],
        compiler_params=pltpu.CompilerParams(collective_id=collective_id, has_side_effects=True),
    )(block)


def scatter_kernel(axis, ring, m, with_sib, parts, x_ref, out_ref, sbuf, rbuf, sibbuf, send_sems, recv_sems, sib_sems):
    mesh_id = pl.DeviceIdType.MESH
    names = ("depth", "rz", "rc", "col")
    me = {a: lax.axis_index(a) for a in names}
    pos = me[axis]
    h = m // 2
    q = h // parts

    def device(**moved):
        return tuple(moved.get(a, me[a]) for a in names)

    right = device(**{axis: lax.rem(pos + 1, ring)})
    left = device(**{axis: lax.rem(pos + ring - 1, ring)})
    sib = device(rc=1 - me["rc"])
    peers = (left, right, sib) if with_sib else (left, right)

    barrier = pltpu.get_barrier_semaphore()
    for peer in peers:
        pl.semaphore_signal(barrier, inc=1, device_id=peer, device_id_type=mesh_id)
    pl.semaphore_wait(barrier, len(peers))

    def rows_of(at, half, part, owner):
        slot = at * 2 + owner if with_sib else at
        return pl.ds(pl.multiple_of(slot * m + half * h + part * q, 8), q)

    def sib_rows(at, half, part):
        return pl.ds(pl.multiple_of(at * m + half * h + part * q, 8), q)

    def remote(src, dst, peer, sems, idx):
        cp = pltpu.make_async_remote_copy(
            src_ref=src,
            dst_ref=dst,
            send_sem=sems[0].at[idx],
            recv_sem=sems[1].at[idx],
            device_id=peer,
            device_id_type=mesh_id,
        )
        cp.start()
        return cp

    def need(s, half):
        sign = -1 if half == 0 else 1
        return lax.rem(pos + sign * (s % ring) + ring * ring, ring)

    sib_copies = {}
    if with_sib:
        order = [(s, half) for s in range(1, ring + 1) for half in (0, 1)]
        for idx, (s, half) in enumerate(order):
            at = need(s, half)
            sib_copies[(s, half)] = remote(
                x_ref.at[pl.ds(pl.multiple_of((at * 2 + 1 - me["rc"]) * m + half * h, 8), h)],
                sibbuf.at[pl.ds(pl.multiple_of(at * m + half * h, 8), h)],
                sib,
                (sib_sems[0], sib_sems[1]),
                idx,
            )

    def contribution(s, half, part):
        at = need(s, half)
        own = x_ref[rows_of(at, half, part, me["rc"])]
        if with_sib:
            if part == 0:
                sib_copies[(s, half)].wait()
            own = own + sibbuf[sib_rows(at, half, part)]
        return own

    ring_copies = {}
    for s in range(1, ring):
        for part in range(parts):
            for half in (0, 1):
                value = contribution(s, half, part)
                if s > 1:
                    ring_copies[(s - 1, half, part)].wait()
                    value = value + rbuf[half, s - 2, part]
                sbuf[half, s - 1, part] = value
                ring_copies[(s, half, part)] = remote(
                    sbuf.at[half, s - 1, part],
                    rbuf.at[half, s - 1, part],
                    right if half == 0 else left,
                    (send_sems, recv_sems),
                    (half * (ring - 1) + s - 1) * parts + part,
                )
    for part in range(parts):
        for half in (0, 1):
            value = contribution(ring, half, part)
            ring_copies[(ring - 1, half, part)].wait()
            out_ref[pl.ds(half * h + part * q, q)] = value + rbuf[half, ring - 2, part]


def ring_scatter(x, axis, ring, with_sib, parts, collective_id):
    total, w = x.shape
    copies = 2 if with_sib else 1
    m = total // (copies * ring)
    sib_rows = ring * m if with_sib else 8
    return pl.pallas_call(
        functools.partial(scatter_kernel, axis, ring, m, with_sib, parts),
        out_shape=jax.ShapeDtypeStruct((m, w), x.dtype),
        in_specs=[pl.BlockSpec(memory_space=pltpu.VMEM)],
        out_specs=pl.BlockSpec(memory_space=pltpu.VMEM),
        scratch_shapes=[
            pltpu.VMEM((2, ring - 1, parts, m // 2 // parts, w), x.dtype),
            pltpu.VMEM((2, ring - 1, parts, m // 2 // parts, w), x.dtype),
            pltpu.VMEM((sib_rows, w), x.dtype),
            pltpu.SemaphoreType.DMA((2 * ring * parts,)),
            pltpu.SemaphoreType.DMA((2 * ring * parts,)),
            (pltpu.SemaphoreType.DMA((2 * ring,)), pltpu.SemaphoreType.DMA((2 * ring,))),
        ],
        compiler_params=pltpu.CompilerParams(
            collective_id=collective_id, has_side_effects=True, vmem_limit_bytes=60 * 1024 * 1024
        ),
    )(x)


def mix_kernel(ring, cols, n, o_ref, wo_ref, out_ref, ogath, part, recv, send_sems, recv_sems, y_send, y_recv):
    mesh_id = pl.DeviceIdType.MESH
    names = ("depth", "rz", "rc", "col")
    me = {a: lax.axis_index(a) for a in names}
    z, c, y = me["rz"], me["rc"], me["col"]
    per_col = 2 * ring // cols

    def device(**moved):
        return tuple(moved.get(a, me[a]) for a in names)

    right = device(rz=lax.rem(z + 1, ring))
    left = device(rz=lax.rem(z + ring - 1, ring))
    sib = device(rc=1 - c)
    peers = [left, right, sib] + [device(col=lax.rem(y + d, cols)) for d in range(1, cols)]

    barrier = pltpu.get_barrier_semaphore()
    for peer in peers:
        pl.semaphore_signal(barrier, inc=1, device_id=peer, device_id_type=mesh_id)
    pl.semaphore_wait(barrier, len(peers))

    def remote(src, dst, peer, send, recv_sem):
        cp = pltpu.make_async_remote_copy(
            src_ref=src, dst_ref=dst, send_sem=send, recv_sem=recv_sem, device_id=peer, device_id_type=mesh_id
        )
        cp.start()
        return cp

    piece = n // cols

    def project(block, k):
        part[k] = jnp.dot(block, wo_ref[...], preferred_element_type=jnp.float32, precision=lax.Precision.HIGH)
        for d in range(1, cols):
            dest = lax.rem(y + d, cols)
            remote(
                part.at[k, pl.ds(pl.multiple_of(dest * piece, 8), piece)],
                recv.at[cols - d, k],
                device(col=dest),
                y_send.at[k * cols + d],
                y_recv.at[(cols - d) * 2 * ring + k],
            )

    def slot(zz, cc):
        return zz * 2 + cc

    def z_copy(src, dst_slot, lo, size, peer, idx):
        return remote(src, ogath.at[dst_slot, pl.ds(lo, size)], peer, send_sems.at[idx], recv_sems.at[idx])

    project(o_ref[...], slot(z, c))
    pending_sib = [(z_copy(o_ref, slot(z, c), 0, n, sib, ring), z)]
    half = ring // 2
    for s in range(1, half + 1):
        origin_r = lax.rem(z - (s - 1) + ring, ring)
        origin_l = lax.rem(z + (s - 1), ring)
        src_r = o_ref if s == 1 else ogath.at[slot(origin_r, c)]
        src_l = o_ref if s == 1 else ogath.at[slot(origin_l, c)]
        if s < half:
            cr = z_copy(src_r, slot(origin_r, c), 0, n, right, 2 * (s - 1))
            cl = z_copy(src_l, slot(origin_l, c), 0, n, left, 2 * (s - 1) + 1)
        else:
            h = n // 2
            cr = z_copy(src_r.at[pl.ds(0, h)], slot(origin_r, c), 0, h, right, 2 * (s - 1))
            cl = z_copy(src_l.at[pl.ds(h, h)], slot(origin_l, c), h, h, left, 2 * (s - 1) + 1)
        for cp, at in pending_sib:
            cp.wait()
            project(ogath[slot(at, 1 - c)], slot(at, 1 - c))
        pending_sib = []
        cr.wait()
        cl.wait()
        if s < half:
            arrived = [(lax.rem(z - s + ring, ring), ring + 2 * s - 1), (lax.rem(z + s, ring), ring + 2 * s)]
        else:
            arrived = [(lax.rem(z + half, ring), ring + 2 * s - 1)]
        for at, idx in arrived:
            pending_sib.append((z_copy(ogath.at[slot(at, c)], slot(at, c), 0, n, sib, idx), at))
            project(ogath[slot(at, c)], slot(at, c))
    for cp, at in pending_sib:
        cp.wait()
        project(ogath[slot(at, 1 - c)], slot(at, 1 - c))
    for k in range(2 * ring):
        total = part[k, pl.ds(pl.multiple_of(y * piece, 8), piece)]
        for d in range(1, cols):
            pltpu.make_async_remote_copy(
                src_ref=part.at[k, pl.ds(0, piece)],
                dst_ref=recv.at[d, k],
                send_sem=y_send.at[0],
                recv_sem=y_recv.at[d * 2 * ring + k],
                device_id=device(col=lax.rem(y + d, cols)),
                device_id_type=mesh_id,
            ).wait_recv()
            total = total + recv[d, k]
        out_ref[pl.ds(k * piece, piece)] = total
    for k in range(2 * ring):
        for d in range(1, cols):
            pltpu.make_async_remote_copy(
                src_ref=part.at[k, pl.ds(0, piece)],
                dst_ref=recv.at[0, 0],
                send_sem=y_send.at[k * cols + d],
                recv_sem=y_recv.at[0],
                device_id=device(col=lax.rem(y + d, cols)),
                device_id_type=mesh_id,
            ).wait_send()


def gather_mix(o, w_out, ring, cols, collective_id):
    n, width = o.shape
    out_w = w_out.shape[1]
    per_col = 2 * ring // cols
    return pl.pallas_call(
        functools.partial(mix_kernel, ring, cols, n),
        out_shape=jax.ShapeDtypeStruct((per_col * n, out_w), jnp.float32),
        in_specs=[pl.BlockSpec(memory_space=pltpu.VMEM), pl.BlockSpec(memory_space=pltpu.VMEM)],
        out_specs=pl.BlockSpec(memory_space=pltpu.VMEM),
        scratch_shapes=[
            pltpu.VMEM((2 * ring, n, width), jnp.float32),
            pltpu.VMEM((2 * ring, n, out_w), jnp.float32),
            pltpu.VMEM((cols, 2 * ring, n // cols, out_w), jnp.float32),
            pltpu.SemaphoreType.DMA((2 * ring,)),
            pltpu.SemaphoreType.DMA((2 * ring,)),
            pltpu.SemaphoreType.DMA((2 * ring * cols,)),
            pltpu.SemaphoreType.DMA((2 * ring * cols,)),
        ],
        compiler_params=pltpu.CompilerParams(
            collective_id=collective_id, has_side_effects=True, vmem_limit_bytes=60 * 1024 * 1024
        ),
    )(o, w_out)


def front_kernel(
    ring, cols, tok_ref, wq_ref, wk_ref, wv_ref, out_ref, kv_out, tg, partial, sibbuf, sbuf, rbuf, kvbuf,
    y_sems, z_sems, sib_sems, kv_sems,
):
    mesh_id = pl.DeviceIdType.MESH
    names = ("depth", "rz", "rc", "col")
    me = {a: lax.axis_index(a) for a in names}
    z, c, y = me["rz"], me["rc"], me["col"]
    rows = tok_ref.shape[0]
    m = rows // (2 * ring)
    h = m // 2

    def device(**moved):
        return tuple(moved.get(a, me[a]) for a in names)

    right = device(rz=lax.rem(z + 1, ring))
    left = device(rz=lax.rem(z + ring - 1, ring))
    sib = device(rc=1 - c)
    y_right = device(col=lax.rem(y + 1, cols))
    y_left = device(col=lax.rem(y + cols - 1, cols))
    peers = [left, right, sib, y_left, y_right]

    barrier = pltpu.get_barrier_semaphore()
    for peer in peers:
        pl.semaphore_signal(barrier, inc=1, device_id=peer, device_id_type=mesh_id)
    pl.semaphore_wait(barrier, len(peers))

    def remote(src, dst, peer, sems, idx):
        cp = pltpu.make_async_remote_copy(
            src_ref=src, dst_ref=dst, send_sem=sems[0].at[idx], recv_sem=sems[1].at[idx],
            device_id=peer, device_id_type=mesh_id,
        )
        cp.start()
        return cp

    def need(s, half):
        sign = -1 if half == 0 else 1
        return lax.rem(z + sign * (s % ring) + ring * ring, ring)

    def round_steps(r, chunk):
        x = partial.at[r]
        base = r * 2 * ring
        sib_copies = {}
        for idx, (s, half) in enumerate((s, half) for s in range(1, ring + 1) for half in (0, 1)):
            at = need(s, half)
            sib_copies[(s, half)] = remote(
                x.at[pl.ds(pl.multiple_of((at * 2 + 1 - c) * m + half * h, 8), h)],
                sibbuf.at[r, pl.ds(pl.multiple_of(at * m + half * h, 8), h)],
                sib, sib_sems, base + idx,
            )
        yield

        def contribution(s, half):
            at = need(s, half)
            sib_copies[(s, half)].wait()
            own = x[pl.ds(pl.multiple_of((at * 2 + c) * m + half * h, 8), h)]
            return own + sibbuf[r, pl.ds(pl.multiple_of(at * m + half * h, 8), h)]

        ring_copies = {}
        for s in range(1, ring):
            for half in (0, 1):
                value = contribution(s, half)
                if s > 1:
                    ring_copies[(s - 1, half)].wait()
                    value = value + rbuf[r, half, s - 2]
                sbuf[r, half, s - 1] = value
                ring_copies[(s, half)] = remote(
                    sbuf.at[r, half, s - 1], rbuf.at[r, half, s - 1],
                    right if half == 0 else left, z_sems, base + half * (ring - 1) + s - 1,
                )
            yield
        for half in (0, 1):
            value = contribution(ring, half)
            ring_copies[(ring - 1, half)].wait()
            value = value + rbuf[r, half, ring - 2]
            out_ref[pl.ds(pl.multiple_of(chunk * m + half * h, 8), h)] = value
            kvbuf[r, z * 2 + c, pl.ds(half * h, h)] = value[:, qw:]
        yield

        def kv_copy(src, at, lo, size, peer, idx):
            return remote(src, kvbuf.at[r, at * 2 + c, pl.ds(lo, size)], peer, kv_sems, base + idx)

        kv_sib = [
            remote(kvbuf.at[r, z * 2 + c], kvbuf.at[r, z * 2 + c], sib, kv_sems, base + ring)
        ]
        half_ring = ring // 2
        for s in range(1, half_ring + 1):
            origin_r = lax.rem(z - (s - 1) + ring, ring)
            origin_l = lax.rem(z + (s - 1), ring)
            src_r = kvbuf.at[r, origin_r * 2 + c]
            src_l = kvbuf.at[r, origin_l * 2 + c]
            if s < half_ring:
                cr = kv_copy(src_r, origin_r, 0, m, right, 2 * (s - 1))
                cl = kv_copy(src_l, origin_l, 0, m, left, 2 * (s - 1) + 1)
            else:
                cr = kv_copy(src_r.at[pl.ds(0, h)], origin_r, 0, h, right, 2 * (s - 1))
                cl = kv_copy(src_l.at[pl.ds(h, h)], origin_l, h, h, left, 2 * (s - 1) + 1)
            yield
            cr.wait()
            cl.wait()
            if s < half_ring:
                got = [(lax.rem(z - s + ring, ring), ring + 2 * s - 1), (lax.rem(z + s, ring), ring + 2 * s)]
            else:
                got = [(lax.rem(z + half_ring, ring), ring + 2 * s - 1)]
            for at, idx in got:
                kv_sib.append(
                    remote(kvbuf.at[r, at * 2 + c], kvbuf.at[r, at * 2 + c], sib, kv_sems, base + idx)
                )
        yield
        for cp in kv_sib:
            cp.wait()
        yield

    qw = wq_ref.shape[1]
    kw = wk_ref.shape[1]

    def project(r, src):
        block = src[...]
        for lo, w_ref in ((0, wq_ref), (qw, wk_ref), (qw + kw, wv_ref)):
            partial[r, :, pl.ds(lo, w_ref.shape[1])] = jnp.dot(
                block, w_ref[...], preferred_element_type=jnp.float32, precision=lax.Precision.HIGH
            )

    y1r = remote(tok_ref, tg.at[1], y_right, y_sems, 0)
    y1l = remote(tok_ref, tg.at[2], y_left, y_sems, 1)
    project(0, tok_ref)
    rounds = [round_steps(0, y)]
    for _ in range(ring):
        next(rounds[0])
    y1r.wait()
    y1l.wait()
    half_rows = rows // 2
    y2r = remote(tg.at[1, pl.ds(0, half_rows)], tg.at[3, pl.ds(0, half_rows)], y_right, y_sems, 2)
    y2l = remote(tg.at[2, pl.ds(half_rows, half_rows)], tg.at[3, pl.ds(half_rows, half_rows)], y_left, y_sems, 3)
    project(1, tg.at[1])
    rounds.append(round_steps(1, lax.rem(y + cols - 1, cols)))
    next(rounds[1])
    project(2, tg.at[2])
    rounds.append(round_steps(2, lax.rem(y + 1, cols)))
    next(rounds[2])
    for _ in range(2):
        for g in rounds:
            next(g, None)
    y2r.wait()
    y2l.wait()
    project(3, tg.at[3])
    rounds.append(round_steps(3, lax.rem(y + 2, cols)))
    next(rounds[3])
    live = list(rounds)
    while live:
        live = [g for g in live if next(g, "done") != "done"]
    kv_out[...] = kvbuf[...]


def front(tokens, w_query, w_key, w_value, ring, cols, collective_id):
    rows, width = tokens.shape
    out_w = w_query.shape[1] + w_key.shape[1] + w_value.shape[1]
    kv_w = w_key.shape[1] + w_value.shape[1]
    m = rows // (2 * ring)
    return pl.pallas_call(
        functools.partial(front_kernel, ring, cols),
        out_shape=(
            jax.ShapeDtypeStruct((cols * m, out_w), jnp.float32),
            jax.ShapeDtypeStruct((cols, 2 * ring, m, kv_w), jnp.float32),
        ),
        in_specs=[pl.BlockSpec(memory_space=pltpu.VMEM)] * 4,
        out_specs=(pl.BlockSpec(memory_space=pltpu.VMEM), pl.BlockSpec(memory_space=pltpu.VMEM)),
        scratch_shapes=[
            pltpu.VMEM((cols, rows, width), jnp.float32),
            pltpu.VMEM((cols, rows, out_w), jnp.float32),
            pltpu.VMEM((cols, ring * m, out_w), jnp.float32),
            pltpu.VMEM((cols, 2, ring - 1, m // 2, out_w), jnp.float32),
            pltpu.VMEM((cols, 2, ring - 1, m // 2, out_w), jnp.float32),
            pltpu.VMEM((cols, 2 * ring, m, kv_w), jnp.float32),
            (pltpu.SemaphoreType.DMA((4,)), pltpu.SemaphoreType.DMA((4,))),
            (pltpu.SemaphoreType.DMA((cols * 2 * ring,)), pltpu.SemaphoreType.DMA((cols * 2 * ring,))),
            (pltpu.SemaphoreType.DMA((cols * 2 * ring,)), pltpu.SemaphoreType.DMA((cols * 2 * ring,))),
            (pltpu.SemaphoreType.DMA((cols * 2 * ring,)), pltpu.SemaphoreType.DMA((cols * 2 * ring,))),
        ],
        compiler_params=pltpu.CompilerParams(
            collective_id=collective_id, has_side_effects=True, vmem_limit_bytes=60 * 1024 * 1024
        ),
    )(tokens, w_query, w_key, w_value)


def on_device(ring, cols, tokens, w_query, w_key, w_value, w_out):
    highest = lax.Precision.HIGH
    q_width = w_query.shape[1]
    kv_width = w_key.shape[1]
    joined, kv_sets = front(tokens, w_query, w_key, w_value, ring, cols, 3)
    query_rows = joined[:, :q_width]
    all_kv = kv_sets.reshape(-1, kv_sets.shape[-1])
    state_end = fold_keys(
        query_rows,
        start_state(query_rows, kv_width),
        (all_kv[:, :kv_width], all_kv[:, kv_width:]),
    )
    return gather_mix(finish(state_end), w_out, ring, cols, 5)


def solution(mesh):
    depth, row, col = (mesh.shape[a] for a in ("depth", "row", "col"))
    split = jax.sharding.Mesh(
        np.asarray(mesh.devices).reshape(depth, row // 2, 2, col), ("depth", "rz", "rc", "col")
    )
    rows = ("rz", "rc")
    placed = (
        P(("depth", "col"), rows),
        P(rows, "col"),
        P(rows, "col"),
        P(rows, "col"),
        P("col", rows),
    )
    return jax.shard_map(
        functools.partial(on_device, row // 2, col),
        mesh=split,
        in_specs=placed,
        out_specs=P(("depth", "col"), rows),
        check_vma=False,
    )
```

```python
import functools
import math

import jax
import numpy as np
import jax.numpy as jnp
from jax import lax
from jax.experimental import pallas as pl
from jax.experimental.pallas import tpu as pltpu
from jax.sharding import PartitionSpec as P

QUERY_HEADS = 32
KEY_VALUE_HEADS = 4
HEAD_SIZE_DIM = 128


def start_state(query_rows, kv_width):
    count_of_heads = kv_width // HEAD_SIZE_DIM
    queries_per_group = QUERY_HEADS // KEY_VALUE_HEADS
    count_of_rows = query_rows.shape[0]
    running_max = jnp.full((count_of_heads, queries_per_group, count_of_rows), -1e30, jnp.float32)
    running_sum = jnp.zeros((count_of_heads, queries_per_group, count_of_rows), jnp.float32)
    weighted = jnp.zeros(
        (count_of_heads, queries_per_group, count_of_rows, HEAD_SIZE_DIM), jnp.float32
    )
    return (running_max, running_sum, weighted)


def fold_keys(query_rows, state_now, block_pair):
    highest = lax.Precision.HIGH
    running_max, running_sum, weighted = state_now
    key_block, value_block = block_pair
    count_of_heads = key_block.shape[1] // HEAD_SIZE_DIM
    count_of_rows = query_rows.shape[0]
    query_head_rows = query_rows.reshape(
        count_of_rows, count_of_heads, QUERY_HEADS // KEY_VALUE_HEADS, HEAD_SIZE_DIM
    )
    key_head_rows = key_block.reshape(-1, count_of_heads, HEAD_SIZE_DIM)
    value_head_rows = value_block.reshape(-1, count_of_heads, HEAD_SIZE_DIM)
    scores = jnp.einsum("rkgd,nkd->kgrn", query_head_rows, key_head_rows, precision=highest) * (
        1.0 / math.sqrt(HEAD_SIZE_DIM)
    )
    newest = jnp.maximum(running_max, jnp.max(scores, axis=-1))
    weights = jnp.exp(scores - newest[..., None])
    running_sum = jnp.sum(weights, axis=-1)
    weighted = jnp.einsum("kgrn,nkd->kgrd", weights, value_head_rows, precision=highest)
    return (newest, running_sum, weighted)


def finish(state_now):
    running_max, running_sum, weighted = state_now
    attention_output = weighted / running_sum[..., None]
    count_of_heads, queries_per_group, count_of_rows, head_size = attention_output.shape
    return attention_output.transpose(2, 0, 1, 3).reshape(
        count_of_rows, count_of_heads * queries_per_group * head_size
    )


def gather_kernel(axis, ring, n, with_sib, x_ref, out_ref, local_sem, send_sems, recv_sems):
    mesh_id = pl.DeviceIdType.MESH
    names = ("depth", "rz", "rc", "col")
    me = {a: lax.axis_index(a) for a in names}
    pos = me[axis]

    def device(**moved):
        return tuple(moved.get(a, me[a]) for a in names)

    right = device(**{axis: lax.rem(pos + 1, ring)})
    left = device(**{axis: lax.rem(pos + ring - 1, ring)})
    sib = device(rc=1 - me["rc"])
    peers = (left, right, sib) if with_sib else (left, right)

    barrier = pltpu.get_barrier_semaphore()
    for peer in peers:
        pl.semaphore_signal(barrier, inc=1, device_id=peer, device_id_type=mesh_id)
    pl.semaphore_wait(barrier, len(peers))

    def rows(at, lo=0, size=n):
        slot = at * 2 + me["rc"] if with_sib else at
        return pl.ds(pl.multiple_of(slot * n + lo, 8), size)

    def remote(src, dst_rows, peer, idx):
        cp = pltpu.make_async_remote_copy(
            src_ref=src,
            dst_ref=out_ref.at[dst_rows],
            send_sem=send_sems.at[idx],
            recv_sem=recv_sems.at[idx],
            device_id=peer,
            device_id_type=mesh_id,
        )
        cp.start()
        return cp

    def to_sib(at, idx):
        if with_sib:
            sib_copies.append(remote(out_ref.at[rows(at)], rows(at), sib, idx))

    local = pltpu.make_async_copy(x_ref, out_ref.at[rows(pos)], local_sem)
    local.start()
    sib_copies = [remote(x_ref, rows(pos), sib, ring)] if with_sib else []
    half = ring // 2
    for s in range(1, half + 1):
        origin_r = lax.rem(pos - (s - 1) + ring, ring)
        origin_l = lax.rem(pos + (s - 1), ring)
        src_r = x_ref if s == 1 else out_ref.at[rows(origin_r)]
        src_l = x_ref if s == 1 else out_ref.at[rows(origin_l)]
        if s < half:
            cr = remote(src_r, rows(origin_r), right, 2 * (s - 1))
            cl = remote(src_l, rows(origin_l), left, 2 * (s - 1) + 1)
            cr.wait()
            cl.wait()
            to_sib(lax.rem(pos - s + ring, ring), ring + 2 * s - 1)
            to_sib(lax.rem(pos + s, ring), ring + 2 * s)
        else:
            h = n // 2
            cr = remote(src_r.at[pl.ds(0, h)], rows(origin_r, 0, h), right, 2 * (s - 1))
            cl = remote(src_l.at[pl.ds(h, h)], rows(origin_l, h, h), left, 2 * (s - 1) + 1)
            cr.wait()
            cl.wait()
            to_sib(lax.rem(pos + half, ring), ring + 2 * s - 1)
    local.wait()
    for cp in sib_copies:
        cp.wait()


def ring_gather(block, axis, ring, with_sib, collective_id):
    n, w = block.shape
    copies = 2 if with_sib else 1
    return pl.pallas_call(
        functools.partial(gather_kernel, axis, ring, n, with_sib),
        out_shape=jax.ShapeDtypeStruct((copies * ring * n, w), block.dtype),
        in_specs=[pl.BlockSpec(memory_space=pl.ANY)],
        out_specs=pl.BlockSpec(memory_space=pl.ANY),
        scratch_shapes=[
            pltpu.SemaphoreType.DMA(()),
            pltpu.SemaphoreType.DMA((2 * ring,)),
            pltpu.SemaphoreType.DMA((2 * ring,)),
        ],
        compiler_params=pltpu.CompilerParams(collective_id=collective_id, has_side_effects=True),
    )(block)


def scatter_kernel(axis, ring, m, with_sib, parts, x_ref, out_ref, sbuf, rbuf, sibbuf, send_sems, recv_sems, sib_sems):
    mesh_id = pl.DeviceIdType.MESH
    names = ("depth", "rz", "rc", "col")
    me = {a: lax.axis_index(a) for a in names}
    pos = me[axis]
    h = m // 2
    q = h // parts

    def device(**moved):
        return tuple(moved.get(a, me[a]) for a in names)

    right = device(**{axis: lax.rem(pos + 1, ring)})
    left = device(**{axis: lax.rem(pos + ring - 1, ring)})
    sib = device(rc=1 - me["rc"])
    peers = (left, right, sib) if with_sib else (left, right)

    barrier = pltpu.get_barrier_semaphore()
    for peer in peers:
        pl.semaphore_signal(barrier, inc=1, device_id=peer, device_id_type=mesh_id)
    pl.semaphore_wait(barrier, len(peers))

    def rows_of(at, half, part, owner):
        slot = at * 2 + owner if with_sib else at
        return pl.ds(pl.multiple_of(slot * m + half * h + part * q, 8), q)

    def sib_rows(at, half, part):
        return pl.ds(pl.multiple_of(at * m + half * h + part * q, 8), q)

    def remote(src, dst, peer, sems, idx):
        cp = pltpu.make_async_remote_copy(
            src_ref=src,
            dst_ref=dst,
            send_sem=sems[0].at[idx],
            recv_sem=sems[1].at[idx],
            device_id=peer,
            device_id_type=mesh_id,
        )
        cp.start()
        return cp

    def need(s, half):
        sign = -1 if half == 0 else 1
        return lax.rem(pos + sign * (s % ring) + ring * ring, ring)

    sib_copies = {}
    if with_sib:
        order = [(s, half) for s in range(1, ring + 1) for half in (0, 1)]
        for idx, (s, half) in enumerate(order):
            at = need(s, half)
            sib_copies[(s, half)] = remote(
                x_ref.at[pl.ds(pl.multiple_of((at * 2 + 1 - me["rc"]) * m + half * h, 8), h)],
                sibbuf.at[pl.ds(pl.multiple_of(at * m + half * h, 8), h)],
                sib,
                (sib_sems[0], sib_sems[1]),
                idx,
            )

    def contribution(s, half, part):
        at = need(s, half)
        own = x_ref[rows_of(at, half, part, me["rc"])]
        if with_sib:
            if part == 0:
                sib_copies[(s, half)].wait()
            own = own + sibbuf[sib_rows(at, half, part)]
        return own

    ring_copies = {}
    for s in range(1, ring):
        for part in range(parts):
            for half in (0, 1):
                value = contribution(s, half, part)
                if s > 1:
                    ring_copies[(s - 1, half, part)].wait()
                    value = value + rbuf[half, s - 2, part]
                sbuf[half, s - 1, part] = value
                ring_copies[(s, half, part)] = remote(
                    sbuf.at[half, s - 1, part],
                    rbuf.at[half, s - 1, part],
                    right if half == 0 else left,
                    (send_sems, recv_sems),
                    (half * (ring - 1) + s - 1) * parts + part,
                )
    for part in range(parts):
        for half in (0, 1):
            value = contribution(ring, half, part)
            ring_copies[(ring - 1, half, part)].wait()
            out_ref[pl.ds(half * h + part * q, q)] = value + rbuf[half, ring - 2, part]


def ring_scatter(x, axis, ring, with_sib, parts, collective_id):
    total, w = x.shape
    copies = 2 if with_sib else 1
    m = total // (copies * ring)
    sib_rows = ring * m if with_sib else 8
    return pl.pallas_call(
        functools.partial(scatter_kernel, axis, ring, m, with_sib, parts),
        out_shape=jax.ShapeDtypeStruct((m, w), x.dtype),
        in_specs=[pl.BlockSpec(memory_space=pltpu.VMEM)],
        out_specs=pl.BlockSpec(memory_space=pltpu.VMEM),
        scratch_shapes=[
            pltpu.VMEM((2, ring - 1, parts, m // 2 // parts, w), x.dtype),
            pltpu.VMEM((2, ring - 1, parts, m // 2 // parts, w), x.dtype),
            pltpu.VMEM((sib_rows, w), x.dtype),
            pltpu.SemaphoreType.DMA((2 * ring * parts,)),
            pltpu.SemaphoreType.DMA((2 * ring * parts,)),
            (pltpu.SemaphoreType.DMA((2 * ring,)), pltpu.SemaphoreType.DMA((2 * ring,))),
        ],
        compiler_params=pltpu.CompilerParams(
            collective_id=collective_id, has_side_effects=True, vmem_limit_bytes=60 * 1024 * 1024
        ),
    )(x)


def mix_kernel(
    ring, cols, n, o_ref, wo_ref, out_ref, ogath, part, fwd_a, fwd_b, comb_l, comb_r, recv_l, recv_r,
    send_sems, recv_sems, fa_sems, fb_sems, cl_sems, cr_sems,
):
    mesh_id = pl.DeviceIdType.MESH
    names = ("depth", "rz", "rc", "col")
    me = {a: lax.axis_index(a) for a in names}
    z, c, y = me["rz"], me["rc"], me["col"]
    piece = n // cols
    hp = piece // 2

    def device(**moved):
        return tuple(moved.get(a, me[a]) for a in names)

    right = device(rz=lax.rem(z + 1, ring))
    left = device(rz=lax.rem(z + ring - 1, ring))
    sib = device(rc=1 - c)
    y_l = lax.rem(y + cols - 1, cols)
    y_r = lax.rem(y + 1, cols)
    y_o = lax.rem(y + 2, cols)
    peers = [left, right, sib, device(col=y_l), device(col=y_r)]

    barrier = pltpu.get_barrier_semaphore()
    for peer in peers:
        pl.semaphore_signal(barrier, inc=1, device_id=peer, device_id_type=mesh_id)
    pl.semaphore_wait(barrier, len(peers))

    def remote(src, dst, peer, sems, idx):
        cp = pltpu.make_async_remote_copy(
            src_ref=src, dst_ref=dst, send_sem=sems[0].at[idx], recv_sem=sems[1].at[idx],
            device_id=peer, device_id_type=mesh_id,
        )
        cp.start()
        return cp

    def rows_at(p, lo, size):
        return pl.ds(pl.multiple_of(p * piece + lo, 8), size)

    y_copies = []
    pending = []

    def combine(k, fa, fb):
        fa.wait_recv()
        comb_l[k, pl.ds(0, hp)] = part[k, rows_at(y_l, 0, hp)] + fwd_a[k]
        comb_l[k, pl.ds(hp, hp)] = part[k, rows_at(y_l, hp, hp)]
        y_copies.append(remote(comb_l.at[k], recv_r.at[k], device(col=y_l), cl_sems, k))
        fb.wait_recv()
        comb_r[k, pl.ds(0, hp)] = part[k, rows_at(y_r, 0, hp)]
        comb_r[k, pl.ds(hp, hp)] = part[k, rows_at(y_r, hp, hp)] + fwd_b[k]
        y_copies.append(remote(comb_r.at[k], recv_l.at[k], device(col=y_r), cr_sems, k))

    def project(block, k):
        part[k] = jnp.dot(block, wo_ref[...], preferred_element_type=jnp.float32, precision=lax.Precision.HIGH)
        fa = remote(part.at[k, rows_at(y_o, 0, hp)], fwd_a.at[k], device(col=y_l), fa_sems, k)
        fb = remote(part.at[k, rows_at(y_o, hp, hp)], fwd_b.at[k], device(col=y_r), fb_sems, k)
        y_copies.extend([fa, fb])
        while pending:
            combine(*pending.pop(0))
        pending.append((k, fa, fb))

    def slot(zz, cc):
        return zz * 2 + cc

    def z_copy(src, dst_slot, lo, size, peer, idx):
        return remote(src, ogath.at[dst_slot, pl.ds(lo, size)], peer, (send_sems, recv_sems), idx)

    project(o_ref[...], slot(z, c))
    pending_sib = [(z_copy(o_ref, slot(z, c), 0, n, sib, ring), z)]
    half = ring // 2
    for s in range(1, half + 1):
        origin_r = lax.rem(z - (s - 1) + ring, ring)
        origin_l = lax.rem(z + (s - 1), ring)
        src_r = o_ref if s == 1 else ogath.at[slot(origin_r, c)]
        src_l = o_ref if s == 1 else ogath.at[slot(origin_l, c)]
        if s < half:
            cr = z_copy(src_r, slot(origin_r, c), 0, n, right, 2 * (s - 1))
            cl = z_copy(src_l, slot(origin_l, c), 0, n, left, 2 * (s - 1) + 1)
        else:
            h = n // 2
            cr = z_copy(src_r.at[pl.ds(0, h)], slot(origin_r, c), 0, h, right, 2 * (s - 1))
            cl = z_copy(src_l.at[pl.ds(h, h)], slot(origin_l, c), h, h, left, 2 * (s - 1) + 1)
        for cp, at in pending_sib:
            cp.wait()
            project(ogath[slot(at, 1 - c)], slot(at, 1 - c))
        pending_sib = []
        cr.wait()
        cl.wait()
        if s < half:
            arrived = [(lax.rem(z - s + ring, ring), ring + 2 * s - 1), (lax.rem(z + s, ring), ring + 2 * s)]
        else:
            arrived = [(lax.rem(z + half, ring), ring + 2 * s - 1)]
        for at, idx in arrived:
            pending_sib.append((z_copy(ogath.at[slot(at, c)], slot(at, c), 0, n, sib, idx), at))
            project(ogath[slot(at, c)], slot(at, c))
    for cp, at in pending_sib:
        cp.wait()
        project(ogath[slot(at, 1 - c)], slot(at, 1 - c))
    while pending:
        combine(*pending.pop(0))
    for k in range(2 * ring):
        for buf, sems, peer in ((recv_l, cr_sems, device(col=y_l)), (recv_r, cl_sems, device(col=y_r))):
            pltpu.make_async_remote_copy(
                src_ref=comb_l.at[k], dst_ref=buf.at[k], send_sem=sems[0].at[k], recv_sem=sems[1].at[k],
                device_id=peer, device_id_type=mesh_id,
            ).wait_recv()
        out_ref[pl.ds(k * piece, piece)] = part[k, rows_at(y, 0, piece)] + recv_l[k] + recv_r[k]
    for cp in y_copies:
        cp.wait_send()


def gather_mix(o, w_out, ring, cols, collective_id):
    n, width = o.shape
    out_w = w_out.shape[1]
    piece = n // cols
    slots = 2 * ring

    def sems():
        return (pltpu.SemaphoreType.DMA((slots,)), pltpu.SemaphoreType.DMA((slots,)))

    return pl.pallas_call(
        functools.partial(mix_kernel, ring, cols, n),
        out_shape=jax.ShapeDtypeStruct((slots * piece, out_w), jnp.float32),
        in_specs=[pl.BlockSpec(memory_space=pltpu.VMEM), pl.BlockSpec(memory_space=pltpu.VMEM)],
        out_specs=pl.BlockSpec(memory_space=pltpu.VMEM),
        scratch_shapes=[
            pltpu.VMEM((slots, n, width), jnp.float32),
            pltpu.VMEM((slots, n, out_w), jnp.float32),
            pltpu.VMEM((slots, piece // 2, out_w), jnp.float32),
            pltpu.VMEM((slots, piece // 2, out_w), jnp.float32),
            pltpu.VMEM((slots, piece, out_w), jnp.float32),
            pltpu.VMEM((slots, piece, out_w), jnp.float32),
            pltpu.VMEM((slots, piece, out_w), jnp.float32),
            pltpu.VMEM((slots, piece, out_w), jnp.float32),
            pltpu.SemaphoreType.DMA((slots,)),
            pltpu.SemaphoreType.DMA((slots,)),
            sems(), sems(), sems(), sems(),
        ],
        compiler_params=pltpu.CompilerParams(
            collective_id=collective_id, has_side_effects=True, vmem_limit_bytes=60 * 1024 * 1024
        ),
    )(o, w_out)


def front_kernel(
    ring, cols, tok_ref, wq_ref, wk_ref, wv_ref, out_ref, kv_out, tg, partial, sibbuf, sbuf, rbuf, kvbuf,
    y_sems, z_sems, sib_sems, kv_sems,
):
    mesh_id = pl.DeviceIdType.MESH
    names = ("depth", "rz", "rc", "col")
    me = {a: lax.axis_index(a) for a in names}
    z, c, y = me["rz"], me["rc"], me["col"]
    rows = tok_ref.shape[0]
    m = rows // (2 * ring)
    h = m // 2

    def device(**moved):
        return tuple(moved.get(a, me[a]) for a in names)

    right = device(rz=lax.rem(z + 1, ring))
    left = device(rz=lax.rem(z + ring - 1, ring))
    sib = device(rc=1 - c)
    y_right = device(col=lax.rem(y + 1, cols))
    y_left = device(col=lax.rem(y + cols - 1, cols))
    peers = [left, right, sib, y_left, y_right]

    barrier = pltpu.get_barrier_semaphore()
    for peer in peers:
        pl.semaphore_signal(barrier, inc=1, device_id=peer, device_id_type=mesh_id)
    pl.semaphore_wait(barrier, len(peers))

    def remote(src, dst, peer, sems, idx):
        cp = pltpu.make_async_remote_copy(
            src_ref=src, dst_ref=dst, send_sem=sems[0].at[idx], recv_sem=sems[1].at[idx],
            device_id=peer, device_id_type=mesh_id,
        )
        cp.start()
        return cp

    def need(s, half):
        sign = -1 if half == 0 else 1
        return lax.rem(z + sign * (s % ring) + ring * ring, ring)

    def round_steps(r, chunk):
        x = partial.at[r]
        base = r * 2 * ring
        sib_copies = {}
        for idx, (s, half) in enumerate((s, half) for s in range(1, ring + 1) for half in (0, 1)):
            at = need(s, half)
            sib_copies[(s, half)] = remote(
                x.at[pl.ds(pl.multiple_of((at * 2 + 1 - c) * m + half * h, 8), h)],
                sibbuf.at[r, pl.ds(pl.multiple_of(at * m + half * h, 8), h)],
                sib, sib_sems, base + idx,
            )
        yield

        def contribution(s, half):
            at = need(s, half)
            sib_copies[(s, half)].wait()
            own = x[pl.ds(pl.multiple_of((at * 2 + c) * m + half * h, 8), h)]
            return own + sibbuf[r, pl.ds(pl.multiple_of(at * m + half * h, 8), h)]

        ring_copies = {}
        for s in range(1, ring):
            for half in (0, 1):
                value = contribution(s, half)
                if s > 1:
                    ring_copies[(s - 1, half)].wait()
                    value = value + rbuf[r, half, s - 2]
                sbuf[r, half, s - 1] = value
                ring_copies[(s, half)] = remote(
                    sbuf.at[r, half, s - 1], rbuf.at[r, half, s - 1],
                    right if half == 0 else left, z_sems, base + half * (ring - 1) + s - 1,
                )
            yield
        for half in (0, 1):
            value = contribution(ring, half)
            ring_copies[(ring - 1, half)].wait()
            value = value + rbuf[r, half, ring - 2]
            out_ref[pl.ds(pl.multiple_of(chunk * m + half * h, 8), h)] = value
            kvbuf[r, z * 2 + c, pl.ds(half * h, h)] = value[:, qw:]
        yield

        def kv_copy(src, at, lo, size, peer, idx):
            return remote(src, kvbuf.at[r, at * 2 + c, pl.ds(lo, size)], peer, kv_sems, base + idx)

        kv_sib = [
            remote(kvbuf.at[r, z * 2 + c], kvbuf.at[r, z * 2 + c], sib, kv_sems, base + ring)
        ]
        half_ring = ring // 2
        for s in range(1, half_ring + 1):
            origin_r = lax.rem(z - (s - 1) + ring, ring)
            origin_l = lax.rem(z + (s - 1), ring)
            src_r = kvbuf.at[r, origin_r * 2 + c]
            src_l = kvbuf.at[r, origin_l * 2 + c]
            if s < half_ring:
                cr = kv_copy(src_r, origin_r, 0, m, right, 2 * (s - 1))
                cl = kv_copy(src_l, origin_l, 0, m, left, 2 * (s - 1) + 1)
            else:
                cr = kv_copy(src_r.at[pl.ds(0, h)], origin_r, 0, h, right, 2 * (s - 1))
                cl = kv_copy(src_l.at[pl.ds(h, h)], origin_l, h, h, left, 2 * (s - 1) + 1)
            yield
            cr.wait()
            cl.wait()
            if s < half_ring:
                got = [(lax.rem(z - s + ring, ring), ring + 2 * s - 1), (lax.rem(z + s, ring), ring + 2 * s)]
            else:
                got = [(lax.rem(z + half_ring, ring), ring + 2 * s - 1)]
            for at, idx in got:
                kv_sib.append(
                    remote(kvbuf.at[r, at * 2 + c], kvbuf.at[r, at * 2 + c], sib, kv_sems, base + idx)
                )
        yield
        for cp in kv_sib:
            cp.wait()
        yield

    qw = wq_ref.shape[1]
    kw = wk_ref.shape[1]

    def project(r, src):
        block = src[...]
        for lo, w_ref in ((0, wq_ref), (qw, wk_ref), (qw + kw, wv_ref)):
            partial[r, :, pl.ds(lo, w_ref.shape[1])] = jnp.dot(
                block, w_ref[...], preferred_element_type=jnp.float32, precision=lax.Precision.HIGH
            )

    y1r = remote(tok_ref, tg.at[1], y_right, y_sems, 0)
    y1l = remote(tok_ref, tg.at[2], y_left, y_sems, 1)
    project(0, tok_ref)
    rounds = [round_steps(0, y)]
    for _ in range(ring):
        next(rounds[0])
    y1r.wait()
    y1l.wait()
    half_rows = rows // 2
    y2r = remote(tg.at[1, pl.ds(0, half_rows)], tg.at[3, pl.ds(0, half_rows)], y_right, y_sems, 2)
    y2l = remote(tg.at[2, pl.ds(half_rows, half_rows)], tg.at[3, pl.ds(half_rows, half_rows)], y_left, y_sems, 3)
    project(1, tg.at[1])
    rounds.append(round_steps(1, lax.rem(y + cols - 1, cols)))
    next(rounds[1])
    project(2, tg.at[2])
    rounds.append(round_steps(2, lax.rem(y + 1, cols)))
    next(rounds[2])
    for _ in range(2):
        for g in rounds:
            next(g, None)
    y2r.wait()
    y2l.wait()
    project(3, tg.at[3])
    rounds.append(round_steps(3, lax.rem(y + 2, cols)))
    next(rounds[3])
    live = list(rounds)
    while live:
        live = [g for g in live if next(g, "done") != "done"]
    kv_out[...] = kvbuf[...]


def front(tokens, w_query, w_key, w_value, ring, cols, collective_id):
    rows, width = tokens.shape
    out_w = w_query.shape[1] + w_key.shape[1] + w_value.shape[1]
    kv_w = w_key.shape[1] + w_value.shape[1]
    m = rows // (2 * ring)
    return pl.pallas_call(
        functools.partial(front_kernel, ring, cols),
        out_shape=(
            jax.ShapeDtypeStruct((cols * m, out_w), jnp.float32),
            jax.ShapeDtypeStruct((cols, 2 * ring, m, kv_w), jnp.float32),
        ),
        in_specs=[pl.BlockSpec(memory_space=pltpu.VMEM)] * 4,
        out_specs=(pl.BlockSpec(memory_space=pltpu.VMEM), pl.BlockSpec(memory_space=pltpu.VMEM)),
        scratch_shapes=[
            pltpu.VMEM((cols, rows, width), jnp.float32),
            pltpu.VMEM((cols, rows, out_w), jnp.float32),
            pltpu.VMEM((cols, ring * m, out_w), jnp.float32),
            pltpu.VMEM((cols, 2, ring - 1, m // 2, out_w), jnp.float32),
            pltpu.VMEM((cols, 2, ring - 1, m // 2, out_w), jnp.float32),
            pltpu.VMEM((cols, 2 * ring, m, kv_w), jnp.float32),
            (pltpu.SemaphoreType.DMA((4,)), pltpu.SemaphoreType.DMA((4,))),
            (pltpu.SemaphoreType.DMA((cols * 2 * ring,)), pltpu.SemaphoreType.DMA((cols * 2 * ring,))),
            (pltpu.SemaphoreType.DMA((cols * 2 * ring,)), pltpu.SemaphoreType.DMA((cols * 2 * ring,))),
            (pltpu.SemaphoreType.DMA((cols * 2 * ring,)), pltpu.SemaphoreType.DMA((cols * 2 * ring,))),
        ],
        compiler_params=pltpu.CompilerParams(
            collective_id=collective_id, has_side_effects=True, vmem_limit_bytes=60 * 1024 * 1024
        ),
    )(tokens, w_query, w_key, w_value)


def on_device(ring, cols, tokens, w_query, w_key, w_value, w_out):
    highest = lax.Precision.HIGH
    q_width = w_query.shape[1]
    kv_width = w_key.shape[1]
    joined, kv_sets = front(tokens, w_query, w_key, w_value, ring, cols, 3)
    query_rows = joined[:, :q_width]
    all_kv = kv_sets.reshape(-1, kv_sets.shape[-1])
    state_end = fold_keys(
        query_rows,
        start_state(query_rows, kv_width),
        (all_kv[:, :kv_width], all_kv[:, kv_width:]),
    )
    return gather_mix(finish(state_end), w_out, ring, cols, 5)


def solution(mesh):
    depth, row, col = (mesh.shape[a] for a in ("depth", "row", "col"))
    split = jax.sharding.Mesh(
        np.asarray(mesh.devices).reshape(depth, row // 2, 2, col), ("depth", "rz", "rc", "col")
    )
    rows = ("rz", "rc")
    placed = (
        P(("depth", "col"), rows),
        P(rows, "col"),
        P(rows, "col"),
        P(rows, "col"),
        P("col", rows),
    )
    return jax.shard_map(
        functools.partial(on_device, row // 2, col),
        mesh=split,
        in_specs=placed,
        out_specs=P(("depth", "col"), rows),
        check_vma=False,
    )
```

```python
import functools
import math

import jax
import numpy as np
import jax.numpy as jnp
from jax import lax
from jax.experimental import pallas as pl
from jax.experimental.pallas import tpu as pltpu
from jax.sharding import PartitionSpec as P

QUERY_HEADS = 32
KEY_VALUE_HEADS = 4
HEAD_SIZE_DIM = 128


def start_state(query_rows, kv_width):
    count_of_heads = kv_width // HEAD_SIZE_DIM
    queries_per_group = QUERY_HEADS // KEY_VALUE_HEADS
    count_of_rows = query_rows.shape[0]
    running_max = jnp.full((count_of_heads, queries_per_group, count_of_rows), -1e30, jnp.float32)
    running_sum = jnp.zeros((count_of_heads, queries_per_group, count_of_rows), jnp.float32)
    weighted = jnp.zeros(
        (count_of_heads, queries_per_group, count_of_rows, HEAD_SIZE_DIM), jnp.float32
    )
    return (running_max, running_sum, weighted)


def fold_keys(query_rows, state_now, block_pair):
    highest = lax.Precision.HIGH
    running_max, running_sum, weighted = state_now
    key_block, value_block = block_pair
    count_of_heads = key_block.shape[1] // HEAD_SIZE_DIM
    count_of_rows = query_rows.shape[0]
    query_head_rows = query_rows.reshape(
        count_of_rows, count_of_heads, QUERY_HEADS // KEY_VALUE_HEADS, HEAD_SIZE_DIM
    )
    key_head_rows = key_block.reshape(-1, count_of_heads, HEAD_SIZE_DIM)
    value_head_rows = value_block.reshape(-1, count_of_heads, HEAD_SIZE_DIM)
    scores = jnp.einsum("rkgd,nkd->kgrn", query_head_rows, key_head_rows, precision=highest) * (
        1.0 / math.sqrt(HEAD_SIZE_DIM)
    )
    newest = jnp.maximum(running_max, jnp.max(scores, axis=-1))
    weights = jnp.exp(scores - newest[..., None])
    running_sum = jnp.sum(weights, axis=-1)
    weighted = jnp.einsum("kgrn,nkd->kgrd", weights, value_head_rows, precision=highest)
    return (newest, running_sum, weighted)


def finish(state_now):
    running_max, running_sum, weighted = state_now
    attention_output = weighted / running_sum[..., None]
    count_of_heads, queries_per_group, count_of_rows, head_size = attention_output.shape
    return attention_output.transpose(2, 0, 1, 3).reshape(
        count_of_rows, count_of_heads * queries_per_group * head_size
    )


def gather_kernel(axis, ring, n, with_sib, x_ref, out_ref, local_sem, send_sems, recv_sems):
    mesh_id = pl.DeviceIdType.MESH
    names = ("depth", "rz", "rc", "col")
    me = {a: lax.axis_index(a) for a in names}
    pos = me[axis]

    def device(**moved):
        return tuple(moved.get(a, me[a]) for a in names)

    right = device(**{axis: lax.rem(pos + 1, ring)})
    left = device(**{axis: lax.rem(pos + ring - 1, ring)})
    sib = device(rc=1 - me["rc"])
    peers = (left, right, sib) if with_sib else (left, right)

    barrier = pltpu.get_barrier_semaphore()
    for peer in peers:
        pl.semaphore_signal(barrier, inc=1, device_id=peer, device_id_type=mesh_id)
    pl.semaphore_wait(barrier, len(peers))

    def rows(at, lo=0, size=n):
        slot = at * 2 + me["rc"] if with_sib else at
        return pl.ds(pl.multiple_of(slot * n + lo, 8), size)

    def remote(src, dst_rows, peer, idx):
        cp = pltpu.make_async_remote_copy(
            src_ref=src,
            dst_ref=out_ref.at[dst_rows],
            send_sem=send_sems.at[idx],
            recv_sem=recv_sems.at[idx],
            device_id=peer,
            device_id_type=mesh_id,
        )
        cp.start()
        return cp

    def to_sib(at, idx):
        if with_sib:
            sib_copies.append(remote(out_ref.at[rows(at)], rows(at), sib, idx))

    local = pltpu.make_async_copy(x_ref, out_ref.at[rows(pos)], local_sem)
    local.start()
    sib_copies = [remote(x_ref, rows(pos), sib, ring)] if with_sib else []
    half = ring // 2
    for s in range(1, half + 1):
        origin_r = lax.rem(pos - (s - 1) + ring, ring)
        origin_l = lax.rem(pos + (s - 1), ring)
        src_r = x_ref if s == 1 else out_ref.at[rows(origin_r)]
        src_l = x_ref if s == 1 else out_ref.at[rows(origin_l)]
        if s < half:
            cr = remote(src_r, rows(origin_r), right, 2 * (s - 1))
            cl = remote(src_l, rows(origin_l), left, 2 * (s - 1) + 1)
            cr.wait()
            cl.wait()
            to_sib(lax.rem(pos - s + ring, ring), ring + 2 * s - 1)
            to_sib(lax.rem(pos + s, ring), ring + 2 * s)
        else:
            h = n // 2
            cr = remote(src_r.at[pl.ds(0, h)], rows(origin_r, 0, h), right, 2 * (s - 1))
            cl = remote(src_l.at[pl.ds(h, h)], rows(origin_l, h, h), left, 2 * (s - 1) + 1)
            cr.wait()
            cl.wait()
            to_sib(lax.rem(pos + half, ring), ring + 2 * s - 1)
    local.wait()
    for cp in sib_copies:
        cp.wait()


def ring_gather(block, axis, ring, with_sib, collective_id):
    n, w = block.shape
    copies = 2 if with_sib else 1
    return pl.pallas_call(
        functools.partial(gather_kernel, axis, ring, n, with_sib),
        out_shape=jax.ShapeDtypeStruct((copies * ring * n, w), block.dtype),
        in_specs=[pl.BlockSpec(memory_space=pl.ANY)],
        out_specs=pl.BlockSpec(memory_space=pl.ANY),
        scratch_shapes=[
            pltpu.SemaphoreType.DMA(()),
            pltpu.SemaphoreType.DMA((2 * ring,)),
            pltpu.SemaphoreType.DMA((2 * ring,)),
        ],
        compiler_params=pltpu.CompilerParams(collective_id=collective_id, has_side_effects=True),
    )(block)


def scatter_kernel(axis, ring, m, with_sib, parts, x_ref, out_ref, sbuf, rbuf, sibbuf, send_sems, recv_sems, sib_sems):
    mesh_id = pl.DeviceIdType.MESH
    names = ("depth", "rz", "rc", "col")
    me = {a: lax.axis_index(a) for a in names}
    pos = me[axis]
    h = m // 2
    q = h // parts

    def device(**moved):
        return tuple(moved.get(a, me[a]) for a in names)

    right = device(**{axis: lax.rem(pos + 1, ring)})
    left = device(**{axis: lax.rem(pos + ring - 1, ring)})
    sib = device(rc=1 - me["rc"])
    peers = (left, right, sib) if with_sib else (left, right)

    barrier = pltpu.get_barrier_semaphore()
    for peer in peers:
        pl.semaphore_signal(barrier, inc=1, device_id=peer, device_id_type=mesh_id)
    pl.semaphore_wait(barrier, len(peers))

    def rows_of(at, half, part, owner):
        slot = at * 2 + owner if with_sib else at
        return pl.ds(pl.multiple_of(slot * m + half * h + part * q, 8), q)

    def sib_rows(at, half, part):
        return pl.ds(pl.multiple_of(at * m + half * h + part * q, 8), q)

    def remote(src, dst, peer, sems, idx):
        cp = pltpu.make_async_remote_copy(
            src_ref=src,
            dst_ref=dst,
            send_sem=sems[0].at[idx],
            recv_sem=sems[1].at[idx],
            device_id=peer,
            device_id_type=mesh_id,
        )
        cp.start()
        return cp

    def need(s, half):
        sign = -1 if half == 0 else 1
        return lax.rem(pos + sign * (s % ring) + ring * ring, ring)

    sib_copies = {}
    if with_sib:
        order = [(s, half) for s in range(1, ring + 1) for half in (0, 1)]
        for idx, (s, half) in enumerate(order):
            at = need(s, half)
            sib_copies[(s, half)] = remote(
                x_ref.at[pl.ds(pl.multiple_of((at * 2 + 1 - me["rc"]) * m + half * h, 8), h)],
                sibbuf.at[pl.ds(pl.multiple_of(at * m + half * h, 8), h)],
                sib,
                (sib_sems[0], sib_sems[1]),
                idx,
            )

    def contribution(s, half, part):
        at = need(s, half)
        own = x_ref[rows_of(at, half, part, me["rc"])]
        if with_sib:
            if part == 0:
                sib_copies[(s, half)].wait()
            own = own + sibbuf[sib_rows(at, half, part)]
        return own

    ring_copies = {}
    for s in range(1, ring):
        for part in range(parts):
            for half in (0, 1):
                value = contribution(s, half, part)
                if s > 1:
                    ring_copies[(s - 1, half, part)].wait()
                    value = value + rbuf[half, s - 2, part]
                sbuf[half, s - 1, part] = value
                ring_copies[(s, half, part)] = remote(
                    sbuf.at[half, s - 1, part],
                    rbuf.at[half, s - 1, part],
                    right if half == 0 else left,
                    (send_sems, recv_sems),
                    (half * (ring - 1) + s - 1) * parts + part,
                )
    for part in range(parts):
        for half in (0, 1):
            value = contribution(ring, half, part)
            ring_copies[(ring - 1, half, part)].wait()
            out_ref[pl.ds(half * h + part * q, q)] = value + rbuf[half, ring - 2, part]


def ring_scatter(x, axis, ring, with_sib, parts, collective_id):
    total, w = x.shape
    copies = 2 if with_sib else 1
    m = total // (copies * ring)
    sib_rows = ring * m if with_sib else 8
    return pl.pallas_call(
        functools.partial(scatter_kernel, axis, ring, m, with_sib, parts),
        out_shape=jax.ShapeDtypeStruct((m, w), x.dtype),
        in_specs=[pl.BlockSpec(memory_space=pltpu.VMEM)],
        out_specs=pl.BlockSpec(memory_space=pltpu.VMEM),
        scratch_shapes=[
            pltpu.VMEM((2, ring - 1, parts, m // 2 // parts, w), x.dtype),
            pltpu.VMEM((2, ring - 1, parts, m // 2 // parts, w), x.dtype),
            pltpu.VMEM((sib_rows, w), x.dtype),
            pltpu.SemaphoreType.DMA((2 * ring * parts,)),
            pltpu.SemaphoreType.DMA((2 * ring * parts,)),
            (pltpu.SemaphoreType.DMA((2 * ring,)), pltpu.SemaphoreType.DMA((2 * ring,))),
        ],
        compiler_params=pltpu.CompilerParams(
            collective_id=collective_id, has_side_effects=True, vmem_limit_bytes=60 * 1024 * 1024
        ),
    )(x)


def mix_kernel(ring, cols, n, o_ref, wo_ref, out_ref, ogath, part, recv, send_sems, recv_sems, y_send, y_recv):
    mesh_id = pl.DeviceIdType.MESH
    names = ("depth", "rz", "rc", "col")
    me = {a: lax.axis_index(a) for a in names}
    z, c, y = me["rz"], me["rc"], me["col"]
    per_col = 2 * ring // cols

    def device(**moved):
        return tuple(moved.get(a, me[a]) for a in names)

    right = device(rz=lax.rem(z + 1, ring))
    left = device(rz=lax.rem(z + ring - 1, ring))
    sib = device(rc=1 - c)
    peers = [left, right, sib] + [device(col=lax.rem(y + d, cols)) for d in range(1, cols)]

    barrier = pltpu.get_barrier_semaphore()
    for peer in peers:
        pl.semaphore_signal(barrier, inc=1, device_id=peer, device_id_type=mesh_id)
    pl.semaphore_wait(barrier, len(peers))

    def remote(src, dst, peer, send, recv_sem):
        cp = pltpu.make_async_remote_copy(
            src_ref=src, dst_ref=dst, send_sem=send, recv_sem=recv_sem, device_id=peer, device_id_type=mesh_id
        )
        cp.start()
        return cp

    piece = n // cols

    def project(block, k):
        part[k] = jnp.dot(block, wo_ref[...], preferred_element_type=jnp.float32, precision=lax.Precision.HIGH)
        for d in range(1, cols):
            dest = lax.rem(y + d, cols)
            remote(
                part.at[k, pl.ds(pl.multiple_of(dest * piece, 8), piece)],
                recv.at[cols - d, k],
                device(col=dest),
                y_send.at[k * cols + d],
                y_recv.at[(cols - d) * 2 * ring + k],
            )

    def slot(zz, cc):
        return zz * 2 + cc

    def z_copy(src, dst_slot, lo, size, peer, idx):
        return remote(src, ogath.at[dst_slot, pl.ds(lo, size)], peer, send_sems.at[idx], recv_sems.at[idx])

    pending_sib = [(z_copy(o_ref, slot(z, c), 0, n, sib, ring), z)]
    to_project = [slot(z, c)]
    half = ring // 2
    for s in range(1, half + 1):
        origin_r = lax.rem(z - (s - 1) + ring, ring)
        origin_l = lax.rem(z + (s - 1), ring)
        src_r = o_ref if s == 1 else ogath.at[slot(origin_r, c)]
        src_l = o_ref if s == 1 else ogath.at[slot(origin_l, c)]
        if s < half:
            cr = z_copy(src_r, slot(origin_r, c), 0, n, right, 2 * (s - 1))
            cl = z_copy(src_l, slot(origin_l, c), 0, n, left, 2 * (s - 1) + 1)
        else:
            h = n // 2
            cr = z_copy(src_r.at[pl.ds(0, h)], slot(origin_r, c), 0, h, right, 2 * (s - 1))
            cl = z_copy(src_l.at[pl.ds(h, h)], slot(origin_l, c), h, h, left, 2 * (s - 1) + 1)
        for k in to_project:
            project(o_ref[...] if s == 1 else ogath[k], k)
        to_project = []
        for cp, at in pending_sib:
            cp.wait()
            project(ogath[slot(at, 1 - c)], slot(at, 1 - c))
        pending_sib = []
        cr.wait()
        cl.wait()
        if s < half:
            arrived = [(lax.rem(z - s + ring, ring), ring + 2 * s - 1), (lax.rem(z + s, ring), ring + 2 * s)]
        else:
            arrived = [(lax.rem(z + half, ring), ring + 2 * s - 1)]
        for at, idx in arrived:
            pending_sib.append((z_copy(ogath.at[slot(at, c)], slot(at, c), 0, n, sib, idx), at))
            to_project.append(slot(at, c))
    for k in to_project:
        project(ogath[k], k)
    for cp, at in pending_sib:
        cp.wait()
        project(ogath[slot(at, 1 - c)], slot(at, 1 - c))
    for k in range(2 * ring):
        total = part[k, pl.ds(pl.multiple_of(y * piece, 8), piece)]
        for d in range(1, cols):
            pltpu.make_async_remote_copy(
                src_ref=part.at[k, pl.ds(0, piece)],
                dst_ref=recv.at[d, k],
                send_sem=y_send.at[0],
                recv_sem=y_recv.at[d * 2 * ring + k],
                device_id=device(col=lax.rem(y + d, cols)),
                device_id_type=mesh_id,
            ).wait_recv()
            total = total + recv[d, k]
        out_ref[pl.ds(k * piece, piece)] = total
    for k in range(2 * ring):
        for d in range(1, cols):
            pltpu.make_async_remote_copy(
                src_ref=part.at[k, pl.ds(0, piece)],
                dst_ref=recv.at[0, 0],
                send_sem=y_send.at[k * cols + d],
                recv_sem=y_recv.at[0],
                device_id=device(col=lax.rem(y + d, cols)),
                device_id_type=mesh_id,
            ).wait_send()


def gather_mix(o, w_out, ring, cols, collective_id):
    n, width = o.shape
    out_w = w_out.shape[1]
    per_col = 2 * ring // cols
    return pl.pallas_call(
        functools.partial(mix_kernel, ring, cols, n),
        out_shape=jax.ShapeDtypeStruct((per_col * n, out_w), jnp.float32),
        in_specs=[pl.BlockSpec(memory_space=pltpu.VMEM), pl.BlockSpec(memory_space=pltpu.VMEM)],
        out_specs=pl.BlockSpec(memory_space=pltpu.VMEM),
        scratch_shapes=[
            pltpu.VMEM((2 * ring, n, width), jnp.float32),
            pltpu.VMEM((2 * ring, n, out_w), jnp.float32),
            pltpu.VMEM((cols, 2 * ring, n // cols, out_w), jnp.float32),
            pltpu.SemaphoreType.DMA((2 * ring,)),
            pltpu.SemaphoreType.DMA((2 * ring,)),
            pltpu.SemaphoreType.DMA((2 * ring * cols,)),
            pltpu.SemaphoreType.DMA((2 * ring * cols,)),
        ],
        compiler_params=pltpu.CompilerParams(
            collective_id=collective_id, has_side_effects=True, vmem_limit_bytes=60 * 1024 * 1024
        ),
    )(o, w_out)


def front_kernel(
    ring, cols, tok_ref, wq_ref, wk_ref, wv_ref, out_ref, kv_out, tg, partial, sibbuf, sbuf, rbuf, kvbuf,
    y_sems, z_sems, sib_sems, kv_sems,
):
    mesh_id = pl.DeviceIdType.MESH
    names = ("depth", "rz", "rc", "col")
    me = {a: lax.axis_index(a) for a in names}
    z, c, y = me["rz"], me["rc"], me["col"]
    rows = tok_ref.shape[0]
    m = rows // (2 * ring)
    h = m // 2

    def device(**moved):
        return tuple(moved.get(a, me[a]) for a in names)

    right = device(rz=lax.rem(z + 1, ring))
    left = device(rz=lax.rem(z + ring - 1, ring))
    sib = device(rc=1 - c)
    y_right = device(col=lax.rem(y + 1, cols))
    y_left = device(col=lax.rem(y + cols - 1, cols))
    peers = [left, right, sib, y_left, y_right]

    barrier = pltpu.get_barrier_semaphore()
    for peer in peers:
        pl.semaphore_signal(barrier, inc=1, device_id=peer, device_id_type=mesh_id)
    pl.semaphore_wait(barrier, len(peers))

    def remote(src, dst, peer, sems, idx):
        cp = pltpu.make_async_remote_copy(
            src_ref=src, dst_ref=dst, send_sem=sems[0].at[idx], recv_sem=sems[1].at[idx],
            device_id=peer, device_id_type=mesh_id,
        )
        cp.start()
        return cp

    def need(s, half):
        sign = -1 if half == 0 else 1
        return lax.rem(z + sign * (s % ring) + ring * ring, ring)

    def round_steps(r, chunk):
        x = partial.at[r]
        base = r * 2 * ring
        sib_copies = {}
        for idx, (s, half) in enumerate((s, half) for s in range(1, ring + 1) for half in (0, 1)):
            at = need(s, half)
            sib_copies[(s, half)] = remote(
                x.at[pl.ds(pl.multiple_of((at * 2 + 1 - c) * m + half * h, 8), h)],
                sibbuf.at[r, pl.ds(pl.multiple_of(at * m + half * h, 8), h)],
                sib, sib_sems, base + idx,
            )
        yield

        def contribution(s, half):
            at = need(s, half)
            sib_copies[(s, half)].wait()
            own = x[pl.ds(pl.multiple_of((at * 2 + c) * m + half * h, 8), h)]
            return own + sibbuf[r, pl.ds(pl.multiple_of(at * m + half * h, 8), h)]

        ring_copies = {}
        for s in range(1, ring):
            for half in (0, 1):
                value = contribution(s, half)
                if s > 1:
                    ring_copies[(s - 1, half)].wait()
                    value = value + rbuf[r, half, s - 2]
                sbuf[r, half, s - 1] = value
                ring_copies[(s, half)] = remote(
                    sbuf.at[r, half, s - 1], rbuf.at[r, half, s - 1],
                    right if half == 0 else left, z_sems, base + half * (ring - 1) + s - 1,
                )
            yield
        for half in (0, 1):
            value = contribution(ring, half)
            ring_copies[(ring - 1, half)].wait()
            value = value + rbuf[r, half, ring - 2]
            out_ref[pl.ds(pl.multiple_of(chunk * m + half * h, 8), h)] = value
            kvbuf[r, z * 2 + c, pl.ds(half * h, h)] = value[:, qw:]
        yield

        def kv_copy(src, at, lo, size, peer, idx):
            return remote(src, kvbuf.at[r, at * 2 + c, pl.ds(lo, size)], peer, kv_sems, base + idx)

        kv_sib = [
            remote(kvbuf.at[r, z * 2 + c], kvbuf.at[r, z * 2 + c], sib, kv_sems, base + ring)
        ]
        half_ring = ring // 2
        for s in range(1, half_ring + 1):
            origin_r = lax.rem(z - (s - 1) + ring, ring)
            origin_l = lax.rem(z + (s - 1), ring)
            src_r = kvbuf.at[r, origin_r * 2 + c]
            src_l = kvbuf.at[r, origin_l * 2 + c]
            if s < half_ring:
                cr = kv_copy(src_r, origin_r, 0, m, right, 2 * (s - 1))
                cl = kv_copy(src_l, origin_l, 0, m, left, 2 * (s - 1) + 1)
            else:
                cr = kv_copy(src_r.at[pl.ds(0, h)], origin_r, 0, h, right, 2 * (s - 1))
                cl = kv_copy(src_l.at[pl.ds(h, h)], origin_l, h, h, left, 2 * (s - 1) + 1)
            yield
            cr.wait()
            cl.wait()
            if s < half_ring:
                got = [(lax.rem(z - s + ring, ring), ring + 2 * s - 1), (lax.rem(z + s, ring), ring + 2 * s)]
            else:
                got = [(lax.rem(z + half_ring, ring), ring + 2 * s - 1)]
            for at, idx in got:
                kv_sib.append(
                    remote(kvbuf.at[r, at * 2 + c], kvbuf.at[r, at * 2 + c], sib, kv_sems, base + idx)
                )
        yield
        for cp in kv_sib:
            cp.wait()
        yield

    qw = wq_ref.shape[1]
    kw = wk_ref.shape[1]

    def project(r, src):
        block = src[...]
        for lo, w_ref in ((0, wq_ref), (qw, wk_ref), (qw + kw, wv_ref)):
            partial[r, :, pl.ds(lo, w_ref.shape[1])] = jnp.dot(
                block, w_ref[...], preferred_element_type=jnp.float32, precision=lax.Precision.HIGH
            )

    y1r = remote(tok_ref, tg.at[1], y_right, y_sems, 0)
    y1l = remote(tok_ref, tg.at[2], y_left, y_sems, 1)
    project(0, tok_ref)
    rounds = [round_steps(0, y)]
    for _ in range(ring):
        next(rounds[0])
    y1r.wait()
    y1l.wait()
    half_rows = rows // 2
    y2r = remote(tg.at[1, pl.ds(0, half_rows)], tg.at[3, pl.ds(0, half_rows)], y_right, y_sems, 2)
    y2l = remote(tg.at[2, pl.ds(half_rows, half_rows)], tg.at[3, pl.ds(half_rows, half_rows)], y_left, y_sems, 3)
    project(1, tg.at[1])
    rounds.append(round_steps(1, lax.rem(y + cols - 1, cols)))
    next(rounds[1])
    project(2, tg.at[2])
    rounds.append(round_steps(2, lax.rem(y + 1, cols)))
    next(rounds[2])
    for _ in range(2):
        for g in rounds:
            next(g, None)
    y2r.wait()
    y2l.wait()
    project(3, tg.at[3])
    rounds.append(round_steps(3, lax.rem(y + 2, cols)))
    next(rounds[3])
    live = list(rounds)
    while live:
        live = [g for g in live if next(g, "done") != "done"]
    kv_out[...] = kvbuf[...]


def front(tokens, w_query, w_key, w_value, ring, cols, collective_id):
    rows, width = tokens.shape
    out_w = w_query.shape[1] + w_key.shape[1] + w_value.shape[1]
    kv_w = w_key.shape[1] + w_value.shape[1]
    m = rows // (2 * ring)
    return pl.pallas_call(
        functools.partial(front_kernel, ring, cols),
        out_shape=(
            jax.ShapeDtypeStruct((cols * m, out_w), jnp.float32),
            jax.ShapeDtypeStruct((cols, 2 * ring, m, kv_w), jnp.float32),
        ),
        in_specs=[pl.BlockSpec(memory_space=pltpu.VMEM)] * 4,
        out_specs=(pl.BlockSpec(memory_space=pltpu.VMEM), pl.BlockSpec(memory_space=pltpu.VMEM)),
        scratch_shapes=[
            pltpu.VMEM((cols, rows, width), jnp.float32),
            pltpu.VMEM((cols, rows, out_w), jnp.float32),
            pltpu.VMEM((cols, ring * m, out_w), jnp.float32),
            pltpu.VMEM((cols, 2, ring - 1, m // 2, out_w), jnp.float32),
            pltpu.VMEM((cols, 2, ring - 1, m // 2, out_w), jnp.float32),
            pltpu.VMEM((cols, 2 * ring, m, kv_w), jnp.float32),
            (pltpu.SemaphoreType.DMA((4,)), pltpu.SemaphoreType.DMA((4,))),
            (pltpu.SemaphoreType.DMA((cols * 2 * ring,)), pltpu.SemaphoreType.DMA((cols * 2 * ring,))),
            (pltpu.SemaphoreType.DMA((cols * 2 * ring,)), pltpu.SemaphoreType.DMA((cols * 2 * ring,))),
            (pltpu.SemaphoreType.DMA((cols * 2 * ring,)), pltpu.SemaphoreType.DMA((cols * 2 * ring,))),
        ],
        compiler_params=pltpu.CompilerParams(
            collective_id=collective_id, has_side_effects=True, vmem_limit_bytes=60 * 1024 * 1024
        ),
    )(tokens, w_query, w_key, w_value)


def on_device(ring, cols, tokens, w_query, w_key, w_value, w_out):
    highest = lax.Precision.HIGH
    q_width = w_query.shape[1]
    kv_width = w_key.shape[1]
    joined, kv_sets = front(tokens, w_query, w_key, w_value, ring, cols, 3)
    query_rows = joined[:, :q_width]
    all_kv = kv_sets.reshape(-1, kv_sets.shape[-1])
    state_end = fold_keys(
        query_rows,
        start_state(query_rows, kv_width),
        (all_kv[:, :kv_width], all_kv[:, kv_width:]),
    )
    return gather_mix(finish(state_end), w_out, ring, cols, 5)


def solution(mesh):
    depth, row, col = (mesh.shape[a] for a in ("depth", "row", "col"))
    split = jax.sharding.Mesh(
        np.asarray(mesh.devices).reshape(depth, row // 2, 2, col), ("depth", "rz", "rc", "col")
    )
    rows = ("rz", "rc")
    placed = (
        P(("depth", "col"), rows),
        P(rows, "col"),
        P(rows, "col"),
        P(rows, "col"),
        P("col", rows),
    )
    return jax.shard_map(
        functools.partial(on_device, row // 2, col),
        mesh=split,
        in_specs=placed,
        out_specs=P(("depth", "col"), rows),
        check_vma=False,
    )
```

```python
import functools
import math

import jax
import numpy as np
import jax.numpy as jnp
from jax import lax
from jax.experimental import pallas as pl
from jax.experimental.pallas import tpu as pltpu
from jax.sharding import PartitionSpec as P

QUERY_HEADS = 32
KEY_VALUE_HEADS = 4
HEAD_SIZE_DIM = 128


def start_state(query_rows, kv_width):
    count_of_heads = kv_width // HEAD_SIZE_DIM
    queries_per_group = QUERY_HEADS // KEY_VALUE_HEADS
    count_of_rows = query_rows.shape[0]
    running_max = jnp.full((count_of_heads, queries_per_group, count_of_rows), -1e30, jnp.float32)
    running_sum = jnp.zeros((count_of_heads, queries_per_group, count_of_rows), jnp.float32)
    weighted = jnp.zeros(
        (count_of_heads, queries_per_group, count_of_rows, HEAD_SIZE_DIM), jnp.float32
    )
    return (running_max, running_sum, weighted)


def fold_keys(query_rows, state_now, block_pair):
    highest = lax.Precision.HIGH
    running_max, running_sum, weighted = state_now
    key_block, value_block = block_pair
    count_of_heads = key_block.shape[1] // HEAD_SIZE_DIM
    count_of_rows = query_rows.shape[0]
    query_head_rows = query_rows.reshape(
        count_of_rows, count_of_heads, QUERY_HEADS // KEY_VALUE_HEADS, HEAD_SIZE_DIM
    )
    key_head_rows = key_block.reshape(-1, count_of_heads, HEAD_SIZE_DIM)
    value_head_rows = value_block.reshape(-1, count_of_heads, HEAD_SIZE_DIM)
    scores = jnp.einsum("rkgd,nkd->kgrn", query_head_rows, key_head_rows, precision=highest) * (
        1.0 / math.sqrt(HEAD_SIZE_DIM)
    )
    newest = jnp.maximum(running_max, jnp.max(scores, axis=-1))
    weights = jnp.exp(scores - newest[..., None])
    running_sum = jnp.sum(weights, axis=-1)
    weighted = jnp.einsum("kgrn,nkd->kgrd", weights, value_head_rows, precision=highest)
    return (newest, running_sum, weighted)


def finish(state_now):
    running_max, running_sum, weighted = state_now
    attention_output = weighted / running_sum[..., None]
    count_of_heads, queries_per_group, count_of_rows, head_size = attention_output.shape
    return attention_output.transpose(2, 0, 1, 3).reshape(
        count_of_rows, count_of_heads * queries_per_group * head_size
    )


def gather_kernel(axis, ring, n, with_sib, x_ref, out_ref, local_sem, send_sems, recv_sems):
    mesh_id = pl.DeviceIdType.MESH
    names = ("depth", "rz", "rc", "col")
    me = {a: lax.axis_index(a) for a in names}
    pos = me[axis]

    def device(**moved):
        return tuple(moved.get(a, me[a]) for a in names)

    right = device(**{axis: lax.rem(pos + 1, ring)})
    left = device(**{axis: lax.rem(pos + ring - 1, ring)})
    sib = device(rc=1 - me["rc"])
    peers = (left, right, sib) if with_sib else (left, right)

    barrier = pltpu.get_barrier_semaphore()
    for peer in peers:
        pl.semaphore_signal(barrier, inc=1, device_id=peer, device_id_type=mesh_id)
    pl.semaphore_wait(barrier, len(peers))

    def rows(at, lo=0, size=n):
        slot = at * 2 + me["rc"] if with_sib else at
        return pl.ds(pl.multiple_of(slot * n + lo, 8), size)

    def remote(src, dst_rows, peer, idx):
        cp = pltpu.make_async_remote_copy(
            src_ref=src,
            dst_ref=out_ref.at[dst_rows],
            send_sem=send_sems.at[idx],
            recv_sem=recv_sems.at[idx],
            device_id=peer,
            device_id_type=mesh_id,
        )
        cp.start()
        return cp

    def to_sib(at, idx):
        if with_sib:
            sib_copies.append(remote(out_ref.at[rows(at)], rows(at), sib, idx))

    local = pltpu.make_async_copy(x_ref, out_ref.at[rows(pos)], local_sem)
    local.start()
    sib_copies = [remote(x_ref, rows(pos), sib, ring)] if with_sib else []
    half = ring // 2
    for s in range(1, half + 1):
        origin_r = lax.rem(pos - (s - 1) + ring, ring)
        origin_l = lax.rem(pos + (s - 1), ring)
        src_r = x_ref if s == 1 else out_ref.at[rows(origin_r)]
        src_l = x_ref if s == 1 else out_ref.at[rows(origin_l)]
        if s < half:
            cr = remote(src_r, rows(origin_r), right, 2 * (s - 1))
            cl = remote(src_l, rows(origin_l), left, 2 * (s - 1) + 1)
            cr.wait()
            cl.wait()
            to_sib(lax.rem(pos - s + ring, ring), ring + 2 * s - 1)
            to_sib(lax.rem(pos + s, ring), ring + 2 * s)
        else:
            h = n // 2
            cr = remote(src_r.at[pl.ds(0, h)], rows(origin_r, 0, h), right, 2 * (s - 1))
            cl = remote(src_l.at[pl.ds(h, h)], rows(origin_l, h, h), left, 2 * (s - 1) + 1)
            cr.wait()
            cl.wait()
            to_sib(lax.rem(pos + half, ring), ring + 2 * s - 1)
    local.wait()
    for cp in sib_copies:
        cp.wait()


def ring_gather(block, axis, ring, with_sib, collective_id):
    n, w = block.shape
    copies = 2 if with_sib else 1
    return pl.pallas_call(
        functools.partial(gather_kernel, axis, ring, n, with_sib),
        out_shape=jax.ShapeDtypeStruct((copies * ring * n, w), block.dtype),
        in_specs=[pl.BlockSpec(memory_space=pl.ANY)],
        out_specs=pl.BlockSpec(memory_space=pl.ANY),
        scratch_shapes=[
            pltpu.SemaphoreType.DMA(()),
            pltpu.SemaphoreType.DMA((2 * ring,)),
            pltpu.SemaphoreType.DMA((2 * ring,)),
        ],
        compiler_params=pltpu.CompilerParams(collective_id=collective_id, has_side_effects=True),
    )(block)


def scatter_kernel(axis, ring, m, with_sib, parts, x_ref, out_ref, sbuf, rbuf, sibbuf, send_sems, recv_sems, sib_sems):
    mesh_id = pl.DeviceIdType.MESH
    names = ("depth", "rz", "rc", "col")
    me = {a: lax.axis_index(a) for a in names}
    pos = me[axis]
    h = m // 2
    q = h // parts

    def device(**moved):
        return tuple(moved.get(a, me[a]) for a in names)

    right = device(**{axis: lax.rem(pos + 1, ring)})
    left = device(**{axis: lax.rem(pos + ring - 1, ring)})
    sib = device(rc=1 - me["rc"])
    peers = (left, right, sib) if with_sib else (left, right)

    barrier = pltpu.get_barrier_semaphore()
    for peer in peers:
        pl.semaphore_signal(barrier, inc=1, device_id=peer, device_id_type=mesh_id)
    pl.semaphore_wait(barrier, len(peers))

    def rows_of(at, half, part, owner):
        slot = at * 2 + owner if with_sib else at
        return pl.ds(pl.multiple_of(slot * m + half * h + part * q, 8), q)

    def sib_rows(at, half, part):
        return pl.ds(pl.multiple_of(at * m + half * h + part * q, 8), q)

    def remote(src, dst, peer, sems, idx):
        cp = pltpu.make_async_remote_copy(
            src_ref=src,
            dst_ref=dst,
            send_sem=sems[0].at[idx],
            recv_sem=sems[1].at[idx],
            device_id=peer,
            device_id_type=mesh_id,
        )
        cp.start()
        return cp

    def need(s, half):
        sign = -1 if half == 0 else 1
        return lax.rem(pos + sign * (s % ring) + ring * ring, ring)

    sib_copies = {}
    if with_sib:
        order = [(s, half) for s in range(1, ring + 1) for half in (0, 1)]
        for idx, (s, half) in enumerate(order):
            at = need(s, half)
            sib_copies[(s, half)] = remote(
                x_ref.at[pl.ds(pl.multiple_of((at * 2 + 1 - me["rc"]) * m + half * h, 8), h)],
                sibbuf.at[pl.ds(pl.multiple_of(at * m + half * h, 8), h)],
                sib,
                (sib_sems[0], sib_sems[1]),
                idx,
            )

    def contribution(s, half, part):
        at = need(s, half)
        own = x_ref[rows_of(at, half, part, me["rc"])]
        if with_sib:
            if part == 0:
                sib_copies[(s, half)].wait()
            own = own + sibbuf[sib_rows(at, half, part)]
        return own

    ring_copies = {}
    for s in range(1, ring):
        for part in range(parts):
            for half in (0, 1):
                value = contribution(s, half, part)
                if s > 1:
                    ring_copies[(s - 1, half, part)].wait()
                    value = value + rbuf[half, s - 2, part]
                sbuf[half, s - 1, part] = value
                ring_copies[(s, half, part)] = remote(
                    sbuf.at[half, s - 1, part],
                    rbuf.at[half, s - 1, part],
                    right if half == 0 else left,
                    (send_sems, recv_sems),
                    (half * (ring - 1) + s - 1) * parts + part,
                )
    for part in range(parts):
        for half in (0, 1):
            value = contribution(ring, half, part)
            ring_copies[(ring - 1, half, part)].wait()
            out_ref[pl.ds(half * h + part * q, q)] = value + rbuf[half, ring - 2, part]


def ring_scatter(x, axis, ring, with_sib, parts, collective_id):
    total, w = x.shape
    copies = 2 if with_sib else 1
    m = total // (copies * ring)
    sib_rows = ring * m if with_sib else 8
    return pl.pallas_call(
        functools.partial(scatter_kernel, axis, ring, m, with_sib, parts),
        out_shape=jax.ShapeDtypeStruct((m, w), x.dtype),
        in_specs=[pl.BlockSpec(memory_space=pltpu.VMEM)],
        out_specs=pl.BlockSpec(memory_space=pltpu.VMEM),
        scratch_shapes=[
            pltpu.VMEM((2, ring - 1, parts, m // 2 // parts, w), x.dtype),
            pltpu.VMEM((2, ring - 1, parts, m // 2 // parts, w), x.dtype),
            pltpu.VMEM((sib_rows, w), x.dtype),
            pltpu.SemaphoreType.DMA((2 * ring * parts,)),
            pltpu.SemaphoreType.DMA((2 * ring * parts,)),
            (pltpu.SemaphoreType.DMA((2 * ring,)), pltpu.SemaphoreType.DMA((2 * ring,))),
        ],
        compiler_params=pltpu.CompilerParams(
            collective_id=collective_id, has_side_effects=True, vmem_limit_bytes=60 * 1024 * 1024
        ),
    )(x)


def mix_kernel(ring, cols, n, o_ref, wo_ref, out_ref, ogath, part, recv, send_sems, recv_sems, y_send, y_recv):
    mesh_id = pl.DeviceIdType.MESH
    names = ("depth", "rz", "rc", "col")
    me = {a: lax.axis_index(a) for a in names}
    z, c, y = me["rz"], me["rc"], me["col"]
    per_col = 2 * ring // cols

    def device(**moved):
        return tuple(moved.get(a, me[a]) for a in names)

    right = device(rz=lax.rem(z + 1, ring))
    left = device(rz=lax.rem(z + ring - 1, ring))
    sib = device(rc=1 - c)
    peers = [left, right, sib] + [device(col=lax.rem(y + d, cols)) for d in range(1, cols)]

    barrier = pltpu.get_barrier_semaphore()
    for peer in peers:
        pl.semaphore_signal(barrier, inc=1, device_id=peer, device_id_type=mesh_id)
    pl.semaphore_wait(barrier, len(peers))

    def remote(src, dst, peer, send, recv_sem):
        cp = pltpu.make_async_remote_copy(
            src_ref=src, dst_ref=dst, send_sem=send, recv_sem=recv_sem, device_id=peer, device_id_type=mesh_id
        )
        cp.start()
        return cp

    piece = n // cols

    def project(block, k):
        part[k] = jnp.dot(block, wo_ref[...], preferred_element_type=jnp.float32, precision=lax.Precision.HIGH)
        for d in range(1, cols):
            dest = lax.rem(y + d, cols)
            remote(
                part.at[k, pl.ds(pl.multiple_of(dest * piece, 8), piece)],
                recv.at[cols - d, k],
                device(col=dest),
                y_send.at[k * cols + d],
                y_recv.at[(cols - d) * 2 * ring + k],
            )

    def slot(zz, cc):
        return zz * 2 + cc

    def z_copy(src, dst_slot, lo, size, peer, idx):
        return remote(src, ogath.at[dst_slot, pl.ds(lo, size)], peer, send_sems.at[idx], recv_sems.at[idx])

    pending_sib = [(z_copy(o_ref, slot(z, c), 0, n, sib, ring), z)]
    to_project = [slot(z, c)]
    half = ring // 2
    for s in range(1, half + 1):
        origin_r = lax.rem(z - (s - 1) + ring, ring)
        origin_l = lax.rem(z + (s - 1), ring)
        src_r = o_ref if s == 1 else ogath.at[slot(origin_r, c)]
        src_l = o_ref if s == 1 else ogath.at[slot(origin_l, c)]
        if s < half:
            cr = z_copy(src_r, slot(origin_r, c), 0, n, right, 2 * (s - 1))
            cl = z_copy(src_l, slot(origin_l, c), 0, n, left, 2 * (s - 1) + 1)
        else:
            h = n // 2
            cr = z_copy(src_r.at[pl.ds(0, h)], slot(origin_r, c), 0, h, right, 2 * (s - 1))
            cl = z_copy(src_l.at[pl.ds(h, h)], slot(origin_l, c), h, h, left, 2 * (s - 1) + 1)
        for k in to_project:
            project(o_ref[...] if s == 1 else ogath[k], k)
        to_project = []
        for cp, at in pending_sib:
            cp.wait()
            project(ogath[slot(at, 1 - c)], slot(at, 1 - c))
        pending_sib = []
        cr.wait()
        cl.wait()
        if s < half:
            arrived = [(lax.rem(z - s + ring, ring), ring + 2 * s - 1), (lax.rem(z + s, ring), ring + 2 * s)]
        else:
            arrived = [(lax.rem(z + half, ring), ring + 2 * s - 1)]
        for at, idx in arrived:
            pending_sib.append((z_copy(ogath.at[slot(at, c)], slot(at, c), 0, n, sib, idx), at))
            to_project.append(slot(at, c))
    for k in to_project:
        project(ogath[k], k)
    for cp, at in pending_sib:
        cp.wait()
        project(ogath[slot(at, 1 - c)], slot(at, 1 - c))
    for k in range(2 * ring):
        total = part[k, pl.ds(pl.multiple_of(y * piece, 8), piece)]
        for d in range(1, cols):
            pltpu.make_async_remote_copy(
                src_ref=part.at[k, pl.ds(0, piece)],
                dst_ref=recv.at[d, k],
                send_sem=y_send.at[0],
                recv_sem=y_recv.at[d * 2 * ring + k],
                device_id=device(col=lax.rem(y + d, cols)),
                device_id_type=mesh_id,
            ).wait_recv()
            total = total + recv[d, k]
        m = piece // 2
        for e in (0, 1):
            out_ref[pl.ds(e * 2 * ring * m + k * m, m)] = total[e * m : (e + 1) * m]
    for k in range(2 * ring):
        for d in range(1, cols):
            pltpu.make_async_remote_copy(
                src_ref=part.at[k, pl.ds(0, piece)],
                dst_ref=recv.at[0, 0],
                send_sem=y_send.at[k * cols + d],
                recv_sem=y_recv.at[0],
                device_id=device(col=lax.rem(y + d, cols)),
                device_id_type=mesh_id,
            ).wait_send()


def gather_mix(o, w_out, ring, cols, collective_id):
    n, width = o.shape
    out_w = w_out.shape[1]
    per_col = 2 * ring // cols
    return pl.pallas_call(
        functools.partial(mix_kernel, ring, cols, n),
        out_shape=jax.ShapeDtypeStruct((per_col * n, out_w), jnp.float32),
        in_specs=[pl.BlockSpec(memory_space=pltpu.VMEM), pl.BlockSpec(memory_space=pltpu.VMEM)],
        out_specs=pl.BlockSpec(memory_space=pltpu.VMEM),
        scratch_shapes=[
            pltpu.VMEM((2 * ring, n, width), jnp.float32),
            pltpu.VMEM((2 * ring, n, out_w), jnp.float32),
            pltpu.VMEM((cols, 2 * ring, n // cols, out_w), jnp.float32),
            pltpu.SemaphoreType.DMA((2 * ring,)),
            pltpu.SemaphoreType.DMA((2 * ring,)),
            pltpu.SemaphoreType.DMA((2 * ring * cols,)),
            pltpu.SemaphoreType.DMA((2 * ring * cols,)),
        ],
        compiler_params=pltpu.CompilerParams(
            collective_id=collective_id, has_side_effects=True, vmem_limit_bytes=60 * 1024 * 1024
        ),
    )(o, w_out)


def front_kernel(
    ring, cols, tok_ref, wq_ref, wk_ref, wv_ref, out_ref, kv_out, tg, partial, sibbuf, sbuf, rbuf, kvbuf,
    y_sems, z_sems, sib_sems, kv_sems,
):
    mesh_id = pl.DeviceIdType.MESH
    names = ("depth", "rz", "rc", "col")
    me = {a: lax.axis_index(a) for a in names}
    z, c, y = me["rz"], me["rc"], me["col"]
    rows = tok_ref.shape[0]
    m = rows // 2 // (2 * ring)
    h = m // 2

    def device(**moved):
        return tuple(moved.get(a, me[a]) for a in names)

    right = device(rz=lax.rem(z + 1, ring))
    left = device(rz=lax.rem(z + ring - 1, ring))
    sib = device(rc=1 - c)
    y_right = device(col=lax.rem(y + 1, cols))
    y_left = device(col=lax.rem(y + cols - 1, cols))
    peers = [left, right, sib, y_left, y_right]

    barrier = pltpu.get_barrier_semaphore()
    for peer in peers:
        pl.semaphore_signal(barrier, inc=1, device_id=peer, device_id_type=mesh_id)
    pl.semaphore_wait(barrier, len(peers))

    def remote(src, dst, peer, sems, idx):
        cp = pltpu.make_async_remote_copy(
            src_ref=src, dst_ref=dst, send_sem=sems[0].at[idx], recv_sem=sems[1].at[idx],
            device_id=peer, device_id_type=mesh_id,
        )
        cp.start()
        return cp

    def need(s, half):
        sign = -1 if half == 0 else 1
        return lax.rem(z + sign * (s % ring) + ring * ring, ring)

    def round_steps(r, chunk):
        x = partial.at[r]
        base = r * 2 * ring
        sib_copies = {}
        for idx, (s, half) in enumerate((s, half) for s in range(1, ring + 1) for half in (0, 1)):
            at = need(s, half)
            sib_copies[(s, half)] = remote(
                x.at[pl.ds(pl.multiple_of((at * 2 + 1 - c) * m + half * h, 8), h)],
                sibbuf.at[r, pl.ds(pl.multiple_of(at * m + half * h, 8), h)],
                sib, sib_sems, base + idx,
            )
        yield

        def contribution(s, half):
            at = need(s, half)
            sib_copies[(s, half)].wait()
            own = x[pl.ds(pl.multiple_of((at * 2 + c) * m + half * h, 8), h)]
            return own + sibbuf[r, pl.ds(pl.multiple_of(at * m + half * h, 8), h)]

        ring_copies = {}
        for s in range(1, ring):
            for half in (0, 1):
                value = contribution(s, half)
                if s > 1:
                    ring_copies[(s - 1, half)].wait()
                    value = value + rbuf[r, half, s - 2]
                sbuf[r, half, s - 1] = value
                ring_copies[(s, half)] = remote(
                    sbuf.at[r, half, s - 1], rbuf.at[r, half, s - 1],
                    right if half == 0 else left, z_sems, base + half * (ring - 1) + s - 1,
                )
            yield
        for half in (0, 1):
            value = contribution(ring, half)
            ring_copies[(ring - 1, half)].wait()
            value = value + rbuf[r, half, ring - 2]
            out_ref[pl.ds(pl.multiple_of(chunk * m + half * h, 8), h)] = value
            kvbuf[r, z * 2 + c, pl.ds(half * h, h)] = value[:, qw:]
        yield

        def kv_copy(src, at, lo, size, peer, idx):
            return remote(src, kvbuf.at[r, at * 2 + c, pl.ds(lo, size)], peer, kv_sems, base + idx)

        kv_sib = [
            remote(kvbuf.at[r, z * 2 + c], kvbuf.at[r, z * 2 + c], sib, kv_sems, base + ring)
        ]
        half_ring = ring // 2
        for s in range(1, half_ring + 1):
            origin_r = lax.rem(z - (s - 1) + ring, ring)
            origin_l = lax.rem(z + (s - 1), ring)
            src_r = kvbuf.at[r, origin_r * 2 + c]
            src_l = kvbuf.at[r, origin_l * 2 + c]
            if s < half_ring:
                cr = kv_copy(src_r, origin_r, 0, m, right, 2 * (s - 1))
                cl = kv_copy(src_l, origin_l, 0, m, left, 2 * (s - 1) + 1)
            else:
                cr = kv_copy(src_r.at[pl.ds(0, h)], origin_r, 0, h, right, 2 * (s - 1))
                cl = kv_copy(src_l.at[pl.ds(h, h)], origin_l, h, h, left, 2 * (s - 1) + 1)
            yield
            cr.wait()
            cl.wait()
            if s < half_ring:
                got = [(lax.rem(z - s + ring, ring), ring + 2 * s - 1), (lax.rem(z + s, ring), ring + 2 * s)]
            else:
                got = [(lax.rem(z + half_ring, ring), ring + 2 * s - 1)]
            for at, idx in got:
                kv_sib.append(
                    remote(kvbuf.at[r, at * 2 + c], kvbuf.at[r, at * 2 + c], sib, kv_sems, base + idx)
                )
        yield
        for cp in kv_sib:
            cp.wait()
        yield

    qw = wq_ref.shape[1]
    kw = wk_ref.shape[1]

    def project(r, src):
        block = src[...]
        for lo, w_ref in ((0, wq_ref), (qw, wk_ref), (qw + kw, wv_ref)):
            partial[r, :, pl.ds(lo, w_ref.shape[1])] = jnp.dot(
                block, w_ref[...], preferred_element_type=jnp.float32, precision=lax.Precision.HIGH
            )

    hr = rows // 2
    chunks = (y, lax.rem(y + cols - 1, cols), lax.rem(y + 1, cols), lax.rem(y + 2, cols))

    def sub(ref, e):
        return ref.at[pl.ds(e * hr, hr)]

    y1 = {}
    for e in (0, 1):
        y1[("r", e)] = remote(sub(tok_ref, e), sub(tg.at[1], e), y_right, y_sems, 2 * e)
        y1[("l", e)] = remote(sub(tok_ref, e), sub(tg.at[2], e), y_left, y_sems, 2 * e + 1)
    rounds = []

    def begin(slot_id, e, src):
        r = 2 * slot_id + e
        project(r, src)
        g = round_steps(r, 2 * chunks[slot_id] + e)
        next(g)
        rounds.append(g)

    def advance(times):
        for _ in range(times):
            for g in list(rounds):
                next(g, None)

    begin(0, 0, sub(tok_ref, 0))
    begin(0, 1, sub(tok_ref, 1))
    advance(ring // 2)
    y1[("r", 0)].wait()
    y2r = remote(sub(tg.at[1], 0), sub(tg.at[3], 0), y_right, y_sems, 4)
    y1[("l", 0)].wait()
    begin(1, 0, sub(tg.at[1], 0))
    begin(2, 0, sub(tg.at[2], 0))
    advance(2)
    y1[("r", 1)].wait()
    y1[("l", 1)].wait()
    y2l = remote(sub(tg.at[2], 1), sub(tg.at[3], 1), y_left, y_sems, 5)
    begin(1, 1, sub(tg.at[1], 1))
    begin(2, 1, sub(tg.at[2], 1))
    advance(2)
    y2r.wait()
    begin(3, 0, sub(tg.at[3], 0))
    y2l.wait()
    begin(3, 1, sub(tg.at[3], 1))
    live = list(rounds)
    while live:
        live = [g for g in live if next(g, "done") != "done"]
    kv_out[...] = kvbuf[...]


def front(tokens, w_query, w_key, w_value, ring, cols, collective_id):
    rows, width = tokens.shape
    out_w = w_query.shape[1] + w_key.shape[1] + w_value.shape[1]
    kv_w = w_key.shape[1] + w_value.shape[1]
    n_rounds = 2 * cols
    hr = rows // 2
    m = hr // (2 * ring)
    return pl.pallas_call(
        functools.partial(front_kernel, ring, cols),
        out_shape=(
            jax.ShapeDtypeStruct((n_rounds * m, out_w), jnp.float32),
            jax.ShapeDtypeStruct((n_rounds, 2 * ring, m, kv_w), jnp.float32),
        ),
        in_specs=[pl.BlockSpec(memory_space=pltpu.VMEM)] * 4,
        out_specs=(pl.BlockSpec(memory_space=pltpu.VMEM), pl.BlockSpec(memory_space=pltpu.VMEM)),
        scratch_shapes=[
            pltpu.VMEM((cols, rows, width), jnp.float32),
            pltpu.VMEM((n_rounds, hr, out_w), jnp.float32),
            pltpu.VMEM((n_rounds, ring * m, out_w), jnp.float32),
            pltpu.VMEM((n_rounds, 2, ring - 1, m // 2, out_w), jnp.float32),
            pltpu.VMEM((n_rounds, 2, ring - 1, m // 2, out_w), jnp.float32),
            pltpu.VMEM((n_rounds, 2 * ring, m, kv_w), jnp.float32),
            (pltpu.SemaphoreType.DMA((6,)), pltpu.SemaphoreType.DMA((6,))),
            (pltpu.SemaphoreType.DMA((n_rounds * 2 * ring,)), pltpu.SemaphoreType.DMA((n_rounds * 2 * ring,))),
            (pltpu.SemaphoreType.DMA((n_rounds * 2 * ring,)), pltpu.SemaphoreType.DMA((n_rounds * 2 * ring,))),
            (pltpu.SemaphoreType.DMA((n_rounds * 2 * ring,)), pltpu.SemaphoreType.DMA((n_rounds * 2 * ring,))),
        ],
        compiler_params=pltpu.CompilerParams(
            collective_id=collective_id, has_side_effects=True, vmem_limit_bytes=60 * 1024 * 1024
        ),
    )(tokens, w_query, w_key, w_value)


def on_device(ring, cols, tokens, w_query, w_key, w_value, w_out):
    highest = lax.Precision.HIGH
    q_width = w_query.shape[1]
    kv_width = w_key.shape[1]
    joined, kv_sets = front(tokens, w_query, w_key, w_value, ring, cols, 3)
    query_rows = joined[:, :q_width]
    all_kv = kv_sets.reshape(-1, kv_sets.shape[-1])
    state_end = fold_keys(
        query_rows,
        start_state(query_rows, kv_width),
        (all_kv[:, :kv_width], all_kv[:, kv_width:]),
    )
    return gather_mix(finish(state_end), w_out, ring, cols, 5)


def solution(mesh):
    depth, row, col = (mesh.shape[a] for a in ("depth", "row", "col"))
    split = jax.sharding.Mesh(
        np.asarray(mesh.devices).reshape(depth, row // 2, 2, col), ("depth", "rz", "rc", "col")
    )
    rows = ("rz", "rc")
    placed = (
        P(("depth", "col"), rows),
        P(rows, "col"),
        P(rows, "col"),
        P(rows, "col"),
        P("col", rows),
    )
    return jax.shard_map(
        functools.partial(on_device, row // 2, col),
        mesh=split,
        in_specs=placed,
        out_specs=P(("depth", "col"), rows),
        check_vma=False,
    )
```

```python
import functools
import math

import jax
import numpy as np
import jax.numpy as jnp
from jax import lax
from jax.experimental import pallas as pl
from jax.experimental.pallas import tpu as pltpu
from jax.sharding import PartitionSpec as P

QUERY_HEADS = 32
KEY_VALUE_HEADS = 4
HEAD_SIZE_DIM = 128


def start_state(query_rows, kv_width):
    count_of_heads = kv_width // HEAD_SIZE_DIM
    queries_per_group = QUERY_HEADS // KEY_VALUE_HEADS
    count_of_rows = query_rows.shape[0]
    running_max = jnp.full((count_of_heads, queries_per_group, count_of_rows), -1e30, jnp.float32)
    running_sum = jnp.zeros((count_of_heads, queries_per_group, count_of_rows), jnp.float32)
    weighted = jnp.zeros(
        (count_of_heads, queries_per_group, count_of_rows, HEAD_SIZE_DIM), jnp.float32
    )
    return (running_max, running_sum, weighted)


def fold_keys(query_rows, state_now, block_pair):
    highest = lax.Precision.HIGH
    running_max, running_sum, weighted = state_now
    key_block, value_block = block_pair
    count_of_heads = key_block.shape[1] // HEAD_SIZE_DIM
    count_of_rows = query_rows.shape[0]
    query_head_rows = query_rows.reshape(
        count_of_rows, count_of_heads, QUERY_HEADS // KEY_VALUE_HEADS, HEAD_SIZE_DIM
    )
    key_head_rows = key_block.reshape(-1, count_of_heads, HEAD_SIZE_DIM)
    value_head_rows = value_block.reshape(-1, count_of_heads, HEAD_SIZE_DIM)
    scores = jnp.einsum("rkgd,nkd->kgrn", query_head_rows, key_head_rows, precision=highest) * (
        1.0 / math.sqrt(HEAD_SIZE_DIM)
    )
    newest = jnp.maximum(running_max, jnp.max(scores, axis=-1))
    weights = jnp.exp(scores - newest[..., None])
    running_sum = jnp.sum(weights, axis=-1)
    weighted = jnp.einsum("kgrn,nkd->kgrd", weights, value_head_rows, precision=highest)
    return (newest, running_sum, weighted)


def finish(state_now):
    running_max, running_sum, weighted = state_now
    attention_output = weighted / running_sum[..., None]
    count_of_heads, queries_per_group, count_of_rows, head_size = attention_output.shape
    return attention_output.transpose(2, 0, 1, 3).reshape(
        count_of_rows, count_of_heads * queries_per_group * head_size
    )


def gather_kernel(axis, ring, n, with_sib, x_ref, out_ref, local_sem, send_sems, recv_sems):
    mesh_id = pl.DeviceIdType.MESH
    names = ("depth", "rz", "rc", "col")
    me = {a: lax.axis_index(a) for a in names}
    pos = me[axis]

    def device(**moved):
        return tuple(moved.get(a, me[a]) for a in names)

    right = device(**{axis: lax.rem(pos + 1, ring)})
    left = device(**{axis: lax.rem(pos + ring - 1, ring)})
    sib = device(rc=1 - me["rc"])
    peers = (left, right, sib) if with_sib else (left, right)

    barrier = pltpu.get_barrier_semaphore()
    for peer in peers:
        pl.semaphore_signal(barrier, inc=1, device_id=peer, device_id_type=mesh_id)
    pl.semaphore_wait(barrier, len(peers))

    def rows(at, lo=0, size=n):
        slot = at * 2 + me["rc"] if with_sib else at
        return pl.ds(pl.multiple_of(slot * n + lo, 8), size)

    def remote(src, dst_rows, peer, idx):
        cp = pltpu.make_async_remote_copy(
            src_ref=src,
            dst_ref=out_ref.at[dst_rows],
            send_sem=send_sems.at[idx],
            recv_sem=recv_sems.at[idx],
            device_id=peer,
            device_id_type=mesh_id,
        )
        cp.start()
        return cp

    def to_sib(at, idx):
        if with_sib:
            sib_copies.append(remote(out_ref.at[rows(at)], rows(at), sib, idx))

    local = pltpu.make_async_copy(x_ref, out_ref.at[rows(pos)], local_sem)
    local.start()
    sib_copies = [remote(x_ref, rows(pos), sib, ring)] if with_sib else []
    half = ring // 2
    for s in range(1, half + 1):
        origin_r = lax.rem(pos - (s - 1) + ring, ring)
        origin_l = lax.rem(pos + (s - 1), ring)
        src_r = x_ref if s == 1 else out_ref.at[rows(origin_r)]
        src_l = x_ref if s == 1 else out_ref.at[rows(origin_l)]
        if s < half:
            cr = remote(src_r, rows(origin_r), right, 2 * (s - 1))
            cl = remote(src_l, rows(origin_l), left, 2 * (s - 1) + 1)
            cr.wait()
            cl.wait()
            to_sib(lax.rem(pos - s + ring, ring), ring + 2 * s - 1)
            to_sib(lax.rem(pos + s, ring), ring + 2 * s)
        else:
            h = n // 2
            cr = remote(src_r.at[pl.ds(0, h)], rows(origin_r, 0, h), right, 2 * (s - 1))
            cl = remote(src_l.at[pl.ds(h, h)], rows(origin_l, h, h), left, 2 * (s - 1) + 1)
            cr.wait()
            cl.wait()
            to_sib(lax.rem(pos + half, ring), ring + 2 * s - 1)
    local.wait()
    for cp in sib_copies:
        cp.wait()


def ring_gather(block, axis, ring, with_sib, collective_id):
    n, w = block.shape
    copies = 2 if with_sib else 1
    return pl.pallas_call(
        functools.partial(gather_kernel, axis, ring, n, with_sib),
        out_shape=jax.ShapeDtypeStruct((copies * ring * n, w), block.dtype),
        in_specs=[pl.BlockSpec(memory_space=pl.ANY)],
        out_specs=pl.BlockSpec(memory_space=pl.ANY),
        scratch_shapes=[
            pltpu.SemaphoreType.DMA(()),
            pltpu.SemaphoreType.DMA((2 * ring,)),
            pltpu.SemaphoreType.DMA((2 * ring,)),
        ],
        compiler_params=pltpu.CompilerParams(collective_id=collective_id, has_side_effects=True),
    )(block)


def scatter_kernel(axis, ring, m, with_sib, parts, x_ref, out_ref, sbuf, rbuf, sibbuf, send_sems, recv_sems, sib_sems):
    mesh_id = pl.DeviceIdType.MESH
    names = ("depth", "rz", "rc", "col")
    me = {a: lax.axis_index(a) for a in names}
    pos = me[axis]
    h = m // 2
    q = h // parts

    def device(**moved):
        return tuple(moved.get(a, me[a]) for a in names)

    right = device(**{axis: lax.rem(pos + 1, ring)})
    left = device(**{axis: lax.rem(pos + ring - 1, ring)})
    sib = device(rc=1 - me["rc"])
    peers = (left, right, sib) if with_sib else (left, right)

    barrier = pltpu.get_barrier_semaphore()
    for peer in peers:
        pl.semaphore_signal(barrier, inc=1, device_id=peer, device_id_type=mesh_id)
    pl.semaphore_wait(barrier, len(peers))

    def rows_of(at, half, part, owner):
        slot = at * 2 + owner if with_sib else at
        return pl.ds(pl.multiple_of(slot * m + half * h + part * q, 8), q)

    def sib_rows(at, half, part):
        return pl.ds(pl.multiple_of(at * m + half * h + part * q, 8), q)

    def remote(src, dst, peer, sems, idx):
        cp = pltpu.make_async_remote_copy(
            src_ref=src,
            dst_ref=dst,
            send_sem=sems[0].at[idx],
            recv_sem=sems[1].at[idx],
            device_id=peer,
            device_id_type=mesh_id,
        )
        cp.start()
        return cp

    def need(s, half):
        sign = -1 if half == 0 else 1
        return lax.rem(pos + sign * (s % ring) + ring * ring, ring)

    sib_copies = {}
    if with_sib:
        order = [(s, half) for s in range(1, ring + 1) for half in (0, 1)]
        for idx, (s, half) in enumerate(order):
            at = need(s, half)
            sib_copies[(s, half)] = remote(
                x_ref.at[pl.ds(pl.multiple_of((at * 2 + 1 - me["rc"]) * m + half * h, 8), h)],
                sibbuf.at[pl.ds(pl.multiple_of(at * m + half * h, 8), h)],
                sib,
                (sib_sems[0], sib_sems[1]),
                idx,
            )

    def contribution(s, half, part):
        at = need(s, half)
        own = x_ref[rows_of(at, half, part, me["rc"])]
        if with_sib:
            if part == 0:
                sib_copies[(s, half)].wait()
            own = own + sibbuf[sib_rows(at, half, part)]
        return own

    ring_copies = {}
    for s in range(1, ring):
        for part in range(parts):
            for half in (0, 1):
                value = contribution(s, half, part)
                if s > 1:
                    ring_copies[(s - 1, half, part)].wait()
                    value = value + rbuf[half, s - 2, part]
                sbuf[half, s - 1, part] = value
                ring_copies[(s, half, part)] = remote(
                    sbuf.at[half, s - 1, part],
                    rbuf.at[half, s - 1, part],
                    right if half == 0 else left,
                    (send_sems, recv_sems),
                    (half * (ring - 1) + s - 1) * parts + part,
                )
    for part in range(parts):
        for half in (0, 1):
            value = contribution(ring, half, part)
            ring_copies[(ring - 1, half, part)].wait()
            out_ref[pl.ds(half * h + part * q, q)] = value + rbuf[half, ring - 2, part]


def ring_scatter(x, axis, ring, with_sib, parts, collective_id):
    total, w = x.shape
    copies = 2 if with_sib else 1
    m = total // (copies * ring)
    sib_rows = ring * m if with_sib else 8
    return pl.pallas_call(
        functools.partial(scatter_kernel, axis, ring, m, with_sib, parts),
        out_shape=jax.ShapeDtypeStruct((m, w), x.dtype),
        in_specs=[pl.BlockSpec(memory_space=pltpu.VMEM)],
        out_specs=pl.BlockSpec(memory_space=pltpu.VMEM),
        scratch_shapes=[
            pltpu.VMEM((2, ring - 1, parts, m // 2 // parts, w), x.dtype),
            pltpu.VMEM((2, ring - 1, parts, m // 2 // parts, w), x.dtype),
            pltpu.VMEM((sib_rows, w), x.dtype),
            pltpu.SemaphoreType.DMA((2 * ring * parts,)),
            pltpu.SemaphoreType.DMA((2 * ring * parts,)),
            (pltpu.SemaphoreType.DMA((2 * ring,)), pltpu.SemaphoreType.DMA((2 * ring,))),
        ],
        compiler_params=pltpu.CompilerParams(
            collective_id=collective_id, has_side_effects=True, vmem_limit_bytes=60 * 1024 * 1024
        ),
    )(x)


def mix_kernel(ring, cols, n, o_ref, wo_ref, out_ref, ogath, part, recv, send_sems, recv_sems, y_send, y_recv):
    mesh_id = pl.DeviceIdType.MESH
    names = ("depth", "rz", "rc", "col")
    me = {a: lax.axis_index(a) for a in names}
    z, c, y = me["rz"], me["rc"], me["col"]
    per_col = 2 * ring // cols

    def device(**moved):
        return tuple(moved.get(a, me[a]) for a in names)

    right = device(rz=lax.rem(z + 1, ring))
    left = device(rz=lax.rem(z + ring - 1, ring))
    sib = device(rc=1 - c)
    peers = [left, right, sib] + [device(col=lax.rem(y + d, cols)) for d in range(1, cols)]

    barrier = pltpu.get_barrier_semaphore()
    for peer in peers:
        pl.semaphore_signal(barrier, inc=1, device_id=peer, device_id_type=mesh_id)
    pl.semaphore_wait(barrier, len(peers))

    def remote(src, dst, peer, send, recv_sem):
        cp = pltpu.make_async_remote_copy(
            src_ref=src, dst_ref=dst, send_sem=send, recv_sem=recv_sem, device_id=peer, device_id_type=mesh_id
        )
        cp.start()
        return cp

    piece = n // cols

    def project(block, k):
        part[k] = jnp.dot(block, wo_ref[...], preferred_element_type=jnp.float32, precision=lax.Precision.HIGH)
        for d in range(1, cols):
            dest = lax.rem(y + d, cols)
            remote(
                part.at[k, pl.ds(pl.multiple_of(dest * piece, 8), piece)],
                recv.at[cols - d, k],
                device(col=dest),
                y_send.at[k * cols + d],
                y_recv.at[(cols - d) * 2 * ring + k],
            )

    def slot(zz, cc):
        return zz * 2 + cc

    def z_copy(src, dst_slot, lo, size, peer, idx):
        return remote(src, ogath.at[dst_slot, pl.ds(lo, size)], peer, send_sems.at[idx], recv_sems.at[idx])

    pending_sib = [(z_copy(o_ref, slot(z, c), 0, n, sib, ring), z)]
    to_project = [slot(z, c)]
    half = ring // 2
    for s in range(1, half + 1):
        origin_r = lax.rem(z - (s - 1) + ring, ring)
        origin_l = lax.rem(z + (s - 1), ring)
        src_r = o_ref if s == 1 else ogath.at[slot(origin_r, c)]
        src_l = o_ref if s == 1 else ogath.at[slot(origin_l, c)]
        if s < half:
            cr = z_copy(src_r, slot(origin_r, c), 0, n, right, 2 * (s - 1))
            cl = z_copy(src_l, slot(origin_l, c), 0, n, left, 2 * (s - 1) + 1)
        else:
            h = n // 2
            cr = z_copy(src_r.at[pl.ds(0, h)], slot(origin_r, c), 0, h, right, 2 * (s - 1))
            cl = z_copy(src_l.at[pl.ds(h, h)], slot(origin_l, c), h, h, left, 2 * (s - 1) + 1)
        for k in to_project:
            project(o_ref[...] if s == 1 else ogath[k], k)
        to_project = []
        for cp, at in pending_sib:
            cp.wait()
            project(ogath[slot(at, 1 - c)], slot(at, 1 - c))
        pending_sib = []
        cr.wait()
        cl.wait()
        if s < half:
            arrived = [(lax.rem(z - s + ring, ring), ring + 2 * s - 1), (lax.rem(z + s, ring), ring + 2 * s)]
        else:
            arrived = [(lax.rem(z + half, ring), ring + 2 * s - 1)]
        for at, idx in arrived:
            pending_sib.append((z_copy(ogath.at[slot(at, c)], slot(at, c), 0, n, sib, idx), at))
            to_project.append(slot(at, c))
    for k in to_project:
        project(ogath[k], k)
    for cp, at in pending_sib:
        cp.wait()
        project(ogath[slot(at, 1 - c)], slot(at, 1 - c))
    for k in range(2 * ring):
        total = part[k, pl.ds(pl.multiple_of(y * piece, 8), piece)]
        for d in range(1, cols):
            pltpu.make_async_remote_copy(
                src_ref=part.at[k, pl.ds(0, piece)],
                dst_ref=recv.at[d, k],
                send_sem=y_send.at[0],
                recv_sem=y_recv.at[d * 2 * ring + k],
                device_id=device(col=lax.rem(y + d, cols)),
                device_id_type=mesh_id,
            ).wait_recv()
            total = total + recv[d, k]
        m = piece // 2
        for e in (0, 1):
            out_ref[pl.ds(e * 2 * ring * m + k * m, m)] = total[e * m : (e + 1) * m]
    for k in range(2 * ring):
        for d in range(1, cols):
            pltpu.make_async_remote_copy(
                src_ref=part.at[k, pl.ds(0, piece)],
                dst_ref=recv.at[0, 0],
                send_sem=y_send.at[k * cols + d],
                recv_sem=y_recv.at[0],
                device_id=device(col=lax.rem(y + d, cols)),
                device_id_type=mesh_id,
            ).wait_send()


def gather_mix(o, w_out, ring, cols, collective_id):
    n, width = o.shape
    out_w = w_out.shape[1]
    per_col = 2 * ring // cols
    return pl.pallas_call(
        functools.partial(mix_kernel, ring, cols, n),
        out_shape=jax.ShapeDtypeStruct((per_col * n, out_w), jnp.float32),
        in_specs=[pl.BlockSpec(memory_space=pltpu.VMEM), pl.BlockSpec(memory_space=pltpu.VMEM)],
        out_specs=pl.BlockSpec(memory_space=pltpu.VMEM),
        scratch_shapes=[
            pltpu.VMEM((2 * ring, n, width), jnp.float32),
            pltpu.VMEM((2 * ring, n, out_w), jnp.float32),
            pltpu.VMEM((cols, 2 * ring, n // cols, out_w), jnp.float32),
            pltpu.SemaphoreType.DMA((2 * ring,)),
            pltpu.SemaphoreType.DMA((2 * ring,)),
            pltpu.SemaphoreType.DMA((2 * ring * cols,)),
            pltpu.SemaphoreType.DMA((2 * ring * cols,)),
        ],
        compiler_params=pltpu.CompilerParams(
            collective_id=collective_id, has_side_effects=True, vmem_limit_bytes=60 * 1024 * 1024
        ),
    )(o, w_out)


def front_kernel(
    ring, cols, tok_ref, wq_ref, wk_ref, wv_ref, out_ref, kv_out, tg, partial, sibbuf, sbuf, rbuf, kvbuf,
    y_sems, z_sems, sib_sems, kv_sems,
):
    mesh_id = pl.DeviceIdType.MESH
    names = ("depth", "rz", "rc", "col")
    me = {a: lax.axis_index(a) for a in names}
    z, c, y = me["rz"], me["rc"], me["col"]
    rows = tok_ref.shape[0]
    m = rows // 2 // (2 * ring)
    h = m // 2

    def device(**moved):
        return tuple(moved.get(a, me[a]) for a in names)

    right = device(rz=lax.rem(z + 1, ring))
    left = device(rz=lax.rem(z + ring - 1, ring))
    sib = device(rc=1 - c)
    y_right = device(col=lax.rem(y + 1, cols))
    y_left = device(col=lax.rem(y + cols - 1, cols))
    peers = [left, right, sib, y_left, y_right]

    barrier = pltpu.get_barrier_semaphore()
    for peer in peers:
        pl.semaphore_signal(barrier, inc=1, device_id=peer, device_id_type=mesh_id)
    pl.semaphore_wait(barrier, len(peers))

    def remote(src, dst, peer, sems, idx):
        cp = pltpu.make_async_remote_copy(
            src_ref=src, dst_ref=dst, send_sem=sems[0].at[idx], recv_sem=sems[1].at[idx],
            device_id=peer, device_id_type=mesh_id,
        )
        cp.start()
        return cp

    def need(s, half):
        sign = -1 if half == 0 else 1
        return lax.rem(z + sign * (s % ring) + ring * ring, ring)

    def round_steps(r, chunk):
        x = partial.at[r]
        base = r * 2 * ring
        sib_copies = {}
        for idx, (s, half) in enumerate((s, half) for s in range(1, ring + 1) for half in (0, 1)):
            at = need(s, half)
            sib_copies[(s, half)] = remote(
                x.at[pl.ds(pl.multiple_of((at * 2 + 1 - c) * m + half * h, 8), h)],
                sibbuf.at[r, pl.ds(pl.multiple_of(at * m + half * h, 8), h)],
                sib, sib_sems, base + idx,
            )
        yield

        def contribution(s, half):
            at = need(s, half)
            sib_copies[(s, half)].wait()
            own = x[pl.ds(pl.multiple_of((at * 2 + c) * m + half * h, 8), h)]
            return own + sibbuf[r, pl.ds(pl.multiple_of(at * m + half * h, 8), h)]

        ring_copies = {}
        for s in range(1, ring):
            for half in (0, 1):
                value = contribution(s, half)
                if s > 1:
                    ring_copies[(s - 1, half)].wait()
                    value = value + rbuf[r, half, s - 2]
                sbuf[r, half, s - 1] = value
                ring_copies[(s, half)] = remote(
                    sbuf.at[r, half, s - 1], rbuf.at[r, half, s - 1],
                    right if half == 0 else left, z_sems, base + half * (ring - 1) + s - 1,
                )
            yield
        for half in (0, 1):
            value = contribution(ring, half)
            ring_copies[(ring - 1, half)].wait()
            value = value + rbuf[r, half, ring - 2]
            out_ref[pl.ds(pl.multiple_of(chunk * m + half * h, 8), h)] = value
            kvbuf[r, z * 2 + c, pl.ds(half * h, h)] = value[:, qw:]
        yield

        def kv_copy(src, at, lo, size, peer, idx):
            return remote(src, kvbuf.at[r, at * 2 + c, pl.ds(lo, size)], peer, kv_sems, base + idx)

        kv_sib = [
            remote(kvbuf.at[r, z * 2 + c], kvbuf.at[r, z * 2 + c], sib, kv_sems, base + ring)
        ]
        half_ring = ring // 2
        for s in range(1, half_ring + 1):
            origin_r = lax.rem(z - (s - 1) + ring, ring)
            origin_l = lax.rem(z + (s - 1), ring)
            src_r = kvbuf.at[r, origin_r * 2 + c]
            src_l = kvbuf.at[r, origin_l * 2 + c]
            if s < half_ring:
                cr = kv_copy(src_r, origin_r, 0, m, right, 2 * (s - 1))
                cl = kv_copy(src_l, origin_l, 0, m, left, 2 * (s - 1) + 1)
            else:
                cr = kv_copy(src_r.at[pl.ds(0, h)], origin_r, 0, h, right, 2 * (s - 1))
                cl = kv_copy(src_l.at[pl.ds(h, h)], origin_l, h, h, left, 2 * (s - 1) + 1)
            yield
            cr.wait()
            cl.wait()
            if s < half_ring:
                got = [(lax.rem(z - s + ring, ring), ring + 2 * s - 1), (lax.rem(z + s, ring), ring + 2 * s)]
            else:
                got = [(lax.rem(z + half_ring, ring), ring + 2 * s - 1)]
            for at, idx in got:
                kv_sib.append(
                    remote(kvbuf.at[r, at * 2 + c], kvbuf.at[r, at * 2 + c], sib, kv_sems, base + idx)
                )
        yield
        for cp in kv_sib:
            cp.wait()
        yield

    qw = wq_ref.shape[1]
    kw = wk_ref.shape[1]

    def project(r, src):
        block = src[...]
        for lo, w_ref in ((0, wq_ref), (qw, wk_ref), (qw + kw, wv_ref)):
            partial[r, :, pl.ds(lo, w_ref.shape[1])] = jnp.dot(
                block, w_ref[...], preferred_element_type=jnp.float32, precision=lax.Precision.HIGH
            )

    hr = rows // 2
    chunks = (y, lax.rem(y + cols - 1, cols), lax.rem(y + 1, cols), lax.rem(y + 2, cols))

    def sub(ref, e):
        return ref.at[pl.ds(e * hr, hr)]

    y1 = {}
    for e in (0, 1):
        y1[("r", e)] = remote(sub(tok_ref, e), sub(tg.at[1], e), y_right, y_sems, 2 * e)
        y1[("l", e)] = remote(sub(tok_ref, e), sub(tg.at[2], e), y_left, y_sems, 2 * e + 1)
    rounds = []

    def begin(slot_id, e, src):
        r = 2 * slot_id + e
        project(r, src)
        g = round_steps(r, 2 * chunks[slot_id] + e)
        next(g)
        rounds.append(g)

    def advance(times):
        for _ in range(times):
            for g in list(rounds):
                next(g, None)

    begin(0, 0, sub(tok_ref, 0))
    begin(0, 1, sub(tok_ref, 1))
    advance(ring // 2)
    y1[("r", 0)].wait()
    y2r = remote(sub(tg.at[1], 0), sub(tg.at[3], 0), y_right, y_sems, 4)
    y1[("l", 0)].wait()
    begin(1, 0, sub(tg.at[1], 0))
    begin(2, 0, sub(tg.at[2], 0))
    advance(2)
    y1[("r", 1)].wait()
    y1[("l", 1)].wait()
    y2l = remote(sub(tg.at[2], 1), sub(tg.at[3], 1), y_left, y_sems, 5)
    begin(1, 1, sub(tg.at[1], 1))
    begin(2, 1, sub(tg.at[2], 1))
    advance(2)
    y2r.wait()
    begin(3, 0, sub(tg.at[3], 0))
    y2l.wait()
    begin(3, 1, sub(tg.at[3], 1))
    live = list(rounds)
    while live:
        live = [g for g in live if next(g, "done") != "done"]
    kv_out[...] = kvbuf[...]


def front(tokens, w_query, w_key, w_value, ring, cols, collective_id):
    rows, width = tokens.shape
    out_w = w_query.shape[1] + w_key.shape[1] + w_value.shape[1]
    kv_w = w_key.shape[1] + w_value.shape[1]
    n_rounds = 2 * cols
    hr = rows // 2
    m = hr // (2 * ring)
    return pl.pallas_call(
        functools.partial(front_kernel, ring, cols),
        out_shape=(
            jax.ShapeDtypeStruct((n_rounds * m, out_w), jnp.float32),
            jax.ShapeDtypeStruct((n_rounds, 2 * ring, m, kv_w), jnp.float32),
        ),
        in_specs=[pl.BlockSpec(memory_space=pltpu.VMEM)] * 4,
        out_specs=(pl.BlockSpec(memory_space=pltpu.VMEM), pl.BlockSpec(memory_space=pltpu.VMEM)),
        scratch_shapes=[
            pltpu.VMEM((cols, rows, width), jnp.float32),
            pltpu.VMEM((n_rounds, hr, out_w), jnp.float32),
            pltpu.VMEM((n_rounds, ring * m, out_w), jnp.float32),
            pltpu.VMEM((n_rounds, 2, ring - 1, m // 2, out_w), jnp.float32),
            pltpu.VMEM((n_rounds, 2, ring - 1, m // 2, out_w), jnp.float32),
            pltpu.VMEM((n_rounds, 2 * ring, m, kv_w), jnp.float32),
            (pltpu.SemaphoreType.DMA((6,)), pltpu.SemaphoreType.DMA((6,))),
            (pltpu.SemaphoreType.DMA((n_rounds * 2 * ring,)), pltpu.SemaphoreType.DMA((n_rounds * 2 * ring,))),
            (pltpu.SemaphoreType.DMA((n_rounds * 2 * ring,)), pltpu.SemaphoreType.DMA((n_rounds * 2 * ring,))),
            (pltpu.SemaphoreType.DMA((n_rounds * 2 * ring,)), pltpu.SemaphoreType.DMA((n_rounds * 2 * ring,))),
        ],
        compiler_params=pltpu.CompilerParams(
            collective_id=collective_id, has_side_effects=True, vmem_limit_bytes=60 * 1024 * 1024
        ),
    )(tokens, w_query, w_key, w_value)


def attend_kernel(q_width, kv_width, q_ref, kv_ref, o_ref):
    scale = 1.0 / math.sqrt(HEAD_SIZE_DIM)
    keys = kv_ref[:, pl.ds(0, kv_width)]
    values = kv_ref[:, pl.ds(kv_width, kv_width)]
    for head in range(q_width // HEAD_SIZE_DIM):
        query = q_ref[:, pl.ds(head * HEAD_SIZE_DIM, HEAD_SIZE_DIM)]
        scores = lax.dot_general(
            query, keys, (((1,), (1,)), ((), ())),
            preferred_element_type=jnp.float32, precision=lax.Precision.HIGH,
        ) * scale
        weights = jnp.exp(scores - jnp.max(scores, axis=-1, keepdims=True))
        total = jnp.sum(weights, axis=-1, keepdims=True)
        weighted = jnp.dot(weights, values, preferred_element_type=jnp.float32, precision=lax.Precision.HIGH)
        o_ref[:, pl.ds(head * HEAD_SIZE_DIM, HEAD_SIZE_DIM)] = weighted / total


def attend(joined, all_kv, q_width, kv_width):
    return pl.pallas_call(
        functools.partial(attend_kernel, q_width, kv_width),
        out_shape=jax.ShapeDtypeStruct((joined.shape[0], q_width), jnp.float32),
        in_specs=[pl.BlockSpec(memory_space=pltpu.VMEM)] * 2,
        out_specs=pl.BlockSpec(memory_space=pltpu.VMEM),
        compiler_params=pltpu.CompilerParams(vmem_limit_bytes=60 * 1024 * 1024),
    )(joined, all_kv)


def on_device(ring, cols, tokens, w_query, w_key, w_value, w_out):
    highest = lax.Precision.HIGH
    q_width = w_query.shape[1]
    kv_width = w_key.shape[1]
    joined, kv_sets = front(tokens, w_query, w_key, w_value, ring, cols, 3)
    all_kv = kv_sets.reshape(-1, kv_sets.shape[-1])
    attended = attend(joined, all_kv, q_width, kv_width)
    return gather_mix(attended, w_out, ring, cols, 5)


def solution(mesh):
    depth, row, col = (mesh.shape[a] for a in ("depth", "row", "col"))
    split = jax.sharding.Mesh(
        np.asarray(mesh.devices).reshape(depth, row // 2, 2, col), ("depth", "rz", "rc", "col")
    )
    rows = ("rz", "rc")
    placed = (
        P(("depth", "col"), rows),
        P(rows, "col"),
        P(rows, "col"),
        P(rows, "col"),
        P("col", rows),
    )
    return jax.shard_map(
        functools.partial(on_device, row // 2, col),
        mesh=split,
        in_specs=placed,
        out_specs=P(("depth", "col"), rows),
        check_vma=False,
    )
```

```python
import functools
import math

import jax
import numpy as np
import jax.numpy as jnp
from jax import lax
from jax.experimental import pallas as pl
from jax.experimental.pallas import tpu as pltpu
from jax.sharding import PartitionSpec as P

QUERY_HEADS = 32
KEY_VALUE_HEADS = 4
HEAD_SIZE_DIM = 128


def start_state(query_rows, kv_width):
    count_of_heads = kv_width // HEAD_SIZE_DIM
    queries_per_group = QUERY_HEADS // KEY_VALUE_HEADS
    count_of_rows = query_rows.shape[0]
    running_max = jnp.full((count_of_heads, queries_per_group, count_of_rows), -1e30, jnp.float32)
    running_sum = jnp.zeros((count_of_heads, queries_per_group, count_of_rows), jnp.float32)
    weighted = jnp.zeros(
        (count_of_heads, queries_per_group, count_of_rows, HEAD_SIZE_DIM), jnp.float32
    )
    return (running_max, running_sum, weighted)


def fold_keys(query_rows, state_now, block_pair):
    highest = lax.Precision.HIGH
    running_max, running_sum, weighted = state_now
    key_block, value_block = block_pair
    count_of_heads = key_block.shape[1] // HEAD_SIZE_DIM
    count_of_rows = query_rows.shape[0]
    query_head_rows = query_rows.reshape(
        count_of_rows, count_of_heads, QUERY_HEADS // KEY_VALUE_HEADS, HEAD_SIZE_DIM
    )
    key_head_rows = key_block.reshape(-1, count_of_heads, HEAD_SIZE_DIM)
    value_head_rows = value_block.reshape(-1, count_of_heads, HEAD_SIZE_DIM)
    scores = jnp.einsum("rkgd,nkd->kgrn", query_head_rows, key_head_rows, precision=highest) * (
        1.0 / math.sqrt(HEAD_SIZE_DIM)
    )
    newest = jnp.maximum(running_max, jnp.max(scores, axis=-1))
    weights = jnp.exp(scores - newest[..., None])
    running_sum = jnp.sum(weights, axis=-1)
    weighted = jnp.einsum("kgrn,nkd->kgrd", weights, value_head_rows, precision=highest)
    return (newest, running_sum, weighted)


def finish(state_now):
    running_max, running_sum, weighted = state_now
    attention_output = weighted / running_sum[..., None]
    count_of_heads, queries_per_group, count_of_rows, head_size = attention_output.shape
    return attention_output.transpose(2, 0, 1, 3).reshape(
        count_of_rows, count_of_heads * queries_per_group * head_size
    )


def gather_kernel(axis, ring, n, with_sib, x_ref, out_ref, local_sem, send_sems, recv_sems):
    mesh_id = pl.DeviceIdType.MESH
    names = ("depth", "rz", "rc", "col")
    me = {a: lax.axis_index(a) for a in names}
    pos = me[axis]

    def device(**moved):
        return tuple(moved.get(a, me[a]) for a in names)

    right = device(**{axis: lax.rem(pos + 1, ring)})
    left = device(**{axis: lax.rem(pos + ring - 1, ring)})
    sib = device(rc=1 - me["rc"])
    peers = (left, right, sib) if with_sib else (left, right)

    barrier = pltpu.get_barrier_semaphore()
    for peer in peers:
        pl.semaphore_signal(barrier, inc=1, device_id=peer, device_id_type=mesh_id)
    pl.semaphore_wait(barrier, len(peers))

    def rows(at, lo=0, size=n):
        slot = at * 2 + me["rc"] if with_sib else at
        return pl.ds(pl.multiple_of(slot * n + lo, 8), size)

    def remote(src, dst_rows, peer, idx):
        cp = pltpu.make_async_remote_copy(
            src_ref=src,
            dst_ref=out_ref.at[dst_rows],
            send_sem=send_sems.at[idx],
            recv_sem=recv_sems.at[idx],
            device_id=peer,
            device_id_type=mesh_id,
        )
        cp.start()
        return cp

    def to_sib(at, idx):
        if with_sib:
            sib_copies.append(remote(out_ref.at[rows(at)], rows(at), sib, idx))

    local = pltpu.make_async_copy(x_ref, out_ref.at[rows(pos)], local_sem)
    local.start()
    sib_copies = [remote(x_ref, rows(pos), sib, ring)] if with_sib else []
    half = ring // 2
    for s in range(1, half + 1):
        origin_r = lax.rem(pos - (s - 1) + ring, ring)
        origin_l = lax.rem(pos + (s - 1), ring)
        src_r = x_ref if s == 1 else out_ref.at[rows(origin_r)]
        src_l = x_ref if s == 1 else out_ref.at[rows(origin_l)]
        if s < half:
            cr = remote(src_r, rows(origin_r), right, 2 * (s - 1))
            cl = remote(src_l, rows(origin_l), left, 2 * (s - 1) + 1)
            cr.wait()
            cl.wait()
            to_sib(lax.rem(pos - s + ring, ring), ring + 2 * s - 1)
            to_sib(lax.rem(pos + s, ring), ring + 2 * s)
        else:
            h = n // 2
            cr = remote(src_r.at[pl.ds(0, h)], rows(origin_r, 0, h), right, 2 * (s - 1))
            cl = remote(src_l.at[pl.ds(h, h)], rows(origin_l, h, h), left, 2 * (s - 1) + 1)
            cr.wait()
            cl.wait()
            to_sib(lax.rem(pos + half, ring), ring + 2 * s - 1)
    local.wait()
    for cp in sib_copies:
        cp.wait()


def ring_gather(block, axis, ring, with_sib, collective_id):
    n, w = block.shape
    copies = 2 if with_sib else 1
    return pl.pallas_call(
        functools.partial(gather_kernel, axis, ring, n, with_sib),
        out_shape=jax.ShapeDtypeStruct((copies * ring * n, w), block.dtype),
        in_specs=[pl.BlockSpec(memory_space=pl.ANY)],
        out_specs=pl.BlockSpec(memory_space=pl.ANY),
        scratch_shapes=[
            pltpu.SemaphoreType.DMA(()),
            pltpu.SemaphoreType.DMA((2 * ring,)),
            pltpu.SemaphoreType.DMA((2 * ring,)),
        ],
        compiler_params=pltpu.CompilerParams(collective_id=collective_id, has_side_effects=True),
    )(block)


def scatter_kernel(axis, ring, m, with_sib, parts, x_ref, out_ref, sbuf, rbuf, sibbuf, send_sems, recv_sems, sib_sems):
    mesh_id = pl.DeviceIdType.MESH
    names = ("depth", "rz", "rc", "col")
    me = {a: lax.axis_index(a) for a in names}
    pos = me[axis]
    h = m // 2
    q = h // parts

    def device(**moved):
        return tuple(moved.get(a, me[a]) for a in names)

    right = device(**{axis: lax.rem(pos + 1, ring)})
    left = device(**{axis: lax.rem(pos + ring - 1, ring)})
    sib = device(rc=1 - me["rc"])
    peers = (left, right, sib) if with_sib else (left, right)

    barrier = pltpu.get_barrier_semaphore()
    for peer in peers:
        pl.semaphore_signal(barrier, inc=1, device_id=peer, device_id_type=mesh_id)
    pl.semaphore_wait(barrier, len(peers))

    def rows_of(at, half, part, owner):
        slot = at * 2 + owner if with_sib else at
        return pl.ds(pl.multiple_of(slot * m + half * h + part * q, 8), q)

    def sib_rows(at, half, part):
        return pl.ds(pl.multiple_of(at * m + half * h + part * q, 8), q)

    def remote(src, dst, peer, sems, idx):
        cp = pltpu.make_async_remote_copy(
            src_ref=src,
            dst_ref=dst,
            send_sem=sems[0].at[idx],
            recv_sem=sems[1].at[idx],
            device_id=peer,
            device_id_type=mesh_id,
        )
        cp.start()
        return cp

    def need(s, half):
        sign = -1 if half == 0 else 1
        return lax.rem(pos + sign * (s % ring) + ring * ring, ring)

    sib_copies = {}
    if with_sib:
        order = [(s, half) for s in range(1, ring + 1) for half in (0, 1)]
        for idx, (s, half) in enumerate(order):
            at = need(s, half)
            sib_copies[(s, half)] = remote(
                x_ref.at[pl.ds(pl.multiple_of((at * 2 + 1 - me["rc"]) * m + half * h, 8), h)],
                sibbuf.at[pl.ds(pl.multiple_of(at * m + half * h, 8), h)],
                sib,
                (sib_sems[0], sib_sems[1]),
                idx,
            )

    def contribution(s, half, part):
        at = need(s, half)
        own = x_ref[rows_of(at, half, part, me["rc"])]
        if with_sib:
            if part == 0:
                sib_copies[(s, half)].wait()
            own = own + sibbuf[sib_rows(at, half, part)]
        return own

    ring_copies = {}
    for s in range(1, ring):
        for part in range(parts):
            for half in (0, 1):
                value = contribution(s, half, part)
                if s > 1:
                    ring_copies[(s - 1, half, part)].wait()
                    value = value + rbuf[half, s - 2, part]
                sbuf[half, s - 1, part] = value
                ring_copies[(s, half, part)] = remote(
                    sbuf.at[half, s - 1, part],
                    rbuf.at[half, s - 1, part],
                    right if half == 0 else left,
                    (send_sems, recv_sems),
                    (half * (ring - 1) + s - 1) * parts + part,
                )
    for part in range(parts):
        for half in (0, 1):
            value = contribution(ring, half, part)
            ring_copies[(ring - 1, half, part)].wait()
            out_ref[pl.ds(half * h + part * q, q)] = value + rbuf[half, ring - 2, part]


def ring_scatter(x, axis, ring, with_sib, parts, collective_id):
    total, w = x.shape
    copies = 2 if with_sib else 1
    m = total // (copies * ring)
    sib_rows = ring * m if with_sib else 8
    return pl.pallas_call(
        functools.partial(scatter_kernel, axis, ring, m, with_sib, parts),
        out_shape=jax.ShapeDtypeStruct((m, w), x.dtype),
        in_specs=[pl.BlockSpec(memory_space=pltpu.VMEM)],
        out_specs=pl.BlockSpec(memory_space=pltpu.VMEM),
        scratch_shapes=[
            pltpu.VMEM((2, ring - 1, parts, m // 2 // parts, w), x.dtype),
            pltpu.VMEM((2, ring - 1, parts, m // 2 // parts, w), x.dtype),
            pltpu.VMEM((sib_rows, w), x.dtype),
            pltpu.SemaphoreType.DMA((2 * ring * parts,)),
            pltpu.SemaphoreType.DMA((2 * ring * parts,)),
            (pltpu.SemaphoreType.DMA((2 * ring,)), pltpu.SemaphoreType.DMA((2 * ring,))),
        ],
        compiler_params=pltpu.CompilerParams(
            collective_id=collective_id, has_side_effects=True, vmem_limit_bytes=60 * 1024 * 1024
        ),
    )(x)


def mix_kernel(ring, cols, n, o_ref, wo_ref, own_ref, out_ref, ogath, part, recv, send_sems, recv_sems, y_send, y_recv):
    mesh_id = pl.DeviceIdType.MESH
    names = ("depth", "rz", "rc", "col")
    me = {a: lax.axis_index(a) for a in names}
    z, c, y = me["rz"], me["rc"], me["col"]
    per_col = 2 * ring // cols

    def device(**moved):
        return tuple(moved.get(a, me[a]) for a in names)

    right = device(rz=lax.rem(z + 1, ring))
    left = device(rz=lax.rem(z + ring - 1, ring))
    sib = device(rc=1 - c)
    peers = [left, right, sib] + [device(col=lax.rem(y + d, cols)) for d in range(1, cols)]

    barrier = pltpu.get_barrier_semaphore()
    for peer in peers:
        pl.semaphore_signal(barrier, inc=1, device_id=peer, device_id_type=mesh_id)
    pl.semaphore_wait(barrier, len(peers))

    def remote(src, dst, peer, send, recv_sem):
        cp = pltpu.make_async_remote_copy(
            src_ref=src, dst_ref=dst, send_sem=send, recv_sem=recv_sem, device_id=peer, device_id_type=mesh_id
        )
        cp.start()
        return cp

    piece = n // cols

    def project(block, k):
        part[k] = jnp.dot(block, wo_ref[...], preferred_element_type=jnp.float32, precision=lax.Precision.HIGH)
        for d in range(1, cols):
            dest = lax.rem(y + d, cols)
            remote(
                part.at[k, pl.ds(pl.multiple_of(dest * piece, 8), piece)],
                recv.at[cols - d, k],
                device(col=dest),
                y_send.at[k * cols + d],
                y_recv.at[(cols - d) * 2 * ring + k],
            )

    def slot(zz, cc):
        return zz * 2 + cc

    def z_copy(src, dst_slot, lo, size, peer, idx):
        return remote(src, ogath.at[dst_slot, pl.ds(lo, size)], peer, send_sems.at[idx], recv_sems.at[idx])

    pending_sib = [(z_copy(o_ref, slot(z, c), 0, n, sib, ring), z)]
    to_project = [slot(z, c)]
    half = ring // 2
    for s in range(1, half + 1):
        origin_r = lax.rem(z - (s - 1) + ring, ring)
        origin_l = lax.rem(z + (s - 1), ring)
        src_r = o_ref if s == 1 else ogath.at[slot(origin_r, c)]
        src_l = o_ref if s == 1 else ogath.at[slot(origin_l, c)]
        if s < half:
            cr = z_copy(src_r, slot(origin_r, c), 0, n, right, 2 * (s - 1))
            cl = z_copy(src_l, slot(origin_l, c), 0, n, left, 2 * (s - 1) + 1)
        else:
            h = n // 2
            cr = z_copy(src_r.at[pl.ds(0, h)], slot(origin_r, c), 0, h, right, 2 * (s - 1))
            cl = z_copy(src_l.at[pl.ds(h, h)], slot(origin_l, c), h, h, left, 2 * (s - 1) + 1)
        for k in to_project:
            project(o_ref[...] if s == 1 else ogath[k], k)
        to_project = []
        for cp, at in pending_sib:
            cp.wait()
            project(ogath[slot(at, 1 - c)], slot(at, 1 - c))
        pending_sib = []
        cr.wait()
        cl.wait()
        if s < half:
            arrived = [(lax.rem(z - s + ring, ring), ring + 2 * s - 1), (lax.rem(z + s, ring), ring + 2 * s)]
        else:
            arrived = [(lax.rem(z + half, ring), ring + 2 * s - 1)]
        for at, idx in arrived:
            pending_sib.append((z_copy(ogath.at[slot(at, c)], slot(at, c), 0, n, sib, idx), at))
            to_project.append(slot(at, c))
    for k in to_project:
        project(ogath[k], k)
    for cp, at in pending_sib:
        cp.wait()
        project(ogath[slot(at, 1 - c)], slot(at, 1 - c))
    for k in range(2 * ring):
        own = part[k, pl.ds(pl.multiple_of(y * piece, 8), piece)]
        total = None
        for d in range(1, cols):
            pltpu.make_async_remote_copy(
                src_ref=part.at[k, pl.ds(0, piece)],
                dst_ref=recv.at[d, k],
                send_sem=y_send.at[0],
                recv_sem=y_recv.at[d * 2 * ring + k],
                device_id=device(col=lax.rem(y + d, cols)),
                device_id_type=mesh_id,
            ).wait_recv()
            total = recv[d, k] if total is None else total + recv[d, k]
        m = piece // 2
        for e in (0, 1):
            out_ref[pl.ds(e * 2 * ring * m + k * m, m)] = total[e * m : (e + 1) * m]
            own_ref[pl.ds(e * 2 * ring * m + k * m, m)] = own[e * m : (e + 1) * m]
    for k in range(2 * ring):
        for d in range(1, cols):
            pltpu.make_async_remote_copy(
                src_ref=part.at[k, pl.ds(0, piece)],
                dst_ref=recv.at[0, 0],
                send_sem=y_send.at[k * cols + d],
                recv_sem=y_recv.at[0],
                device_id=device(col=lax.rem(y + d, cols)),
                device_id_type=mesh_id,
            ).wait_send()


def gather_mix(o, w_out, ring, cols, collective_id):
    n, width = o.shape
    out_w = w_out.shape[1]
    per_col = 2 * ring // cols
    return pl.pallas_call(
        functools.partial(mix_kernel, ring, cols, n),
        out_shape=(
            jax.ShapeDtypeStruct((per_col * n, out_w), jnp.float32),
            jax.ShapeDtypeStruct((per_col * n, out_w), jnp.float32),
        ),
        in_specs=[pl.BlockSpec(memory_space=pltpu.VMEM), pl.BlockSpec(memory_space=pltpu.VMEM)],
        out_specs=(pl.BlockSpec(memory_space=pltpu.VMEM), pl.BlockSpec(memory_space=pltpu.VMEM)),
        scratch_shapes=[
            pltpu.VMEM((2 * ring, n, width), jnp.float32),
            pltpu.VMEM((2 * ring, n, out_w), jnp.float32),
            pltpu.VMEM((cols, 2 * ring, n // cols, out_w), jnp.float32),
            pltpu.SemaphoreType.DMA((2 * ring,)),
            pltpu.SemaphoreType.DMA((2 * ring,)),
            pltpu.SemaphoreType.DMA((2 * ring * cols,)),
            pltpu.SemaphoreType.DMA((2 * ring * cols,)),
        ],
        compiler_params=pltpu.CompilerParams(
            collective_id=collective_id, has_side_effects=True, vmem_limit_bytes=60 * 1024 * 1024
        ),
    )(o, w_out)


def front_kernel(
    ring, cols, tok_ref, wq_ref, wk_ref, wv_ref, out_ref, kv_out, tg, partial, sibbuf, sbuf, rbuf, kvbuf,
    y_sems, z_sems, sib_sems, kv_sems,
):
    mesh_id = pl.DeviceIdType.MESH
    names = ("depth", "rz", "rc", "col")
    me = {a: lax.axis_index(a) for a in names}
    z, c, y = me["rz"], me["rc"], me["col"]
    rows = tok_ref.shape[0]
    m = rows // 2 // (2 * ring)
    h = m // 2

    def device(**moved):
        return tuple(moved.get(a, me[a]) for a in names)

    right = device(rz=lax.rem(z + 1, ring))
    left = device(rz=lax.rem(z + ring - 1, ring))
    sib = device(rc=1 - c)
    y_right = device(col=lax.rem(y + 1, cols))
    y_left = device(col=lax.rem(y + cols - 1, cols))
    peers = [left, right, sib, y_left, y_right]

    barrier = pltpu.get_barrier_semaphore()
    for peer in peers:
        pl.semaphore_signal(barrier, inc=1, device_id=peer, device_id_type=mesh_id)
    pl.semaphore_wait(barrier, len(peers))

    def remote(src, dst, peer, sems, idx):
        cp = pltpu.make_async_remote_copy(
            src_ref=src, dst_ref=dst, send_sem=sems[0].at[idx], recv_sem=sems[1].at[idx],
            device_id=peer, device_id_type=mesh_id,
        )
        cp.start()
        return cp

    def need(s, half):
        sign = -1 if half == 0 else 1
        return lax.rem(z + sign * (s % ring) + ring * ring, ring)

    def round_steps(r, chunk):
        x = partial.at[r]
        base = r * 2 * ring
        sib_copies = {}
        for idx, (s, half) in enumerate((s, half) for s in range(1, ring + 1) for half in (0, 1)):
            at = need(s, half)
            sib_copies[(s, half)] = remote(
                x.at[pl.ds(pl.multiple_of((at * 2 + 1 - c) * m + half * h, 8), h)],
                sibbuf.at[r, pl.ds(pl.multiple_of(at * m + half * h, 8), h)],
                sib, sib_sems, base + idx,
            )
        yield

        def contribution(s, half):
            at = need(s, half)
            sib_copies[(s, half)].wait()
            own = x[pl.ds(pl.multiple_of((at * 2 + c) * m + half * h, 8), h)]
            return own + sibbuf[r, pl.ds(pl.multiple_of(at * m + half * h, 8), h)]

        ring_copies = {}
        for s in range(1, ring):
            for half in (0, 1):
                value = contribution(s, half)
                if s > 1:
                    ring_copies[(s - 1, half)].wait()
                    value = value + rbuf[r, half, s - 2]
                sbuf[r, half, s - 1] = value
                ring_copies[(s, half)] = remote(
                    sbuf.at[r, half, s - 1], rbuf.at[r, half, s - 1],
                    right if half == 0 else left, z_sems, base + half * (ring - 1) + s - 1,
                )
            yield
        for half in (0, 1):
            value = contribution(ring, half)
            ring_copies[(ring - 1, half)].wait()
            value = value + rbuf[r, half, ring - 2]
            out_ref[pl.ds(pl.multiple_of(chunk * m + half * h, 8), h)] = value
            kvbuf[r, z * 2 + c, pl.ds(half * h, h)] = value[:, qw:]
        yield

        def kv_copy(src, at, lo, size, peer, idx):
            return remote(src, kvbuf.at[r, at * 2 + c, pl.ds(lo, size)], peer, kv_sems, base + idx)

        kv_sib = [
            remote(kvbuf.at[r, z * 2 + c], kvbuf.at[r, z * 2 + c], sib, kv_sems, base + ring)
        ]
        half_ring = ring // 2
        for s in range(1, half_ring + 1):
            origin_r = lax.rem(z - (s - 1) + ring, ring)
            origin_l = lax.rem(z + (s - 1), ring)
            src_r = kvbuf.at[r, origin_r * 2 + c]
            src_l = kvbuf.at[r, origin_l * 2 + c]
            if s < half_ring:
                cr = kv_copy(src_r, origin_r, 0, m, right, 2 * (s - 1))
                cl = kv_copy(src_l, origin_l, 0, m, left, 2 * (s - 1) + 1)
            else:
                cr = kv_copy(src_r.at[pl.ds(0, h)], origin_r, 0, h, right, 2 * (s - 1))
                cl = kv_copy(src_l.at[pl.ds(h, h)], origin_l, h, h, left, 2 * (s - 1) + 1)
            yield
            cr.wait()
            cl.wait()
            if s < half_ring:
                got = [(lax.rem(z - s + ring, ring), ring + 2 * s - 1), (lax.rem(z + s, ring), ring + 2 * s)]
            else:
                got = [(lax.rem(z + half_ring, ring), ring + 2 * s - 1)]
            for at, idx in got:
                kv_sib.append(
                    remote(kvbuf.at[r, at * 2 + c], kvbuf.at[r, at * 2 + c], sib, kv_sems, base + idx)
                )
        yield
        for cp in kv_sib:
            cp.wait()
        yield

    qw = wq_ref.shape[1]
    kw = wk_ref.shape[1]

    def project(r, src):
        block = src[...]
        for lo, w_ref in ((0, wq_ref), (qw, wk_ref), (qw + kw, wv_ref)):
            partial[r, :, pl.ds(lo, w_ref.shape[1])] = jnp.dot(
                block, w_ref[...], preferred_element_type=jnp.float32, precision=lax.Precision.HIGH
            )

    hr = rows // 2
    chunks = (y, lax.rem(y + cols - 1, cols), lax.rem(y + 1, cols), lax.rem(y + 2, cols))

    def sub(ref, e):
        return ref.at[pl.ds(e * hr, hr)]

    y1 = {}
    for e in (0, 1):
        y1[("r", e)] = remote(sub(tok_ref, e), sub(tg.at[1], e), y_right, y_sems, 2 * e)
        y1[("l", e)] = remote(sub(tok_ref, e), sub(tg.at[2], e), y_left, y_sems, 2 * e + 1)
    rounds = []

    def begin(slot_id, e, src):
        r = 2 * slot_id + e
        project(r, src)
        g = round_steps(r, 2 * chunks[slot_id] + e)
        next(g)
        rounds.append(g)

    def advance(times):
        for _ in range(times):
            for g in list(rounds):
                next(g, None)

    begin(0, 0, sub(tok_ref, 0))
    begin(0, 1, sub(tok_ref, 1))
    advance(ring // 2)
    y1[("r", 0)].wait()
    y2r = remote(sub(tg.at[1], 0), sub(tg.at[3], 0), y_right, y_sems, 4)
    y1[("l", 0)].wait()
    begin(1, 0, sub(tg.at[1], 0))
    begin(2, 0, sub(tg.at[2], 0))
    advance(2)
    y1[("r", 1)].wait()
    y1[("l", 1)].wait()
    y2l = remote(sub(tg.at[2], 1), sub(tg.at[3], 1), y_left, y_sems, 5)
    begin(1, 1, sub(tg.at[1], 1))
    begin(2, 1, sub(tg.at[2], 1))
    advance(2)
    y2r.wait()
    begin(3, 0, sub(tg.at[3], 0))
    y2l.wait()
    begin(3, 1, sub(tg.at[3], 1))
    live = list(rounds)
    while live:
        live = [g for g in live if next(g, "done") != "done"]
    kv_out[...] = kvbuf[...]


def front(tokens, w_query, w_key, w_value, ring, cols, collective_id):
    rows, width = tokens.shape
    out_w = w_query.shape[1] + w_key.shape[1] + w_value.shape[1]
    kv_w = w_key.shape[1] + w_value.shape[1]
    n_rounds = 2 * cols
    hr = rows // 2
    m = hr // (2 * ring)
    return pl.pallas_call(
        functools.partial(front_kernel, ring, cols),
        out_shape=(
            jax.ShapeDtypeStruct((n_rounds * m, out_w), jnp.float32),
            jax.ShapeDtypeStruct((n_rounds, 2 * ring, m, kv_w), jnp.float32),
        ),
        in_specs=[pl.BlockSpec(memory_space=pltpu.VMEM)] * 4,
        out_specs=(pl.BlockSpec(memory_space=pltpu.VMEM), pl.BlockSpec(memory_space=pltpu.VMEM)),
        scratch_shapes=[
            pltpu.VMEM((cols, rows, width), jnp.float32),
            pltpu.VMEM((n_rounds, hr, out_w), jnp.float32),
            pltpu.VMEM((n_rounds, ring * m, out_w), jnp.float32),
            pltpu.VMEM((n_rounds, 2, ring - 1, m // 2, out_w), jnp.float32),
            pltpu.VMEM((n_rounds, 2, ring - 1, m // 2, out_w), jnp.float32),
            pltpu.VMEM((n_rounds, 2 * ring, m, kv_w), jnp.float32),
            (pltpu.SemaphoreType.DMA((6,)), pltpu.SemaphoreType.DMA((6,))),
            (pltpu.SemaphoreType.DMA((n_rounds * 2 * ring,)), pltpu.SemaphoreType.DMA((n_rounds * 2 * ring,))),
            (pltpu.SemaphoreType.DMA((n_rounds * 2 * ring,)), pltpu.SemaphoreType.DMA((n_rounds * 2 * ring,))),
            (pltpu.SemaphoreType.DMA((n_rounds * 2 * ring,)), pltpu.SemaphoreType.DMA((n_rounds * 2 * ring,))),
        ],
        compiler_params=pltpu.CompilerParams(
            collective_id=collective_id, has_side_effects=True, vmem_limit_bytes=60 * 1024 * 1024
        ),
    )(tokens, w_query, w_key, w_value)


def on_device(ring, cols, tokens, w_query, w_key, w_value, w_out):
    highest = lax.Precision.HIGH
    q_width = w_query.shape[1]
    kv_width = w_key.shape[1]
    joined, kv_sets = front(tokens, w_query, w_key, w_value, ring, cols, 3)
    query_rows = joined[:, :q_width]
    all_kv = kv_sets.reshape(-1, kv_sets.shape[-1])
    state_end = fold_keys(
        query_rows,
        start_state(query_rows, kv_width),
        (all_kv[:, :kv_width], all_kv[:, kv_width:]),
    )
    own, rest = gather_mix(finish(state_end), w_out, ring, cols, 5)
    return own + rest


def solution(mesh):
    depth, row, col = (mesh.shape[a] for a in ("depth", "row", "col"))
    split = jax.sharding.Mesh(
        np.asarray(mesh.devices).reshape(depth, row // 2, 2, col), ("depth", "rz", "rc", "col")
    )
    rows = ("rz", "rc")
    placed = (
        P(("depth", "col"), rows),
        P(rows, "col"),
        P(rows, "col"),
        P(rows, "col"),
        P("col", rows),
    )
    return jax.shard_map(
        functools.partial(on_device, row // 2, col),
        mesh=split,
        in_specs=placed,
        out_specs=P(("depth", "col"), rows),
        check_vma=False,
    )
```

```python
import functools
import math

import jax
import numpy as np
import jax.numpy as jnp
from jax import lax
from jax.experimental import pallas as pl
from jax.experimental.pallas import tpu as pltpu
from jax.sharding import PartitionSpec as P

QUERY_HEADS = 32
KEY_VALUE_HEADS = 4
HEAD_SIZE_DIM = 128


def start_state(query_rows, kv_width):
    count_of_heads = kv_width // HEAD_SIZE_DIM
    queries_per_group = QUERY_HEADS // KEY_VALUE_HEADS
    count_of_rows = query_rows.shape[0]
    running_max = jnp.full((count_of_heads, queries_per_group, count_of_rows), -1e30, jnp.float32)
    running_sum = jnp.zeros((count_of_heads, queries_per_group, count_of_rows), jnp.float32)
    weighted = jnp.zeros(
        (count_of_heads, queries_per_group, count_of_rows, HEAD_SIZE_DIM), jnp.float32
    )
    return (running_max, running_sum, weighted)


def fold_keys(query_rows, state_now, block_pair):
    highest = lax.Precision.HIGH
    running_max, running_sum, weighted = state_now
    key_block, value_block = block_pair
    count_of_heads = key_block.shape[1] // HEAD_SIZE_DIM
    count_of_rows = query_rows.shape[0]
    query_head_rows = query_rows.reshape(
        count_of_rows, count_of_heads, QUERY_HEADS // KEY_VALUE_HEADS, HEAD_SIZE_DIM
    )
    key_head_rows = key_block.reshape(-1, count_of_heads, HEAD_SIZE_DIM)
    value_head_rows = value_block.reshape(-1, count_of_heads, HEAD_SIZE_DIM)
    scores = jnp.einsum("rkgd,nkd->kgrn", query_head_rows, key_head_rows, precision=highest) * (
        1.0 / math.sqrt(HEAD_SIZE_DIM)
    )
    newest = jnp.maximum(running_max, jnp.max(scores, axis=-1))
    weights = jnp.exp(scores - newest[..., None])
    running_sum = jnp.sum(weights, axis=-1)
    weighted = jnp.einsum("kgrn,nkd->kgrd", weights, value_head_rows, precision=highest)
    return (newest, running_sum, weighted)


def finish(state_now):
    running_max, running_sum, weighted = state_now
    attention_output = weighted / running_sum[..., None]
    count_of_heads, queries_per_group, count_of_rows, head_size = attention_output.shape
    return attention_output.transpose(2, 0, 1, 3).reshape(
        count_of_rows, count_of_heads * queries_per_group * head_size
    )


def gather_kernel(axis, ring, n, with_sib, x_ref, out_ref, local_sem, send_sems, recv_sems):
    mesh_id = pl.DeviceIdType.MESH
    names = ("depth", "rz", "rc", "col")
    me = {a: lax.axis_index(a) for a in names}
    pos = me[axis]

    def device(**moved):
        return tuple(moved.get(a, me[a]) for a in names)

    right = device(**{axis: lax.rem(pos + 1, ring)})
    left = device(**{axis: lax.rem(pos + ring - 1, ring)})
    sib = device(rc=1 - me["rc"])
    peers = (left, right, sib) if with_sib else (left, right)

    barrier = pltpu.get_barrier_semaphore()
    for peer in peers:
        pl.semaphore_signal(barrier, inc=1, device_id=peer, device_id_type=mesh_id)
    pl.semaphore_wait(barrier, len(peers))

    def rows(at, lo=0, size=n):
        slot = at * 2 + me["rc"] if with_sib else at
        return pl.ds(pl.multiple_of(slot * n + lo, 8), size)

    def remote(src, dst_rows, peer, idx):
        cp = pltpu.make_async_remote_copy(
            src_ref=src,
            dst_ref=out_ref.at[dst_rows],
            send_sem=send_sems.at[idx],
            recv_sem=recv_sems.at[idx],
            device_id=peer,
            device_id_type=mesh_id,
        )
        cp.start()
        return cp

    def to_sib(at, idx):
        if with_sib:
            sib_copies.append(remote(out_ref.at[rows(at)], rows(at), sib, idx))

    local = pltpu.make_async_copy(x_ref, out_ref.at[rows(pos)], local_sem)
    local.start()
    sib_copies = [remote(x_ref, rows(pos), sib, ring)] if with_sib else []
    half = ring // 2
    for s in range(1, half + 1):
        origin_r = lax.rem(pos - (s - 1) + ring, ring)
        origin_l = lax.rem(pos + (s - 1), ring)
        src_r = x_ref if s == 1 else out_ref.at[rows(origin_r)]
        src_l = x_ref if s == 1 else out_ref.at[rows(origin_l)]
        if s < half:
            cr = remote(src_r, rows(origin_r), right, 2 * (s - 1))
            cl = remote(src_l, rows(origin_l), left, 2 * (s - 1) + 1)
            cr.wait()
            cl.wait()
            to_sib(lax.rem(pos - s + ring, ring), ring + 2 * s - 1)
            to_sib(lax.rem(pos + s, ring), ring + 2 * s)
        else:
            h = n // 2
            cr = remote(src_r.at[pl.ds(0, h)], rows(origin_r, 0, h), right, 2 * (s - 1))
            cl = remote(src_l.at[pl.ds(h, h)], rows(origin_l, h, h), left, 2 * (s - 1) + 1)
            cr.wait()
            cl.wait()
            to_sib(lax.rem(pos + half, ring), ring + 2 * s - 1)
    local.wait()
    for cp in sib_copies:
        cp.wait()


def ring_gather(block, axis, ring, with_sib, collective_id):
    n, w = block.shape
    copies = 2 if with_sib else 1
    return pl.pallas_call(
        functools.partial(gather_kernel, axis, ring, n, with_sib),
        out_shape=jax.ShapeDtypeStruct((copies * ring * n, w), block.dtype),
        in_specs=[pl.BlockSpec(memory_space=pl.ANY)],
        out_specs=pl.BlockSpec(memory_space=pl.ANY),
        scratch_shapes=[
            pltpu.SemaphoreType.DMA(()),
            pltpu.SemaphoreType.DMA((2 * ring,)),
            pltpu.SemaphoreType.DMA((2 * ring,)),
        ],
        compiler_params=pltpu.CompilerParams(collective_id=collective_id, has_side_effects=True),
    )(block)


def scatter_kernel(axis, ring, m, with_sib, parts, x_ref, out_ref, sbuf, rbuf, sibbuf, send_sems, recv_sems, sib_sems):
    mesh_id = pl.DeviceIdType.MESH
    names = ("depth", "rz", "rc", "col")
    me = {a: lax.axis_index(a) for a in names}
    pos = me[axis]
    h = m // 2
    q = h // parts

    def device(**moved):
        return tuple(moved.get(a, me[a]) for a in names)

    right = device(**{axis: lax.rem(pos + 1, ring)})
    left = device(**{axis: lax.rem(pos + ring - 1, ring)})
    sib = device(rc=1 - me["rc"])
    peers = (left, right, sib) if with_sib else (left, right)

    barrier = pltpu.get_barrier_semaphore()
    for peer in peers:
        pl.semaphore_signal(barrier, inc=1, device_id=peer, device_id_type=mesh_id)
    pl.semaphore_wait(barrier, len(peers))

    def rows_of(at, half, part, owner):
        slot = at * 2 + owner if with_sib else at
        return pl.ds(pl.multiple_of(slot * m + half * h + part * q, 8), q)

    def sib_rows(at, half, part):
        return pl.ds(pl.multiple_of(at * m + half * h + part * q, 8), q)

    def remote(src, dst, peer, sems, idx):
        cp = pltpu.make_async_remote_copy(
            src_ref=src,
            dst_ref=dst,
            send_sem=sems[0].at[idx],
            recv_sem=sems[1].at[idx],
            device_id=peer,
            device_id_type=mesh_id,
        )
        cp.start()
        return cp

    def need(s, half):
        sign = -1 if half == 0 else 1
        return lax.rem(pos + sign * (s % ring) + ring * ring, ring)

    sib_copies = {}
    if with_sib:
        order = [(s, half) for s in range(1, ring + 1) for half in (0, 1)]
        for idx, (s, half) in enumerate(order):
            at = need(s, half)
            sib_copies[(s, half)] = remote(
                x_ref.at[pl.ds(pl.multiple_of((at * 2 + 1 - me["rc"]) * m + half * h, 8), h)],
                sibbuf.at[pl.ds(pl.multiple_of(at * m + half * h, 8), h)],
                sib,
                (sib_sems[0], sib_sems[1]),
                idx,
            )

    def contribution(s, half, part):
        at = need(s, half)
        own = x_ref[rows_of(at, half, part, me["rc"])]
        if with_sib:
            if part == 0:
                sib_copies[(s, half)].wait()
            own = own + sibbuf[sib_rows(at, half, part)]
        return own

    ring_copies = {}
    for s in range(1, ring):
        for part in range(parts):
            for half in (0, 1):
                value = contribution(s, half, part)
                if s > 1:
                    ring_copies[(s - 1, half, part)].wait()
                    value = value + rbuf[half, s - 2, part]
                sbuf[half, s - 1, part] = value
                ring_copies[(s, half, part)] = remote(
                    sbuf.at[half, s - 1, part],
                    rbuf.at[half, s - 1, part],
                    right if half == 0 else left,
                    (send_sems, recv_sems),
                    (half * (ring - 1) + s - 1) * parts + part,
                )
    for part in range(parts):
        for half in (0, 1):
            value = contribution(ring, half, part)
            ring_copies[(ring - 1, half, part)].wait()
            out_ref[pl.ds(half * h + part * q, q)] = value + rbuf[half, ring - 2, part]


def ring_scatter(x, axis, ring, with_sib, parts, collective_id):
    total, w = x.shape
    copies = 2 if with_sib else 1
    m = total // (copies * ring)
    sib_rows = ring * m if with_sib else 8
    return pl.pallas_call(
        functools.partial(scatter_kernel, axis, ring, m, with_sib, parts),
        out_shape=jax.ShapeDtypeStruct((m, w), x.dtype),
        in_specs=[pl.BlockSpec(memory_space=pltpu.VMEM)],
        out_specs=pl.BlockSpec(memory_space=pltpu.VMEM),
        scratch_shapes=[
            pltpu.VMEM((2, ring - 1, parts, m // 2 // parts, w), x.dtype),
            pltpu.VMEM((2, ring - 1, parts, m // 2 // parts, w), x.dtype),
            pltpu.VMEM((sib_rows, w), x.dtype),
            pltpu.SemaphoreType.DMA((2 * ring * parts,)),
            pltpu.SemaphoreType.DMA((2 * ring * parts,)),
            (pltpu.SemaphoreType.DMA((2 * ring,)), pltpu.SemaphoreType.DMA((2 * ring,))),
        ],
        compiler_params=pltpu.CompilerParams(
            collective_id=collective_id, has_side_effects=True, vmem_limit_bytes=60 * 1024 * 1024
        ),
    )(x)


def mix_kernel(ring, cols, n, o_ref, wo_ref, out_ref, ogath, part, recv, send_sems, recv_sems, y_send, y_recv):
    mesh_id = pl.DeviceIdType.MESH
    names = ("depth", "rz", "rc", "col")
    me = {a: lax.axis_index(a) for a in names}
    z, c, y = me["rz"], me["rc"], me["col"]
    per_col = 2 * ring // cols

    def device(**moved):
        return tuple(moved.get(a, me[a]) for a in names)

    right = device(rz=lax.rem(z + 1, ring))
    left = device(rz=lax.rem(z + ring - 1, ring))
    sib = device(rc=1 - c)
    peers = [left, right, sib] + [device(col=lax.rem(y + d, cols)) for d in range(1, cols)]

    barrier = pltpu.get_barrier_semaphore()
    for peer in peers:
        pl.semaphore_signal(barrier, inc=1, device_id=peer, device_id_type=mesh_id)
    pl.semaphore_wait(barrier, len(peers))

    def remote(src, dst, peer, send, recv_sem):
        cp = pltpu.make_async_remote_copy(
            src_ref=src, dst_ref=dst, send_sem=send, recv_sem=recv_sem, device_id=peer, device_id_type=mesh_id
        )
        cp.start()
        return cp

    piece = n // cols

    def project(block, k):
        part[k] = jnp.dot(block, wo_ref[...], preferred_element_type=jnp.float32, precision=lax.Precision.HIGH)
        for d in range(1, cols):
            dest = lax.rem(y + d, cols)
            remote(
                part.at[k, pl.ds(pl.multiple_of(dest * piece, 8), piece)],
                recv.at[cols - d, k],
                device(col=dest),
                y_send.at[k * cols + d],
                y_recv.at[(cols - d) * 2 * ring + k],
            )

    def slot(zz, cc):
        return zz * 2 + cc

    def z_copy(src, dst_slot, lo, size, peer, idx):
        return remote(src, ogath.at[dst_slot, pl.ds(lo, size)], peer, send_sems.at[idx], recv_sems.at[idx])

    pending_sib = [(z_copy(o_ref, slot(z, c), 0, n, sib, ring), z)]
    to_project = [slot(z, c)]
    half = ring // 2
    for s in range(1, half + 1):
        origin_r = lax.rem(z - (s - 1) + ring, ring)
        origin_l = lax.rem(z + (s - 1), ring)
        src_r = o_ref if s == 1 else ogath.at[slot(origin_r, c)]
        src_l = o_ref if s == 1 else ogath.at[slot(origin_l, c)]
        if s < half:
            cr = z_copy(src_r, slot(origin_r, c), 0, n, right, 2 * (s - 1))
            cl = z_copy(src_l, slot(origin_l, c), 0, n, left, 2 * (s - 1) + 1)
        else:
            h = n // 2
            cr = z_copy(src_r.at[pl.ds(0, h)], slot(origin_r, c), 0, h, right, 2 * (s - 1))
            cl = z_copy(src_l.at[pl.ds(h, h)], slot(origin_l, c), h, h, left, 2 * (s - 1) + 1)
        for k in to_project:
            project(o_ref[...] if s == 1 else ogath[k], k)
        to_project = []
        for cp, at in pending_sib:
            cp.wait()
            project(ogath[slot(at, 1 - c)], slot(at, 1 - c))
        pending_sib = []
        cr.wait()
        cl.wait()
        if s < half:
            arrived = [(lax.rem(z - s + ring, ring), ring + 2 * s - 1), (lax.rem(z + s, ring), ring + 2 * s)]
        else:
            arrived = [(lax.rem(z + half, ring), ring + 2 * s - 1)]
        for at, idx in arrived:
            pending_sib.append((z_copy(ogath.at[slot(at, c)], slot(at, c), 0, n, sib, idx), at))
            to_project.append(slot(at, c))
    for k in to_project:
        project(ogath[k], k)
    for cp, at in pending_sib:
        cp.wait()
        project(ogath[slot(at, 1 - c)], slot(at, 1 - c))
    for k in range(2 * ring):
        total = part[k, pl.ds(pl.multiple_of(y * piece, 8), piece)]
        for d in range(1, cols):
            pltpu.make_async_remote_copy(
                src_ref=part.at[k, pl.ds(0, piece)],
                dst_ref=recv.at[d, k],
                send_sem=y_send.at[0],
                recv_sem=y_recv.at[d * 2 * ring + k],
                device_id=device(col=lax.rem(y + d, cols)),
                device_id_type=mesh_id,
            ).wait_recv()
            total = total + recv[d, k]
        m = piece // 2
        for e in (0, 1):
            out_ref[pl.ds(e * 2 * ring * m + k * m, m)] = total[e * m : (e + 1) * m]
    for k in range(2 * ring):
        for d in range(1, cols):
            pltpu.make_async_remote_copy(
                src_ref=part.at[k, pl.ds(0, piece)],
                dst_ref=recv.at[0, 0],
                send_sem=y_send.at[k * cols + d],
                recv_sem=y_recv.at[0],
                device_id=device(col=lax.rem(y + d, cols)),
                device_id_type=mesh_id,
            ).wait_send()


def gather_mix(o, w_out, ring, cols, collective_id):
    n, width = o.shape
    out_w = w_out.shape[1]
    per_col = 2 * ring // cols
    return pl.pallas_call(
        functools.partial(mix_kernel, ring, cols, n),
        out_shape=jax.ShapeDtypeStruct((per_col * n, out_w), jnp.float32),
        in_specs=[pl.BlockSpec(memory_space=pltpu.VMEM), pl.BlockSpec(memory_space=pltpu.VMEM)],
        out_specs=pl.BlockSpec(memory_space=pltpu.VMEM),
        scratch_shapes=[
            pltpu.VMEM((2 * ring, n, width), jnp.float32),
            pltpu.VMEM((2 * ring, n, out_w), jnp.float32),
            pltpu.VMEM((cols, 2 * ring, n // cols, out_w), jnp.float32),
            pltpu.SemaphoreType.DMA((2 * ring,)),
            pltpu.SemaphoreType.DMA((2 * ring,)),
            pltpu.SemaphoreType.DMA((2 * ring * cols,)),
            pltpu.SemaphoreType.DMA((2 * ring * cols,)),
        ],
        compiler_params=pltpu.CompilerParams(
            collective_id=collective_id, has_side_effects=True, vmem_limit_bytes=60 * 1024 * 1024
        ),
    )(o, w_out)


def front_kernel(
    ring, cols, tok_ref, wq_ref, wk_ref, wv_ref, out_ref, kv_out, tg, partial, sibbuf, sbuf, rbuf, kvbuf,
    y_sems, z_sems, sib_sems, kv_sems,
):
    mesh_id = pl.DeviceIdType.MESH
    names = ("depth", "rz", "rc", "col")
    me = {a: lax.axis_index(a) for a in names}
    z, c, y = me["rz"], me["rc"], me["col"]
    rows = tok_ref.shape[0]
    m = rows // 2 // (2 * ring)
    h = m // 2

    def device(**moved):
        return tuple(moved.get(a, me[a]) for a in names)

    right = device(rz=lax.rem(z + 1, ring))
    left = device(rz=lax.rem(z + ring - 1, ring))
    sib = device(rc=1 - c)
    y_right = device(col=lax.rem(y + 1, cols))
    y_left = device(col=lax.rem(y + cols - 1, cols))
    peers = [left, right, sib, y_left, y_right]

    barrier = pltpu.get_barrier_semaphore()
    for peer in peers:
        pl.semaphore_signal(barrier, inc=1, device_id=peer, device_id_type=mesh_id)
    pl.semaphore_wait(barrier, len(peers))

    def remote(src, dst, peer, sems, idx):
        cp = pltpu.make_async_remote_copy(
            src_ref=src, dst_ref=dst, send_sem=sems[0].at[idx], recv_sem=sems[1].at[idx],
            device_id=peer, device_id_type=mesh_id,
        )
        cp.start()
        return cp

    def need(s, half):
        sign = -1 if half == 0 else 1
        return lax.rem(z + sign * (s % ring) + ring * ring, ring)

    def round_steps(r, chunk):
        x = partial.at[r]
        base = r * 2 * ring
        sib_copies = {}
        for idx, (s, half) in enumerate((s, half) for s in range(1, ring + 1) for half in (0, 1)):
            at = need(s, half)
            sib_copies[(s, half)] = remote(
                x.at[pl.ds(pl.multiple_of((at * 2 + 1 - c) * m + half * h, 8), h)],
                sibbuf.at[r, pl.ds(pl.multiple_of(at * m + half * h, 8), h)],
                sib, sib_sems, base + idx,
            )
        yield

        def contribution(s, half):
            at = need(s, half)
            sib_copies[(s, half)].wait()
            own = x[pl.ds(pl.multiple_of((at * 2 + c) * m + half * h, 8), h)]
            return own + sibbuf[r, pl.ds(pl.multiple_of(at * m + half * h, 8), h)]

        ring_copies = {}
        for s in range(1, ring):
            for half in (0, 1):
                value = contribution(s, half)
                if s > 1:
                    ring_copies[(s - 1, half)].wait()
                    value = value + rbuf[r, half, s - 2]
                sbuf[r, half, s - 1] = value
                ring_copies[(s, half)] = remote(
                    sbuf.at[r, half, s - 1], rbuf.at[r, half, s - 1],
                    right if half == 0 else left, z_sems, base + half * (ring - 1) + s - 1,
                )
            yield
        for half in (0, 1):
            value = contribution(ring, half)
            ring_copies[(ring - 1, half)].wait()
            value = value + rbuf[r, half, ring - 2]
            out_ref[pl.ds(pl.multiple_of(chunk * m + half * h, 8), h)] = value
            kvbuf[r, z * 2 + c, pl.ds(half * h, h)] = value[:, qw:]
        yield

        def kv_copy(src, at, lo, size, peer, idx):
            return remote(src, kvbuf.at[r, at * 2 + c, pl.ds(lo, size)], peer, kv_sems, base + idx)

        kv_sib = [
            remote(kvbuf.at[r, z * 2 + c], kvbuf.at[r, z * 2 + c], sib, kv_sems, base + ring)
        ]
        half_ring = ring // 2
        for s in range(1, half_ring + 1):
            origin_r = lax.rem(z - (s - 1) + ring, ring)
            origin_l = lax.rem(z + (s - 1), ring)
            src_r = kvbuf.at[r, origin_r * 2 + c]
            src_l = kvbuf.at[r, origin_l * 2 + c]
            if s < half_ring:
                cr = kv_copy(src_r, origin_r, 0, m, right, 2 * (s - 1))
                cl = kv_copy(src_l, origin_l, 0, m, left, 2 * (s - 1) + 1)
            else:
                cr = kv_copy(src_r.at[pl.ds(0, h)], origin_r, 0, h, right, 2 * (s - 1))
                cl = kv_copy(src_l.at[pl.ds(h, h)], origin_l, h, h, left, 2 * (s - 1) + 1)
            yield
            cr.wait()
            cl.wait()
            if s < half_ring:
                got = [(lax.rem(z - s + ring, ring), ring + 2 * s - 1), (lax.rem(z + s, ring), ring + 2 * s)]
            else:
                got = [(lax.rem(z + half_ring, ring), ring + 2 * s - 1)]
            for at, idx in got:
                kv_sib.append(
                    remote(kvbuf.at[r, at * 2 + c], kvbuf.at[r, at * 2 + c], sib, kv_sems, base + idx)
                )
        yield
        for cp in kv_sib:
            cp.wait()
        yield

    qw = wq_ref.shape[1]
    kw = wk_ref.shape[1]

    def project(r, src):
        block = src[...]
        for lo, w_ref in ((0, wq_ref), (qw, wk_ref), (qw + kw, wv_ref)):
            partial[r, :, pl.ds(lo, w_ref.shape[1])] = jnp.dot(
                block, w_ref[...], preferred_element_type=jnp.float32, precision=lax.Precision.HIGH
            )

    hr = rows // 2
    chunks = (y, lax.rem(y + cols - 1, cols), lax.rem(y + 1, cols), lax.rem(y + 2, cols))

    def sub(ref, e):
        return ref.at[pl.ds(e * hr, hr)]

    y1 = {}
    for e in (0, 1):
        y1[("r", e)] = remote(sub(tok_ref, e), sub(tg.at[1], e), y_right, y_sems, 2 * e)
        y1[("l", e)] = remote(sub(tok_ref, e), sub(tg.at[2], e), y_left, y_sems, 2 * e + 1)
    rounds = []

    def begin(slot_id, e, src):
        r = 2 * slot_id + e
        project(r, src)
        g = round_steps(r, 2 * chunks[slot_id] + e)
        next(g)
        rounds.append(g)

    def advance(times):
        for _ in range(times):
            for g in list(rounds):
                next(g, None)

    begin(0, 0, sub(tok_ref, 0))
    begin(0, 1, sub(tok_ref, 1))
    advance(ring - 1)
    y1[("r", 0)].wait()
    y2r = remote(sub(tg.at[1], 0), sub(tg.at[3], 0), y_right, y_sems, 4)
    y1[("l", 0)].wait()
    begin(1, 0, sub(tg.at[1], 0))
    begin(2, 0, sub(tg.at[2], 0))
    advance(2)
    y1[("r", 1)].wait()
    y1[("l", 1)].wait()
    y2l = remote(sub(tg.at[2], 1), sub(tg.at[3], 1), y_left, y_sems, 5)
    begin(1, 1, sub(tg.at[1], 1))
    begin(2, 1, sub(tg.at[2], 1))
    advance(2)
    y2r.wait()
    begin(3, 0, sub(tg.at[3], 0))
    y2l.wait()
    begin(3, 1, sub(tg.at[3], 1))
    live = list(rounds)
    while live:
        live = [g for g in live if next(g, "done") != "done"]
    kv_out[...] = kvbuf[...]


def front(tokens, w_query, w_key, w_value, ring, cols, collective_id):
    rows, width = tokens.shape
    out_w = w_query.shape[1] + w_key.shape[1] + w_value.shape[1]
    kv_w = w_key.shape[1] + w_value.shape[1]
    n_rounds = 2 * cols
    hr = rows // 2
    m = hr // (2 * ring)
    return pl.pallas_call(
        functools.partial(front_kernel, ring, cols),
        out_shape=(
            jax.ShapeDtypeStruct((n_rounds * m, out_w), jnp.float32),
            jax.ShapeDtypeStruct((n_rounds, 2 * ring, m, kv_w), jnp.float32),
        ),
        in_specs=[pl.BlockSpec(memory_space=pltpu.VMEM)] * 4,
        out_specs=(pl.BlockSpec(memory_space=pltpu.VMEM), pl.BlockSpec(memory_space=pltpu.VMEM)),
        scratch_shapes=[
            pltpu.VMEM((cols, rows, width), jnp.float32),
            pltpu.VMEM((n_rounds, hr, out_w), jnp.float32),
            pltpu.VMEM((n_rounds, ring * m, out_w), jnp.float32),
            pltpu.VMEM((n_rounds, 2, ring - 1, m // 2, out_w), jnp.float32),
            pltpu.VMEM((n_rounds, 2, ring - 1, m // 2, out_w), jnp.float32),
            pltpu.VMEM((n_rounds, 2 * ring, m, kv_w), jnp.float32),
            (pltpu.SemaphoreType.DMA((6,)), pltpu.SemaphoreType.DMA((6,))),
            (pltpu.SemaphoreType.DMA((n_rounds * 2 * ring,)), pltpu.SemaphoreType.DMA((n_rounds * 2 * ring,))),
            (pltpu.SemaphoreType.DMA((n_rounds * 2 * ring,)), pltpu.SemaphoreType.DMA((n_rounds * 2 * ring,))),
            (pltpu.SemaphoreType.DMA((n_rounds * 2 * ring,)), pltpu.SemaphoreType.DMA((n_rounds * 2 * ring,))),
        ],
        compiler_params=pltpu.CompilerParams(
            collective_id=collective_id, has_side_effects=True, vmem_limit_bytes=60 * 1024 * 1024
        ),
    )(tokens, w_query, w_key, w_value)


def on_device(ring, cols, tokens, w_query, w_key, w_value, w_out):
    highest = lax.Precision.HIGH
    q_width = w_query.shape[1]
    kv_width = w_key.shape[1]
    joined, kv_sets = front(tokens, w_query, w_key, w_value, ring, cols, 3)
    query_rows = joined[:, :q_width]
    all_kv = kv_sets.reshape(-1, kv_sets.shape[-1])
    state_end = fold_keys(
        query_rows,
        start_state(query_rows, kv_width),
        (all_kv[:, :kv_width], all_kv[:, kv_width:]),
    )
    return gather_mix(finish(state_end), w_out, ring, cols, 5)


def solution(mesh):
    depth, row, col = (mesh.shape[a] for a in ("depth", "row", "col"))
    split = jax.sharding.Mesh(
        np.asarray(mesh.devices).reshape(depth, row // 2, 2, col), ("depth", "rz", "rc", "col")
    )
    rows = ("rz", "rc")
    placed = (
        P(("depth", "col"), rows),
        P(rows, "col"),
        P(rows, "col"),
        P(rows, "col"),
        P("col", rows),
    )
    return jax.shard_map(
        functools.partial(on_device, row // 2, col),
        mesh=split,
        in_specs=placed,
        out_specs=P(("depth", "col"), rows),
        check_vma=False,
    )
```

```python
import functools
import math

import jax
import numpy as np
import jax.numpy as jnp
from jax import lax
from jax.experimental import pallas as pl
from jax.experimental.pallas import tpu as pltpu
from jax.sharding import PartitionSpec as P

QUERY_HEADS = 32
KEY_VALUE_HEADS = 4
HEAD_SIZE_DIM = 128


def start_state(query_rows, kv_width):
    count_of_heads = kv_width // HEAD_SIZE_DIM
    queries_per_group = QUERY_HEADS // KEY_VALUE_HEADS
    count_of_rows = query_rows.shape[0]
    running_max = jnp.full((count_of_heads, queries_per_group, count_of_rows), -1e30, jnp.float32)
    running_sum = jnp.zeros((count_of_heads, queries_per_group, count_of_rows), jnp.float32)
    weighted = jnp.zeros(
        (count_of_heads, queries_per_group, count_of_rows, HEAD_SIZE_DIM), jnp.float32
    )
    return (running_max, running_sum, weighted)


def fold_keys(query_rows, state_now, block_pair):
    highest = lax.Precision.HIGH
    running_max, running_sum, weighted = state_now
    key_block, value_block = block_pair
    count_of_heads = key_block.shape[1] // HEAD_SIZE_DIM
    count_of_rows = query_rows.shape[0]
    query_head_rows = query_rows.reshape(
        count_of_rows, count_of_heads, QUERY_HEADS // KEY_VALUE_HEADS, HEAD_SIZE_DIM
    )
    key_head_rows = key_block.reshape(-1, count_of_heads, HEAD_SIZE_DIM)
    value_head_rows = value_block.reshape(-1, count_of_heads, HEAD_SIZE_DIM)
    scores = jnp.einsum("rkgd,nkd->kgrn", query_head_rows, key_head_rows, precision=highest) * (
        1.0 / math.sqrt(HEAD_SIZE_DIM)
    )
    newest = jnp.maximum(running_max, jnp.max(scores, axis=-1))
    weights = jnp.exp(scores - newest[..., None])
    running_sum = jnp.sum(weights, axis=-1)
    weighted = jnp.einsum("kgrn,nkd->kgrd", weights, value_head_rows, precision=highest)
    return (newest, running_sum, weighted)


def finish(state_now):
    running_max, running_sum, weighted = state_now
    attention_output = weighted / running_sum[..., None]
    count_of_heads, queries_per_group, count_of_rows, head_size = attention_output.shape
    return attention_output.transpose(2, 0, 1, 3).reshape(
        count_of_rows, count_of_heads * queries_per_group * head_size
    )


def gather_kernel(axis, ring, n, with_sib, x_ref, out_ref, local_sem, send_sems, recv_sems):
    mesh_id = pl.DeviceIdType.MESH
    names = ("depth", "rz", "rc", "col")
    me = {a: lax.axis_index(a) for a in names}
    pos = me[axis]

    def device(**moved):
        return tuple(moved.get(a, me[a]) for a in names)

    right = device(**{axis: lax.rem(pos + 1, ring)})
    left = device(**{axis: lax.rem(pos + ring - 1, ring)})
    sib = device(rc=1 - me["rc"])
    peers = (left, right, sib) if with_sib else (left, right)

    barrier = pltpu.get_barrier_semaphore()
    for peer in peers:
        pl.semaphore_signal(barrier, inc=1, device_id=peer, device_id_type=mesh_id)
    pl.semaphore_wait(barrier, len(peers))

    def rows(at, lo=0, size=n):
        slot = at * 2 + me["rc"] if with_sib else at
        return pl.ds(pl.multiple_of(slot * n + lo, 8), size)

    def remote(src, dst_rows, peer, idx):
        cp = pltpu.make_async_remote_copy(
            src_ref=src,
            dst_ref=out_ref.at[dst_rows],
            send_sem=send_sems.at[idx],
            recv_sem=recv_sems.at[idx],
            device_id=peer,
            device_id_type=mesh_id,
        )
        cp.start()
        return cp

    def to_sib(at, idx):
        if with_sib:
            sib_copies.append(remote(out_ref.at[rows(at)], rows(at), sib, idx))

    local = pltpu.make_async_copy(x_ref, out_ref.at[rows(pos)], local_sem)
    local.start()
    sib_copies = [remote(x_ref, rows(pos), sib, ring)] if with_sib else []
    half = ring // 2
    for s in range(1, half + 1):
        origin_r = lax.rem(pos - (s - 1) + ring, ring)
        origin_l = lax.rem(pos + (s - 1), ring)
        src_r = x_ref if s == 1 else out_ref.at[rows(origin_r)]
        src_l = x_ref if s == 1 else out_ref.at[rows(origin_l)]
        if s < half:
            cr = remote(src_r, rows(origin_r), right, 2 * (s - 1))
            cl = remote(src_l, rows(origin_l), left, 2 * (s - 1) + 1)
            cr.wait()
            cl.wait()
            to_sib(lax.rem(pos - s + ring, ring), ring + 2 * s - 1)
            to_sib(lax.rem(pos + s, ring), ring + 2 * s)
        else:
            h = n // 2
            cr = remote(src_r.at[pl.ds(0, h)], rows(origin_r, 0, h), right, 2 * (s - 1))
            cl = remote(src_l.at[pl.ds(h, h)], rows(origin_l, h, h), left, 2 * (s - 1) + 1)
            cr.wait()
            cl.wait()
            to_sib(lax.rem(pos + half, ring), ring + 2 * s - 1)
    local.wait()
    for cp in sib_copies:
        cp.wait()


def ring_gather(block, axis, ring, with_sib, collective_id):
    n, w = block.shape
    copies = 2 if with_sib else 1
    return pl.pallas_call(
        functools.partial(gather_kernel, axis, ring, n, with_sib),
        out_shape=jax.ShapeDtypeStruct((copies * ring * n, w), block.dtype),
        in_specs=[pl.BlockSpec(memory_space=pl.ANY)],
        out_specs=pl.BlockSpec(memory_space=pl.ANY),
        scratch_shapes=[
            pltpu.SemaphoreType.DMA(()),
            pltpu.SemaphoreType.DMA((2 * ring,)),
            pltpu.SemaphoreType.DMA((2 * ring,)),
        ],
        compiler_params=pltpu.CompilerParams(collective_id=collective_id, has_side_effects=True),
    )(block)


def scatter_kernel(axis, ring, m, with_sib, parts, x_ref, out_ref, sbuf, rbuf, sibbuf, send_sems, recv_sems, sib_sems):
    mesh_id = pl.DeviceIdType.MESH
    names = ("depth", "rz", "rc", "col")
    me = {a: lax.axis_index(a) for a in names}
    pos = me[axis]
    h = m // 2
    q = h // parts

    def device(**moved):
        return tuple(moved.get(a, me[a]) for a in names)

    right = device(**{axis: lax.rem(pos + 1, ring)})
    left = device(**{axis: lax.rem(pos + ring - 1, ring)})
    sib = device(rc=1 - me["rc"])
    peers = (left, right, sib) if with_sib else (left, right)

    barrier = pltpu.get_barrier_semaphore()
    for peer in peers:
        pl.semaphore_signal(barrier, inc=1, device_id=peer, device_id_type=mesh_id)
    pl.semaphore_wait(barrier, len(peers))

    def rows_of(at, half, part, owner):
        slot = at * 2 + owner if with_sib else at
        return pl.ds(pl.multiple_of(slot * m + half * h + part * q, 8), q)

    def sib_rows(at, half, part):
        return pl.ds(pl.multiple_of(at * m + half * h + part * q, 8), q)

    def remote(src, dst, peer, sems, idx):
        cp = pltpu.make_async_remote_copy(
            src_ref=src,
            dst_ref=dst,
            send_sem=sems[0].at[idx],
            recv_sem=sems[1].at[idx],
            device_id=peer,
            device_id_type=mesh_id,
        )
        cp.start()
        return cp

    def need(s, half):
        sign = -1 if half == 0 else 1
        return lax.rem(pos + sign * (s % ring) + ring * ring, ring)

    sib_copies = {}
    if with_sib:
        order = [(s, half) for s in range(1, ring + 1) for half in (0, 1)]
        for idx, (s, half) in enumerate(order):
            at = need(s, half)
            sib_copies[(s, half)] = remote(
                x_ref.at[pl.ds(pl.multiple_of((at * 2 + 1 - me["rc"]) * m + half * h, 8), h)],
                sibbuf.at[pl.ds(pl.multiple_of(at * m + half * h, 8), h)],
                sib,
                (sib_sems[0], sib_sems[1]),
                idx,
            )

    def contribution(s, half, part):
        at = need(s, half)
        own = x_ref[rows_of(at, half, part, me["rc"])]
        if with_sib:
            if part == 0:
                sib_copies[(s, half)].wait()
            own = own + sibbuf[sib_rows(at, half, part)]
        return own

    ring_copies = {}
    for s in range(1, ring):
        for part in range(parts):
            for half in (0, 1):
                value = contribution(s, half, part)
                if s > 1:
                    ring_copies[(s - 1, half, part)].wait()
                    value = value + rbuf[half, s - 2, part]
                sbuf[half, s - 1, part] = value
                ring_copies[(s, half, part)] = remote(
                    sbuf.at[half, s - 1, part],
                    rbuf.at[half, s - 1, part],
                    right if half == 0 else left,
                    (send_sems, recv_sems),
                    (half * (ring - 1) + s - 1) * parts + part,
                )
    for part in range(parts):
        for half in (0, 1):
            value = contribution(ring, half, part)
            ring_copies[(ring - 1, half, part)].wait()
            out_ref[pl.ds(half * h + part * q, q)] = value + rbuf[half, ring - 2, part]


def ring_scatter(x, axis, ring, with_sib, parts, collective_id):
    total, w = x.shape
    copies = 2 if with_sib else 1
    m = total // (copies * ring)
    sib_rows = ring * m if with_sib else 8
    return pl.pallas_call(
        functools.partial(scatter_kernel, axis, ring, m, with_sib, parts),
        out_shape=jax.ShapeDtypeStruct((m, w), x.dtype),
        in_specs=[pl.BlockSpec(memory_space=pltpu.VMEM)],
        out_specs=pl.BlockSpec(memory_space=pltpu.VMEM),
        scratch_shapes=[
            pltpu.VMEM((2, ring - 1, parts, m // 2 // parts, w), x.dtype),
            pltpu.VMEM((2, ring - 1, parts, m // 2 // parts, w), x.dtype),
            pltpu.VMEM((sib_rows, w), x.dtype),
            pltpu.SemaphoreType.DMA((2 * ring * parts,)),
            pltpu.SemaphoreType.DMA((2 * ring * parts,)),
            (pltpu.SemaphoreType.DMA((2 * ring,)), pltpu.SemaphoreType.DMA((2 * ring,))),
        ],
        compiler_params=pltpu.CompilerParams(
            collective_id=collective_id, has_side_effects=True, vmem_limit_bytes=60 * 1024 * 1024
        ),
    )(x)


def mix_kernel(ring, cols, n, o_ref, wo_ref, out_ref, ogath, part, recv, send_sems, recv_sems, y_send, y_recv):
    mesh_id = pl.DeviceIdType.MESH
    names = ("depth", "rz", "rc", "col")
    me = {a: lax.axis_index(a) for a in names}
    z, c, y = me["rz"], me["rc"], me["col"]
    per_col = 2 * ring // cols

    def device(**moved):
        return tuple(moved.get(a, me[a]) for a in names)

    right = device(rz=lax.rem(z + 1, ring))
    left = device(rz=lax.rem(z + ring - 1, ring))
    sib = device(rc=1 - c)
    peers = [left, right, sib] + [device(col=lax.rem(y + d, cols)) for d in range(1, cols)]

    barrier = pltpu.get_barrier_semaphore()
    for peer in peers:
        pl.semaphore_signal(barrier, inc=1, device_id=peer, device_id_type=mesh_id)
    pl.semaphore_wait(barrier, len(peers))

    def remote(src, dst, peer, send, recv_sem):
        cp = pltpu.make_async_remote_copy(
            src_ref=src, dst_ref=dst, send_sem=send, recv_sem=recv_sem, device_id=peer, device_id_type=mesh_id
        )
        cp.start()
        return cp

    piece = n // cols

    def project(block, k):
        part[k] = jnp.dot(block, wo_ref[...], preferred_element_type=jnp.float32, precision=lax.Precision.HIGH)
        for d in range(1, cols):
            dest = lax.rem(y + d, cols)
            remote(
                part.at[k, pl.ds(pl.multiple_of(dest * piece, 8), piece)],
                recv.at[cols - d, k],
                device(col=dest),
                y_send.at[k * cols + d],
                y_recv.at[(cols - d) * 2 * ring + k],
            )

    def slot(zz, cc):
        return zz * 2 + cc

    def z_copy(src, dst_slot, lo, size, peer, idx):
        return remote(src, ogath.at[dst_slot, pl.ds(lo, size)], peer, send_sems.at[idx], recv_sems.at[idx])

    pending_sib = [(z_copy(o_ref, slot(z, c), 0, n, sib, ring), z)]
    to_project = [slot(z, c)]
    half = ring // 2
    for s in range(1, half + 1):
        origin_r = lax.rem(z - (s - 1) + ring, ring)
        origin_l = lax.rem(z + (s - 1), ring)
        src_r = o_ref if s == 1 else ogath.at[slot(origin_r, c)]
        src_l = o_ref if s == 1 else ogath.at[slot(origin_l, c)]
        if s < half:
            cr = z_copy(src_r, slot(origin_r, c), 0, n, right, 2 * (s - 1))
            cl = z_copy(src_l, slot(origin_l, c), 0, n, left, 2 * (s - 1) + 1)
        else:
            h = n // 2
            cr = z_copy(src_r.at[pl.ds(0, h)], slot(origin_r, c), 0, h, right, 2 * (s - 1))
            cl = z_copy(src_l.at[pl.ds(h, h)], slot(origin_l, c), h, h, left, 2 * (s - 1) + 1)
        for k in to_project:
            project(o_ref[...] if s == 1 else ogath[k], k)
        to_project = []
        for cp, at in pending_sib:
            cp.wait()
            project(ogath[slot(at, 1 - c)], slot(at, 1 - c))
        pending_sib = []
        cr.wait()
        cl.wait()
        if s < half:
            arrived = [(lax.rem(z - s + ring, ring), ring + 2 * s - 1), (lax.rem(z + s, ring), ring + 2 * s)]
        else:
            arrived = [(lax.rem(z + half, ring), ring + 2 * s - 1)]
        for at, idx in arrived:
            pending_sib.append((z_copy(ogath.at[slot(at, c)], slot(at, c), 0, n, sib, idx), at))
            to_project.append(slot(at, c))
    for k in to_project:
        project(ogath[k], k)
    for cp, at in pending_sib:
        cp.wait()
        project(ogath[slot(at, 1 - c)], slot(at, 1 - c))
    for k in range(2 * ring):
        total = part[k, pl.ds(pl.multiple_of(y * piece, 8), piece)]
        for d in range(1, cols):
            pltpu.make_async_remote_copy(
                src_ref=part.at[k, pl.ds(0, piece)],
                dst_ref=recv.at[d, k],
                send_sem=y_send.at[0],
                recv_sem=y_recv.at[d * 2 * ring + k],
                device_id=device(col=lax.rem(y + d, cols)),
                device_id_type=mesh_id,
            ).wait_recv()
            total = total + recv[d, k]
        m = piece // 2
        for e in (0, 1):
            out_ref[pl.ds(e * 2 * ring * m + k * m, m)] = total[e * m : (e + 1) * m]
    for k in range(2 * ring):
        for d in range(1, cols):
            pltpu.make_async_remote_copy(
                src_ref=part.at[k, pl.ds(0, piece)],
                dst_ref=recv.at[0, 0],
                send_sem=y_send.at[k * cols + d],
                recv_sem=y_recv.at[0],
                device_id=device(col=lax.rem(y + d, cols)),
                device_id_type=mesh_id,
            ).wait_send()


def gather_mix(o, w_out, ring, cols, collective_id):
    n, width = o.shape
    out_w = w_out.shape[1]
    per_col = 2 * ring // cols
    return pl.pallas_call(
        functools.partial(mix_kernel, ring, cols, n),
        out_shape=jax.ShapeDtypeStruct((per_col * n, out_w), jnp.float32),
        in_specs=[pl.BlockSpec(memory_space=pltpu.VMEM), pl.BlockSpec(memory_space=pltpu.VMEM)],
        out_specs=pl.BlockSpec(memory_space=pltpu.VMEM),
        scratch_shapes=[
            pltpu.VMEM((2 * ring, n, width), jnp.float32),
            pltpu.VMEM((2 * ring, n, out_w), jnp.float32),
            pltpu.VMEM((cols, 2 * ring, n // cols, out_w), jnp.float32),
            pltpu.SemaphoreType.DMA((2 * ring,)),
            pltpu.SemaphoreType.DMA((2 * ring,)),
            pltpu.SemaphoreType.DMA((2 * ring * cols,)),
            pltpu.SemaphoreType.DMA((2 * ring * cols,)),
        ],
        compiler_params=pltpu.CompilerParams(
            collective_id=collective_id, has_side_effects=True, vmem_limit_bytes=60 * 1024 * 1024
        ),
    )(o, w_out)


def front_kernel(
    ring, cols, tok_ref, wq_ref, wk_ref, wv_ref, out_ref, kv_out, tg, partial, sibbuf, sbuf, rbuf, kvbuf,
    y_sems, z_sems, sib_sems, kv_sems,
):
    mesh_id = pl.DeviceIdType.MESH
    names = ("depth", "rz", "rc", "col")
    me = {a: lax.axis_index(a) for a in names}
    z, c, y = me["rz"], me["rc"], me["col"]
    rows = tok_ref.shape[0]
    m = rows // 2 // (2 * ring)
    h = m // 2

    def device(**moved):
        return tuple(moved.get(a, me[a]) for a in names)

    right = device(rz=lax.rem(z + 1, ring))
    left = device(rz=lax.rem(z + ring - 1, ring))
    sib = device(rc=1 - c)
    y_right = device(col=lax.rem(y + 1, cols))
    y_left = device(col=lax.rem(y + cols - 1, cols))
    peers = [left, right, sib, y_left, y_right]

    barrier = pltpu.get_barrier_semaphore()
    for peer in peers:
        pl.semaphore_signal(barrier, inc=1, device_id=peer, device_id_type=mesh_id)
    pl.semaphore_wait(barrier, len(peers))

    def remote(src, dst, peer, sems, idx):
        cp = pltpu.make_async_remote_copy(
            src_ref=src, dst_ref=dst, send_sem=sems[0].at[idx], recv_sem=sems[1].at[idx],
            device_id=peer, device_id_type=mesh_id,
        )
        cp.start()
        return cp

    def need(s, half):
        sign = -1 if half == 0 else 1
        return lax.rem(z + sign * (s % ring) + ring * ring, ring)

    def round_steps(r, chunk):
        x = partial.at[r]
        base = r * 2 * ring
        sib_copies = {}
        for idx, (s, half) in enumerate((s, half) for s in range(1, ring + 1) for half in (0, 1)):
            at = need(s, half)
            sib_copies[(s, half)] = remote(
                x.at[pl.ds(pl.multiple_of((at * 2 + 1 - c) * m + half * h, 8), h)],
                sibbuf.at[r, pl.ds(pl.multiple_of(at * m + half * h, 8), h)],
                sib, sib_sems, base + idx,
            )
        yield

        def contribution(s, half):
            at = need(s, half)
            sib_copies[(s, half)].wait()
            own = x[pl.ds(pl.multiple_of((at * 2 + c) * m + half * h, 8), h)]
            return own + sibbuf[r, pl.ds(pl.multiple_of(at * m + half * h, 8), h)]

        ring_copies = {}
        for s in range(1, ring):
            for half in (0, 1):
                value = contribution(s, half)
                if s > 1:
                    ring_copies[(s - 1, half)].wait()
                    value = value + rbuf[r, half, s - 2]
                sbuf[r, half, s - 1] = value
                ring_copies[(s, half)] = remote(
                    sbuf.at[r, half, s - 1], rbuf.at[r, half, s - 1],
                    right if half == 0 else left, z_sems, base + half * (ring - 1) + s - 1,
                )
            yield
        for half in (0, 1):
            value = contribution(ring, half)
            ring_copies[(ring - 1, half)].wait()
            value = value + rbuf[r, half, ring - 2]
            out_ref[pl.ds(pl.multiple_of(chunk * m + half * h, 8), h)] = value
            kvbuf[r, z * 2 + c, pl.ds(half * h, h)] = value[:, qw:]
        yield

        def kv_copy(src, at, lo, size, peer, idx):
            return remote(src, kvbuf.at[r, at * 2 + c, pl.ds(lo, size)], peer, kv_sems, base + idx)

        kv_sib = [
            remote(kvbuf.at[r, z * 2 + c], kvbuf.at[r, z * 2 + c], sib, kv_sems, base + ring)
        ]
        half_ring = ring // 2
        for s in range(1, half_ring + 1):
            origin_r = lax.rem(z - (s - 1) + ring, ring)
            origin_l = lax.rem(z + (s - 1), ring)
            src_r = kvbuf.at[r, origin_r * 2 + c]
            src_l = kvbuf.at[r, origin_l * 2 + c]
            if s < half_ring:
                cr = kv_copy(src_r, origin_r, 0, m, right, 2 * (s - 1))
                cl = kv_copy(src_l, origin_l, 0, m, left, 2 * (s - 1) + 1)
            else:
                cr = kv_copy(src_r.at[pl.ds(0, h)], origin_r, 0, h, right, 2 * (s - 1))
                cl = kv_copy(src_l.at[pl.ds(h, h)], origin_l, h, h, left, 2 * (s - 1) + 1)
            yield
            cr.wait()
            cl.wait()
            if s < half_ring:
                got = [(lax.rem(z - s + ring, ring), ring + 2 * s - 1), (lax.rem(z + s, ring), ring + 2 * s)]
            else:
                got = [(lax.rem(z + half_ring, ring), ring + 2 * s - 1)]
            for at, idx in got:
                kv_sib.append(
                    remote(kvbuf.at[r, at * 2 + c], kvbuf.at[r, at * 2 + c], sib, kv_sems, base + idx)
                )
        yield
        for cp in kv_sib:
            cp.wait()
        yield

    qw = wq_ref.shape[1]
    kw = wk_ref.shape[1]

    def project(r, src):
        block = src[...]
        for lo, w_ref in ((0, wq_ref), (qw, wk_ref), (qw + kw, wv_ref)):
            partial[r, :, pl.ds(lo, w_ref.shape[1])] = jnp.dot(
                block, w_ref[...], preferred_element_type=jnp.float32, precision=lax.Precision.HIGH
            )

    hr = rows // 2
    chunks = (y, lax.rem(y + cols - 1, cols), lax.rem(y + 1, cols), lax.rem(y + 2, cols))

    def sub(ref, e):
        return ref.at[pl.ds(e * hr, hr)]

    y1 = {}
    for e in (0, 1):
        y1[("r", e)] = remote(sub(tok_ref, e), sub(tg.at[1], e), y_right, y_sems, 2 * e)
        y1[("l", e)] = remote(sub(tok_ref, e), sub(tg.at[2], e), y_left, y_sems, 2 * e + 1)
    rounds = []

    def begin(slot_id, e, src):
        r = 2 * slot_id + e
        project(r, src)
        g = round_steps(r, 2 * chunks[slot_id] + e)
        next(g)
        rounds.append(g)

    def advance(times):
        for _ in range(times):
            for g in list(rounds):
                next(g, None)

    begin(0, 0, sub(tok_ref, 0))
    begin(0, 1, sub(tok_ref, 1))
    advance(2)
    y1[("r", 0)].wait()
    y2r = remote(sub(tg.at[1], 0), sub(tg.at[3], 0), y_right, y_sems, 4)
    y1[("l", 0)].wait()
    begin(1, 0, sub(tg.at[1], 0))
    begin(2, 0, sub(tg.at[2], 0))
    advance(2)
    y1[("r", 1)].wait()
    y1[("l", 1)].wait()
    y2l = remote(sub(tg.at[2], 1), sub(tg.at[3], 1), y_left, y_sems, 5)
    begin(1, 1, sub(tg.at[1], 1))
    begin(2, 1, sub(tg.at[2], 1))
    advance(2)
    y2r.wait()
    begin(3, 0, sub(tg.at[3], 0))
    y2l.wait()
    begin(3, 1, sub(tg.at[3], 1))
    live = list(rounds)
    while live:
        live = [g for g in live if next(g, "done") != "done"]
    kv_out[...] = kvbuf[...]


def front(tokens, w_query, w_key, w_value, ring, cols, collective_id):
    rows, width = tokens.shape
    out_w = w_query.shape[1] + w_key.shape[1] + w_value.shape[1]
    kv_w = w_key.shape[1] + w_value.shape[1]
    n_rounds = 2 * cols
    hr = rows // 2
    m = hr // (2 * ring)
    return pl.pallas_call(
        functools.partial(front_kernel, ring, cols),
        out_shape=(
            jax.ShapeDtypeStruct((n_rounds * m, out_w), jnp.float32),
            jax.ShapeDtypeStruct((n_rounds, 2 * ring, m, kv_w), jnp.float32),
        ),
        in_specs=[pl.BlockSpec(memory_space=pltpu.VMEM)] * 4,
        out_specs=(pl.BlockSpec(memory_space=pltpu.VMEM), pl.BlockSpec(memory_space=pltpu.VMEM)),
        scratch_shapes=[
            pltpu.VMEM((cols, rows, width), jnp.float32),
            pltpu.VMEM((n_rounds, hr, out_w), jnp.float32),
            pltpu.VMEM((n_rounds, ring * m, out_w), jnp.float32),
            pltpu.VMEM((n_rounds, 2, ring - 1, m // 2, out_w), jnp.float32),
            pltpu.VMEM((n_rounds, 2, ring - 1, m // 2, out_w), jnp.float32),
            pltpu.VMEM((n_rounds, 2 * ring, m, kv_w), jnp.float32),
            (pltpu.SemaphoreType.DMA((6,)), pltpu.SemaphoreType.DMA((6,))),
            (pltpu.SemaphoreType.DMA((n_rounds * 2 * ring,)), pltpu.SemaphoreType.DMA((n_rounds * 2 * ring,))),
            (pltpu.SemaphoreType.DMA((n_rounds * 2 * ring,)), pltpu.SemaphoreType.DMA((n_rounds * 2 * ring,))),
            (pltpu.SemaphoreType.DMA((n_rounds * 2 * ring,)), pltpu.SemaphoreType.DMA((n_rounds * 2 * ring,))),
        ],
        compiler_params=pltpu.CompilerParams(
            collective_id=collective_id, has_side_effects=True, vmem_limit_bytes=60 * 1024 * 1024
        ),
    )(tokens, w_query, w_key, w_value)


def on_device(ring, cols, tokens, w_query, w_key, w_value, w_out):
    highest = lax.Precision.HIGH
    q_width = w_query.shape[1]
    kv_width = w_key.shape[1]
    joined, kv_sets = front(tokens, w_query, w_key, w_value, ring, cols, 3)
    query_rows = joined[:, :q_width]
    all_kv = kv_sets.reshape(-1, kv_sets.shape[-1])
    state_end = fold_keys(
        query_rows,
        start_state(query_rows, kv_width),
        (all_kv[:, :kv_width], all_kv[:, kv_width:]),
    )
    return gather_mix(finish(state_end), w_out, ring, cols, 5)


def solution(mesh):
    depth, row, col = (mesh.shape[a] for a in ("depth", "row", "col"))
    split = jax.sharding.Mesh(
        np.asarray(mesh.devices).reshape(depth, row // 2, 2, col), ("depth", "rz", "rc", "col")
    )
    rows = ("rz", "rc")
    placed = (
        P(("depth", "col"), rows),
        P(rows, "col"),
        P(rows, "col"),
        P(rows, "col"),
        P("col", rows),
    )
    return jax.shard_map(
        functools.partial(on_device, row // 2, col),
        mesh=split,
        in_specs=placed,
        out_specs=P(("depth", "col"), rows),
        check_vma=False,
    )
```

```python
import functools
import math

import jax
import numpy as np
import jax.numpy as jnp
from jax import lax
from jax.experimental import pallas as pl
from jax.experimental.pallas import tpu as pltpu
from jax.sharding import PartitionSpec as P

QUERY_HEADS = 32
KEY_VALUE_HEADS = 4
HEAD_SIZE_DIM = 128


def start_state(query_rows, kv_width):
    count_of_heads = kv_width // HEAD_SIZE_DIM
    queries_per_group = QUERY_HEADS // KEY_VALUE_HEADS
    count_of_rows = query_rows.shape[0]
    running_max = jnp.full((count_of_heads, queries_per_group, count_of_rows), -1e30, jnp.float32)
    running_sum = jnp.zeros((count_of_heads, queries_per_group, count_of_rows), jnp.float32)
    weighted = jnp.zeros(
        (count_of_heads, queries_per_group, count_of_rows, HEAD_SIZE_DIM), jnp.float32
    )
    return (running_max, running_sum, weighted)


def fold_keys(query_rows, state_now, block_pair):
    highest = lax.Precision.HIGH
    running_max, running_sum, weighted = state_now
    key_block, value_block = block_pair
    count_of_heads = key_block.shape[1] // HEAD_SIZE_DIM
    count_of_rows = query_rows.shape[0]
    query_head_rows = query_rows.reshape(
        count_of_rows, count_of_heads, QUERY_HEADS // KEY_VALUE_HEADS, HEAD_SIZE_DIM
    )
    key_head_rows = key_block.reshape(-1, count_of_heads, HEAD_SIZE_DIM)
    value_head_rows = value_block.reshape(-1, count_of_heads, HEAD_SIZE_DIM)
    scores = jnp.einsum("rkgd,nkd->kgrn", query_head_rows, key_head_rows, precision=highest) * (
        1.0 / math.sqrt(HEAD_SIZE_DIM)
    )
    newest = jnp.maximum(running_max, jnp.max(scores, axis=-1))
    weights = jnp.exp(scores - newest[..., None])
    running_sum = jnp.sum(weights, axis=-1)
    weighted = jnp.einsum("kgrn,nkd->kgrd", weights, value_head_rows, precision=highest)
    return (newest, running_sum, weighted)


def finish(state_now):
    running_max, running_sum, weighted = state_now
    attention_output = weighted / running_sum[..., None]
    count_of_heads, queries_per_group, count_of_rows, head_size = attention_output.shape
    return attention_output.transpose(2, 0, 1, 3).reshape(
        count_of_rows, count_of_heads * queries_per_group * head_size
    )


def gather_kernel(axis, ring, n, with_sib, x_ref, out_ref, local_sem, send_sems, recv_sems):
    mesh_id = pl.DeviceIdType.MESH
    names = ("depth", "rz", "rc", "col")
    me = {a: lax.axis_index(a) for a in names}
    pos = me[axis]

    def device(**moved):
        return tuple(moved.get(a, me[a]) for a in names)

    right = device(**{axis: lax.rem(pos + 1, ring)})
    left = device(**{axis: lax.rem(pos + ring - 1, ring)})
    sib = device(rc=1 - me["rc"])
    peers = (left, right, sib) if with_sib else (left, right)

    barrier = pltpu.get_barrier_semaphore()
    for peer in peers:
        pl.semaphore_signal(barrier, inc=1, device_id=peer, device_id_type=mesh_id)
    pl.semaphore_wait(barrier, len(peers))

    def rows(at, lo=0, size=n):
        slot = at * 2 + me["rc"] if with_sib else at
        return pl.ds(pl.multiple_of(slot * n + lo, 8), size)

    def remote(src, dst_rows, peer, idx):
        cp = pltpu.make_async_remote_copy(
            src_ref=src,
            dst_ref=out_ref.at[dst_rows],
            send_sem=send_sems.at[idx],
            recv_sem=recv_sems.at[idx],
            device_id=peer,
            device_id_type=mesh_id,
        )
        cp.start()
        return cp

    def to_sib(at, idx):
        if with_sib:
            sib_copies.append(remote(out_ref.at[rows(at)], rows(at), sib, idx))

    local = pltpu.make_async_copy(x_ref, out_ref.at[rows(pos)], local_sem)
    local.start()
    sib_copies = [remote(x_ref, rows(pos), sib, ring)] if with_sib else []
    half = ring // 2
    for s in range(1, half + 1):
        origin_r = lax.rem(pos - (s - 1) + ring, ring)
        origin_l = lax.rem(pos + (s - 1), ring)
        src_r = x_ref if s == 1 else out_ref.at[rows(origin_r)]
        src_l = x_ref if s == 1 else out_ref.at[rows(origin_l)]
        if s < half:
            cr = remote(src_r, rows(origin_r), right, 2 * (s - 1))
            cl = remote(src_l, rows(origin_l), left, 2 * (s - 1) + 1)
            cr.wait()
            cl.wait()
            to_sib(lax.rem(pos - s + ring, ring), ring + 2 * s - 1)
            to_sib(lax.rem(pos + s, ring), ring + 2 * s)
        else:
            h = n // 2
            cr = remote(src_r.at[pl.ds(0, h)], rows(origin_r, 0, h), right, 2 * (s - 1))
            cl = remote(src_l.at[pl.ds(h, h)], rows(origin_l, h, h), left, 2 * (s - 1) + 1)
            cr.wait()
            cl.wait()
            to_sib(lax.rem(pos + half, ring), ring + 2 * s - 1)
    local.wait()
    for cp in sib_copies:
        cp.wait()


def ring_gather(block, axis, ring, with_sib, collective_id):
    n, w = block.shape
    copies = 2 if with_sib else 1
    return pl.pallas_call(
        functools.partial(gather_kernel, axis, ring, n, with_sib),
        out_shape=jax.ShapeDtypeStruct((copies * ring * n, w), block.dtype),
        in_specs=[pl.BlockSpec(memory_space=pl.ANY)],
        out_specs=pl.BlockSpec(memory_space=pl.ANY),
        scratch_shapes=[
            pltpu.SemaphoreType.DMA(()),
            pltpu.SemaphoreType.DMA((2 * ring,)),
            pltpu.SemaphoreType.DMA((2 * ring,)),
        ],
        compiler_params=pltpu.CompilerParams(collective_id=collective_id, has_side_effects=True),
    )(block)


def scatter_kernel(axis, ring, m, with_sib, parts, x_ref, out_ref, sbuf, rbuf, sibbuf, send_sems, recv_sems, sib_sems):
    mesh_id = pl.DeviceIdType.MESH
    names = ("depth", "rz", "rc", "col")
    me = {a: lax.axis_index(a) for a in names}
    pos = me[axis]
    h = m // 2
    q = h // parts

    def device(**moved):
        return tuple(moved.get(a, me[a]) for a in names)

    right = device(**{axis: lax.rem(pos + 1, ring)})
    left = device(**{axis: lax.rem(pos + ring - 1, ring)})
    sib = device(rc=1 - me["rc"])
    peers = (left, right, sib) if with_sib else (left, right)

    barrier = pltpu.get_barrier_semaphore()
    for peer in peers:
        pl.semaphore_signal(barrier, inc=1, device_id=peer, device_id_type=mesh_id)
    pl.semaphore_wait(barrier, len(peers))

    def rows_of(at, half, part, owner):
        slot = at * 2 + owner if with_sib else at
        return pl.ds(pl.multiple_of(slot * m + half * h + part * q, 8), q)

    def sib_rows(at, half, part):
        return pl.ds(pl.multiple_of(at * m + half * h + part * q, 8), q)

    def remote(src, dst, peer, sems, idx):
        cp = pltpu.make_async_remote_copy(
            src_ref=src,
            dst_ref=dst,
            send_sem=sems[0].at[idx],
            recv_sem=sems[1].at[idx],
            device_id=peer,
            device_id_type=mesh_id,
        )
        cp.start()
        return cp

    def need(s, half):
        sign = -1 if half == 0 else 1
        return lax.rem(pos + sign * (s % ring) + ring * ring, ring)

    sib_copies = {}
    if with_sib:
        order = [(s, half) for s in range(1, ring + 1) for half in (0, 1)]
        for idx, (s, half) in enumerate(order):
            at = need(s, half)
            sib_copies[(s, half)] = remote(
                x_ref.at[pl.ds(pl.multiple_of((at * 2 + 1 - me["rc"]) * m + half * h, 8), h)],
                sibbuf.at[pl.ds(pl.multiple_of(at * m + half * h, 8), h)],
                sib,
                (sib_sems[0], sib_sems[1]),
                idx,
            )

    def contribution(s, half, part):
        at = need(s, half)
        own = x_ref[rows_of(at, half, part, me["rc"])]
        if with_sib:
            if part == 0:
                sib_copies[(s, half)].wait()
            own = own + sibbuf[sib_rows(at, half, part)]
        return own

    ring_copies = {}
    for s in range(1, ring):
        for part in range(parts):
            for half in (0, 1):
                value = contribution(s, half, part)
                if s > 1:
                    ring_copies[(s - 1, half, part)].wait()
                    value = value + rbuf[half, s - 2, part]
                sbuf[half, s - 1, part] = value
                ring_copies[(s, half, part)] = remote(
                    sbuf.at[half, s - 1, part],
                    rbuf.at[half, s - 1, part],
                    right if half == 0 else left,
                    (send_sems, recv_sems),
                    (half * (ring - 1) + s - 1) * parts + part,
                )
    for part in range(parts):
        for half in (0, 1):
            value = contribution(ring, half, part)
            ring_copies[(ring - 1, half, part)].wait()
            out_ref[pl.ds(half * h + part * q, q)] = value + rbuf[half, ring - 2, part]


def ring_scatter(x, axis, ring, with_sib, parts, collective_id):
    total, w = x.shape
    copies = 2 if with_sib else 1
    m = total // (copies * ring)
    sib_rows = ring * m if with_sib else 8
    return pl.pallas_call(
        functools.partial(scatter_kernel, axis, ring, m, with_sib, parts),
        out_shape=jax.ShapeDtypeStruct((m, w), x.dtype),
        in_specs=[pl.BlockSpec(memory_space=pltpu.VMEM)],
        out_specs=pl.BlockSpec(memory_space=pltpu.VMEM),
        scratch_shapes=[
            pltpu.VMEM((2, ring - 1, parts, m // 2 // parts, w), x.dtype),
            pltpu.VMEM((2, ring - 1, parts, m // 2 // parts, w), x.dtype),
            pltpu.VMEM((sib_rows, w), x.dtype),
            pltpu.SemaphoreType.DMA((2 * ring * parts,)),
            pltpu.SemaphoreType.DMA((2 * ring * parts,)),
            (pltpu.SemaphoreType.DMA((2 * ring,)), pltpu.SemaphoreType.DMA((2 * ring,))),
        ],
        compiler_params=pltpu.CompilerParams(
            collective_id=collective_id, has_side_effects=True, vmem_limit_bytes=60 * 1024 * 1024
        ),
    )(x)


def mix_kernel(ring, cols, n, o_ref, wo_ref, out_ref, ogath, part, recv, send_sems, recv_sems, y_send, y_recv):
    mesh_id = pl.DeviceIdType.MESH
    names = ("depth", "rz", "rc", "col")
    me = {a: lax.axis_index(a) for a in names}
    z, c, y = me["rz"], me["rc"], me["col"]
    per_col = 2 * ring // cols

    def device(**moved):
        return tuple(moved.get(a, me[a]) for a in names)

    right = device(rz=lax.rem(z + 1, ring))
    left = device(rz=lax.rem(z + ring - 1, ring))
    sib = device(rc=1 - c)
    peers = [left, right, sib] + [device(col=lax.rem(y + d, cols)) for d in range(1, cols)]

    barrier = pltpu.get_barrier_semaphore()
    for peer in peers:
        pl.semaphore_signal(barrier, inc=1, device_id=peer, device_id_type=mesh_id)
    pl.semaphore_wait(barrier, len(peers))

    def remote(src, dst, peer, send, recv_sem):
        cp = pltpu.make_async_remote_copy(
            src_ref=src, dst_ref=dst, send_sem=send, recv_sem=recv_sem, device_id=peer, device_id_type=mesh_id
        )
        cp.start()
        return cp

    piece = n // cols

    def project(block, k):
        part[k] = jnp.dot(block, wo_ref[...], preferred_element_type=jnp.float32, precision=lax.Precision.HIGH)
        for d in range(1, cols):
            dest = lax.rem(y + d, cols)
            remote(
                part.at[k, pl.ds(pl.multiple_of(dest * piece, 8), piece)],
                recv.at[cols - d, k],
                device(col=dest),
                y_send.at[k * cols + d],
                y_recv.at[(cols - d) * 2 * ring + k],
            )

    def slot(zz, cc):
        return zz * 2 + cc

    def z_copy(src, dst_slot, lo, size, peer, idx):
        return remote(src, ogath.at[dst_slot, pl.ds(lo, size)], peer, send_sems.at[idx], recv_sems.at[idx])

    pending_sib = [(z_copy(o_ref, slot(z, c), 0, n, sib, ring), z)]
    to_project = [slot(z, c)]
    half = ring // 2
    for s in range(1, half + 1):
        origin_r = lax.rem(z - (s - 1) + ring, ring)
        origin_l = lax.rem(z + (s - 1), ring)
        src_r = o_ref if s == 1 else ogath.at[slot(origin_r, c)]
        src_l = o_ref if s == 1 else ogath.at[slot(origin_l, c)]
        if s < half:
            cr = z_copy(src_r, slot(origin_r, c), 0, n, right, 2 * (s - 1))
            cl = z_copy(src_l, slot(origin_l, c), 0, n, left, 2 * (s - 1) + 1)
        else:
            h = n // 2
            cr = z_copy(src_r.at[pl.ds(0, h)], slot(origin_r, c), 0, h, right, 2 * (s - 1))
            cl = z_copy(src_l.at[pl.ds(h, h)], slot(origin_l, c), h, h, left, 2 * (s - 1) + 1)
        for k in to_project:
            project(o_ref[...] if s == 1 else ogath[k], k)
        to_project = []
        for cp, at in pending_sib:
            cp.wait()
            project(ogath[slot(at, 1 - c)], slot(at, 1 - c))
        pending_sib = []
        cr.wait()
        cl.wait()
        if s < half:
            arrived = [(lax.rem(z - s + ring, ring), ring + 2 * s - 1), (lax.rem(z + s, ring), ring + 2 * s)]
        else:
            arrived = [(lax.rem(z + half, ring), ring + 2 * s - 1)]
        for at, idx in arrived:
            pending_sib.append((z_copy(ogath.at[slot(at, c)], slot(at, c), 0, n, sib, idx), at))
            to_project.append(slot(at, c))
    for k in to_project:
        project(ogath[k], k)
    for cp, at in pending_sib:
        cp.wait()
        project(ogath[slot(at, 1 - c)], slot(at, 1 - c))
    for k in range(2 * ring):
        total = part[k, pl.ds(pl.multiple_of(y * piece, 8), piece)]
        for d in range(1, cols):
            pltpu.make_async_remote_copy(
                src_ref=part.at[k, pl.ds(0, piece)],
                dst_ref=recv.at[d, k],
                send_sem=y_send.at[0],
                recv_sem=y_recv.at[d * 2 * ring + k],
                device_id=device(col=lax.rem(y + d, cols)),
                device_id_type=mesh_id,
            ).wait_recv()
            total = total + recv[d, k]
        m = piece // 2
        for e in (0, 1):
            out_ref[pl.ds(e * 2 * ring * m + k * m, m)] = total[e * m : (e + 1) * m]
    for k in range(2 * ring):
        for d in range(1, cols):
            pltpu.make_async_remote_copy(
                src_ref=part.at[k, pl.ds(0, piece)],
                dst_ref=recv.at[0, 0],
                send_sem=y_send.at[k * cols + d],
                recv_sem=y_recv.at[0],
                device_id=device(col=lax.rem(y + d, cols)),
                device_id_type=mesh_id,
            ).wait_send()


def gather_mix(o, w_out, ring, cols, collective_id):
    n, width = o.shape
    out_w = w_out.shape[1]
    per_col = 2 * ring // cols
    return pl.pallas_call(
        functools.partial(mix_kernel, ring, cols, n),
        out_shape=jax.ShapeDtypeStruct((per_col * n, out_w), jnp.float32),
        in_specs=[pl.BlockSpec(memory_space=pltpu.VMEM), pl.BlockSpec(memory_space=pltpu.VMEM)],
        out_specs=pl.BlockSpec(memory_space=pltpu.VMEM),
        scratch_shapes=[
            pltpu.VMEM((2 * ring, n, width), jnp.float32),
            pltpu.VMEM((2 * ring, n, out_w), jnp.float32),
            pltpu.VMEM((cols, 2 * ring, n // cols, out_w), jnp.float32),
            pltpu.SemaphoreType.DMA((2 * ring,)),
            pltpu.SemaphoreType.DMA((2 * ring,)),
            pltpu.SemaphoreType.DMA((2 * ring * cols,)),
            pltpu.SemaphoreType.DMA((2 * ring * cols,)),
        ],
        compiler_params=pltpu.CompilerParams(
            collective_id=collective_id, has_side_effects=True, vmem_limit_bytes=60 * 1024 * 1024
        ),
    )(o, w_out)


def front_kernel(
    ring, cols, tok_ref, wq_ref, wk_ref, wv_ref, out_ref, kv_out, tg, partial, sibbuf, sbuf, rbuf, kvbuf,
    y_sems, z_sems, sib_sems, kv_sems,
):
    mesh_id = pl.DeviceIdType.MESH
    names = ("depth", "rz", "rc", "col")
    me = {a: lax.axis_index(a) for a in names}
    z, c, y = me["rz"], me["rc"], me["col"]
    rows = tok_ref.shape[0]
    m = rows // 2 // (2 * ring)
    h = m // 2

    def device(**moved):
        return tuple(moved.get(a, me[a]) for a in names)

    right = device(rz=lax.rem(z + 1, ring))
    left = device(rz=lax.rem(z + ring - 1, ring))
    sib = device(rc=1 - c)
    y_right = device(col=lax.rem(y + 1, cols))
    y_left = device(col=lax.rem(y + cols - 1, cols))
    peers = [left, right, sib, y_left, y_right]

    barrier = pltpu.get_barrier_semaphore()
    for peer in peers:
        pl.semaphore_signal(barrier, inc=1, device_id=peer, device_id_type=mesh_id)
    pl.semaphore_wait(barrier, len(peers))

    def remote(src, dst, peer, sems, idx):
        cp = pltpu.make_async_remote_copy(
            src_ref=src, dst_ref=dst, send_sem=sems[0].at[idx], recv_sem=sems[1].at[idx],
            device_id=peer, device_id_type=mesh_id,
        )
        cp.start()
        return cp

    def need(s, half):
        sign = -1 if half == 0 else 1
        return lax.rem(z + sign * (s % ring) + ring * ring, ring)

    def round_steps(r, chunk):
        x = partial.at[r]
        base = r * 2 * ring
        sib_copies = {}
        for idx, (s, half) in enumerate((s, half) for s in range(1, ring + 1) for half in (0, 1)):
            at = need(s, half)
            sib_copies[(s, half)] = remote(
                x.at[pl.ds(pl.multiple_of((at * 2 + 1 - c) * m + half * h, 8), h)],
                sibbuf.at[r, pl.ds(pl.multiple_of(at * m + half * h, 8), h)],
                sib, sib_sems, base + idx,
            )
        yield

        def contribution(s, half):
            at = need(s, half)
            sib_copies[(s, half)].wait()
            own = x[pl.ds(pl.multiple_of((at * 2 + c) * m + half * h, 8), h)]
            return own + sibbuf[r, pl.ds(pl.multiple_of(at * m + half * h, 8), h)]

        ring_copies = {}
        for s in range(1, ring):
            for half in (0, 1):
                value = contribution(s, half)
                if s > 1:
                    ring_copies[(s - 1, half)].wait()
                    value = value + rbuf[r, half, s - 2]
                sbuf[r, half, s - 1] = value
                ring_copies[(s, half)] = remote(
                    sbuf.at[r, half, s - 1], rbuf.at[r, half, s - 1],
                    right if half == 0 else left, z_sems, base + half * (ring - 1) + s - 1,
                )
            yield
        for half in (0, 1):
            value = contribution(ring, half)
            ring_copies[(ring - 1, half)].wait()
            value = value + rbuf[r, half, ring - 2]
            out_ref[pl.ds(pl.multiple_of(chunk * m + half * h, 8), h)] = value
            kvbuf[r, z * 2 + c, pl.ds(half * h, h)] = value[:, qw:]
        yield

        def kv_copy(src, at, lo, size, peer, idx):
            return remote(src, kvbuf.at[r, at * 2 + c, pl.ds(lo, size)], peer, kv_sems, base + idx)

        kv_sib = [
            remote(kvbuf.at[r, z * 2 + c], kvbuf.at[r, z * 2 + c], sib, kv_sems, base + ring)
        ]
        half_ring = ring // 2
        for s in range(1, half_ring + 1):
            origin_r = lax.rem(z - (s - 1) + ring, ring)
            origin_l = lax.rem(z + (s - 1), ring)
            src_r = kvbuf.at[r, origin_r * 2 + c]
            src_l = kvbuf.at[r, origin_l * 2 + c]
            if s < half_ring:
                cr = kv_copy(src_r, origin_r, 0, m, right, 2 * (s - 1))
                cl = kv_copy(src_l, origin_l, 0, m, left, 2 * (s - 1) + 1)
            else:
                cr = kv_copy(src_r.at[pl.ds(0, h)], origin_r, 0, h, right, 2 * (s - 1))
                cl = kv_copy(src_l.at[pl.ds(h, h)], origin_l, h, h, left, 2 * (s - 1) + 1)
            yield
            cr.wait()
            cl.wait()
            if s < half_ring:
                got = [(lax.rem(z - s + ring, ring), ring + 2 * s - 1), (lax.rem(z + s, ring), ring + 2 * s)]
            else:
                got = [(lax.rem(z + half_ring, ring), ring + 2 * s - 1)]
            for at, idx in got:
                kv_sib.append(
                    remote(kvbuf.at[r, at * 2 + c], kvbuf.at[r, at * 2 + c], sib, kv_sems, base + idx)
                )
        yield
        for cp in kv_sib:
            cp.wait()
        yield

    qw = wq_ref.shape[1]
    kw = wk_ref.shape[1]

    def project(r, src):
        block = src[...]
        for lo, w_ref in ((0, wq_ref), (qw, wk_ref), (qw + kw, wv_ref)):
            partial[r, :, pl.ds(lo, w_ref.shape[1])] = jnp.dot(
                block, w_ref[...], preferred_element_type=jnp.float32, precision=lax.Precision.HIGH
            )

    hr = rows // 2
    chunks = (y, lax.rem(y + cols - 1, cols), lax.rem(y + 1, cols), lax.rem(y + 2, cols))

    def sub(ref, e):
        return ref.at[pl.ds(e * hr, hr)]

    y1 = {}
    for e in (0, 1):
        y1[("r", e)] = remote(sub(tok_ref, e), sub(tg.at[1], e), y_right, y_sems, 2 * e)
        y1[("l", e)] = remote(sub(tok_ref, e), sub(tg.at[2], e), y_left, y_sems, 2 * e + 1)
    rounds = []

    def begin(slot_id, e, src):
        r = 2 * slot_id + e
        project(r, src)
        g = round_steps(r, 2 * chunks[slot_id] + e)
        next(g)
        rounds.append(g)

    def advance(times):
        for _ in range(times):
            for g in list(rounds):
                next(g, None)

    begin(0, 0, sub(tok_ref, 0))
    begin(0, 1, sub(tok_ref, 1))
    advance(ring // 2)
    y1[("r", 0)].wait()
    y2r = remote(sub(tg.at[1], 0), sub(tg.at[3], 0), y_right, y_sems, 4)
    y1[("l", 0)].wait()
    begin(1, 0, sub(tg.at[1], 0))
    begin(2, 0, sub(tg.at[2], 0))
    advance(3)
    y1[("r", 1)].wait()
    y1[("l", 1)].wait()
    y2l = remote(sub(tg.at[2], 1), sub(tg.at[3], 1), y_left, y_sems, 5)
    begin(1, 1, sub(tg.at[1], 1))
    begin(2, 1, sub(tg.at[2], 1))
    advance(2)
    y2r.wait()
    begin(3, 0, sub(tg.at[3], 0))
    y2l.wait()
    begin(3, 1, sub(tg.at[3], 1))
    live = list(rounds)
    while live:
        live = [g for g in live if next(g, "done") != "done"]
    kv_out[...] = kvbuf[...]


def front(tokens, w_query, w_key, w_value, ring, cols, collective_id):
    rows, width = tokens.shape
    out_w = w_query.shape[1] + w_key.shape[1] + w_value.shape[1]
    kv_w = w_key.shape[1] + w_value.shape[1]
    n_rounds = 2 * cols
    hr = rows // 2
    m = hr // (2 * ring)
    return pl.pallas_call(
        functools.partial(front_kernel, ring, cols),
        out_shape=(
            jax.ShapeDtypeStruct((n_rounds * m, out_w), jnp.float32),
            jax.ShapeDtypeStruct((n_rounds, 2 * ring, m, kv_w), jnp.float32),
        ),
        in_specs=[pl.BlockSpec(memory_space=pltpu.VMEM)] * 4,
        out_specs=(pl.BlockSpec(memory_space=pltpu.VMEM), pl.BlockSpec(memory_space=pltpu.VMEM)),
        scratch_shapes=[
            pltpu.VMEM((cols, rows, width), jnp.float32),
            pltpu.VMEM((n_rounds, hr, out_w), jnp.float32),
            pltpu.VMEM((n_rounds, ring * m, out_w), jnp.float32),
            pltpu.VMEM((n_rounds, 2, ring - 1, m // 2, out_w), jnp.float32),
            pltpu.VMEM((n_rounds, 2, ring - 1, m // 2, out_w), jnp.float32),
            pltpu.VMEM((n_rounds, 2 * ring, m, kv_w), jnp.float32),
            (pltpu.SemaphoreType.DMA((6,)), pltpu.SemaphoreType.DMA((6,))),
            (pltpu.SemaphoreType.DMA((n_rounds * 2 * ring,)), pltpu.SemaphoreType.DMA((n_rounds * 2 * ring,))),
            (pltpu.SemaphoreType.DMA((n_rounds * 2 * ring,)), pltpu.SemaphoreType.DMA((n_rounds * 2 * ring,))),
            (pltpu.SemaphoreType.DMA((n_rounds * 2 * ring,)), pltpu.SemaphoreType.DMA((n_rounds * 2 * ring,))),
        ],
        compiler_params=pltpu.CompilerParams(
            collective_id=collective_id, has_side_effects=True, vmem_limit_bytes=60 * 1024 * 1024
        ),
    )(tokens, w_query, w_key, w_value)


def on_device(ring, cols, tokens, w_query, w_key, w_value, w_out):
    highest = lax.Precision.HIGH
    q_width = w_query.shape[1]
    kv_width = w_key.shape[1]
    joined, kv_sets = front(tokens, w_query, w_key, w_value, ring, cols, 3)
    query_rows = joined[:, :q_width]
    all_kv = kv_sets.reshape(-1, kv_sets.shape[-1])
    state_end = fold_keys(
        query_rows,
        start_state(query_rows, kv_width),
        (all_kv[:, :kv_width], all_kv[:, kv_width:]),
    )
    return gather_mix(finish(state_end), w_out, ring, cols, 5)


def solution(mesh):
    depth, row, col = (mesh.shape[a] for a in ("depth", "row", "col"))
    split = jax.sharding.Mesh(
        np.asarray(mesh.devices).reshape(depth, row // 2, 2, col), ("depth", "rz", "rc", "col")
    )
    rows = ("rz", "rc")
    placed = (
        P(("depth", "col"), rows),
        P(rows, "col"),
        P(rows, "col"),
        P(rows, "col"),
        P("col", rows),
    )
    return jax.shard_map(
        functools.partial(on_device, row // 2, col),
        mesh=split,
        in_specs=placed,
        out_specs=P(("depth", "col"), rows),
        check_vma=False,
    )
```

```python
import functools
import math

import jax
import numpy as np
import jax.numpy as jnp
from jax import lax
from jax.experimental import pallas as pl
from jax.experimental.pallas import tpu as pltpu
from jax.sharding import PartitionSpec as P

QUERY_HEADS = 32
KEY_VALUE_HEADS = 4
HEAD_SIZE_DIM = 128


def start_state(query_rows, kv_width):
    count_of_heads = kv_width // HEAD_SIZE_DIM
    queries_per_group = QUERY_HEADS // KEY_VALUE_HEADS
    count_of_rows = query_rows.shape[0]
    running_max = jnp.full((count_of_heads, queries_per_group, count_of_rows), -1e30, jnp.float32)
    running_sum = jnp.zeros((count_of_heads, queries_per_group, count_of_rows), jnp.float32)
    weighted = jnp.zeros(
        (count_of_heads, queries_per_group, count_of_rows, HEAD_SIZE_DIM), jnp.float32
    )
    return (running_max, running_sum, weighted)


def fold_keys(query_rows, state_now, block_pair):
    highest = lax.Precision.HIGH
    running_max, running_sum, weighted = state_now
    key_block, value_block = block_pair
    count_of_heads = key_block.shape[1] // HEAD_SIZE_DIM
    count_of_rows = query_rows.shape[0]
    query_head_rows = query_rows.reshape(
        count_of_rows, count_of_heads, QUERY_HEADS // KEY_VALUE_HEADS, HEAD_SIZE_DIM
    )
    key_head_rows = key_block.reshape(-1, count_of_heads, HEAD_SIZE_DIM)
    value_head_rows = value_block.reshape(-1, count_of_heads, HEAD_SIZE_DIM)
    scores = jnp.einsum("rkgd,nkd->kgrn", query_head_rows, key_head_rows, precision=highest) * (
        1.0 / math.sqrt(HEAD_SIZE_DIM)
    )
    newest = jnp.maximum(running_max, jnp.max(scores, axis=-1))
    weights = jnp.exp(scores - newest[..., None])
    running_sum = jnp.sum(weights, axis=-1)
    weighted = jnp.einsum("kgrn,nkd->kgrd", weights, value_head_rows, precision=highest)
    return (newest, running_sum, weighted)


def finish(state_now):
    running_max, running_sum, weighted = state_now
    attention_output = weighted / running_sum[..., None]
    count_of_heads, queries_per_group, count_of_rows, head_size = attention_output.shape
    return attention_output.transpose(2, 0, 1, 3).reshape(
        count_of_rows, count_of_heads * queries_per_group * head_size
    )


def gather_kernel(axis, ring, n, with_sib, x_ref, out_ref, local_sem, send_sems, recv_sems):
    mesh_id = pl.DeviceIdType.MESH
    names = ("depth", "rz", "rc", "col")
    me = {a: lax.axis_index(a) for a in names}
    pos = me[axis]

    def device(**moved):
        return tuple(moved.get(a, me[a]) for a in names)

    right = device(**{axis: lax.rem(pos + 1, ring)})
    left = device(**{axis: lax.rem(pos + ring - 1, ring)})
    sib = device(rc=1 - me["rc"])
    peers = (left, right, sib) if with_sib else (left, right)

    barrier = pltpu.get_barrier_semaphore()
    for peer in peers:
        pl.semaphore_signal(barrier, inc=1, device_id=peer, device_id_type=mesh_id)
    pl.semaphore_wait(barrier, len(peers))

    def rows(at, lo=0, size=n):
        slot = at * 2 + me["rc"] if with_sib else at
        return pl.ds(pl.multiple_of(slot * n + lo, 8), size)

    def remote(src, dst_rows, peer, idx):
        cp = pltpu.make_async_remote_copy(
            src_ref=src,
            dst_ref=out_ref.at[dst_rows],
            send_sem=send_sems.at[idx],
            recv_sem=recv_sems.at[idx],
            device_id=peer,
            device_id_type=mesh_id,
        )
        cp.start()
        return cp

    def to_sib(at, idx):
        if with_sib:
            sib_copies.append(remote(out_ref.at[rows(at)], rows(at), sib, idx))

    local = pltpu.make_async_copy(x_ref, out_ref.at[rows(pos)], local_sem)
    local.start()
    sib_copies = [remote(x_ref, rows(pos), sib, ring)] if with_sib else []
    half = ring // 2
    for s in range(1, half + 1):
        origin_r = lax.rem(pos - (s - 1) + ring, ring)
        origin_l = lax.rem(pos + (s - 1), ring)
        src_r = x_ref if s == 1 else out_ref.at[rows(origin_r)]
        src_l = x_ref if s == 1 else out_ref.at[rows(origin_l)]
        if s < half:
            cr = remote(src_r, rows(origin_r), right, 2 * (s - 1))
            cl = remote(src_l, rows(origin_l), left, 2 * (s - 1) + 1)
            cr.wait()
            cl.wait()
            to_sib(lax.rem(pos - s + ring, ring), ring + 2 * s - 1)
            to_sib(lax.rem(pos + s, ring), ring + 2 * s)
        else:
            h = n // 2
            cr = remote(src_r.at[pl.ds(0, h)], rows(origin_r, 0, h), right, 2 * (s - 1))
            cl = remote(src_l.at[pl.ds(h, h)], rows(origin_l, h, h), left, 2 * (s - 1) + 1)
            cr.wait()
            cl.wait()
            to_sib(lax.rem(pos + half, ring), ring + 2 * s - 1)
    local.wait()
    for cp in sib_copies:
        cp.wait()


def ring_gather(block, axis, ring, with_sib, collective_id):
    n, w = block.shape
    copies = 2 if with_sib else 1
    return pl.pallas_call(
        functools.partial(gather_kernel, axis, ring, n, with_sib),
        out_shape=jax.ShapeDtypeStruct((copies * ring * n, w), block.dtype),
        in_specs=[pl.BlockSpec(memory_space=pl.ANY)],
        out_specs=pl.BlockSpec(memory_space=pl.ANY),
        scratch_shapes=[
            pltpu.SemaphoreType.DMA(()),
            pltpu.SemaphoreType.DMA((2 * ring,)),
            pltpu.SemaphoreType.DMA((2 * ring,)),
        ],
        compiler_params=pltpu.CompilerParams(collective_id=collective_id, has_side_effects=True),
    )(block)


def scatter_kernel(axis, ring, m, with_sib, parts, x_ref, out_ref, sbuf, rbuf, sibbuf, send_sems, recv_sems, sib_sems):
    mesh_id = pl.DeviceIdType.MESH
    names = ("depth", "rz", "rc", "col")
    me = {a: lax.axis_index(a) for a in names}
    pos = me[axis]
    h = m // 2
    q = h // parts

    def device(**moved):
        return tuple(moved.get(a, me[a]) for a in names)

    right = device(**{axis: lax.rem(pos + 1, ring)})
    left = device(**{axis: lax.rem(pos + ring - 1, ring)})
    sib = device(rc=1 - me["rc"])
    peers = (left, right, sib) if with_sib else (left, right)

    barrier = pltpu.get_barrier_semaphore()
    for peer in peers:
        pl.semaphore_signal(barrier, inc=1, device_id=peer, device_id_type=mesh_id)
    pl.semaphore_wait(barrier, len(peers))

    def rows_of(at, half, part, owner):
        slot = at * 2 + owner if with_sib else at
        return pl.ds(pl.multiple_of(slot * m + half * h + part * q, 8), q)

    def sib_rows(at, half, part):
        return pl.ds(pl.multiple_of(at * m + half * h + part * q, 8), q)

    def remote(src, dst, peer, sems, idx):
        cp = pltpu.make_async_remote_copy(
            src_ref=src,
            dst_ref=dst,
            send_sem=sems[0].at[idx],
            recv_sem=sems[1].at[idx],
            device_id=peer,
            device_id_type=mesh_id,
        )
        cp.start()
        return cp

    def need(s, half):
        sign = -1 if half == 0 else 1
        return lax.rem(pos + sign * (s % ring) + ring * ring, ring)

    sib_copies = {}
    if with_sib:
        order = [(s, half) for s in range(1, ring + 1) for half in (0, 1)]
        for idx, (s, half) in enumerate(order):
            at = need(s, half)
            sib_copies[(s, half)] = remote(
                x_ref.at[pl.ds(pl.multiple_of((at * 2 + 1 - me["rc"]) * m + half * h, 8), h)],
                sibbuf.at[pl.ds(pl.multiple_of(at * m + half * h, 8), h)],
                sib,
                (sib_sems[0], sib_sems[1]),
                idx,
            )

    def contribution(s, half, part):
        at = need(s, half)
        own = x_ref[rows_of(at, half, part, me["rc"])]
        if with_sib:
            if part == 0:
                sib_copies[(s, half)].wait()
            own = own + sibbuf[sib_rows(at, half, part)]
        return own

    ring_copies = {}
    for s in range(1, ring):
        for part in range(parts):
            for half in (0, 1):
                value = contribution(s, half, part)
                if s > 1:
                    ring_copies[(s - 1, half, part)].wait()
                    value = value + rbuf[half, s - 2, part]
                sbuf[half, s - 1, part] = value
                ring_copies[(s, half, part)] = remote(
                    sbuf.at[half, s - 1, part],
                    rbuf.at[half, s - 1, part],
                    right if half == 0 else left,
                    (send_sems, recv_sems),
                    (half * (ring - 1) + s - 1) * parts + part,
                )
    for part in range(parts):
        for half in (0, 1):
            value = contribution(ring, half, part)
            ring_copies[(ring - 1, half, part)].wait()
            out_ref[pl.ds(half * h + part * q, q)] = value + rbuf[half, ring - 2, part]


def ring_scatter(x, axis, ring, with_sib, parts, collective_id):
    total, w = x.shape
    copies = 2 if with_sib else 1
    m = total // (copies * ring)
    sib_rows = ring * m if with_sib else 8
    return pl.pallas_call(
        functools.partial(scatter_kernel, axis, ring, m, with_sib, parts),
        out_shape=jax.ShapeDtypeStruct((m, w), x.dtype),
        in_specs=[pl.BlockSpec(memory_space=pltpu.VMEM)],
        out_specs=pl.BlockSpec(memory_space=pltpu.VMEM),
        scratch_shapes=[
            pltpu.VMEM((2, ring - 1, parts, m // 2 // parts, w), x.dtype),
            pltpu.VMEM((2, ring - 1, parts, m // 2 // parts, w), x.dtype),
            pltpu.VMEM((sib_rows, w), x.dtype),
            pltpu.SemaphoreType.DMA((2 * ring * parts,)),
            pltpu.SemaphoreType.DMA((2 * ring * parts,)),
            (pltpu.SemaphoreType.DMA((2 * ring,)), pltpu.SemaphoreType.DMA((2 * ring,))),
        ],
        compiler_params=pltpu.CompilerParams(
            collective_id=collective_id, has_side_effects=True, vmem_limit_bytes=60 * 1024 * 1024
        ),
    )(x)


def mix_kernel(ring, cols, n, o_ref, wo_ref, out_ref, ogath, part, recv, send_sems, recv_sems, y_send, y_recv):
    mesh_id = pl.DeviceIdType.MESH
    names = ("depth", "rz", "rc", "col")
    me = {a: lax.axis_index(a) for a in names}
    z, c, y = me["rz"], me["rc"], me["col"]
    per_col = 2 * ring // cols

    def device(**moved):
        return tuple(moved.get(a, me[a]) for a in names)

    right = device(rz=lax.rem(z + 1, ring))
    left = device(rz=lax.rem(z + ring - 1, ring))
    sib = device(rc=1 - c)
    peers = [left, right, sib] + [device(col=lax.rem(y + d, cols)) for d in range(1, cols)]

    barrier = pltpu.get_barrier_semaphore()
    for peer in peers:
        pl.semaphore_signal(barrier, inc=1, device_id=peer, device_id_type=mesh_id)
    pl.semaphore_wait(barrier, len(peers))

    def remote(src, dst, peer, send, recv_sem):
        cp = pltpu.make_async_remote_copy(
            src_ref=src, dst_ref=dst, send_sem=send, recv_sem=recv_sem, device_id=peer, device_id_type=mesh_id
        )
        cp.start()
        return cp

    piece = n // cols

    def project(block, k):
        part[k] = jnp.dot(block, wo_ref[...], preferred_element_type=jnp.float32, precision=lax.Precision.HIGH)
        for d in range(1, cols):
            dest = lax.rem(y + d, cols)
            remote(
                part.at[k, pl.ds(pl.multiple_of(dest * piece, 8), piece)],
                recv.at[cols - d, k],
                device(col=dest),
                y_send.at[k * cols + d],
                y_recv.at[(cols - d) * 2 * ring + k],
            )

    def slot(zz, cc):
        return zz * 2 + cc

    def z_copy(src, dst_slot, lo, size, peer, idx):
        return remote(src, ogath.at[dst_slot, pl.ds(lo, size)], peer, send_sems.at[idx], recv_sems.at[idx])

    pending_sib = [(z_copy(o_ref, slot(z, c), 0, n, sib, ring), z)]
    to_project = [slot(z, c)]
    half = ring // 2
    for s in range(1, half + 1):
        origin_r = lax.rem(z - (s - 1) + ring, ring)
        origin_l = lax.rem(z + (s - 1), ring)
        src_r = o_ref if s == 1 else ogath.at[slot(origin_r, c)]
        src_l = o_ref if s == 1 else ogath.at[slot(origin_l, c)]
        if s < half:
            cr = z_copy(src_r, slot(origin_r, c), 0, n, right, 2 * (s - 1))
            cl = z_copy(src_l, slot(origin_l, c), 0, n, left, 2 * (s - 1) + 1)
        else:
            h = n // 2
            cr = z_copy(src_r.at[pl.ds(0, h)], slot(origin_r, c), 0, h, right, 2 * (s - 1))
            cl = z_copy(src_l.at[pl.ds(h, h)], slot(origin_l, c), h, h, left, 2 * (s - 1) + 1)
        for k in to_project:
            project(o_ref[...] if s == 1 else ogath[k], k)
        to_project = []
        for cp, at in pending_sib:
            cp.wait()
            project(ogath[slot(at, 1 - c)], slot(at, 1 - c))
        pending_sib = []
        cr.wait()
        cl.wait()
        if s < half:
            arrived = [(lax.rem(z - s + ring, ring), ring + 2 * s - 1), (lax.rem(z + s, ring), ring + 2 * s)]
        else:
            arrived = [(lax.rem(z + half, ring), ring + 2 * s - 1)]
        for at, idx in arrived:
            pending_sib.append((z_copy(ogath.at[slot(at, c)], slot(at, c), 0, n, sib, idx), at))
            to_project.append(slot(at, c))
    for k in to_project:
        project(ogath[k], k)
    for cp, at in pending_sib:
        cp.wait()
        project(ogath[slot(at, 1 - c)], slot(at, 1 - c))
    for k in range(2 * ring):
        total = part[k, pl.ds(pl.multiple_of(y * piece, 8), piece)]
        for d in range(1, cols):
            pltpu.make_async_remote_copy(
                src_ref=part.at[k, pl.ds(0, piece)],
                dst_ref=recv.at[d, k],
                send_sem=y_send.at[0],
                recv_sem=y_recv.at[d * 2 * ring + k],
                device_id=device(col=lax.rem(y + d, cols)),
                device_id_type=mesh_id,
            ).wait_recv()
            total = total + recv[d, k]
        m = piece // 2
        for e in (0, 1):
            out_ref[pl.ds(e * 2 * ring * m + k * m, m)] = total[e * m : (e + 1) * m]
    for k in range(2 * ring):
        for d in range(1, cols):
            pltpu.make_async_remote_copy(
                src_ref=part.at[k, pl.ds(0, piece)],
                dst_ref=recv.at[0, 0],
                send_sem=y_send.at[k * cols + d],
                recv_sem=y_recv.at[0],
                device_id=device(col=lax.rem(y + d, cols)),
                device_id_type=mesh_id,
            ).wait_send()


def gather_mix(o, w_out, ring, cols, collective_id):
    n, width = o.shape
    out_w = w_out.shape[1]
    per_col = 2 * ring // cols
    return pl.pallas_call(
        functools.partial(mix_kernel, ring, cols, n),
        out_shape=jax.ShapeDtypeStruct((per_col * n, out_w), jnp.float32),
        in_specs=[pl.BlockSpec(memory_space=pltpu.VMEM), pl.BlockSpec(memory_space=pltpu.VMEM)],
        out_specs=pl.BlockSpec(memory_space=pltpu.VMEM),
        scratch_shapes=[
            pltpu.VMEM((2 * ring, n, width), jnp.float32),
            pltpu.VMEM((2 * ring, n, out_w), jnp.float32),
            pltpu.VMEM((cols, 2 * ring, n // cols, out_w), jnp.float32),
            pltpu.SemaphoreType.DMA((2 * ring,)),
            pltpu.SemaphoreType.DMA((2 * ring,)),
            pltpu.SemaphoreType.DMA((2 * ring * cols,)),
            pltpu.SemaphoreType.DMA((2 * ring * cols,)),
        ],
        compiler_params=pltpu.CompilerParams(
            collective_id=collective_id, has_side_effects=True, vmem_limit_bytes=60 * 1024 * 1024
        ),
    )(o, w_out)


def front_kernel(
    ring, cols, tok_ref, wq_ref, wk_ref, wv_ref, out_ref, kv_out, tg, partial, sibbuf, sbuf, rbuf, kvbuf,
    y_sems, z_sems, sib_sems, kv_sems,
):
    mesh_id = pl.DeviceIdType.MESH
    names = ("depth", "rz", "rc", "col")
    me = {a: lax.axis_index(a) for a in names}
    z, c, y = me["rz"], me["rc"], me["col"]
    rows = tok_ref.shape[0]
    m = rows // 2 // (2 * ring)
    h = m // 2

    def device(**moved):
        return tuple(moved.get(a, me[a]) for a in names)

    right = device(rz=lax.rem(z + 1, ring))
    left = device(rz=lax.rem(z + ring - 1, ring))
    sib = device(rc=1 - c)
    y_right = device(col=lax.rem(y + 1, cols))
    y_left = device(col=lax.rem(y + cols - 1, cols))
    peers = [left, right, sib, y_left, y_right]

    barrier = pltpu.get_barrier_semaphore()
    for peer in peers:
        pl.semaphore_signal(barrier, inc=1, device_id=peer, device_id_type=mesh_id)
    pl.semaphore_wait(barrier, len(peers))

    def remote(src, dst, peer, sems, idx):
        cp = pltpu.make_async_remote_copy(
            src_ref=src, dst_ref=dst, send_sem=sems[0].at[idx], recv_sem=sems[1].at[idx],
            device_id=peer, device_id_type=mesh_id,
        )
        cp.start()
        return cp

    def need(s, half):
        sign = -1 if half == 0 else 1
        return lax.rem(z + sign * (s % ring) + ring * ring, ring)

    def round_steps(r, chunk):
        x = partial.at[r]
        base = r * 2 * ring
        sib_copies = {}
        for idx, (s, half) in enumerate((s, half) for s in range(1, ring + 1) for half in (0, 1)):
            at = need(s, half)
            sib_copies[(s, half)] = remote(
                x.at[pl.ds(pl.multiple_of((at * 2 + 1 - c) * m + half * h, 8), h)],
                sibbuf.at[r, pl.ds(pl.multiple_of(at * m + half * h, 8), h)],
                sib, sib_sems, base + idx,
            )
        yield

        def contribution(s, half):
            at = need(s, half)
            sib_copies[(s, half)].wait()
            own = x[pl.ds(pl.multiple_of((at * 2 + c) * m + half * h, 8), h)]
            return own + sibbuf[r, pl.ds(pl.multiple_of(at * m + half * h, 8), h)]

        ring_copies = {}
        for s in range(1, ring):
            for half in (0, 1):
                value = contribution(s, half)
                if s > 1:
                    ring_copies[(s - 1, half)].wait()
                    value = value + rbuf[r, half, s - 2]
                sbuf[r, half, s - 1] = value
                ring_copies[(s, half)] = remote(
                    sbuf.at[r, half, s - 1], rbuf.at[r, half, s - 1],
                    right if half == 0 else left, z_sems, base + half * (ring - 1) + s - 1,
                )
            yield
        for half in (0, 1):
            value = contribution(ring, half)
            ring_copies[(ring - 1, half)].wait()
            value = value + rbuf[r, half, ring - 2]
            out_ref[pl.ds(pl.multiple_of(chunk * m + half * h, 8), h)] = value
            kvbuf[r, z * 2 + c, pl.ds(half * h, h)] = value[:, qw:]
        yield

        def kv_copy(src, at, lo, size, peer, idx):
            return remote(src, kvbuf.at[r, at * 2 + c, pl.ds(lo, size)], peer, kv_sems, base + idx)

        kv_sib = [
            remote(kvbuf.at[r, z * 2 + c], kvbuf.at[r, z * 2 + c], sib, kv_sems, base + ring)
        ]
        half_ring = ring // 2
        for s in range(1, half_ring + 1):
            origin_r = lax.rem(z - (s - 1) + ring, ring)
            origin_l = lax.rem(z + (s - 1), ring)
            src_r = kvbuf.at[r, origin_r * 2 + c]
            src_l = kvbuf.at[r, origin_l * 2 + c]
            if s < half_ring:
                cr = kv_copy(src_r, origin_r, 0, m, right, 2 * (s - 1))
                cl = kv_copy(src_l, origin_l, 0, m, left, 2 * (s - 1) + 1)
            else:
                cr = kv_copy(src_r.at[pl.ds(0, h)], origin_r, 0, h, right, 2 * (s - 1))
                cl = kv_copy(src_l.at[pl.ds(h, h)], origin_l, h, h, left, 2 * (s - 1) + 1)
            yield
            cr.wait()
            cl.wait()
            if s < half_ring:
                got = [(lax.rem(z - s + ring, ring), ring + 2 * s - 1), (lax.rem(z + s, ring), ring + 2 * s)]
            else:
                got = [(lax.rem(z + half_ring, ring), ring + 2 * s - 1)]
            for at, idx in got:
                kv_sib.append(
                    remote(kvbuf.at[r, at * 2 + c], kvbuf.at[r, at * 2 + c], sib, kv_sems, base + idx)
                )
        yield
        for cp in kv_sib:
            cp.wait()
        yield

    qw = wq_ref.shape[1]
    kw = wk_ref.shape[1]

    def project(r, src):
        block = src[...]
        for lo, w_ref in ((0, wq_ref), (qw, wk_ref), (qw + kw, wv_ref)):
            partial[r, :, pl.ds(lo, w_ref.shape[1])] = jnp.dot(
                block, w_ref[...], preferred_element_type=jnp.float32, precision=lax.Precision.HIGH
            )

    hr = rows // 2
    chunks = (y, lax.rem(y + cols - 1, cols), lax.rem(y + 1, cols), lax.rem(y + 2, cols))

    def sub(ref, e):
        return ref.at[pl.ds(e * hr, hr)]

    y1 = {}
    for e in (0, 1):
        y1[("r", e)] = remote(sub(tok_ref, e), sub(tg.at[1], e), y_right, y_sems, 2 * e)
        y1[("l", e)] = remote(sub(tok_ref, e), sub(tg.at[2], e), y_left, y_sems, 2 * e + 1)
    rounds = []

    def begin(slot_id, e, src):
        r = 2 * slot_id + e
        project(r, src)
        g = round_steps(r, 2 * chunks[slot_id] + e)
        next(g)
        rounds.append(g)

    def advance(times):
        for _ in range(times):
            for g in list(rounds):
                next(g, None)

    begin(0, 0, sub(tok_ref, 0))
    begin(0, 1, sub(tok_ref, 1))
    advance(ring // 2)
    y1[("r", 0)].wait()
    y2r = remote(sub(tg.at[1], 0), sub(tg.at[3], 0), y_right, y_sems, 4)
    y1[("l", 0)].wait()
    begin(1, 0, sub(tg.at[1], 0))
    begin(2, 0, sub(tg.at[2], 0))
    advance(3)
    y1[("r", 1)].wait()
    y1[("l", 1)].wait()
    y2l = remote(sub(tg.at[2], 1), sub(tg.at[3], 1), y_left, y_sems, 5)
    begin(1, 1, sub(tg.at[1], 1))
    begin(2, 1, sub(tg.at[2], 1))
    advance(3)
    y2r.wait()
    begin(3, 0, sub(tg.at[3], 0))
    y2l.wait()
    begin(3, 1, sub(tg.at[3], 1))
    live = list(rounds)
    while live:
        live = [g for g in live if next(g, "done") != "done"]
    kv_out[...] = kvbuf[...]


def front(tokens, w_query, w_key, w_value, ring, cols, collective_id):
    rows, width = tokens.shape
    out_w = w_query.shape[1] + w_key.shape[1] + w_value.shape[1]
    kv_w = w_key.shape[1] + w_value.shape[1]
    n_rounds = 2 * cols
    hr = rows // 2
    m = hr // (2 * ring)
    return pl.pallas_call(
        functools.partial(front_kernel, ring, cols),
        out_shape=(
            jax.ShapeDtypeStruct((n_rounds * m, out_w), jnp.float32),
            jax.ShapeDtypeStruct((n_rounds, 2 * ring, m, kv_w), jnp.float32),
        ),
        in_specs=[pl.BlockSpec(memory_space=pltpu.VMEM)] * 4,
        out_specs=(pl.BlockSpec(memory_space=pltpu.VMEM), pl.BlockSpec(memory_space=pltpu.VMEM)),
        scratch_shapes=[
            pltpu.VMEM((cols, rows, width), jnp.float32),
            pltpu.VMEM((n_rounds, hr, out_w), jnp.float32),
            pltpu.VMEM((n_rounds, ring * m, out_w), jnp.float32),
            pltpu.VMEM((n_rounds, 2, ring - 1, m // 2, out_w), jnp.float32),
            pltpu.VMEM((n_rounds, 2, ring - 1, m // 2, out_w), jnp.float32),
            pltpu.VMEM((n_rounds, 2 * ring, m, kv_w), jnp.float32),
            (pltpu.SemaphoreType.DMA((6,)), pltpu.SemaphoreType.DMA((6,))),
            (pltpu.SemaphoreType.DMA((n_rounds * 2 * ring,)), pltpu.SemaphoreType.DMA((n_rounds * 2 * ring,))),
            (pltpu.SemaphoreType.DMA((n_rounds * 2 * ring,)), pltpu.SemaphoreType.DMA((n_rounds * 2 * ring,))),
            (pltpu.SemaphoreType.DMA((n_rounds * 2 * ring,)), pltpu.SemaphoreType.DMA((n_rounds * 2 * ring,))),
        ],
        compiler_params=pltpu.CompilerParams(
            collective_id=collective_id, has_side_effects=True, vmem_limit_bytes=60 * 1024 * 1024
        ),
    )(tokens, w_query, w_key, w_value)


def on_device(ring, cols, tokens, w_query, w_key, w_value, w_out):
    highest = lax.Precision.HIGH
    q_width = w_query.shape[1]
    kv_width = w_key.shape[1]
    joined, kv_sets = front(tokens, w_query, w_key, w_value, ring, cols, 3)
    query_rows = joined[:, :q_width]
    all_kv = kv_sets.reshape(-1, kv_sets.shape[-1])
    state_end = fold_keys(
        query_rows,
        start_state(query_rows, kv_width),
        (all_kv[:, :kv_width], all_kv[:, kv_width:]),
    )
    return gather_mix(finish(state_end), w_out, ring, cols, 5)


def solution(mesh):
    depth, row, col = (mesh.shape[a] for a in ("depth", "row", "col"))
    split = jax.sharding.Mesh(
        np.asarray(mesh.devices).reshape(depth, row // 2, 2, col), ("depth", "rz", "rc", "col")
    )
    rows = ("rz", "rc")
    placed = (
        P(("depth", "col"), rows),
        P(rows, "col"),
        P(rows, "col"),
        P(rows, "col"),
        P("col", rows),
    )
    return jax.shard_map(
        functools.partial(on_device, row // 2, col),
        mesh=split,
        in_specs=placed,
        out_specs=P(("depth", "col"), rows),
        check_vma=False,
    )
```

```python
import functools
import math

import jax
import numpy as np
import jax.numpy as jnp
from jax import lax
from jax.experimental import pallas as pl
from jax.experimental.pallas import tpu as pltpu
from jax.sharding import PartitionSpec as P

QUERY_HEADS = 32
KEY_VALUE_HEADS = 4
HEAD_SIZE_DIM = 128


def start_state(query_rows, kv_width):
    count_of_heads = kv_width // HEAD_SIZE_DIM
    queries_per_group = QUERY_HEADS // KEY_VALUE_HEADS
    count_of_rows = query_rows.shape[0]
    running_max = jnp.full((count_of_heads, queries_per_group, count_of_rows), -1e30, jnp.float32)
    running_sum = jnp.zeros((count_of_heads, queries_per_group, count_of_rows), jnp.float32)
    weighted = jnp.zeros(
        (count_of_heads, queries_per_group, count_of_rows, HEAD_SIZE_DIM), jnp.float32
    )
    return (running_max, running_sum, weighted)


def fold_keys(query_rows, state_now, block_pair):
    highest = lax.Precision.HIGH
    running_max, running_sum, weighted = state_now
    key_block, value_block = block_pair
    count_of_heads = key_block.shape[1] // HEAD_SIZE_DIM
    count_of_rows = query_rows.shape[0]
    query_head_rows = query_rows.reshape(
        count_of_rows, count_of_heads, QUERY_HEADS // KEY_VALUE_HEADS, HEAD_SIZE_DIM
    )
    key_head_rows = key_block.reshape(-1, count_of_heads, HEAD_SIZE_DIM)
    value_head_rows = value_block.reshape(-1, count_of_heads, HEAD_SIZE_DIM)
    scores = jnp.einsum("rkgd,nkd->kgrn", query_head_rows, key_head_rows, precision=highest) * (
        1.0 / math.sqrt(HEAD_SIZE_DIM)
    )
    newest = jnp.maximum(running_max, jnp.max(scores, axis=-1))
    weights = jnp.exp(scores - newest[..., None])
    running_sum = jnp.sum(weights, axis=-1)
    weighted = jnp.einsum("kgrn,nkd->kgrd", weights, value_head_rows, precision=highest)
    return (newest, running_sum, weighted)


def finish(state_now):
    running_max, running_sum, weighted = state_now
    attention_output = weighted / running_sum[..., None]
    count_of_heads, queries_per_group, count_of_rows, head_size = attention_output.shape
    return attention_output.transpose(2, 0, 1, 3).reshape(
        count_of_rows, count_of_heads * queries_per_group * head_size
    )


def gather_kernel(axis, ring, n, with_sib, x_ref, out_ref, local_sem, send_sems, recv_sems):
    mesh_id = pl.DeviceIdType.MESH
    names = ("depth", "rz", "rc", "col")
    me = {a: lax.axis_index(a) for a in names}
    pos = me[axis]

    def device(**moved):
        return tuple(moved.get(a, me[a]) for a in names)

    right = device(**{axis: lax.rem(pos + 1, ring)})
    left = device(**{axis: lax.rem(pos + ring - 1, ring)})
    sib = device(rc=1 - me["rc"])
    peers = (left, right, sib) if with_sib else (left, right)

    barrier = pltpu.get_barrier_semaphore()
    for peer in peers:
        pl.semaphore_signal(barrier, inc=1, device_id=peer, device_id_type=mesh_id)
    pl.semaphore_wait(barrier, len(peers))

    def rows(at, lo=0, size=n):
        slot = at * 2 + me["rc"] if with_sib else at
        return pl.ds(pl.multiple_of(slot * n + lo, 8), size)

    def remote(src, dst_rows, peer, idx):
        cp = pltpu.make_async_remote_copy(
            src_ref=src,
            dst_ref=out_ref.at[dst_rows],
            send_sem=send_sems.at[idx],
            recv_sem=recv_sems.at[idx],
            device_id=peer,
            device_id_type=mesh_id,
        )
        cp.start()
        return cp

    def to_sib(at, idx):
        if with_sib:
            sib_copies.append(remote(out_ref.at[rows(at)], rows(at), sib, idx))

    local = pltpu.make_async_copy(x_ref, out_ref.at[rows(pos)], local_sem)
    local.start()
    sib_copies = [remote(x_ref, rows(pos), sib, ring)] if with_sib else []
    half = ring // 2
    for s in range(1, half + 1):
        origin_r = lax.rem(pos - (s - 1) + ring, ring)
        origin_l = lax.rem(pos + (s - 1), ring)
        src_r = x_ref if s == 1 else out_ref.at[rows(origin_r)]
        src_l = x_ref if s == 1 else out_ref.at[rows(origin_l)]
        if s < half:
            cr = remote(src_r, rows(origin_r), right, 2 * (s - 1))
            cl = remote(src_l, rows(origin_l), left, 2 * (s - 1) + 1)
            cr.wait()
            cl.wait()
            to_sib(lax.rem(pos - s + ring, ring), ring + 2 * s - 1)
            to_sib(lax.rem(pos + s, ring), ring + 2 * s)
        else:
            h = n // 2
            cr = remote(src_r.at[pl.ds(0, h)], rows(origin_r, 0, h), right, 2 * (s - 1))
            cl = remote(src_l.at[pl.ds(h, h)], rows(origin_l, h, h), left, 2 * (s - 1) + 1)
            cr.wait()
            cl.wait()
            to_sib(lax.rem(pos + half, ring), ring + 2 * s - 1)
    local.wait()
    for cp in sib_copies:
        cp.wait()


def ring_gather(block, axis, ring, with_sib, collective_id):
    n, w = block.shape
    copies = 2 if with_sib else 1
    return pl.pallas_call(
        functools.partial(gather_kernel, axis, ring, n, with_sib),
        out_shape=jax.ShapeDtypeStruct((copies * ring * n, w), block.dtype),
        in_specs=[pl.BlockSpec(memory_space=pl.ANY)],
        out_specs=pl.BlockSpec(memory_space=pl.ANY),
        scratch_shapes=[
            pltpu.SemaphoreType.DMA(()),
            pltpu.SemaphoreType.DMA((2 * ring,)),
            pltpu.SemaphoreType.DMA((2 * ring,)),
        ],
        compiler_params=pltpu.CompilerParams(collective_id=collective_id, has_side_effects=True),
    )(block)


def scatter_kernel(axis, ring, m, with_sib, parts, x_ref, out_ref, sbuf, rbuf, sibbuf, send_sems, recv_sems, sib_sems):
    mesh_id = pl.DeviceIdType.MESH
    names = ("depth", "rz", "rc", "col")
    me = {a: lax.axis_index(a) for a in names}
    pos = me[axis]
    h = m // 2
    q = h // parts

    def device(**moved):
        return tuple(moved.get(a, me[a]) for a in names)

    right = device(**{axis: lax.rem(pos + 1, ring)})
    left = device(**{axis: lax.rem(pos + ring - 1, ring)})
    sib = device(rc=1 - me["rc"])
    peers = (left, right, sib) if with_sib else (left, right)

    barrier = pltpu.get_barrier_semaphore()
    for peer in peers:
        pl.semaphore_signal(barrier, inc=1, device_id=peer, device_id_type=mesh_id)
    pl.semaphore_wait(barrier, len(peers))

    def rows_of(at, half, part, owner):
        slot = at * 2 + owner if with_sib else at
        return pl.ds(pl.multiple_of(slot * m + half * h + part * q, 8), q)

    def sib_rows(at, half, part):
        return pl.ds(pl.multiple_of(at * m + half * h + part * q, 8), q)

    def remote(src, dst, peer, sems, idx):
        cp = pltpu.make_async_remote_copy(
            src_ref=src,
            dst_ref=dst,
            send_sem=sems[0].at[idx],
            recv_sem=sems[1].at[idx],
            device_id=peer,
            device_id_type=mesh_id,
        )
        cp.start()
        return cp

    def need(s, half):
        sign = -1 if half == 0 else 1
        return lax.rem(pos + sign * (s % ring) + ring * ring, ring)

    sib_copies = {}
    if with_sib:
        order = [(s, half) for s in range(1, ring + 1) for half in (0, 1)]
        for idx, (s, half) in enumerate(order):
            at = need(s, half)
            sib_copies[(s, half)] = remote(
                x_ref.at[pl.ds(pl.multiple_of((at * 2 + 1 - me["rc"]) * m + half * h, 8), h)],
                sibbuf.at[pl.ds(pl.multiple_of(at * m + half * h, 8), h)],
                sib,
                (sib_sems[0], sib_sems[1]),
                idx,
            )

    def contribution(s, half, part):
        at = need(s, half)
        own = x_ref[rows_of(at, half, part, me["rc"])]
        if with_sib:
            if part == 0:
                sib_copies[(s, half)].wait()
            own = own + sibbuf[sib_rows(at, half, part)]
        return own

    ring_copies = {}
    for s in range(1, ring):
        for part in range(parts):
            for half in (0, 1):
                value = contribution(s, half, part)
                if s > 1:
                    ring_copies[(s - 1, half, part)].wait()
                    value = value + rbuf[half, s - 2, part]
                sbuf[half, s - 1, part] = value
                ring_copies[(s, half, part)] = remote(
                    sbuf.at[half, s - 1, part],
                    rbuf.at[half, s - 1, part],
                    right if half == 0 else left,
                    (send_sems, recv_sems),
                    (half * (ring - 1) + s - 1) * parts + part,
                )
    for part in range(parts):
        for half in (0, 1):
            value = contribution(ring, half, part)
            ring_copies[(ring - 1, half, part)].wait()
            out_ref[pl.ds(half * h + part * q, q)] = value + rbuf[half, ring - 2, part]


def ring_scatter(x, axis, ring, with_sib, parts, collective_id):
    total, w = x.shape
    copies = 2 if with_sib else 1
    m = total // (copies * ring)
    sib_rows = ring * m if with_sib else 8
    return pl.pallas_call(
        functools.partial(scatter_kernel, axis, ring, m, with_sib, parts),
        out_shape=jax.ShapeDtypeStruct((m, w), x.dtype),
        in_specs=[pl.BlockSpec(memory_space=pltpu.VMEM)],
        out_specs=pl.BlockSpec(memory_space=pltpu.VMEM),
        scratch_shapes=[
            pltpu.VMEM((2, ring - 1, parts, m // 2 // parts, w), x.dtype),
            pltpu.VMEM((2, ring - 1, parts, m // 2 // parts, w), x.dtype),
            pltpu.VMEM((sib_rows, w), x.dtype),
            pltpu.SemaphoreType.DMA((2 * ring * parts,)),
            pltpu.SemaphoreType.DMA((2 * ring * parts,)),
            (pltpu.SemaphoreType.DMA((2 * ring,)), pltpu.SemaphoreType.DMA((2 * ring,))),
        ],
        compiler_params=pltpu.CompilerParams(
            collective_id=collective_id, has_side_effects=True, vmem_limit_bytes=60 * 1024 * 1024
        ),
    )(x)


def mix_kernel(ring, cols, n, o_ref, wo_ref, out_ref, ogath, part, recv, send_sems, recv_sems, y_send, y_recv):
    mesh_id = pl.DeviceIdType.MESH
    names = ("depth", "rz", "rc", "col")
    me = {a: lax.axis_index(a) for a in names}
    z, c, y = me["rz"], me["rc"], me["col"]
    per_col = 2 * ring // cols

    def device(**moved):
        return tuple(moved.get(a, me[a]) for a in names)

    right = device(rz=lax.rem(z + 1, ring))
    left = device(rz=lax.rem(z + ring - 1, ring))
    sib = device(rc=1 - c)
    peers = [left, right, sib] + [device(col=lax.rem(y + d, cols)) for d in range(1, cols)]

    barrier = pltpu.get_barrier_semaphore()
    for peer in peers:
        pl.semaphore_signal(barrier, inc=1, device_id=peer, device_id_type=mesh_id)
    pl.semaphore_wait(barrier, len(peers))

    def remote(src, dst, peer, send, recv_sem):
        cp = pltpu.make_async_remote_copy(
            src_ref=src, dst_ref=dst, send_sem=send, recv_sem=recv_sem, device_id=peer, device_id_type=mesh_id
        )
        cp.start()
        return cp

    piece = n // cols

    def project(block, k):
        part[k] = jnp.dot(block, wo_ref[...], preferred_element_type=jnp.float32, precision=lax.Precision.HIGH)
        for d in range(1, cols):
            dest = lax.rem(y + d, cols)
            remote(
                part.at[k, pl.ds(pl.multiple_of(dest * piece, 8), piece)],
                recv.at[cols - d, k],
                device(col=dest),
                y_send.at[k * cols + d],
                y_recv.at[(cols - d) * 2 * ring + k],
            )

    def slot(zz, cc):
        return zz * 2 + cc

    def z_copy(src, dst_slot, lo, size, peer, idx):
        return remote(src, ogath.at[dst_slot, pl.ds(lo, size)], peer, send_sems.at[idx], recv_sems.at[idx])

    pending_sib = [(z_copy(o_ref, slot(z, c), 0, n, sib, ring), z)]
    to_project = [slot(z, c)]
    half = ring // 2
    for s in range(1, half + 1):
        origin_r = lax.rem(z - (s - 1) + ring, ring)
        origin_l = lax.rem(z + (s - 1), ring)
        src_r = o_ref if s == 1 else ogath.at[slot(origin_r, c)]
        src_l = o_ref if s == 1 else ogath.at[slot(origin_l, c)]
        if s < half:
            cr = z_copy(src_r, slot(origin_r, c), 0, n, right, 2 * (s - 1))
            cl = z_copy(src_l, slot(origin_l, c), 0, n, left, 2 * (s - 1) + 1)
        else:
            h = n // 2
            cr = z_copy(src_r.at[pl.ds(0, h)], slot(origin_r, c), 0, h, right, 2 * (s - 1))
            cl = z_copy(src_l.at[pl.ds(h, h)], slot(origin_l, c), h, h, left, 2 * (s - 1) + 1)
        for k in to_project:
            project(o_ref[...] if s == 1 else ogath[k], k)
        to_project = []
        for cp, at in pending_sib:
            cp.wait()
            project(ogath[slot(at, 1 - c)], slot(at, 1 - c))
        pending_sib = []
        cr.wait()
        cl.wait()
        if s < half:
            arrived = [(lax.rem(z - s + ring, ring), ring + 2 * s - 1), (lax.rem(z + s, ring), ring + 2 * s)]
        else:
            arrived = [(lax.rem(z + half, ring), ring + 2 * s - 1)]
        for at, idx in arrived:
            pending_sib.append((z_copy(ogath.at[slot(at, c)], slot(at, c), 0, n, sib, idx), at))
            to_project.append(slot(at, c))
    for k in to_project:
        project(ogath[k], k)
    for cp, at in pending_sib:
        cp.wait()
        project(ogath[slot(at, 1 - c)], slot(at, 1 - c))
    for k in range(2 * ring):
        total = part[k, pl.ds(pl.multiple_of(y * piece, 8), piece)]
        for d in range(1, cols):
            pltpu.make_async_remote_copy(
                src_ref=part.at[k, pl.ds(0, piece)],
                dst_ref=recv.at[d, k],
                send_sem=y_send.at[0],
                recv_sem=y_recv.at[d * 2 * ring + k],
                device_id=device(col=lax.rem(y + d, cols)),
                device_id_type=mesh_id,
            ).wait_recv()
            total = total + recv[d, k]
        m = piece // 2
        for e in (0, 1):
            out_ref[pl.ds(e * 2 * ring * m + k * m, m)] = total[e * m : (e + 1) * m]
    for k in range(2 * ring):
        for d in range(1, cols):
            pltpu.make_async_remote_copy(
                src_ref=part.at[k, pl.ds(0, piece)],
                dst_ref=recv.at[0, 0],
                send_sem=y_send.at[k * cols + d],
                recv_sem=y_recv.at[0],
                device_id=device(col=lax.rem(y + d, cols)),
                device_id_type=mesh_id,
            ).wait_send()


def gather_mix(o, w_out, ring, cols, collective_id):
    n, width = o.shape
    out_w = w_out.shape[1]
    per_col = 2 * ring // cols
    return pl.pallas_call(
        functools.partial(mix_kernel, ring, cols, n),
        out_shape=jax.ShapeDtypeStruct((per_col * n, out_w), jnp.float32),
        in_specs=[pl.BlockSpec(memory_space=pltpu.VMEM), pl.BlockSpec(memory_space=pltpu.VMEM)],
        out_specs=pl.BlockSpec(memory_space=pltpu.VMEM),
        scratch_shapes=[
            pltpu.VMEM((2 * ring, n, width), jnp.float32),
            pltpu.VMEM((2 * ring, n, out_w), jnp.float32),
            pltpu.VMEM((cols, 2 * ring, n // cols, out_w), jnp.float32),
            pltpu.SemaphoreType.DMA((2 * ring,)),
            pltpu.SemaphoreType.DMA((2 * ring,)),
            pltpu.SemaphoreType.DMA((2 * ring * cols,)),
            pltpu.SemaphoreType.DMA((2 * ring * cols,)),
        ],
        compiler_params=pltpu.CompilerParams(
            collective_id=collective_id, has_side_effects=True, vmem_limit_bytes=60 * 1024 * 1024
        ),
    )(o, w_out)


def front_kernel(
    ring, cols, tok_ref, wq_ref, wk_ref, wv_ref, out_ref, kv_out, tg, partial, sibbuf, sbuf, rbuf, kvbuf,
    y_sems, z_sems, sib_sems, kv_sems,
):
    mesh_id = pl.DeviceIdType.MESH
    names = ("depth", "rz", "rc", "col")
    me = {a: lax.axis_index(a) for a in names}
    z, c, y = me["rz"], me["rc"], me["col"]
    rows = tok_ref.shape[0]
    m = rows // 2 // (2 * ring)
    h = m // 2

    def device(**moved):
        return tuple(moved.get(a, me[a]) for a in names)

    right = device(rz=lax.rem(z + 1, ring))
    left = device(rz=lax.rem(z + ring - 1, ring))
    sib = device(rc=1 - c)
    y_right = device(col=lax.rem(y + 1, cols))
    y_left = device(col=lax.rem(y + cols - 1, cols))
    peers = [left, right, sib, y_left, y_right]

    barrier = pltpu.get_barrier_semaphore()
    for peer in peers:
        pl.semaphore_signal(barrier, inc=1, device_id=peer, device_id_type=mesh_id)
    pl.semaphore_wait(barrier, len(peers))

    def remote(src, dst, peer, sems, idx):
        cp = pltpu.make_async_remote_copy(
            src_ref=src, dst_ref=dst, send_sem=sems[0].at[idx], recv_sem=sems[1].at[idx],
            device_id=peer, device_id_type=mesh_id,
        )
        cp.start()
        return cp

    def need(s, half):
        sign = -1 if half == 0 else 1
        return lax.rem(z + sign * (s % ring) + ring * ring, ring)

    def round_steps(r, chunk):
        x = partial.at[r]
        base = r * 2 * ring
        sib_copies = {}
        for idx, (s, half) in enumerate((s, half) for s in range(1, ring + 1) for half in (0, 1)):
            at = need(s, half)
            sib_copies[(s, half)] = remote(
                x.at[pl.ds(pl.multiple_of((at * 2 + 1 - c) * m + half * h, 8), h)],
                sibbuf.at[r, pl.ds(pl.multiple_of(at * m + half * h, 8), h)],
                sib, sib_sems, base + idx,
            )
        yield

        def contribution(s, half):
            at = need(s, half)
            sib_copies[(s, half)].wait()
            own = x[pl.ds(pl.multiple_of((at * 2 + c) * m + half * h, 8), h)]
            return own + sibbuf[r, pl.ds(pl.multiple_of(at * m + half * h, 8), h)]

        ring_copies = {}
        for s in range(1, ring):
            for half in (0, 1):
                value = contribution(s, half)
                if s > 1:
                    ring_copies[(s - 1, half)].wait()
                    value = value + rbuf[r, half, s - 2]
                sbuf[r, half, s - 1] = value
                ring_copies[(s, half)] = remote(
                    sbuf.at[r, half, s - 1], rbuf.at[r, half, s - 1],
                    right if half == 0 else left, z_sems, base + half * (ring - 1) + s - 1,
                )
            yield
        for half in (0, 1):
            value = contribution(ring, half)
            ring_copies[(ring - 1, half)].wait()
            value = value + rbuf[r, half, ring - 2]
            out_ref[pl.ds(pl.multiple_of(chunk * m + half * h, 8), h)] = value
            kvbuf[r, z * 2 + c, pl.ds(half * h, h)] = value[:, qw:]
        yield

        def kv_copy(src, at, lo, size, peer, idx):
            return remote(src, kvbuf.at[r, at * 2 + c, pl.ds(lo, size)], peer, kv_sems, base + idx)

        kv_sib = [
            remote(kvbuf.at[r, z * 2 + c], kvbuf.at[r, z * 2 + c], sib, kv_sems, base + ring)
        ]
        half_ring = ring // 2
        for s in range(1, half_ring + 1):
            origin_r = lax.rem(z - (s - 1) + ring, ring)
            origin_l = lax.rem(z + (s - 1), ring)
            src_r = kvbuf.at[r, origin_r * 2 + c]
            src_l = kvbuf.at[r, origin_l * 2 + c]
            if s < half_ring:
                cr = kv_copy(src_r, origin_r, 0, m, right, 2 * (s - 1))
                cl = kv_copy(src_l, origin_l, 0, m, left, 2 * (s - 1) + 1)
            else:
                cr = kv_copy(src_r.at[pl.ds(0, h)], origin_r, 0, h, right, 2 * (s - 1))
                cl = kv_copy(src_l.at[pl.ds(h, h)], origin_l, h, h, left, 2 * (s - 1) + 1)
            yield
            cr.wait()
            cl.wait()
            if s < half_ring:
                got = [(lax.rem(z - s + ring, ring), ring + 2 * s - 1), (lax.rem(z + s, ring), ring + 2 * s)]
            else:
                got = [(lax.rem(z + half_ring, ring), ring + 2 * s - 1)]
            for at, idx in got:
                kv_sib.append(
                    remote(kvbuf.at[r, at * 2 + c], kvbuf.at[r, at * 2 + c], sib, kv_sems, base + idx)
                )
        yield
        for cp in kv_sib:
            cp.wait()
        yield

    qw = wq_ref.shape[1]
    kw = wk_ref.shape[1]

    def project(r, src):
        block = src[...]
        for lo, w_ref in ((0, wq_ref), (qw, wk_ref), (qw + kw, wv_ref)):
            partial[r, :, pl.ds(lo, w_ref.shape[1])] = jnp.dot(
                block, w_ref[...], preferred_element_type=jnp.float32, precision=lax.Precision.HIGH
            )

    hr = rows // 2
    chunks = (y, lax.rem(y + cols - 1, cols), lax.rem(y + 1, cols), lax.rem(y + 2, cols))

    def sub(ref, e):
        return ref.at[pl.ds(e * hr, hr)]

    y1 = {}
    for e in (0, 1):
        y1[("r", e)] = remote(sub(tok_ref, e), sub(tg.at[1], e), y_right, y_sems, 2 * e)
        y1[("l", e)] = remote(sub(tok_ref, e), sub(tg.at[2], e), y_left, y_sems, 2 * e + 1)
    rounds = []

    def begin(slot_id, e, src):
        r = 2 * slot_id + e
        project(r, src)
        g = round_steps(r, 2 * chunks[slot_id] + e)
        next(g)
        rounds.append(g)

    def advance(times):
        for _ in range(times):
            for g in list(rounds):
                next(g, None)

    begin(0, 0, sub(tok_ref, 0))
    begin(0, 1, sub(tok_ref, 1))
    advance(ring // 2)
    y1[("r", 0)].wait()
    y2r = remote(sub(tg.at[1], 0), sub(tg.at[3], 0), y_right, y_sems, 4)
    y1[("l", 0)].wait()
    begin(1, 0, sub(tg.at[1], 0))
    begin(2, 0, sub(tg.at[2], 0))
    advance(4)
    y1[("r", 1)].wait()
    y1[("l", 1)].wait()
    y2l = remote(sub(tg.at[2], 1), sub(tg.at[3], 1), y_left, y_sems, 5)
    begin(1, 1, sub(tg.at[1], 1))
    begin(2, 1, sub(tg.at[2], 1))
    advance(2)
    y2r.wait()
    begin(3, 0, sub(tg.at[3], 0))
    y2l.wait()
    begin(3, 1, sub(tg.at[3], 1))
    live = list(rounds)
    while live:
        live = [g for g in live if next(g, "done") != "done"]
    kv_out[...] = kvbuf[...]


def front(tokens, w_query, w_key, w_value, ring, cols, collective_id):
    rows, width = tokens.shape
    out_w = w_query.shape[1] + w_key.shape[1] + w_value.shape[1]
    kv_w = w_key.shape[1] + w_value.shape[1]
    n_rounds = 2 * cols
    hr = rows // 2
    m = hr // (2 * ring)
    return pl.pallas_call(
        functools.partial(front_kernel, ring, cols),
        out_shape=(
            jax.ShapeDtypeStruct((n_rounds * m, out_w), jnp.float32),
            jax.ShapeDtypeStruct((n_rounds, 2 * ring, m, kv_w), jnp.float32),
        ),
        in_specs=[pl.BlockSpec(memory_space=pltpu.VMEM)] * 4,
        out_specs=(pl.BlockSpec(memory_space=pltpu.VMEM), pl.BlockSpec(memory_space=pltpu.VMEM)),
        scratch_shapes=[
            pltpu.VMEM((cols, rows, width), jnp.float32),
            pltpu.VMEM((n_rounds, hr, out_w), jnp.float32),
            pltpu.VMEM((n_rounds, ring * m, out_w), jnp.float32),
            pltpu.VMEM((n_rounds, 2, ring - 1, m // 2, out_w), jnp.float32),
            pltpu.VMEM((n_rounds, 2, ring - 1, m // 2, out_w), jnp.float32),
            pltpu.VMEM((n_rounds, 2 * ring, m, kv_w), jnp.float32),
            (pltpu.SemaphoreType.DMA((6,)), pltpu.SemaphoreType.DMA((6,))),
            (pltpu.SemaphoreType.DMA((n_rounds * 2 * ring,)), pltpu.SemaphoreType.DMA((n_rounds * 2 * ring,))),
            (pltpu.SemaphoreType.DMA((n_rounds * 2 * ring,)), pltpu.SemaphoreType.DMA((n_rounds * 2 * ring,))),
            (pltpu.SemaphoreType.DMA((n_rounds * 2 * ring,)), pltpu.SemaphoreType.DMA((n_rounds * 2 * ring,))),
        ],
        compiler_params=pltpu.CompilerParams(
            collective_id=collective_id, has_side_effects=True, vmem_limit_bytes=60 * 1024 * 1024
        ),
    )(tokens, w_query, w_key, w_value)


def on_device(ring, cols, tokens, w_query, w_key, w_value, w_out):
    highest = lax.Precision.HIGH
    q_width = w_query.shape[1]
    kv_width = w_key.shape[1]
    joined, kv_sets = front(tokens, w_query, w_key, w_value, ring, cols, 3)
    query_rows = joined[:, :q_width]
    all_kv = kv_sets.reshape(-1, kv_sets.shape[-1])
    state_end = fold_keys(
        query_rows,
        start_state(query_rows, kv_width),
        (all_kv[:, :kv_width], all_kv[:, kv_width:]),
    )
    return gather_mix(finish(state_end), w_out, ring, cols, 5)


def solution(mesh):
    depth, row, col = (mesh.shape[a] for a in ("depth", "row", "col"))
    split = jax.sharding.Mesh(
        np.asarray(mesh.devices).reshape(depth, row // 2, 2, col), ("depth", "rz", "rc", "col")
    )
    rows = ("rz", "rc")
    placed = (
        P(("depth", "col"), rows),
        P(rows, "col"),
        P(rows, "col"),
        P(rows, "col"),
        P("col", rows),
    )
    return jax.shard_map(
        functools.partial(on_device, row // 2, col),
        mesh=split,
        in_specs=placed,
        out_specs=P(("depth", "col"), rows),
        check_vma=False,
    )
```
